128 devices in a mesh: row: 16 (over y_lo, z, core), col: 8 (over x, y_hi).
Axes of the slice: x: 4, y: 4 (y_hi: 2, y_lo: 2; y = y_hi * 2 + y_lo), z: 4, core: 2. Of those that a mesh axis runs over, the one named last changes fastest.
Arguments:
- tokens: bfloat16 [2, 256, 256, 1024], P(None, 'row', 'col'), may hold values from -36 to 36
- norm_gain: float32 [1024], replicated, may hold values from 0.1 to 1.9
- w_query: bfloat16 [1024, 512], replicated, as said below
- w_kv: bfloat16 [1024, 1024], replicated, as said below
- w_out: bfloat16 [512, 1024], replicated, may hold values from -0.25 to 0.25
- w_pool: bfloat16 [4, 1024, 512], replicated, may hold values from -0.1875 to 0.1875
- w_join: bfloat16 [3, 3, 3072, 256], replicated, may hold values from -0.0390625 to 0.0390625
Outputs:
- joined: bfloat16 [2, 256, 256, 256], P(None, 'row', 'col')
The draws below stay inside these ranges and needn't reach their ends.
Inputs may be any that keep to these rules, and one draw needn't show every extreme that they name: `w_query`: entries within 6 / sqrt(1024) + 10 / 1024 of zero. `w_kv`: entries within 6 / sqrt(1024) + 10 / 1024 of zero.
All inputs are finite; a program needn't handle non-finite values.
Results may differ from the reference program's by a relative error of at most 0.003.
The reference program's roundings to bfloat16 on the way count: a program that leaves them out, or rounds other values in their place, can miss the bound.
Values may be sent and summed in bfloat16 or wider, within the bound.
No kernel may reach another device: no remote copies, remote signals or barrier semaphores. Data moves between devices by JAX's collectives and lax.ppermute only.
A program may use at most 192 MiB of HBM per device.

```python
import math
import jax
import jax.numpy as jnp
from jax import lax

D = 1024
HEAD_DIM = 32
INNER = 512
BLOCK = 8
HALO = 2
PPM_CH = 512
CAT = 3072
JOIN_OUT = 256
SHEETS = 2
ROWS_DEV = 16
COLS_DEV = 32
GRID_H = 256
GRID_W = 256


def channel_normal(key):
    return jax.random.normal(jax.random.fold_in(key, 101), (D,), jnp.float32)


def draw_tokens(key, part):
    key_noise = jax.random.fold_in(key, 11)
    key_amplitude = jax.random.fold_in(key, 12)
    key_tile = jax.random.fold_in(key, 13)
    key_rowline = jax.random.fold_in(key, 14)
    key_colline = jax.random.fold_in(key, 15)
    key_rowstrength = jax.random.fold_in(key, 16)
    key_colstrength = jax.random.fold_in(key, 17)
    full_shape = (SHEETS, GRID_H, GRID_W, D)
    tiles_h = GRID_H // ROWS_DEV
    tiles_w = GRID_W // COLS_DEV
    channel_pattern = jnp.clip(channel_normal(key), -3.0, 3.0)
    token_noise = jnp.clip(jax.random.normal(key_noise, full_shape, jnp.float32), -4.0, 4.0)
    amplitude = jax.random.uniform(key_amplitude, (SHEETS, tiles_h, tiles_w), jnp.float32, 0.5, 1.5)
    tile_pattern = jnp.clip(jax.random.normal(key_tile, (SHEETS, tiles_h, tiles_w, D), jnp.float32), -2.5, 2.5)
    row_lines = jnp.clip(jax.random.normal(key_rowline, (SHEETS, GRID_H, D), jnp.float32), -2.0, 2.0)
    col_lines = jnp.clip(jax.random.normal(key_colline, (SHEETS, GRID_W, D), jnp.float32), -2.0, 2.0)
    row_strength = jax.random.uniform(key_rowstrength, (SHEETS, GRID_H, 1), jnp.float32, 2.0, 3.0)
    col_strength = jax.random.uniform(key_colstrength, (SHEETS, GRID_W, 1), jnp.float32, 2.0, 3.0)
    row_ramp = 1.0 + 2.0 * jnp.arange(tiles_h, dtype=jnp.float32) / max(tiles_h - 1, 1)
    amplitude = amplitude * row_ramp[None, :, None]
    amplitude = jnp.repeat(jnp.repeat(amplitude, ROWS_DEV, axis=1), COLS_DEV, axis=2)
    tile_part = jnp.repeat(jnp.repeat(tile_pattern, ROWS_DEV, axis=1), COLS_DEV, axis=2)
    line_part = (row_lines * row_strength)[:, :, None, :] + (col_lines * col_strength)[:, None, :, :]
    total = token_noise + amplitude[..., None] * channel_pattern + tile_part + line_part
    return total.astype(jnp.bfloat16)


def draw_w_query(key, part):
    random_part = jnp.clip(jax.random.normal(jax.random.fold_in(key, 202), (D, INNER), jnp.float32), -6.0, 6.0) * D ** (-0.5)
    return random_part.astype(jnp.bfloat16)


def draw_w_kv(key, part):
    random_part = jnp.clip(jax.random.normal(jax.random.fold_in(key, 303), (D, 2 * INNER), jnp.float32), -6.0, 6.0) * D ** (-0.5)
    return random_part.astype(jnp.bfloat16)


def normal_values(stream_key, shape, width, limit, kind=jnp.bfloat16):
    drawn = jax.random.normal(stream_key, shape, jnp.float32) * width
    return jnp.minimum(jnp.maximum(drawn, -limit), limit).astype(kind)


def setup_inputs(seed: int = 0) -> dict:
    arg_keys = jax.random.split(jax.random.key(seed), 8)
    tokens = draw_tokens(jax.random.fold_in(arg_keys[7], 71), 0)
    norm_gain = jnp.clip(1.0 + 0.18 * jax.random.normal(arg_keys[1], (D,), jnp.float32), 0.1, 1.9)
    w_query = draw_w_query(jax.random.fold_in(arg_keys[7], 71), 0)
    w_kv = draw_w_kv(jax.random.fold_in(arg_keys[7], 71), 0)
    w_out = normal_values(arg_keys[4], (INNER, D), INNER ** -0.5, 0.25)
    w_pool = normal_values(arg_keys[5], (4, D, PPM_CH), D ** -0.5, 0.1875)
    w_join = normal_values(arg_keys[6], (3, 3, CAT, JOIN_OUT), (9 * CAT) ** -0.5, 0.0390625)
    return dict(tokens=tokens, norm_gain=norm_gain, w_query=w_query, w_kv=w_kv, w_out=w_out, w_pool=w_pool, w_join=w_join)


EPS = 1e-05
pool_levels = (1, 2, 3, 6)

def unfold(extended, axis, count):
    pad_spec = [(0, 0)] * extended.ndim
    pad_spec[axis] = (0, BLOCK - 2 * HALO)
    extended = jnp.pad(extended, pad_spec)
    nblocks = count // BLOCK
    head_part = lax.slice_in_dim(extended, 0, count, axis=axis)
    tail_part = lax.slice_in_dim(extended, BLOCK, count + BLOCK, axis=axis)
    new_shape = extended.shape[:axis] + (nblocks, BLOCK) + extended.shape[axis + 1:]
    head_part = head_part.reshape(new_shape)
    tail_part = lax.slice_in_dim(tail_part.reshape(new_shape), 0, 2 * HALO, axis=axis + 1)
    return jnp.concatenate([head_part, tail_part], axis=axis + 1)

def attend(query_blocks, windows, row_ok, col_ok):
    sheets, nbr, _, nbc, _, inner = query_blocks.shape
    heads = inner // HEAD_DIM
    span = BLOCK + 2 * HALO
    queries = query_blocks.transpose(0, 1, 3, 2, 4, 5).reshape(sheets, nbr, nbc, BLOCK * BLOCK, heads, HEAD_DIM)
    window_kv = windows.transpose(0, 1, 3, 2, 4, 5).reshape(sheets, nbr, nbc, span * span, 2, heads, HEAD_DIM)
    keys = window_kv[:, :, :, :, 0]
    values = window_kv[:, :, :, :, 1]
    scores = jnp.einsum('sabqhe,sabkhe->sabhqk', queries.astype(jnp.float32), keys.astype(jnp.float32)) / math.sqrt(HEAD_DIM)
    allowed = row_ok[:, :, None, None] & col_ok[None, None, :, :]
    allowed = allowed.transpose(0, 2, 1, 3).reshape(nbr, nbc, 1, 1, span * span)
    scores = jnp.where(allowed[None], scores, -1e+30)
    top = lax.optimization_barrier(jnp.max(scores, axis=-1, keepdims=True))
    expon = jnp.exp(scores - top)
    weights = (expon / lax.optimization_barrier(jnp.sum(expon, axis=-1, keepdims=True))).astype(jnp.bfloat16)
    context = jnp.einsum('sabhqk,sabkhe->sabqhe', weights.astype(jnp.float32), values.astype(jnp.float32))
    context = context.astype(jnp.bfloat16).reshape(sheets, nbr, nbc, BLOCK, BLOCK, inner)
    return context.transpose(0, 1, 3, 2, 4, 5).reshape(sheets, nbr * BLOCK, nbc * BLOCK, inner)

def pool_matrix(level, length, first, count):
    places = first + jnp.arange(count)
    cells = jnp.arange(level)
    starts = cells * length // level
    ends = ((cells + 1) * length + level - 1) // level
    member = (places[None, :] >= starts[:, None]) & (places[None, :] < ends[:, None])
    return (member, ends - starts)

def upsample_matrix(level, length, first, count):
    places = first + jnp.arange(count)
    numer = jnp.maximum((2 * places + 1) * level - length, 0)
    lower = numer // (2 * length)
    frac = (numer - lower * 2 * length).astype(jnp.float32) / (2.0 * length)
    upper = jnp.minimum(lower + 1, level - 1)
    cells = jnp.arange(level)[None, :]
    weight = (cells == lower[:, None]) * (1.0 - frac)[:, None] + (cells == upper[:, None]) * frac[:, None]
    inside = ((places >= 0) & (places < length)).astype(jnp.float32)
    return weight * inside[:, None]

def reference(tokens, norm_gain, w_query, w_kv, w_out, w_pool, w_join):
    tokens_f = tokens.astype(jnp.float32)
    center = lax.optimization_barrier(jnp.mean(tokens_f, axis=-1, keepdims=True))
    spread = lax.optimization_barrier(jnp.mean((tokens_f - center) ** 2, axis=-1, keepdims=True))
    normed = ((tokens_f - center) * lax.rsqrt(spread + EPS) * norm_gain.astype(jnp.float32)).astype(jnp.bfloat16)
    queries = jnp.dot(normed, w_query, preferred_element_type=jnp.float32).astype(jnp.bfloat16)
    keyvals = jnp.dot(normed, w_kv, preferred_element_type=jnp.float32).astype(jnp.bfloat16)
    kv_padded = jnp.pad(keyvals, ((0, 0), (HALO, HALO), (HALO, HALO), (0, 0)))
    col_places = jnp.arange(GRID_W + 2 * HALO) - HALO
    col_ok = unfold((col_places >= 0) & (col_places < GRID_W), 0, GRID_W)

    def band_attend(band):
        query_band = lax.dynamic_slice_in_dim(queries, band * BLOCK, BLOCK, 1)
        query_blocks = query_band.reshape(SHEETS, 1, BLOCK, GRID_W // BLOCK, BLOCK, INNER)
        kv_band = lax.dynamic_slice_in_dim(kv_padded, band * BLOCK, BLOCK + 2 * HALO, 1)
        kv_band = kv_band.reshape(SHEETS, 1, BLOCK + 2 * HALO, GRID_W + 2 * HALO, 2 * INNER)
        windows = unfold(kv_band, 3, GRID_W)
        row_places = band * BLOCK - HALO + jnp.arange(BLOCK + 2 * HALO)
        row_ok = ((row_places >= 0) & (row_places < GRID_H))[None, :]
        return attend(query_blocks, windows, row_ok, col_ok)[:, 0:BLOCK]
    context = lax.map(band_attend, jnp.arange(GRID_H // BLOCK))
    context = context.transpose(1, 0, 2, 3, 4).reshape(SHEETS, GRID_H, GRID_W, INNER)
    attended = (tokens_f + jnp.dot(context, w_out, preferred_element_type=jnp.float32)).astype(jnp.bfloat16)
    branches = []
    for index, level in enumerate(pool_levels):
        rows_in, rows_count = pool_matrix(level, GRID_H, 0, GRID_H)
        cols_in, cols_count = pool_matrix(level, GRID_W, 0, GRID_W)
        row_sums = jnp.einsum('ir,srcd->sicd', rows_in.astype(attended.dtype), attended, preferred_element_type=jnp.float32)
        sums = jnp.einsum('jc,sicd->sijd', cols_in.astype(jnp.float32), row_sums, precision=lax.Precision.HIGHEST)
        counts = (rows_count[:, None] * cols_count[None, :]).astype(jnp.float32)
        pooled = sums / counts[None, :, :, None]
        branch = jnp.einsum('sijd,dp->sijp', pooled, w_pool[index].astype(jnp.float32), precision=lax.Precision.HIGHEST)
        branches.append(jnp.maximum(branch, 0.0))
    att_padded = jnp.pad(attended, ((0, 0), (1, 1), (1, 1), (0, 0)))
    col_maps = [upsample_matrix(level, GRID_W, -1, GRID_W + 2) for level in pool_levels]

    def join_band(band):
        first = band * ROWS_DEV
        pieces = [lax.dynamic_slice_in_dim(att_padded, first, ROWS_DEV + 2, 1)]
        for index, level in enumerate(pool_levels):
            row_map = upsample_matrix(level, GRID_H, first - 1, ROWS_DEV + 2)
            grown = jnp.einsum('ri,sijc,wj->srwc', row_map, branches[index], col_maps[index], precision=lax.Precision.HIGHEST)
            pieces.append(grown.astype(jnp.bfloat16))
        stacked = jnp.concatenate(pieces, axis=-1)
        total = jnp.zeros((SHEETS, ROWS_DEV, GRID_W, JOIN_OUT), jnp.float32)
        for shift_row in range(3):
            for shift_col in range(3):
                total = total + jnp.dot(stacked[:, shift_row:shift_row + ROWS_DEV, shift_col:shift_col + GRID_W], w_join[shift_row, shift_col], preferred_element_type=jnp.float32)
        return total.astype(jnp.bfloat16)
    joined = lax.map(join_band, jnp.arange(GRID_H // ROWS_DEV))
    return joined.transpose(1, 0, 2, 3, 4).reshape(SHEETS, GRID_H, GRID_W, JOIN_OUT)
```

```python
import math

import jax
import jax.numpy as jnp
import numpy as np
from jax import lax
from jax.experimental import pallas as pl
from jax.experimental.pallas import tpu as pltpu
from jax.sharding import PartitionSpec as P

HEAD_DIM = 32
BLOCK = 8
HALO = 2
EPS = 1e-05
LEVELS = (1, 2, 3, 6)
CODED = (6, 3, 2)
UNITS = 8
STRIP_UNITS = 24
STRIP_AT = {6: 0, 3: 12, 2: 18}
SLOTS = {1: 8, 2: 8, 3: 16, 6: 40}
TAPS = 9
f32 = jnp.float32
bf16 = jnp.bfloat16


def bins_of(level, length, first, count):
    places = first + np.arange(count)
    found = []
    for cell in range(level):
        start = cell * length // level
        end = ((cell + 1) * length + level - 1) // level
        mask = (places >= start) & (places < end)
        if mask.any():
            found.append((cell, mask))
    return found


def pool_tables(rows, row_strips, cols, col_strips):
    grid_h, grid_w = rows * row_strips, cols * col_strips
    row_masks = np.zeros((row_strips, col_strips, UNITS, rows), np.float32)
    col_masks = np.zeros((row_strips, col_strips, UNITS, cols), np.float32)
    strip = np.zeros((col_strips, 2 * STRIP_UNITS, row_strips, 2 * UNITS), np.float32)
    slots = 2 * sum(SLOTS.values())
    bins = np.zeros((slots, col_strips, 2 * STRIP_UNITS), np.float32)
    scale = np.zeros((slots, 1), np.float32)
    for c in range(col_strips):
        for r in range(row_strips):
            units = []
            for level in CODED:
                for i, row_mask in bins_of(level, grid_h, r * rows, rows):
                    for g, (j, col_mask) in enumerate(bins_of(level, grid_w, c * cols, cols)):
                        key = (row_mask.tobytes(), col_mask.tobytes())
                        if key not in units:
                            units.append(key)
                            at = len(units) - 1
                            row_masks[r, c, at] = row_mask
                            col_masks[r, c, at] = col_mask
                        at = units.index(key)
                        width = 1 if level == 2 else 2
                        for s in range(2):
                            target = s * STRIP_UNITS + STRIP_AT[level] + i * width + g
                            strip[c, target, r, s * UNITS + at] = 1.0
            assert len(units) <= UNITS
        base = 0
        for level in LEVELS:
            source = 2 if level == 1 else level
            for g, (j, _) in enumerate(bins_of(source, grid_w, c * cols, cols)):
                for i in range(source):
                    for s in range(2):
                        cell = 0 if level == 1 else i * level + j
                        row = base + s * SLOTS[level] + cell
                        width = 1 if source == 2 else 2
                        bins[row, c, s * STRIP_UNITS + STRIP_AT[source] + i * width + g] = 1.0
            base += 2 * SLOTS[level]
    base = 0
    for level in LEVELS:
        row_all = bins_of(level, grid_h, 0, grid_h)
        col_all = bins_of(level, grid_w, 0, grid_w)
        for s in range(2):
            for i, row_mask in row_all:
                for j, col_mask in col_all:
                    row = base + s * SLOTS[level] + i * level + j
                    scale[row, 0] = 1.0 / (row_mask.sum() * col_mask.sum())
        base += 2 * SLOTS[level]
    return row_masks, col_masks, strip.reshape(col_strips, 2 * STRIP_UNITS, -1), bins.reshape(slots, -1), scale


def upsample_weights(level, length, first, count):
    places = first + np.arange(count)
    numer = np.maximum((2 * places + 1) * level - length, 0)
    lower = numer // (2 * length)
    frac = (numer - lower * 2 * length).astype(np.float32) / np.float32(2.0 * length)
    upper = np.minimum(lower + 1, level - 1)
    cells = np.arange(level)[None, :]
    weight = (cells == lower[:, None]) * (1.0 - frac)[:, None] + (cells == upper[:, None]) * frac[:, None]
    inside = (places >= 0) & (places < length)
    return (weight * inside[:, None]).astype(np.float32)


def upsample_tables(rows, row_strips, cols, col_strips):
    grid_h, grid_w = rows * row_strips, cols * col_strips
    width = TAPS * sum(SLOTS.values())
    by_row = np.zeros((row_strips, rows, width), np.float32)
    by_col = np.zeros((col_strips, cols, width), np.float32)
    base = 0
    for level in LEVELS:
        for a in range(3):
            for c in range(3):
                at = base + (a * 3 + c) * SLOTS[level]
                for strip in range(row_strips):
                    w = upsample_weights(level, grid_h, strip * rows + a - 1, rows)
                    by_row[strip, :, at : at + level * level] = np.repeat(w, level, axis=1)
                for strip in range(col_strips):
                    w = upsample_weights(level, grid_w, strip * cols + c - 1, cols)
                    by_col[strip, :, at : at + level * level] = np.tile(w, (1, level))
        base += TAPS * SLOTS[level]
    return by_row, by_col


def layer_norm(tokens, gain):
    x = tokens.astype(f32)
    center = jnp.mean(x, axis=-1, keepdims=True)
    x = x - center
    spread = jnp.mean(x * x, axis=-1, keepdims=True)
    return (x * lax.rsqrt(spread + EPS) * gain).astype(bf16)


def dot(a, b):
    return jnp.dot(a, b, preferred_element_type=f32)


def project_kernel(tokens_ref, gain_ref, wq_ref, wkv_ref, q_ref, kv_ref):
    normed = layer_norm(tokens_ref[...], gain_ref[...])
    q_ref[...] = dot(normed, wq_ref[...]).astype(bf16)
    kv_ref[...] = dot(normed, wkv_ref[...]).astype(bf16)


def attend_kernel(
    q_ref, kv_ref, rows_ref, sides_ref, tokens_ref, gain_ref, wkv_ref, wout_ref, bias_ref, pool_ref,
    attended_ref, sums_ref, ext, queries, context,
):
    rows, cols = queries.shape[0], queries.shape[1]
    inner = queries.shape[2]
    wide = 2 * inner
    groups = cols // BLOCK
    span = BLOCK + 2 * HALO
    gain = gain_ref[...]
    wkv = wkv_ref[...]
    halo = dot(layer_norm(rows_ref[...], gain), wkv).astype(bf16).astype(f32)
    halo = halo.reshape(2 * HALO, cols, wide)
    ext[0:HALO, BLOCK : BLOCK + cols, :] = halo[0:HALO]
    ext[rows + HALO :, BLOCK : BLOCK + cols, :] = halo[HALO:]
    sides = dot(layer_norm(sides_ref[...], gain), wkv).astype(bf16).astype(f32)
    sides = sides.reshape(rows + 2 * HALO, BLOCK, wide)
    ext[:, 0:BLOCK, :] = sides
    ext[:, BLOCK + cols :, :] = sides
    ext[HALO : rows + HALO, BLOCK : BLOCK + cols, :] = kv_ref[...].astype(f32).reshape(rows, cols, wide)
    queries[...] = q_ref[...].astype(f32).reshape(rows, cols, inner)

    half = inner // 2
    heads = half // HEAD_DIM
    count = BLOCK * BLOCK
    head_of_row = lax.broadcasted_iota(jnp.int32, (heads, count, half), 0)
    head_of_lane = lax.broadcasted_iota(jnp.int32, (heads, count, half), 2) // HEAD_DIM
    own = (head_of_row == head_of_lane).astype(f32).astype(bf16).reshape(heads * count, half)
    lane = lax.broadcasted_iota(jnp.int32, (count, 128), 1)
    place = lax.broadcasted_iota(jnp.int32, (span // 2, BLOCK, wide), 1)
    factor = math.log2(math.e) / math.sqrt(HEAD_DIM)

    def column(b, carry):
        left = pl.multiple_of(b * BLOCK, BLOCK)
        mid = pl.multiple_of(b * BLOCK + BLOCK, BLOCK)
        right = pl.multiple_of(b * BLOCK + 2 * BLOCK, BLOCK)
        for a in range(rows // BLOCK):
            at = a * BLOCK
            main = ext[at : at + span, pl.ds(mid, BLOCK), :].reshape(span * BLOCK, wide)
            west = ext[at : at + span, pl.ds(left, BLOCK), :].reshape(span // 2, 2, BLOCK, wide)
            east = ext[at : at + span, pl.ds(right, BLOCK), :].reshape(span // 2, 2, BLOCK, wide)
            even = jnp.where(place >= 6, west[:, 0], east[:, 0])
            odd = jnp.where(place >= 6, west[:, 1], east[:, 1])
            odd = pltpu.roll(odd, 4, 1)
            extra = jnp.where((place >= 6) | (place < 2), even, odd).reshape(span * 4, wide)
            window = jnp.concatenate([main, extra], axis=0).astype(bf16)
            block = queries[at : at + BLOCK, pl.ds(left, BLOCK), :].reshape(count, inner).astype(bf16)
            bias = bias_ref[a, b]
            pieces = []
            for h in range(2):
                q = block[:, h * half : (h + 1) * half]
                q = jnp.concatenate([q] * heads, axis=0) * own
                keys = window[:, h * half : (h + 1) * half]
                values = window[:, inner + h * half : inner + (h + 1) * half]
                scores = lax.dot_general(keys, q, (((1,), (1,)), ((), ())), preferred_element_type=f32)
                scores = scores + jnp.concatenate([bias] * (heads * count // 128), axis=1)
                top = jnp.max(scores, axis=0, keepdims=True)
                expon = jnp.exp2((scores - top) * factor)
                weights = (expon * (1.0 / jnp.sum(expon, axis=0, keepdims=True))).astype(bf16)
                mixed = lax.dot_general(weights, values, (((0,), (0,)), ((), ())), preferred_element_type=f32)
                mixed = mixed.reshape(heads, count, half)
                for t in range(half // 128):
                    lanes = slice(t * 128, (t + 1) * 128)
                    per = 128 // HEAD_DIM
                    piece = mixed[t * per, :, lanes]
                    for k in range(1, per):
                        piece = jnp.where(lane >= k * HEAD_DIM, mixed[t * per + k, :, lanes], piece)
                    pieces.append(piece)
            done = jnp.concatenate(pieces, axis=1).reshape(BLOCK, BLOCK, inner)
            context[at : at + BLOCK, pl.ds(left, BLOCK), :] = done
        return carry

    lax.fori_loop(0, groups, column, 0)
    mixed = context[...].reshape(rows * cols, inner).astype(bf16)
    attended = (tokens_ref[...].astype(f32) + dot(mixed, wout_ref[...])).astype(bf16)
    attended_ref[...] = attended
    sums_ref[...] = dot(pool_ref[...], attended).astype(bf16)


def combine_kernel(table_ref, parts_ref, out_ref):
    out_ref[...] = dot(table_ref[...], parts_ref[...]).astype(bf16)


def conv_kernel(attended_ref, top_ref, bottom_ref, left_ref, right_ref, w_ref, out_ref, ext):
    cols = top_ref.shape[0]
    rows = attended_ref.shape[0] // cols
    ext[0:cols] = top_ref[...]
    ext[cols : cols + rows * cols] = attended_ref[...]
    ext[cols + rows * cols :] = bottom_ref[...]

    def edge(ref, c):
        total = 0.0
        for a in range(3):
            total = total + dot(ref[...], w_ref[a, c])[a : a + rows]
        return total.reshape(rows, 1, total.shape[-1])

    def middle(c):
        total = dot(ext[0 : rows * cols], w_ref[0, c])
        for a in range(1, 3):
            total = total + dot(ext[a * cols : a * cols + rows * cols], w_ref[a, c])
        return total.reshape(rows, cols, total.shape[-1])

    place = lax.broadcasted_iota(jnp.int32, (rows, cols, w_ref.shape[-1]), 1)
    total = middle(1)
    total = total + jnp.where(place == 0, edge(left_ref, 0), pltpu.roll(middle(0), 1, 1))
    total = total + jnp.where(place == cols - 1, edge(right_ref, 2), pltpu.roll(middle(2), cols - 1, 1))
    out_ref[...] = total.reshape(rows * cols, -1)


def split(x):
    high = x.astype(bf16)
    return high, (x - high.astype(f32)).astype(bf16)


def tail_kernel(
    table_ref, scale_ref, parts_ref, wpool_ref, w1_ref, w2_ref, w3_ref, w6_ref, by_row_ref, by_col_ref, conv_ref,
    out_ref, taps,
):
    pooled = dot(table_ref[...], parts_ref[...]) * scale_ref[...]
    row = 0
    at = 0
    for index, (level, w_ref) in enumerate(zip(LEVELS, (w1_ref, w2_ref, w3_ref, w6_ref))):
        slots = SLOTS[level]
        high, low = split(pooled[row : row + 2 * slots])
        both = dot(jnp.concatenate([high, low], axis=0), wpool_ref[index])
        branch = jnp.maximum(both[: 2 * slots] + both[2 * slots :], 0.0)
        high, low = split(branch)
        both = jnp.concatenate([high, low], axis=0)
        for a in range(3):
            for c in range(3):
                tap = dot(both, w_ref[a, c])
                tap = tap[: 2 * slots] + tap[2 * slots :]
                start = at + (a * 3 + c) * slots
                for s in range(2):
                    taps[s, start : start + slots, :] = tap[s * slots : (s + 1) * slots]
        row += 2 * slots
        at += TAPS * slots
    rows, cols = by_row_ref.shape[0], by_col_ref.shape[0]
    grid = by_row_ref[...][:, None, :] * by_col_ref[...][None, :, :]
    grid_high, grid_low = split(grid.reshape(rows * cols, -1))
    for s in range(2):
        high, low = split(taps[s])
        total = conv_ref[s] + dot(grid_high, high) + dot(grid_low, high) + dot(grid_high, low)
        out_ref[s] = total.astype(bf16)


def cost(flops, nbytes, transcendentals=0):
    return pl.CostEstimate(flops=int(flops), bytes_accessed=int(nbytes), transcendentals=int(transcendentals))


def params(mib):
    return pltpu.CompilerParams(vmem_limit_bytes=mib * 2**20)


def whole(shape):
    return pl.BlockSpec(shape, lambda *_: (0,) * len(shape))


def shifts(axis):
    count = lax.axis_size(axis)
    forward = [(i, i + 1) for i in range(count - 1)]
    return forward, [(j, i) for i, j in forward]


def body(tokens, norm_gain, w_query, w_kv, w_out, w_pool, w_join):
    sheets, rows, cols, width = tokens.shape
    inner = w_query.shape[1]
    wide = w_kv.shape[1]
    out_ch = w_join.shape[-1]
    ppm = w_pool.shape[-1]
    area = rows * cols
    row_count, col_count = lax.axis_size("row"), lax.axis_size("col")
    r, c = lax.axis_index("row"), lax.axis_index("col")
    grid_h, grid_w = rows * row_count, cols * col_count
    gain = norm_gain.reshape(1, width)
    row_masks, col_masks, strip_table, bin_table, bin_scale = pool_tables(rows, row_count, cols, col_count)
    by_row, by_col = upsample_tables(rows, row_count, cols, col_count)

    def pick(table, index):
        return lax.dynamic_index_in_dim(jnp.asarray(table), index, 0, keepdims=False)

    row_fwd, row_bwd = shifts("row")
    col_fwd, col_bwd = shifts("col")
    above = lax.ppermute(tokens[:, rows - HALO :], "row", row_fwd)
    below = lax.ppermute(tokens[:, :HALO], "row", row_bwd)
    flat = tokens.reshape(sheets, area, width)
    q, kv = pl.pallas_call(
        project_kernel,
        grid=(sheets,),
        in_specs=[
            pl.BlockSpec((None, area, width), lambda s: (s, 0, 0)),
            whole((1, width)), whole((width, inner)), whole((width, wide)),
        ],
        out_specs=[
            pl.BlockSpec((None, area, inner), lambda s: (s, 0, 0)),
            pl.BlockSpec((None, area, wide), lambda s: (s, 0, 0)),
        ],
        out_shape=[
            jax.ShapeDtypeStruct((sheets, area, inner), bf16),
            jax.ShapeDtypeStruct((sheets, area, wide), bf16),
        ],
        compiler_params=params(40),
        cost_estimate=cost(2 * sheets * area * width * (inner + wide), 2 * (width * (inner + wide) + 3 * sheets * area * width)),
        name="project",
    )(flat, gain, w_query, w_kv)

    def edges(first):
        return jnp.concatenate([x[:, :, first : first + HALO] for x in (above, tokens, below)], axis=1)

    west = lax.ppermute(edges(cols - HALO), "col", col_fwd)
    east = lax.ppermute(edges(0), "col", col_bwd)
    blank = jnp.zeros((sheets, rows + 2 * HALO, BLOCK - 2 * HALO, width), bf16)
    sides = jnp.concatenate([east, blank, west], axis=2).reshape(sheets, (rows + 2 * HALO) * BLOCK, width)
    row_halo = jnp.concatenate([above, below], axis=1).reshape(sheets, 2 * HALO * cols, width)

    span = BLOCK + 2 * HALO
    k = np.arange(span * span)
    e = k - span * BLOCK
    lane8 = e % 8
    odd = (lane8 >= 2) & (lane8 < 6)
    is_west = (lane8 >= 6) | ((lane8 >= 2) & (lane8 < 4))
    key_row = np.where(e < 0, k // BLOCK, 2 * (e // 8) + odd) - HALO
    key_col = np.where(e < 0, k % BLOCK, np.where(is_west, lane8 % 2 - HALO, BLOCK + lane8 % 2))
    row_at = r * rows + jnp.arange(0, rows, BLOCK)[:, None] + jnp.asarray(key_row)[None, :]
    col_at = c * cols + jnp.arange(0, cols, BLOCK)[:, None] + jnp.asarray(key_col)[None, :]
    row_ok = (row_at >= 0) & (row_at < grid_h)
    col_ok = (col_at >= 0) & (col_at < grid_w)
    ok = row_ok[:, None, :, None] & col_ok[None, :, :, None]
    bias = jnp.broadcast_to(jnp.where(ok, 0.0, -1e30).astype(f32), ok.shape[:3] + (128,))
    row_mask = pick(row_masks.reshape(-1, UNITS, rows), r * col_count + c)
    col_mask = pick(col_masks.reshape(-1, UNITS, cols), r * col_count + c)
    pool = (row_mask[:, :, None] * col_mask[:, None, :]).reshape(UNITS, area).astype(bf16)

    blocks = (rows // BLOCK) * (cols // BLOCK)
    attended, sums = pl.pallas_call(
        attend_kernel,
        grid=(sheets,),
        in_specs=[
            pl.BlockSpec((None, area, inner), lambda s: (s, 0, 0)),
            pl.BlockSpec((None, area, wide), lambda s: (s, 0, 0)),
            pl.BlockSpec((None, 2 * HALO * cols, width), lambda s: (s, 0, 0)),
            pl.BlockSpec((None, (rows + 2 * HALO) * BLOCK, width), lambda s: (s, 0, 0)),
            pl.BlockSpec((None, area, width), lambda s: (s, 0, 0)),
            whole((1, width)), whole((width, wide)), whole((inner, width)),
            whole(bias.shape), whole((UNITS, area)),
        ],
        out_specs=[
            pl.BlockSpec((None, area, width), lambda s: (s, 0, 0)),
            pl.BlockSpec((None, UNITS, width), lambda s: (s, 0, 0)),
        ],
        out_shape=[
            jax.ShapeDtypeStruct((sheets, area, width), bf16),
            jax.ShapeDtypeStruct((sheets, UNITS, width), bf16),
        ],
        scratch_shapes=[
            pltpu.VMEM((rows + 2 * HALO, cols + 2 * BLOCK, wide), f32),
            pltpu.VMEM((rows, cols, inner), f32),
            pltpu.VMEM((rows, cols, inner), f32),
        ],
        compiler_params=params(48),
        cost_estimate=cost(2 * sheets * area * inner * width * 4, 2 * sheets * area * width * 4, sheets * blocks * 144 * 1024),
        name="attend",
    )(q, kv, row_halo, sides, flat, gain, w_kv, w_out, bias, pool)

    att = attended.reshape(sheets, rows, cols, width)
    att_above = lax.ppermute(att[:, rows - 1 :], "row", row_fwd)
    att_below = lax.ppermute(att[:, :1], "row", row_bwd)

    parts = jnp.broadcast_to(sums.reshape(1, sheets * UNITS, width), (row_count, sheets * UNITS, width))
    parts = lax.all_to_all(parts, "row", 0, 0, tiled=True).reshape(row_count * sheets * UNITS, width)
    strip_rows = sheets * STRIP_UNITS
    strips = pl.pallas_call(
        combine_kernel,
        out_shape=jax.ShapeDtypeStruct((strip_rows, width), bf16),
        compiler_params=params(8),
        name="combine",
    )(pick(strip_table, c).astype(bf16), parts)

    def att_edges(first):
        return jnp.concatenate([x[:, :, first] for x in (att_above, att, att_below)], axis=1)

    att_west = lax.ppermute(att_edges(cols - 1), "col", col_fwd)
    att_east = lax.ppermute(att_edges(0), "col", col_bwd)
    pad = ((0, 0), (0, 6), (0, 0))
    att_west, att_east = jnp.pad(att_west, pad), jnp.pad(att_east, pad)

    strips = jnp.broadcast_to(strips[None], (col_count, strip_rows, width))
    strips = lax.all_to_all(strips, "col", 0, 0, tiled=True).reshape(col_count * strip_rows, width)

    def per_sheet(*dims):
        return pl.BlockSpec((None,) + dims, lambda s: (s,) + (0,) * len(dims))

    conv = pl.pallas_call(
        conv_kernel,
        grid=(sheets,),
        in_specs=[
            per_sheet(area, width), per_sheet(cols, width), per_sheet(cols, width),
            per_sheet(rows + 8, width), per_sheet(rows + 8, width),
            pl.BlockSpec((3, 3, width, out_ch), lambda s: (0, 0, 0, 0)),
        ],
        out_specs=per_sheet(area, out_ch),
        out_shape=jax.ShapeDtypeStruct((sheets, area, out_ch), f32),
        scratch_shapes=[pltpu.VMEM((area + 2 * cols, width), bf16)],
        compiler_params=params(32),
        cost_estimate=cost(2 * sheets * area * width * 9 * out_ch, 2 * 9 * width * out_ch + 2 * sheets * area * width),
        name="conv",
    )(attended, att_above.reshape(sheets, cols, width), att_below.reshape(sheets, cols, width), att_west, att_east, w_join)

    first = width // ppm

    def level_spec(index):
        return pl.BlockSpec((3, 3, ppm, out_ch), lambda *_: (0, 0, first + index, 0), pipeline_mode=pl.Buffered(1))

    depth = TAPS * sum(SLOTS.values())
    bin_rows = 2 * sum(SLOTS.values())
    out = pl.pallas_call(
        tail_kernel,
        grid=(1,),
        in_specs=[
            whole((bin_rows, col_count * strip_rows)), whole((bin_rows, 1)), whole((col_count * strip_rows, width)),
            whole(w_pool.shape), level_spec(0), level_spec(1), level_spec(2), level_spec(3),
            whole((rows, depth)), whole((cols, depth)), whole((sheets, area, out_ch)),
        ],
        out_specs=whole((sheets, area, out_ch)),
        out_shape=jax.ShapeDtypeStruct((sheets, area, out_ch), bf16),
        scratch_shapes=[pltpu.VMEM((sheets, depth, out_ch), f32)],
        compiler_params=params(56),
        name="tail",
    )(
        jnp.asarray(bin_table).astype(bf16), jnp.asarray(bin_scale), strips,
        w_pool, w_join, w_join, w_join, w_join, pick(by_row, r), pick(by_col, c), conv,
    )
    return out.reshape(sheets, rows, cols, out_ch)


def solution(mesh):
    placed = (P(None, "row", "col", None), P(), P(), P(), P(), P(), P())
    return jax.shard_map(
        body, mesh=mesh, in_specs=placed, out_specs=P(None, "row", "col", None), check_vma=False
    )
```

```python
import math

import jax
import jax.numpy as jnp
import numpy as np
from jax import lax
from jax.experimental import pallas as pl
from jax.experimental.pallas import tpu as pltpu
from jax.sharding import PartitionSpec as P

HEAD_DIM = 32
BLOCK = 8
HALO = 2
EPS = 1e-05
LEVELS = (1, 2, 3, 6)
CODED = (6, 3, 2)
UNITS = 8
STRIP_UNITS = 24
STRIP_AT = {6: 0, 3: 12, 2: 18}
SLOTS = {1: 8, 2: 8, 3: 16, 6: 40}
TAPS = 9
f32 = jnp.float32
bf16 = jnp.bfloat16


def bins_of(level, length, first, count):
    places = first + np.arange(count)
    found = []
    for cell in range(level):
        start = cell * length // level
        end = ((cell + 1) * length + level - 1) // level
        mask = (places >= start) & (places < end)
        if mask.any():
            found.append((cell, mask))
    return found


def pool_tables(rows, row_strips, cols, col_strips):
    grid_h, grid_w = rows * row_strips, cols * col_strips
    row_masks = np.zeros((row_strips, col_strips, UNITS, rows), np.float32)
    col_masks = np.zeros((row_strips, col_strips, UNITS, cols), np.float32)
    strip = np.zeros((col_strips, 2 * STRIP_UNITS, row_strips, 2 * UNITS), np.float32)
    slots = 2 * sum(SLOTS.values())
    bins = np.zeros((slots, col_strips, 2 * STRIP_UNITS), np.float32)
    scale = np.zeros((slots, 1), np.float32)
    for c in range(col_strips):
        for r in range(row_strips):
            units = []
            for level in CODED:
                for i, row_mask in bins_of(level, grid_h, r * rows, rows):
                    for g, (j, col_mask) in enumerate(bins_of(level, grid_w, c * cols, cols)):
                        key = (row_mask.tobytes(), col_mask.tobytes())
                        if key not in units:
                            units.append(key)
                            at = len(units) - 1
                            row_masks[r, c, at] = row_mask
                            col_masks[r, c, at] = col_mask
                        at = units.index(key)
                        width = 1 if level == 2 else 2
                        for s in range(2):
                            target = s * STRIP_UNITS + STRIP_AT[level] + i * width + g
                            strip[c, target, r, s * UNITS + at] = 1.0
            assert len(units) <= UNITS
        base = 0
        for level in LEVELS:
            source = 2 if level == 1 else level
            for g, (j, _) in enumerate(bins_of(source, grid_w, c * cols, cols)):
                for i in range(source):
                    for s in range(2):
                        cell = 0 if level == 1 else i * level + j
                        row = base + s * SLOTS[level] + cell
                        width = 1 if source == 2 else 2
                        bins[row, c, s * STRIP_UNITS + STRIP_AT[source] + i * width + g] = 1.0
            base += 2 * SLOTS[level]
    base = 0
    for level in LEVELS:
        row_all = bins_of(level, grid_h, 0, grid_h)
        col_all = bins_of(level, grid_w, 0, grid_w)
        for s in range(2):
            for i, row_mask in row_all:
                for j, col_mask in col_all:
                    row = base + s * SLOTS[level] + i * level + j
                    scale[row, 0] = 1.0 / (row_mask.sum() * col_mask.sum())
        base += 2 * SLOTS[level]
    return row_masks, col_masks, strip.reshape(col_strips, 2 * STRIP_UNITS, -1), bins.reshape(slots, -1), scale


def upsample_weights(level, length, first, count):
    places = first + np.arange(count)
    numer = np.maximum((2 * places + 1) * level - length, 0)
    lower = numer // (2 * length)
    frac = (numer - lower * 2 * length).astype(np.float32) / np.float32(2.0 * length)
    upper = np.minimum(lower + 1, level - 1)
    cells = np.arange(level)[None, :]
    weight = (cells == lower[:, None]) * (1.0 - frac)[:, None] + (cells == upper[:, None]) * frac[:, None]
    inside = (places >= 0) & (places < length)
    return (weight * inside[:, None]).astype(np.float32)


def upsample_tables(rows, row_strips, cols, col_strips):
    grid_h, grid_w = rows * row_strips, cols * col_strips
    width = TAPS * sum(SLOTS.values())
    cells = sum(LEVELS)
    by_row = np.zeros((row_strips, rows, 64), np.float32)
    by_col = np.zeros((col_strips, cols, 64), np.float32)
    spread = np.zeros((2, 64, width), np.float32)
    base, first = 0, 0
    for level in LEVELS:
        for a in range(3):
            for strip in range(row_strips):
                w = upsample_weights(level, grid_h, strip * rows + a - 1, rows)
                by_row[strip, :, a * cells + first : a * cells + first + level] = w
            for strip in range(col_strips):
                w = upsample_weights(level, grid_w, strip * cols + a - 1, cols)
                by_col[strip, :, a * cells + first : a * cells + first + level] = w
            for c in range(3):
                for i in range(level):
                    for j in range(level):
                        at = base + (a * 3 + c) * SLOTS[level] + i * level + j
                        spread[0, a * cells + first + i, at] = 1.0
                        spread[1, c * cells + first + j, at] = 1.0
        base += TAPS * SLOTS[level]
        first += level
    return by_row, by_col, spread


def layer_norm(tokens, gain):
    x = tokens.astype(f32)
    center = jnp.mean(x, axis=-1, keepdims=True)
    x = x - center
    spread = jnp.mean(x * x, axis=-1, keepdims=True)
    return (x * lax.rsqrt(spread + EPS) * gain).astype(bf16)


def dot(a, b):
    return jnp.dot(a, b, preferred_element_type=f32)


def project_kernel(tokens_ref, above_ref, below_ref, gain_ref, wq_ref, wkv_ref, q_ref, kv_ref):
    rows, cols, inner = q_ref.shape
    gain, wkv = gain_ref[...], wkv_ref[...]
    normed = layer_norm(tokens_ref[...], gain)
    q_ref[...] = dot(normed, wq_ref[...]).astype(bf16).astype(f32).reshape(rows, cols, inner)
    kv_ref[HALO : rows + HALO] = dot(normed, wkv).astype(bf16).astype(f32).reshape(rows, cols, -1)
    edge = layer_norm(jnp.concatenate([above_ref[...], below_ref[...]], axis=0), gain)
    edge = dot(edge, wkv).astype(bf16).astype(f32).reshape(2 * HALO, cols, -1)
    kv_ref[0:HALO] = edge[:HALO]
    kv_ref[rows + HALO :] = edge[HALO:]


def window_bias(bias, first_row, first_col, grid_h, grid_w):
    span = BLOCK + 2 * HALO
    key = lax.broadcasted_iota(jnp.int32, bias.shape[2:], 0)
    extra = key - span * BLOCK
    lane = extra & 7
    odd = ((lane >= 2) & (lane < 6)).astype(jnp.int32)
    west = (lane >= 6) | ((lane >= 2) & (lane < 4))
    main = key < span * BLOCK
    row = jnp.where(main, key >> 3, 2 * (extra >> 3) + odd) - HALO
    col = jnp.where(main, key & 7, (key & 1) + jnp.where(west, -HALO, BLOCK))
    for a in range(bias.shape[0]):
        at = row + (first_row + a * BLOCK)
        row_ok = (at >= 0) & (at < grid_h)
        for b in range(bias.shape[1]):
            at = col + (first_col + b * BLOCK)
            bias[a, b] = jnp.where(row_ok & (at >= 0) & (at < grid_w), 0.0, -1e30)


def attend_kernel(
    grid_shape, place_ref, q_ref, kv_ref, sides_ref, tokens_ref, gain_ref, wkv_ref, wout_ref, masks_ref,
    attended_ref, sums_ref, sides, context, bias, pool, scores, weights,
):
    rows, cols, inner = q_ref.shape
    groups = cols // BLOCK
    span = BLOCK + 2 * HALO

    @pl.when(pl.program_id(0) == 0)
    def _():
        window_bias(bias, place_ref[0] * rows, place_ref[1] * cols, *grid_shape)
        masks = masks_ref[...].astype(bf16)
        unit = lax.broadcasted_iota(jnp.int32, (masks.shape[1], rows * cols), 0)
        token = lax.broadcasted_iota(jnp.int32, (masks.shape[1], rows * cols), 1)
        to_row = (unit == token // cols).astype(f32).astype(bf16)
        to_col = (unit - rows == token % cols).astype(f32).astype(bf16)
        pool[...] = (dot(masks, to_row) * dot(masks, to_col)).astype(bf16)
        ends = layer_norm(sides_ref[...].reshape(-1, sides_ref.shape[-1]), gain_ref[...])
        ends = dot(ends, wkv_ref[...]).astype(bf16).astype(f32)
        sides[...] = ends.reshape(sides.shape)

    sheet = pl.program_id(0)
    count = BLOCK * BLOCK
    heads = 128 // HEAD_DIM
    head_of_row = lax.broadcasted_iota(jnp.int32, (heads, count, 128), 0)
    head_of_lane = lax.broadcasted_iota(jnp.int32, (heads, count, 128), 2) // HEAD_DIM
    own = (head_of_row == head_of_lane).astype(f32).astype(bf16).reshape(heads * count, 128)
    lane = lax.broadcasted_iota(jnp.int32, (count, 128), 1)
    place = lax.broadcasted_iota(jnp.int32, (span // 2, BLOCK, 128), 1)
    factor = math.log2(math.e) / math.sqrt(HEAD_DIM)

    def band(a, carry):
        at = pl.multiple_of(a * BLOCK, BLOCK)

        def keys_of(b, lanes):
            mid = slice(b * BLOCK, (b + 1) * BLOCK)
            main = kv_ref[pl.ds(at, span), mid, lanes].reshape(span * BLOCK, 128)

            def beside(g):
                if g < 0 or g >= groups:
                    found = sides[sheet, pl.ds(at, span), :, lanes]
                else:
                    found = kv_ref[pl.ds(at, span), g * BLOCK : (g + 1) * BLOCK, lanes]
                return found.reshape(span // 2, 2, BLOCK, 128)

            west, east = beside(b - 1), beside(b + 1)
            even = jnp.where(place >= 6, west[:, 0], east[:, 0])
            odd = pltpu.roll(jnp.where(place >= 6, west[:, 1], east[:, 1]), 4, 1)
            extra = jnp.where((place >= 6) | (place < 2), even, odd).reshape(span * 4, 128)
            return jnp.concatenate([main, extra], axis=0).astype(bf16)

        tiles = inner // 128

        def score(b, slot):
            mid = slice(b * BLOCK, (b + 1) * BLOCK)
            low = bias[a, b]
            for t in range(tiles):
                lanes = slice(t * 128, (t + 1) * 128)
                q = q_ref[pl.ds(at, BLOCK), mid, lanes].reshape(count, 128).astype(bf16)
                q = jnp.concatenate([q] * heads, axis=0) * own
                found = lax.dot_general(keys_of(b, lanes), q, (((1,), (1,)), ((), ())), preferred_element_type=f32)
                scores[slot, t] = found + jnp.concatenate([low] * (heads * count // 128), axis=1)

        def soften(slot):
            for t in range(tiles):
                for h in range(heads * count // 128):
                    lanes = slice(h * 128, (h + 1) * 128)
                    found = scores[slot, t, :, lanes]
                    top = jnp.max(found, axis=0, keepdims=True)
                    expon = jnp.exp2((found - top) * factor)
                    weights[slot, t, :, lanes] = (expon * (1.0 / jnp.sum(expon, axis=0, keepdims=True))).astype(bf16)

        def mix(b, slot):
            mid = slice(b * BLOCK, (b + 1) * BLOCK)
            for t in range(tiles):
                lanes = slice(t * 128, (t + 1) * 128)
                values = keys_of(b, slice(inner + t * 128, inner + (t + 1) * 128))
                mixed = lax.dot_general(weights[slot, t], values, (((0,), (0,)), ((), ())), preferred_element_type=f32)
                mixed = mixed.reshape(heads, count, 128)
                piece = mixed[0]
                for k in range(1, heads):
                    piece = jnp.where(lane >= k * HEAD_DIM, mixed[k], piece)
                context[pl.ds(at, BLOCK), mid, lanes] = piece.reshape(BLOCK, BLOCK, 128)

        score(0, 0)
        for b in range(groups):
            if b + 1 < groups:
                score(b + 1, (b + 1) % 2)
            soften(b % 2)
            mix(b, b % 2)
        return carry

    lax.fori_loop(0, rows // BLOCK, band, 0)
    mixed = context[...].reshape(rows * cols, inner).astype(bf16)
    attended = (tokens_ref[...].astype(f32) + dot(mixed, wout_ref[...])).astype(bf16)
    attended_ref[...] = attended
    sums = dot(pool[...], attended).astype(bf16)
    sums_ref[...] = jnp.broadcast_to(sums[None], sums_ref.shape)


def combine_kernel(place_ref, table_ref, parts_ref, out_ref):
    added = dot(table_ref[...].astype(bf16), parts_ref[...]).astype(bf16)
    out_ref[...] = jnp.broadcast_to(added[None], out_ref.shape)


def conv_kernel(attended_ref, top_ref, bottom_ref, left_ref, right_ref, w_ref, out_ref, ext):
    sheets, area, _ = attended_ref.shape
    cols = top_ref.shape[1]
    rows = area // cols
    out_ch = out_ref.shape[-1]
    step = pl.program_id(0)

    def edge(ref, s):
        total = 0.0
        for a in range(3):
            total = total + dot(ref[s], w_ref[a])[a : a + rows]
        return total.reshape(rows, 1, out_ch)

    def middle(s):
        total = dot(ext[s, 0:area], w_ref[0])
        for a in range(1, 3):
            total = total + dot(ext[s, a * cols : a * cols + area], w_ref[a])
        return total.reshape(rows, cols, out_ch)

    @pl.when(step == 0)
    def _():
        place = lax.broadcasted_iota(jnp.int32, (rows, cols, out_ch), 1)
        for s in range(sheets):
            ext[s, 0:cols] = top_ref[s]
            ext[s, cols : cols + area] = attended_ref[s]
            ext[s, cols + area :] = bottom_ref[s]
            part = jnp.where(place == 0, edge(left_ref, s), pltpu.roll(middle(s), 1, 1))
            out_ref[s] = part.reshape(area, out_ch)

    @pl.when(step == 1)
    def _():
        for s in range(sheets):
            out_ref[s] += middle(s).reshape(area, out_ch)

    @pl.when(step == 2)
    def _():
        place = lax.broadcasted_iota(jnp.int32, (rows, cols, out_ch), 1)
        for s in range(sheets):
            part = jnp.where(place == cols - 1, edge(right_ref, s), pltpu.roll(middle(s), cols - 1, 1))
            out_ref[s] += part.reshape(area, out_ch)


def split(x):
    high = x.astype(bf16)
    return high, (x - high.astype(f32)).astype(bf16)


def tail_kernel(
    place_ref, table_ref, scale_ref, parts_ref, wpool_hbm, wjoin_hbm, by_row_ref, by_col_ref, spread_ref, conv_ref,
    out_ref, taps, wpool, wjoin, sems,
):
    width, ppm = wpool.shape[1], wpool.shape[2]
    copies = []
    for index in range(len(LEVELS)):
        copies.append((
            pltpu.make_async_copy(wpool_hbm.at[index], wpool.at[index], sems.at[0, index]),
            pltpu.make_async_copy(
                wjoin_hbm.at[:, :, width + index * ppm : width + (index + 1) * ppm, :], wjoin.at[index], sems.at[1, index]
            ),
        ))
    for pair in copies:
        for copy in pair:
            copy.start()
    pooled = dot(table_ref[...], parts_ref[...]) * scale_ref[...]
    row = 0
    at = 0
    for index, level in enumerate(LEVELS):
        slots = SLOTS[level]
        high, low = split(pooled[row : row + 2 * slots])
        copies[index][0].wait()
        both = dot(jnp.concatenate([high, low], axis=0), wpool[index])
        branch = jnp.maximum(both[: 2 * slots] + both[2 * slots :], 0.0)
        high, low = split(branch)
        both = jnp.concatenate([high, low], axis=0)
        copies[index][1].wait()
        for a in range(3):
            for c in range(3):
                tap = dot(both, wjoin[index, a, c])
                tap = tap[: 2 * slots] + tap[2 * slots :]
                start = at + (a * 3 + c) * slots
                for s in range(2):
                    taps[s, start : start + slots, :] = tap[s * slots : (s + 1) * slots]
        row += 2 * slots
        at += TAPS * slots
    rows, cols = by_row_ref.shape[0], by_col_ref.shape[0]

    def along(ref, axis):
        high, low = split(ref[...])
        return dot(high, spread_ref[axis]) + dot(low, spread_ref[axis])

    grid = along(by_row_ref, 0)[:, None, :] * along(by_col_ref, 1)[None, :, :]
    grid_high, grid_low = split(grid.reshape(rows * cols, -1))
    for s in range(2):
        high, low = split(taps[s])
        total = conv_ref[s] + dot(grid_high, high) + dot(grid_low, high) + dot(grid_high, low)
        out_ref[s] = total.astype(bf16)


def cost(flops, nbytes, transcendentals=0):
    return pl.CostEstimate(flops=int(flops), bytes_accessed=int(nbytes), transcendentals=int(transcendentals))


def params(mib):
    return pltpu.CompilerParams(vmem_limit_bytes=mib * 2**20)


def whole(shape):
    return pl.BlockSpec(shape, lambda *_: (0,) * len(shape))


def shifts(axis):
    count = lax.axis_size(axis)
    forward = [(i, i + 1) for i in range(count - 1)]
    return forward, [(j, i) for i, j in forward]


def layer(tokens, norm_gain, w_query, w_kv, w_out, w_pool, w_join):
    sheets, rows, cols, width = tokens.shape
    inner = w_query.shape[1]
    wide = w_kv.shape[1]
    out_ch = w_join.shape[-1]
    ppm = w_pool.shape[-1]
    area = rows * cols
    row_count, col_count = lax.axis_size("row"), lax.axis_size("col")
    r, c = lax.axis_index("row"), lax.axis_index("col")
    grid_h, grid_w = rows * row_count, cols * col_count
    gain = norm_gain.reshape(1, width)
    row_masks, col_masks, strip_table, bin_table, bin_scale = pool_tables(rows, row_count, cols, col_count)
    by_row, by_col, spread = upsample_tables(rows, row_count, cols, col_count)
    masks = np.concatenate([row_masks, col_masks], axis=-1).reshape(row_count * col_count, UNITS, rows + cols)

    at = jnp.stack([r, c]).astype(jnp.int32)
    row_fwd, row_bwd = shifts("row")
    col_fwd, col_bwd = shifts("col")
    above = lax.ppermute(tokens[:, rows - HALO :], "row", row_fwd)
    below = lax.ppermute(tokens[:, :HALO], "row", row_bwd)

    def edges(first):
        return jnp.concatenate([x[:, :, first : first + HALO] for x in (above, tokens, below)], axis=1)

    west = lax.ppermute(edges(cols - HALO), "col", col_fwd)
    east = lax.ppermute(edges(0), "col", col_bwd)

    def per_sheet(*dims):
        return pl.BlockSpec((None,) + dims, lambda s: (s,) + (0,) * len(dims))

    flat = tokens.reshape(sheets, area, width)
    edge = HALO * cols
    q, kv = pl.pallas_call(
        project_kernel,
        grid=(sheets,),
        in_specs=[
            per_sheet(area, width), per_sheet(edge, width), per_sheet(edge, width),
            whole((1, width)), whole((width, inner)), whole((width, wide)),
        ],
        out_specs=[per_sheet(rows, cols, inner), per_sheet(rows + 2 * HALO, cols, wide)],
        out_shape=[
            jax.ShapeDtypeStruct((sheets, rows, cols, inner), f32),
            jax.ShapeDtypeStruct((sheets, rows + 2 * HALO, cols, wide), f32),
        ],
        compiler_params=params(28),
        cost_estimate=cost(2 * sheets * area * width * (inner + wide), 2 * (width * (inner + wide) + 5 * sheets * area * width)),
        name="project",
    )(flat, above.reshape(sheets, edge, width), below.reshape(sheets, edge, width), gain, w_query, w_kv)

    blank = jnp.zeros((sheets, rows + 2 * HALO, BLOCK - 2 * HALO, width), bf16)
    sides = jnp.concatenate([east, blank, west], axis=2).reshape(sheets, (rows + 2 * HALO) * BLOCK, width)
    blocks = (rows // BLOCK) * (cols // BLOCK)
    keys = (BLOCK + 2 * HALO) ** 2

    def fixed(*dims):
        return whole(dims)

    attended, sums = pl.pallas_call(
        lambda *refs: attend_kernel((grid_h, grid_w), *refs),
        grid_spec=pltpu.PrefetchScalarGridSpec(
            num_scalar_prefetch=1,
            grid=(sheets,),
            in_specs=[
                pl.BlockSpec((None, rows, cols, inner), lambda s, _: (s, 0, 0, 0)),
                pl.BlockSpec((None, rows + 2 * HALO, cols, wide), lambda s, _: (s, 0, 0, 0)),
                fixed(sheets, (rows + 2 * HALO) * BLOCK, width),
                pl.BlockSpec((None, area, width), lambda s, _: (s, 0, 0)),
                fixed(1, width), fixed(width, wide), fixed(inner, width),
                pl.BlockSpec((None, UNITS, rows + cols), lambda s, p: (p[0] * col_count + p[1], 0, 0)),
            ],
            out_specs=[
                pl.BlockSpec((None, area, width), lambda s, _: (s, 0, 0)),
                pl.BlockSpec((row_count, UNITS, width), lambda s, _: (0, s, 0)),
            ],
            scratch_shapes=[
                pltpu.VMEM((sheets, rows + 2 * HALO, BLOCK, wide), f32),
                pltpu.VMEM((rows, cols, inner), f32),
                pltpu.VMEM((rows // BLOCK, cols // BLOCK, keys, 128), f32),
                pltpu.VMEM((UNITS, area), bf16),
                pltpu.VMEM((2, inner // 128, keys, 256), f32),
                pltpu.VMEM((2, inner // 128, keys, 256), bf16),
            ],
        ),
        out_shape=[
            jax.ShapeDtypeStruct((sheets, area, width), bf16),
            jax.ShapeDtypeStruct((row_count, sheets * UNITS, width), bf16),
        ],
        compiler_params=params(32),
        cost_estimate=cost(2 * sheets * area * inner * width * 4, 2 * sheets * area * width * 4, sheets * blocks * keys * 1024),
        name="attend",
    )(at, q, kv, sides, flat, gain, w_kv, w_out, jnp.asarray(masks))

    att = attended.reshape(sheets, rows, cols, width)
    strip_rows = sheets * STRIP_UNITS
    att_above = lax.ppermute(att[:, rows - 1 :], "row", row_fwd)
    att_below = lax.ppermute(att[:, :1], "row", row_bwd)
    parts = lax.all_to_all(sums, "row", 0, 0, tiled=True).reshape(row_count * sheets * UNITS, width)

    def att_edges(first):
        return jnp.concatenate([x[:, :, first] for x in (att_above, att, att_below)], axis=1)

    att_west = lax.ppermute(att_edges(cols - 1), "col", col_fwd)
    att_east = lax.ppermute(att_edges(0), "col", col_bwd)
    pad = ((0, 0), (0, 6), (0, 0))
    att_west, att_east = jnp.pad(att_west, pad), jnp.pad(att_east, pad)

    strips = pl.pallas_call(
        combine_kernel,
        grid_spec=pltpu.PrefetchScalarGridSpec(
            num_scalar_prefetch=1,
            grid=(1,),
            in_specs=[
                pl.BlockSpec((None,) + strip_table.shape[1:], lambda k, p: (p[1], 0, 0)),
                fixed(row_count * sheets * UNITS, width),
            ],
            out_specs=fixed(col_count, strip_rows, width),
        ),
        out_shape=jax.ShapeDtypeStruct((col_count, strip_rows, width), bf16),
        compiler_params=params(8),
        name="combine",
    )(at, jnp.asarray(strip_table).astype(bf16), parts)
    strips = lax.all_to_all(strips, "col", 0, 0, tiled=True).reshape(col_count * strip_rows, width)

    conv = pl.pallas_call(
        conv_kernel,
        grid=(3,),
        in_specs=[
            whole((sheets, area, width)), whole((sheets, cols, width)), whole((sheets, cols, width)),
            whole((sheets, rows + 8, width)), whole((sheets, rows + 8, width)),
            pl.BlockSpec((3, None, width, out_ch), lambda k: (0, k, 0, 0)),
        ],
        out_specs=whole((sheets, area, out_ch)),
        out_shape=jax.ShapeDtypeStruct((sheets, area, out_ch), f32),
        scratch_shapes=[pltpu.VMEM((sheets, area + 2 * cols, width), bf16)],
        compiler_params=params(52),
        cost_estimate=cost(2 * sheets * area * width * 9 * out_ch, 2 * 9 * width * out_ch + 2 * sheets * area * width),
        name="conv",
    )(attended, att_above.reshape(sheets, cols, width), att_below.reshape(sheets, cols, width), att_west, att_east, w_join)

    depth = TAPS * sum(SLOTS.values())
    bin_rows = 2 * sum(SLOTS.values())
    out = pl.pallas_call(
        tail_kernel,
        grid_spec=pltpu.PrefetchScalarGridSpec(
            num_scalar_prefetch=1,
            grid=(1,),
            in_specs=[
                fixed(bin_rows, col_count * strip_rows), fixed(bin_rows, 1), fixed(col_count * strip_rows, width),
                pl.BlockSpec(memory_space=pl.ANY), pl.BlockSpec(memory_space=pl.ANY),
                pl.BlockSpec((None, rows, 64), lambda k, p: (p[0], 0, 0)),
                pl.BlockSpec((None, cols, 64), lambda k, p: (p[1], 0, 0)),
                fixed(2, 64, depth), fixed(sheets, area, out_ch),
            ],
            out_specs=fixed(sheets, area, out_ch),
            scratch_shapes=[
                pltpu.VMEM((sheets, depth, out_ch), f32),
                pltpu.VMEM(w_pool.shape, bf16),
                pltpu.VMEM((len(LEVELS), 3, 3, ppm, out_ch), bf16),
                pltpu.SemaphoreType.DMA((2, len(LEVELS))),
            ],
        ),
        out_shape=jax.ShapeDtypeStruct((sheets, area, out_ch), bf16),
        compiler_params=params(56),
        cost_estimate=cost(4e9, 2 * (w_pool.size + 9 * 4 * ppm * out_ch)),
        name="tail",
    )(
        at, jnp.asarray(bin_table).astype(bf16), jnp.asarray(bin_scale), strips,
        w_pool, w_join, jnp.asarray(by_row), jnp.asarray(by_col), jnp.asarray(spread).astype(bf16), conv,
    )
    return out.reshape(sheets, rows, cols, out_ch)


def solution(mesh):
    placed = (P(None, "row", "col", None), P(), P(), P(), P(), P(), P())
    return jax.shard_map(layer, mesh=mesh, in_specs=placed, out_specs=P(None, "row", "col", None), check_vma=False)
```

```python
import math

import jax
import jax.numpy as jnp
import numpy as np
from jax import lax
from jax.experimental import pallas as pl
from jax.experimental.pallas import tpu as pltpu
from jax.sharding import PartitionSpec as P

HEAD_DIM = 32
BLOCK = 8
HALO = 2
EPS = 1e-05
LEVELS = (1, 2, 3, 6)
CODED = (6, 3, 2)
UNITS = 8
STRIP_ALL = 24
STRIP_ALL_AT = {6: 0, 3: 12, 2: 18}
STRIP_UNITS = 16
STRIP_AT = {6: 0, 3: 6, 2: 12}
NEAR = {1: 1, 2: 2, 3: 3, 6: 3}
SLOTS = {1: 8, 2: 8, 3: 16, 6: 16}
TAPS = 9
f32 = jnp.float32
bf16 = jnp.bfloat16


def bins_of(level, length, first, count):
    places = first + np.arange(count)
    found = []
    for cell in range(level):
        start = cell * length // level
        end = ((cell + 1) * length + level - 1) // level
        mask = (places >= start) & (places < end)
        if mask.any():
            found.append((cell, mask))
    return found


def lower_bin(level, length, place):
    return max((2 * place + 1) * level - length, 0) // (2 * length)


def first_bin(level, length, first, count):
    start = min(lower_bin(level, length, first - 1), level - NEAR[level])
    assert min(lower_bin(level, length, first + count) + 1, level - 1) < start + NEAR[level]
    return start


def pool_tables(rows, row_strips, cols, col_strips):
    grid_h, grid_w = rows * row_strips, cols * col_strips
    row_masks = np.zeros((row_strips, col_strips, UNITS, rows), np.float32)
    col_masks = np.zeros((row_strips, col_strips, UNITS, cols), np.float32)
    strip = np.zeros((col_strips, 2 * STRIP_ALL, row_strips, 2 * UNITS), np.float32)
    near = np.zeros((row_strips, 2 * STRIP_UNITS, 2 * STRIP_ALL), np.float32)
    slots = 2 * sum(SLOTS.values())
    bins = np.zeros((col_strips, slots, col_strips, 2 * STRIP_UNITS), np.float32)
    row_scale = np.zeros((row_strips, 1, slots), np.float32)
    col_scale = np.zeros((col_strips, 1, slots), np.float32)
    for c in range(col_strips):
        for r in range(row_strips):
            units = []
            for level in CODED:
                for i, row_mask in bins_of(level, grid_h, r * rows, rows):
                    for g, (j, col_mask) in enumerate(bins_of(level, grid_w, c * cols, cols)):
                        key = (row_mask.tobytes(), col_mask.tobytes())
                        if key not in units:
                            units.append(key)
                            at = len(units) - 1
                            row_masks[r, c, at] = row_mask
                            col_masks[r, c, at] = col_mask
                        at = units.index(key)
                        width = 1 if level == 2 else 2
                        for s in range(2):
                            target = s * STRIP_ALL + STRIP_ALL_AT[level] + i * width + g
                            strip[c, target, r, s * UNITS + at] = 1.0
            assert len(units) <= UNITS
    for r in range(row_strips):
        for level in CODED:
            width = 1 if level == 2 else 2
            start = first_bin(level, grid_h, r * rows, rows)
            for k in range(NEAR[level] * width):
                for s in range(2):
                    source = s * STRIP_ALL + STRIP_ALL_AT[level] + start * width + k
                    near[r, s * STRIP_UNITS + STRIP_AT[level] + k, source] = 1.0
    for c in range(col_strips):
        base = 0
        for level in LEVELS:
            source = 2 if level == 1 else level
            width = 1 if source == 2 else 2
            start = first_bin(level, grid_w, c * cols, cols)
            for p in range(col_strips):
                for g, (j, _) in enumerate(bins_of(source, grid_w, p * cols, cols)):
                    j = 0 if level == 1 else j - start
                    if not 0 <= j < NEAR[level]:
                        continue
                    for i in range(NEAR[source]):
                        for s in range(2):
                            cell = 0 if level == 1 else i * NEAR[level] + j
                            at = base + s * SLOTS[level] + cell
                            bins[c, at, p, s * STRIP_UNITS + STRIP_AT[source] + i * width + g] = 1.0
            base += 2 * SLOTS[level]
    for table, strips, size, along_rows in ((row_scale, row_strips, rows, True), (col_scale, col_strips, cols, False)):
        for at in range(strips):
            base = 0
            for level in LEVELS:
                length = size * strips
                start = first_bin(level, length, at * size, size)
                sizes = [mask.sum() for _, mask in bins_of(level, length, 0, length)]
                for i in range(NEAR[level]):
                    for j in range(NEAR[level]):
                        for s in range(2):
                            k = base + s * SLOTS[level] + i * NEAR[level] + j
                            table[at, 0, k] = 1.0 / sizes[start + (i if along_rows else j)]
                base += 2 * SLOTS[level]
    strip = strip.reshape(col_strips, 2 * STRIP_ALL, -1)
    return row_masks, col_masks, strip, near, bins.reshape(col_strips, slots, -1), row_scale, col_scale


def upsample_weights(level, length, first, count):
    places = first + np.arange(count)
    numer = np.maximum((2 * places + 1) * level - length, 0)
    lower = numer // (2 * length)
    frac = (numer - lower * 2 * length).astype(np.float32) / np.float32(2.0 * length)
    upper = np.minimum(lower + 1, level - 1)
    cells = np.arange(level)[None, :]
    weight = (cells == lower[:, None]) * (1.0 - frac)[:, None] + (cells == upper[:, None]) * frac[:, None]
    inside = (places >= 0) & (places < length)
    return (weight * inside[:, None]).astype(np.float32)


def upsample_tables(rows, row_strips, cols, col_strips):
    width = TAPS * sum(SLOTS.values())
    cells = sum(NEAR.values())
    spread = np.zeros((2, 64, width), np.float32)

    def strips_of(size, strips):
        table = np.zeros((strips, size, 64), np.float32)
        length = size * strips
        for strip in range(strips):
            first = 0
            for level in LEVELS:
                start = first_bin(level, length, strip * size, size)
                for a in range(3):
                    w = upsample_weights(level, length, strip * size + a - 1, size)
                    at = a * cells + first
                    table[strip, :, at : at + NEAR[level]] = w[:, start : start + NEAR[level]]
                first += NEAR[level]
        return table

    base, first = 0, 0
    for level in LEVELS:
        for a in range(3):
            for c in range(3):
                for i in range(NEAR[level]):
                    for j in range(NEAR[level]):
                        at = base + (a * 3 + c) * SLOTS[level] + i * NEAR[level] + j
                        spread[0, a * cells + first + i, at] = 1.0
                        spread[1, c * cells + first + j, at] = 1.0
        base += TAPS * SLOTS[level]
        first += NEAR[level]
    return strips_of(rows, row_strips), strips_of(cols, col_strips), spread


def layer_norm(tokens, gain):
    x = tokens.astype(f32)
    center = jnp.mean(x, axis=-1, keepdims=True)
    x = x - center
    spread = jnp.mean(x * x, axis=-1, keepdims=True)
    return (x * lax.rsqrt(spread + EPS) * gain).astype(bf16)


def dot(a, b):
    return jnp.dot(a, b, preferred_element_type=f32)


def project_kernel(tokens_ref, above_ref, below_ref, gain_ref, wq_hbm, wkv_hbm, q_ref, kv_ref, wq, wkv, sems):
    rows, cols, inner = q_ref.shape
    first = pl.program_id(0) == 0
    fetches = (
        pltpu.make_async_copy(wq_hbm, wq, sems.at[0]),
        pltpu.make_async_copy(wkv_hbm, wkv, sems.at[1]),
    )

    @pl.when(first)
    def _():
        for fetch in fetches:
            fetch.start()

    gain = gain_ref[...]
    normed = layer_norm(tokens_ref[...], gain)
    edge = layer_norm(jnp.concatenate([above_ref[...], below_ref[...]], axis=0), gain)

    @pl.when(first)
    def _():
        for fetch in fetches:
            fetch.wait()

    q_ref[...] = dot(normed, wq[...]).astype(bf16).astype(f32).reshape(rows, cols, inner)
    kv_ref[HALO : rows + HALO] = dot(normed, wkv[...]).astype(bf16).astype(f32).reshape(rows, cols, -1)
    edge = dot(edge, wkv[...]).astype(bf16).astype(f32).reshape(2 * HALO, cols, -1)
    kv_ref[0:HALO] = edge[:HALO]
    kv_ref[rows + HALO :] = edge[HALO:]


def window_bias(bias, first_row, first_col, grid_h, grid_w):
    span = BLOCK + 2 * HALO
    key = lax.broadcasted_iota(jnp.int32, bias.shape[2:], 0)
    extra = key - span * BLOCK
    lane = extra & 7
    odd = ((lane >= 2) & (lane < 6)).astype(jnp.int32)
    west = (lane >= 6) | ((lane >= 2) & (lane < 4))
    main = key < span * BLOCK
    row = jnp.where(main, key >> 3, 2 * (extra >> 3) + odd) - HALO
    col = jnp.where(main, key & 7, (key & 1) + jnp.where(west, -HALO, BLOCK))
    for a in range(bias.shape[0]):
        at = row + (first_row + a * BLOCK)
        row_ok = (at >= 0) & (at < grid_h)
        for b in range(bias.shape[1]):
            at = col + (first_col + b * BLOCK)
            bias[a, b] = jnp.where(row_ok & (at >= 0) & (at < grid_w), 0.0, -1e30)


def attend_kernel(
    grid_shape, place_ref, q_ref, kv_ref, sides_ref, tokens_ref, gain_ref, wkv_ref, wout_ref, masks_ref,
    attended_ref, sums_ref, sides, context, bias, pool, scores, weights,
):
    rows, cols, inner = q_ref.shape
    groups = cols // BLOCK
    span = BLOCK + 2 * HALO

    @pl.when(pl.program_id(0) == 0)
    def _():
        window_bias(bias, place_ref[0] * rows, place_ref[1] * cols, *grid_shape)
        masks = masks_ref[...].astype(bf16)
        unit = lax.broadcasted_iota(jnp.int32, (masks.shape[1], rows * cols), 0)
        token = lax.broadcasted_iota(jnp.int32, (masks.shape[1], rows * cols), 1)
        to_row = (unit == token // cols).astype(f32).astype(bf16)
        to_col = (unit - rows == token % cols).astype(f32).astype(bf16)
        pool[...] = (dot(masks, to_row) * dot(masks, to_col)).astype(bf16)
        ends = layer_norm(sides_ref[...].reshape(-1, sides_ref.shape[-1]), gain_ref[...])
        ends = dot(ends, wkv_ref[...]).astype(bf16).astype(f32)
        sides[...] = ends.reshape(sides.shape)

    sheet = pl.program_id(0)
    count = BLOCK * BLOCK
    heads = 128 // HEAD_DIM
    head_of_row = lax.broadcasted_iota(jnp.int32, (heads, count, 128), 0)
    head_of_lane = lax.broadcasted_iota(jnp.int32, (heads, count, 128), 2) // HEAD_DIM
    own = (head_of_row == head_of_lane).astype(f32).astype(bf16).reshape(heads * count, 128)
    lane = lax.broadcasted_iota(jnp.int32, (count, 128), 1)
    place = lax.broadcasted_iota(jnp.int32, (span // 2, BLOCK, 128), 1)
    factor = math.log2(math.e) / math.sqrt(HEAD_DIM)

    def band(a, carry):
        at = pl.multiple_of(a * BLOCK, BLOCK)

        def keys_of(b, lanes):
            mid = slice(b * BLOCK, (b + 1) * BLOCK)
            main = kv_ref[pl.ds(at, span), mid, lanes].reshape(span * BLOCK, 128)

            def beside(g):
                if g < 0 or g >= groups:
                    found = sides[sheet, pl.ds(at, span), :, lanes]
                else:
                    found = kv_ref[pl.ds(at, span), g * BLOCK : (g + 1) * BLOCK, lanes]
                return found.reshape(span // 2, 2, BLOCK, 128)

            west, east = beside(b - 1), beside(b + 1)
            even = jnp.where(place >= 6, west[:, 0], east[:, 0])
            odd = pltpu.roll(jnp.where(place >= 6, west[:, 1], east[:, 1]), 4, 1)
            extra = jnp.where((place >= 6) | (place < 2), even, odd).reshape(span * 4, 128)
            return jnp.concatenate([main, extra], axis=0).astype(bf16)

        tiles = inner // 128

        def score(b, slot):
            mid = slice(b * BLOCK, (b + 1) * BLOCK)
            low = bias[a, b]
            for t in range(tiles):
                lanes = slice(t * 128, (t + 1) * 128)
                q = q_ref[pl.ds(at, BLOCK), mid, lanes].reshape(count, 128).astype(bf16)
                q = jnp.concatenate([q] * heads, axis=0) * own
                found = lax.dot_general(keys_of(b, lanes), q, (((1,), (1,)), ((), ())), preferred_element_type=f32)
                scores[slot, t] = found + jnp.concatenate([low] * (heads * count // 128), axis=1)

        def soften(slot):
            for t in range(tiles):
                for h in range(heads * count // 128):
                    lanes = slice(h * 128, (h + 1) * 128)
                    found = scores[slot, t, :, lanes]
                    top = jnp.max(found, axis=0, keepdims=True)
                    expon = jnp.exp2((found - top) * factor)
                    weights[slot, t, :, lanes] = (expon * (1.0 / jnp.sum(expon, axis=0, keepdims=True))).astype(bf16)

        def mix(b, slot):
            mid = slice(b * BLOCK, (b + 1) * BLOCK)
            for t in range(tiles):
                lanes = slice(t * 128, (t + 1) * 128)
                values = keys_of(b, slice(inner + t * 128, inner + (t + 1) * 128))
                mixed = lax.dot_general(weights[slot, t], values, (((0,), (0,)), ((), ())), preferred_element_type=f32)
                mixed = mixed.reshape(heads, count, 128)
                piece = mixed[0]
                for k in range(1, heads):
                    piece = jnp.where(lane >= k * HEAD_DIM, mixed[k], piece)
                context[pl.ds(at, BLOCK), mid, lanes] = piece.reshape(BLOCK, BLOCK, 128)

        score(0, 0)
        for b in range(groups):
            if b + 1 < groups:
                score(b + 1, (b + 1) % 2)
            soften(b % 2)
            mix(b, b % 2)
        return carry

    lax.fori_loop(0, rows // BLOCK, band, 0)
    mixed = context[...].reshape(rows * cols, inner).astype(bf16)
    attended = (tokens_ref[...].astype(f32) + dot(mixed, wout_ref[...])).astype(bf16)
    attended_ref[...] = attended
    sums = dot(pool[...], attended).astype(bf16)
    sums_ref[...] = jnp.broadcast_to(sums[None], sums_ref.shape)


def combine_kernel(place_ref, near_ref, table_ref, parts_ref, out_ref):
    table = dot(near_ref[...], table_ref[...]).astype(bf16)
    added = dot(table, parts_ref[...]).astype(bf16)
    out_ref[...] = jnp.broadcast_to(added[None], out_ref.shape)


def conv_kernel(attended_ref, top_ref, bottom_ref, left_ref, right_ref, w_ref, out_ref, ext):
    sheets, area, _ = attended_ref.shape
    cols = top_ref.shape[1]
    rows = area // cols
    out_ch = out_ref.shape[-1]
    step = pl.program_id(0)

    def edge(ref, s):
        total = 0.0
        for a in range(3):
            total = total + dot(ref[s], w_ref[a])[a : a + rows]
        return total.reshape(rows, 1, out_ch)

    def middle(s):
        total = dot(ext[s, 0:area], w_ref[0])
        for a in range(1, 3):
            total = total + dot(ext[s, a * cols : a * cols + area], w_ref[a])
        return total.reshape(rows, cols, out_ch)

    @pl.when(step == 0)
    def _():
        place = lax.broadcasted_iota(jnp.int32, (rows, cols, out_ch), 1)
        for s in range(sheets):
            ext[s, 0:cols] = top_ref[s]
            ext[s, cols : cols + area] = attended_ref[s]
            ext[s, cols + area :] = bottom_ref[s]
            part = jnp.where(place == 0, edge(left_ref, s), pltpu.roll(middle(s), 1, 1))
            out_ref[s] = part.reshape(area, out_ch)

    @pl.when(step == 1)
    def _():
        for s in range(sheets):
            out_ref[s] += middle(s).reshape(area, out_ch)

    @pl.when(step == 2)
    def _():
        place = lax.broadcasted_iota(jnp.int32, (rows, cols, out_ch), 1)
        for s in range(sheets):
            part = jnp.where(place == cols - 1, edge(right_ref, s), pltpu.roll(middle(s), cols - 1, 1))
            out_ref[s] += part.reshape(area, out_ch)


def split(x):
    high = x.astype(bf16)
    return high, (x - high.astype(f32)).astype(bf16)


def tail_kernel(
    place_ref, table_ref, row_scale_ref, col_scale_ref, parts_ref, wpool_hbm, wjoin_hbm, by_row_ref, by_col_ref,
    spread_ref, conv_hbm, out_ref, taps, wpool, wjoin, conv, sems,
):
    width, ppm = wpool.shape[1], wpool.shape[2]
    count = len(LEVELS)
    copies = [pltpu.make_async_copy(wpool_hbm.at[k], wpool.at[k], sems.at[k]) for k in range(count)]
    for k in range(count):
        lines = slice(width + k * ppm, width + (k + 1) * ppm)
        copies.append(pltpu.make_async_copy(wjoin_hbm.at[:, :, lines, :], wjoin.at[k], sems.at[count + k]))
    copies.append(pltpu.make_async_copy(conv_hbm, conv, sems.at[2 * count]))
    ahead = 3
    for copy in copies[:ahead]:
        copy.start()

    def ready(k):
        copies[k].wait()
        if k + ahead < len(copies):
            copies[k + ahead].start()

    rows, cols = by_row_ref.shape[0], by_col_ref.shape[0]

    def along(ref, axis):
        high, low = split(ref[...])
        return dot(high, spread_ref[axis]) + dot(low, spread_ref[axis])

    grid = along(by_row_ref, 0)[:, None, :] * along(by_col_ref, 1)[None, :, :]
    grid_high, grid_low = split(grid.reshape(rows * cols, -1))
    scale = row_scale_ref[...] * col_scale_ref[...]
    scale = jnp.broadcast_to(scale, (128, scale.shape[1])).T[:, :1]
    pooled = dot(table_ref[...], parts_ref[...]) * scale
    branches = []
    row = 0
    for index, level in enumerate(LEVELS):
        slots = SLOTS[level]
        high, low = split(pooled[row : row + 2 * slots])
        ready(index)
        both = dot(jnp.concatenate([high, low], axis=0), wpool[index])
        high, low = split(jnp.maximum(both[: 2 * slots] + both[2 * slots :], 0.0))
        branches.append(jnp.concatenate([high, low], axis=0))
        row += 2 * slots
    at = 0
    for index, level in enumerate(LEVELS):
        slots = SLOTS[level]
        ready(count + index)
        for a in range(3):
            for c in range(3):
                tap = dot(branches[index], wjoin[index, a, c])
                tap = tap[: 2 * slots] + tap[2 * slots :]
                start = at + (a * 3 + c) * slots
                for s in range(2):
                    taps[s, start : start + slots, :] = tap[s * slots : (s + 1) * slots]
        at += TAPS * slots
    ready(2 * count)
    for s in range(2):
        high, low = split(taps[s])
        total = conv[s] + dot(grid_high, high) + dot(grid_low, high) + dot(grid_high, low)
        out_ref[s] = total.astype(bf16)


def cost(flops, nbytes, transcendentals=0):
    return pl.CostEstimate(flops=int(flops), bytes_accessed=int(nbytes), transcendentals=int(transcendentals))


def params(mib):
    return pltpu.CompilerParams(vmem_limit_bytes=mib * 2**20)


def whole(shape):
    return pl.BlockSpec(shape, lambda *_: (0,) * len(shape))


def in_hbm(x):
    return pltpu.with_memory_space_constraint(x, pltpu.HBM)


def shifts(axis):
    count = lax.axis_size(axis)
    forward = [(i, i + 1) for i in range(count - 1)]
    return forward, [(j, i) for i, j in forward]


def layer(tokens, norm_gain, w_query, w_kv, w_out, w_pool, w_join):
    sheets, rows, cols, width = tokens.shape
    inner = w_query.shape[1]
    wide = w_kv.shape[1]
    out_ch = w_join.shape[-1]
    ppm = w_pool.shape[-1]
    area = rows * cols
    row_count, col_count = lax.axis_size("row"), lax.axis_size("col")
    r, c = lax.axis_index("row"), lax.axis_index("col")
    grid_h, grid_w = rows * row_count, cols * col_count
    gain = norm_gain.reshape(1, width)
    tables = pool_tables(rows, row_count, cols, col_count)
    row_masks, col_masks, strip_table, near_table, bin_table, row_scale, col_scale = tables
    by_row, by_col, spread = upsample_tables(rows, row_count, cols, col_count)
    masks = np.concatenate([row_masks, col_masks], axis=-1).reshape(row_count * col_count, UNITS, rows + cols)

    at = jnp.stack([r, c]).astype(jnp.int32)
    row_fwd, row_bwd = shifts("row")
    col_fwd, col_bwd = shifts("col")
    above = lax.ppermute(tokens[:, rows - HALO :], "row", row_fwd)
    below = lax.ppermute(tokens[:, :HALO], "row", row_bwd)

    def edges(first):
        return jnp.concatenate([x[:, :, first : first + HALO] for x in (above, tokens, below)], axis=1)

    west = lax.ppermute(edges(cols - HALO), "col", col_fwd)
    east = lax.ppermute(edges(0), "col", col_bwd)

    def per_sheet(*dims):
        return pl.BlockSpec((None,) + dims, lambda s: (s,) + (0,) * len(dims))

    flat = tokens.reshape(sheets, area, width)
    edge = HALO * cols
    q, kv = pl.pallas_call(
        project_kernel,
        grid=(sheets,),
        in_specs=[
            per_sheet(area, width), per_sheet(edge, width), per_sheet(edge, width),
            whole((1, width)), pl.BlockSpec(memory_space=pl.ANY), pl.BlockSpec(memory_space=pl.ANY),
        ],
        out_specs=[per_sheet(rows, cols, inner), per_sheet(rows + 2 * HALO, cols, wide)],
        out_shape=[
            jax.ShapeDtypeStruct((sheets, rows, cols, inner), f32),
            jax.ShapeDtypeStruct((sheets, rows + 2 * HALO, cols, wide), f32),
        ],
        scratch_shapes=[
            pltpu.VMEM((width, inner), bf16), pltpu.VMEM((width, wide), bf16), pltpu.SemaphoreType.DMA((2,)),
        ],
        compiler_params=params(28),
        cost_estimate=cost(2 * sheets * area * width * (inner + wide), 2 * (width * (inner + wide) + 5 * sheets * area * width)),
        name="project",
    )(flat, above.reshape(sheets, edge, width), below.reshape(sheets, edge, width), gain, in_hbm(w_query), in_hbm(w_kv))

    blank = jnp.zeros((sheets, rows + 2 * HALO, BLOCK - 2 * HALO, width), bf16)
    sides = jnp.concatenate([east, blank, west], axis=2).reshape(sheets, (rows + 2 * HALO) * BLOCK, width)
    blocks = (rows // BLOCK) * (cols // BLOCK)
    keys = (BLOCK + 2 * HALO) ** 2

    def fixed(*dims):
        return whole(dims)

    attended, sums = pl.pallas_call(
        lambda *refs: attend_kernel((grid_h, grid_w), *refs),
        grid_spec=pltpu.PrefetchScalarGridSpec(
            num_scalar_prefetch=1,
            grid=(sheets,),
            in_specs=[
                pl.BlockSpec((None, rows, cols, inner), lambda s, _: (s, 0, 0, 0)),
                pl.BlockSpec((None, rows + 2 * HALO, cols, wide), lambda s, _: (s, 0, 0, 0)),
                fixed(sheets, (rows + 2 * HALO) * BLOCK, width),
                pl.BlockSpec((None, area, width), lambda s, _: (s, 0, 0)),
                fixed(1, width), fixed(width, wide), fixed(inner, width),
                pl.BlockSpec((None, UNITS, rows + cols), lambda s, p: (p[0] * col_count + p[1], 0, 0)),
            ],
            out_specs=[
                pl.BlockSpec((None, area, width), lambda s, _: (s, 0, 0)),
                pl.BlockSpec((row_count, UNITS, width), lambda s, _: (0, s, 0)),
            ],
            scratch_shapes=[
                pltpu.VMEM((sheets, rows + 2 * HALO, BLOCK, wide), f32),
                pltpu.VMEM((rows, cols, inner), f32),
                pltpu.VMEM((rows // BLOCK, cols // BLOCK, keys, 128), f32),
                pltpu.VMEM((UNITS, area), bf16),
                pltpu.VMEM((2, inner // 128, keys, 256), f32),
                pltpu.VMEM((2, inner // 128, keys, 256), bf16),
            ],
        ),
        out_shape=[
            jax.ShapeDtypeStruct((sheets, area, width), bf16),
            jax.ShapeDtypeStruct((row_count, sheets * UNITS, width), bf16),
        ],
        compiler_params=params(32),
        cost_estimate=cost(2 * sheets * area * inner * width * 4, 2 * sheets * area * width * 4, sheets * blocks * keys * 1024),
        name="attend",
    )(at, q, kv, sides, flat, gain, w_kv, w_out, jnp.asarray(masks))

    att = attended.reshape(sheets, rows, cols, width)
    strip_rows = sheets * STRIP_UNITS
    att_above = lax.ppermute(att[:, rows - 1 :], "row", row_fwd)
    att_below = lax.ppermute(att[:, :1], "row", row_bwd)
    parts = lax.all_to_all(sums, "row", 0, 0, tiled=True).reshape(row_count * sheets * UNITS, width)

    def att_edges(first):
        return jnp.concatenate([x[:, :, first] for x in (att_above, att, att_below)], axis=1)

    att_west = lax.ppermute(att_edges(cols - 1), "col", col_fwd)
    att_east = lax.ppermute(att_edges(0), "col", col_bwd)
    pad = ((0, 0), (0, 6), (0, 0))
    att_west, att_east = jnp.pad(att_west, pad), jnp.pad(att_east, pad)

    strips = pl.pallas_call(
        combine_kernel,
        grid_spec=pltpu.PrefetchScalarGridSpec(
            num_scalar_prefetch=1,
            grid=(1,),
            in_specs=[
                pl.BlockSpec((None,) + near_table.shape[1:], lambda k, p: (p[0], 0, 0)),
                pl.BlockSpec((None,) + strip_table.shape[1:], lambda k, p: (p[1], 0, 0)),
                fixed(row_count * sheets * UNITS, width),
            ],
            out_specs=fixed(col_count, strip_rows, width),
        ),
        out_shape=jax.ShapeDtypeStruct((col_count, strip_rows, width), bf16),
        compiler_params=params(8),
        name="combine",
    )(at, near_table.astype(bf16), strip_table.astype(bf16), parts)
    strips = lax.all_to_all(strips, "col", 0, 0, tiled=True).reshape(col_count * strip_rows, width)

    conv = pl.pallas_call(
        conv_kernel,
        grid=(3,),
        in_specs=[
            whole((sheets, area, width)), whole((sheets, cols, width)), whole((sheets, cols, width)),
            whole((sheets, rows + 8, width)), whole((sheets, rows + 8, width)),
            pl.BlockSpec((3, None, width, out_ch), lambda k: (0, k, 0, 0)),
        ],
        out_specs=whole((sheets, area, out_ch)),
        out_shape=pltpu.HBM((sheets, area, out_ch), f32),
        scratch_shapes=[pltpu.VMEM((sheets, area + 2 * cols, width), bf16)],
        compiler_params=params(52),
        cost_estimate=cost(2 * sheets * area * width * 9 * out_ch, 2 * 9 * width * out_ch + 2 * sheets * area * width),
        name="conv",
    )(attended, att_above.reshape(sheets, cols, width), att_below.reshape(sheets, cols, width), att_west, att_east, w_join)

    depth = TAPS * sum(SLOTS.values())
    bin_rows = 2 * sum(SLOTS.values())
    out = pl.pallas_call(
        tail_kernel,
        grid_spec=pltpu.PrefetchScalarGridSpec(
            num_scalar_prefetch=1,
            grid=(1,),
            in_specs=[
                pl.BlockSpec((None,) + bin_table.shape[1:], lambda k, p: (p[1], 0, 0)),
                pl.BlockSpec((None, 1, bin_rows), lambda k, p: (p[0], 0, 0)),
                pl.BlockSpec((None, 1, bin_rows), lambda k, p: (p[1], 0, 0)),
                fixed(col_count * strip_rows, width),
                pl.BlockSpec(memory_space=pl.ANY), pl.BlockSpec(memory_space=pl.ANY),
                pl.BlockSpec((None, rows, 64), lambda k, p: (p[0], 0, 0)),
                pl.BlockSpec((None, cols, 64), lambda k, p: (p[1], 0, 0)),
                fixed(2, 64, depth), pl.BlockSpec(memory_space=pl.ANY),
            ],
            out_specs=fixed(sheets, area, out_ch),
            scratch_shapes=[
                pltpu.VMEM((sheets, depth, out_ch), f32),
                pltpu.VMEM(w_pool.shape, bf16),
                pltpu.VMEM((len(LEVELS), 3, 3, ppm, out_ch), bf16),
                pltpu.VMEM((sheets, area, out_ch), f32),
                pltpu.SemaphoreType.DMA((2 * len(LEVELS) + 1,)),
            ],
        ),
        out_shape=jax.ShapeDtypeStruct((sheets, area, out_ch), bf16),
        compiler_params=params(56),
        cost_estimate=cost(4e9, 2 * (w_pool.size + 9 * 4 * ppm * out_ch)),
        name="tail",
    )(
        at, bin_table.astype(bf16), row_scale, col_scale, strips, in_hbm(w_pool), in_hbm(w_join),
        by_row, by_col, spread.astype(bf16), in_hbm(conv),
    )
    return out.reshape(sheets, rows, cols, out_ch)


def solution(mesh):
    placed = (P(None, "row", "col", None), P(), P(), P(), P(), P(), P())
    return jax.shard_map(layer, mesh=mesh, in_specs=placed, out_specs=P(None, "row", "col", None), check_vma=False)
```

```python
import math

import jax
import jax.numpy as jnp
import numpy as np
from jax import lax
from jax.experimental import pallas as pl
from jax.experimental.pallas import tpu as pltpu
from jax.sharding import PartitionSpec as P

HEAD_DIM = 32
BLOCK = 8
HALO = 2
EPS = 1e-05
LEVELS = (1, 2, 3, 6)
CODED = (6, 3, 2)
UNITS = 8
STRIP_ALL = 24
STRIP_ALL_AT = {6: 0, 3: 12, 2: 18}
STRIP_UNITS = 16
STRIP_AT = {6: 0, 3: 6, 2: 12}
NEAR = {1: 1, 2: 2, 3: 3, 6: 3}
SLOTS = {1: 8, 2: 8, 3: 16, 6: 16}
TAPS = 9
f32 = jnp.float32
bf16 = jnp.bfloat16


def bins_of(level, length, first, count):
    places = first + np.arange(count)
    found = []
    for cell in range(level):
        start = cell * length // level
        end = ((cell + 1) * length + level - 1) // level
        mask = (places >= start) & (places < end)
        if mask.any():
            found.append((cell, mask))
    return found


def lower_bin(level, length, place):
    return max((2 * place + 1) * level - length, 0) // (2 * length)


def first_bin(level, length, first, count):
    start = min(lower_bin(level, length, first - 1), level - NEAR[level])
    assert min(lower_bin(level, length, first + count) + 1, level - 1) < start + NEAR[level]
    return start


def pool_tables(rows, row_strips, cols, col_strips):
    grid_h, grid_w = rows * row_strips, cols * col_strips
    row_masks = np.zeros((row_strips, col_strips, UNITS, rows), np.float32)
    col_masks = np.zeros((row_strips, col_strips, UNITS, cols), np.float32)
    strip = np.zeros((col_strips, 2 * STRIP_ALL, row_strips, 2 * UNITS), np.float32)
    near = np.zeros((row_strips, 2 * STRIP_UNITS, 2 * STRIP_ALL), np.float32)
    slots = 2 * sum(SLOTS.values())
    bins = np.zeros((col_strips, slots, col_strips, 2 * STRIP_UNITS), np.float32)
    row_scale = np.zeros((row_strips, 1, slots), np.float32)
    col_scale = np.zeros((col_strips, 1, slots), np.float32)
    for c in range(col_strips):
        for r in range(row_strips):
            units = []
            for level in CODED:
                for i, row_mask in bins_of(level, grid_h, r * rows, rows):
                    for g, (j, col_mask) in enumerate(bins_of(level, grid_w, c * cols, cols)):
                        key = (row_mask.tobytes(), col_mask.tobytes())
                        if key not in units:
                            units.append(key)
                            at = len(units) - 1
                            row_masks[r, c, at] = row_mask
                            col_masks[r, c, at] = col_mask
                        at = units.index(key)
                        width = 1 if level == 2 else 2
                        for s in range(2):
                            target = s * STRIP_ALL + STRIP_ALL_AT[level] + i * width + g
                            strip[c, target, r, s * UNITS + at] = 1.0
            assert len(units) <= UNITS
    for r in range(row_strips):
        for level in CODED:
            width = 1 if level == 2 else 2
            start = first_bin(level, grid_h, r * rows, rows)
            for k in range(NEAR[level] * width):
                for s in range(2):
                    source = s * STRIP_ALL + STRIP_ALL_AT[level] + start * width + k
                    near[r, s * STRIP_UNITS + STRIP_AT[level] + k, source] = 1.0
    for c in range(col_strips):
        base = 0
        for level in LEVELS:
            source = 2 if level == 1 else level
            width = 1 if source == 2 else 2
            start = first_bin(level, grid_w, c * cols, cols)
            for p in range(col_strips):
                for g, (j, _) in enumerate(bins_of(source, grid_w, p * cols, cols)):
                    j = 0 if level == 1 else j - start
                    if not 0 <= j < NEAR[level]:
                        continue
                    for i in range(NEAR[source]):
                        for s in range(2):
                            cell = 0 if level == 1 else i * NEAR[level] + j
                            at = base + s * SLOTS[level] + cell
                            bins[c, at, p, s * STRIP_UNITS + STRIP_AT[source] + i * width + g] = 1.0
            base += 2 * SLOTS[level]
    for table, strips, size, along_rows in ((row_scale, row_strips, rows, True), (col_scale, col_strips, cols, False)):
        for at in range(strips):
            base = 0
            for level in LEVELS:
                length = size * strips
                start = first_bin(level, length, at * size, size)
                sizes = [mask.sum() for _, mask in bins_of(level, length, 0, length)]
                for i in range(NEAR[level]):
                    for j in range(NEAR[level]):
                        for s in range(2):
                            k = base + s * SLOTS[level] + i * NEAR[level] + j
                            table[at, 0, k] = 1.0 / sizes[start + (i if along_rows else j)]
                base += 2 * SLOTS[level]
    strip = strip.reshape(col_strips, 2 * STRIP_ALL, -1)
    return row_masks, col_masks, strip, near, bins.reshape(col_strips, slots, -1), row_scale, col_scale


def upsample_weights(level, length, first, count):
    places = first + np.arange(count)
    numer = np.maximum((2 * places + 1) * level - length, 0)
    lower = numer // (2 * length)
    frac = (numer - lower * 2 * length).astype(np.float32) / np.float32(2.0 * length)
    upper = np.minimum(lower + 1, level - 1)
    cells = np.arange(level)[None, :]
    weight = (cells == lower[:, None]) * (1.0 - frac)[:, None] + (cells == upper[:, None]) * frac[:, None]
    inside = (places >= 0) & (places < length)
    return (weight * inside[:, None]).astype(np.float32)


def upsample_tables(rows, row_strips, cols, col_strips):
    width = TAPS * sum(SLOTS.values())
    cells = sum(NEAR.values())
    spread = np.zeros((2, 64, width), np.float32)

    def strips_of(size, strips):
        table = np.zeros((strips, size, 64), np.float32)
        length = size * strips
        for strip in range(strips):
            first = 0
            for level in LEVELS:
                start = first_bin(level, length, strip * size, size)
                for a in range(3):
                    w = upsample_weights(level, length, strip * size + a - 1, size)
                    at = a * cells + first
                    table[strip, :, at : at + NEAR[level]] = w[:, start : start + NEAR[level]]
                first += NEAR[level]
        return table

    base, first = 0, 0
    for level in LEVELS:
        for a in range(3):
            for c in range(3):
                for i in range(NEAR[level]):
                    for j in range(NEAR[level]):
                        at = base + (a * 3 + c) * SLOTS[level] + i * NEAR[level] + j
                        spread[0, a * cells + first + i, at] = 1.0
                        spread[1, c * cells + first + j, at] = 1.0
        base += TAPS * SLOTS[level]
        first += NEAR[level]
    return strips_of(rows, row_strips), strips_of(cols, col_strips), spread


def layer_norm(tokens, gain):
    x = tokens.astype(f32)
    center = jnp.mean(x, axis=-1, keepdims=True)
    x = x - center
    spread = jnp.mean(x * x, axis=-1, keepdims=True)
    return (x * lax.rsqrt(spread + EPS) * gain).astype(bf16)


def dot(a, b):
    return jnp.dot(a, b, preferred_element_type=f32)


def warm_kernel(gain_ref, wq_ref, wkv_ref, out_ref):
    out_ref[...] = gain_ref[...]


def project_kernel(tokens_ref, above_ref, below_ref, gain_ref, wq, wkv, q_ref, kv_ref):
    rows, cols, inner = q_ref.shape
    gain = gain_ref[...]
    normed = layer_norm(tokens_ref[...], gain)
    q_ref[...] = dot(normed, wq[...]).astype(bf16).astype(f32).reshape(rows, cols, inner)
    kv_ref[HALO : rows + HALO] = dot(normed, wkv[...]).astype(bf16).astype(f32).reshape(rows, cols, -1)
    edge = layer_norm(jnp.concatenate([above_ref[...], below_ref[...]], axis=0), gain)
    edge = dot(edge, wkv[...]).astype(bf16).astype(f32).reshape(2 * HALO, cols, -1)
    kv_ref[0:HALO] = edge[:HALO]
    kv_ref[rows + HALO :] = edge[HALO:]


def window_bias(bias, first_row, first_col, grid_h, grid_w):
    span = BLOCK + 2 * HALO
    key = lax.broadcasted_iota(jnp.int32, bias.shape[2:], 0)
    extra = key - span * BLOCK
    lane = extra & 7
    odd = ((lane >= 2) & (lane < 6)).astype(jnp.int32)
    west = (lane >= 6) | ((lane >= 2) & (lane < 4))
    main = key < span * BLOCK
    row = jnp.where(main, key >> 3, 2 * (extra >> 3) + odd) - HALO
    col = jnp.where(main, key & 7, (key & 1) + jnp.where(west, -HALO, BLOCK))
    for a in range(bias.shape[0]):
        at = row + (first_row + a * BLOCK)
        row_ok = (at >= 0) & (at < grid_h)
        for b in range(bias.shape[1]):
            at = col + (first_col + b * BLOCK)
            bias[a, b] = jnp.where(row_ok & (at >= 0) & (at < grid_w), 0.0, -1e30)


def attend_kernel(
    grid_shape, place_ref, q_ref, kv_ref, sides_ref, tokens_ref, gain_ref, wkv_ref, wout_ref, masks_ref,
    attended_ref, sums_ref, sides, context, bias, pool, scores, weights,
):
    rows, cols, inner = q_ref.shape
    groups = cols // BLOCK
    span = BLOCK + 2 * HALO

    @pl.when(pl.program_id(0) == 0)
    def _():
        window_bias(bias, place_ref[0] * rows, place_ref[1] * cols, *grid_shape)
        masks = masks_ref[...].astype(bf16)
        unit = lax.broadcasted_iota(jnp.int32, (masks.shape[1], rows * cols), 0)
        token = lax.broadcasted_iota(jnp.int32, (masks.shape[1], rows * cols), 1)
        to_row = (unit == token // cols).astype(f32).astype(bf16)
        to_col = (unit - rows == token % cols).astype(f32).astype(bf16)
        pool[...] = (dot(masks, to_row) * dot(masks, to_col)).astype(bf16)
        ends = layer_norm(sides_ref[...].reshape(-1, sides_ref.shape[-1]), gain_ref[...])
        ends = dot(ends, wkv_ref[...]).astype(bf16).astype(f32)
        sides[...] = ends.reshape(sides.shape)

    sheet = pl.program_id(0)
    count = BLOCK * BLOCK
    heads = 128 // HEAD_DIM
    head_of_row = lax.broadcasted_iota(jnp.int32, (heads, count, 128), 0)
    head_of_lane = lax.broadcasted_iota(jnp.int32, (heads, count, 128), 2) // HEAD_DIM
    own = (head_of_row == head_of_lane).astype(f32).astype(bf16).reshape(heads * count, 128)
    lane = lax.broadcasted_iota(jnp.int32, (count, 128), 1)
    place = lax.broadcasted_iota(jnp.int32, (span // 2, BLOCK, 128), 1)
    factor = math.log2(math.e) / math.sqrt(HEAD_DIM)

    def band(a, carry):
        at = pl.multiple_of(a * BLOCK, BLOCK)

        def keys_of(b, lanes):
            mid = slice(b * BLOCK, (b + 1) * BLOCK)
            main = kv_ref[pl.ds(at, span), mid, lanes].reshape(span * BLOCK, 128)

            def beside(g):
                if g < 0 or g >= groups:
                    found = sides[sheet, pl.ds(at, span), :, lanes]
                else:
                    found = kv_ref[pl.ds(at, span), g * BLOCK : (g + 1) * BLOCK, lanes]
                return found.reshape(span // 2, 2, BLOCK, 128)

            west, east = beside(b - 1), beside(b + 1)
            even = jnp.where(place >= 6, west[:, 0], east[:, 0])
            odd = pltpu.roll(jnp.where(place >= 6, west[:, 1], east[:, 1]), 4, 1)
            extra = jnp.where((place >= 6) | (place < 2), even, odd).reshape(span * 4, 128)
            return jnp.concatenate([main, extra], axis=0).astype(bf16)

        tiles = inner // 128

        def score(b, slot):
            mid = slice(b * BLOCK, (b + 1) * BLOCK)
            low = bias[a, b]
            for t in range(tiles):
                lanes = slice(t * 128, (t + 1) * 128)
                q = q_ref[pl.ds(at, BLOCK), mid, lanes].reshape(count, 128).astype(bf16)
                q = jnp.concatenate([q] * heads, axis=0) * own
                found = lax.dot_general(keys_of(b, lanes), q, (((1,), (1,)), ((), ())), preferred_element_type=f32)
                scores[slot, t] = found + jnp.concatenate([low] * (heads * count // 128), axis=1)

        def soften(slot):
            for t in range(tiles):
                for h in range(heads * count // 128):
                    lanes = slice(h * 128, (h + 1) * 128)
                    found = scores[slot, t, :, lanes]
                    top = jnp.max(found, axis=0, keepdims=True)
                    expon = jnp.exp2((found - top) * factor)
                    weights[slot, t, :, lanes] = (expon * (1.0 / jnp.sum(expon, axis=0, keepdims=True))).astype(bf16)

        def mix(b, slot):
            mid = slice(b * BLOCK, (b + 1) * BLOCK)
            for t in range(tiles):
                lanes = slice(t * 128, (t + 1) * 128)
                values = keys_of(b, slice(inner + t * 128, inner + (t + 1) * 128))
                mixed = lax.dot_general(weights[slot, t], values, (((0,), (0,)), ((), ())), preferred_element_type=f32)
                mixed = mixed.reshape(heads, count, 128)
                piece = mixed[0]
                for k in range(1, heads):
                    piece = jnp.where(lane >= k * HEAD_DIM, mixed[k], piece)
                context[pl.ds(at, BLOCK), mid, lanes] = piece.reshape(BLOCK, BLOCK, 128)

        score(0, 0)
        for b in range(groups):
            if b + 1 < groups:
                score(b + 1, (b + 1) % 2)
            soften(b % 2)
            mix(b, b % 2)
        return carry

    lax.fori_loop(0, rows // BLOCK, band, 0)
    mixed = context[...].reshape(rows * cols, inner).astype(bf16)
    attended = (tokens_ref[...].astype(f32) + dot(mixed, wout_ref[...])).astype(bf16)
    attended_ref[...] = attended
    sums = dot(pool[...], attended).astype(bf16)
    sums_ref[...] = jnp.broadcast_to(sums[None], sums_ref.shape)


def combine_kernel(place_ref, near_ref, table_ref, parts_ref, out_ref):
    table = dot(near_ref[...], table_ref[...]).astype(bf16)
    added = dot(table, parts_ref[...]).astype(bf16)
    out_ref[...] = jnp.broadcast_to(added[None], out_ref.shape)


def conv_kernel(attended_hbm, top_hbm, bottom_hbm, left_hbm, right_hbm, w_hbm, out_hbm, ext, ends, w, out, sems):
    sheets, area, width = attended_hbm.shape
    cols = top_hbm.shape[1]
    rows = area // cols
    out_ch = out.shape[-1]

    def tokens(s):
        return (
            pltpu.make_async_copy(attended_hbm.at[s], ext.at[s, cols : cols + area], sems.at[0, s]),
            pltpu.make_async_copy(top_hbm.at[s], ext.at[s, 0:cols], sems.at[1, s]),
            pltpu.make_async_copy(bottom_hbm.at[s], ext.at[s, cols + area :], sems.at[2, s]),
            pltpu.make_async_copy(left_hbm.at[s], ends.at[0, s], sems.at[3, s]),
            pltpu.make_async_copy(right_hbm.at[s], ends.at[1, s], sems.at[4, s]),
        )

    def taps(c):
        return pltpu.make_async_copy(w_hbm.at[:, c, 0:width, :], w.at[:, c], sems.at[5, c])

    def result(s):
        return pltpu.make_async_copy(out.at[s], out_hbm.at[s], sems.at[6, s])

    for copy in tokens(0):
        copy.start()
    for c in (1, 0, 2):
        taps(c).start()
    for s in range(1, sheets):
        for copy in tokens(s):
            copy.start()
    place = lax.broadcasted_iota(jnp.int32, (rows, cols, out_ch), 1)

    def sheet(s, carry):
        for copy in tokens(s):
            copy.wait()

        def edge(side, c):
            total = 0.0
            for a in range(3):
                total = total + dot(ends[side, s], w[a, c])[a : a + rows]
            return total.reshape(rows, 1, out_ch)

        def middle(c):
            @pl.when(s == 0)
            def _():
                taps(c).wait()

            total = dot(ext[s, 0:area], w[0, c])
            for a in range(1, 3):
                total = total + dot(ext[s, a * cols : a * cols + area], w[a, c])
            return total.reshape(rows, cols, out_ch)

        out[s] = middle(1).reshape(area, out_ch)
        part = pltpu.roll(middle(0), 1, 1)
        out[s] += jnp.where(place == 0, edge(0, 0), part).reshape(area, out_ch)
        part = pltpu.roll(middle(2), cols - 1, 1)
        out[s] += jnp.where(place == cols - 1, edge(1, 2), part).reshape(area, out_ch)
        result(s).start()
        return carry

    lax.fori_loop(0, sheets, sheet, 0)
    for s in range(sheets):
        result(s).wait()


def split(x):
    high = x.astype(bf16)
    return high, (x - high.astype(f32)).astype(bf16)


def tail_kernel(
    place_ref, table_hbm, row_scale_hbm, col_scale_hbm, parts_hbm, wpool_hbm, wjoin_hbm, by_row_hbm, by_col_hbm,
    spread_hbm, conv_hbm, out_hbm,
    table, row_scale, col_scale, parts, by_row, by_col, spread, wpool, wjoin, conv, taps, out, sems,
):
    width, ppm = wpool.shape[1], wpool.shape[2]
    count = len(LEVELS)
    r, c = place_ref[0], place_ref[1]
    small = [
        pltpu.make_async_copy(source, target, sems.at[0, k])
        for k, (source, target) in enumerate((
            (parts_hbm, parts), (table_hbm.at[c], table), (row_scale_hbm.at[r], row_scale),
            (col_scale_hbm.at[c], col_scale), (by_row_hbm.at[r], by_row), (by_col_hbm.at[c], by_col), (spread_hbm, spread),
        ))
    ]
    large = [pltpu.make_async_copy(wpool_hbm.at[k], wpool.at[k], sems.at[1, k]) for k in range(count)]
    for k in range(count):
        lines = slice(width + k * ppm, width + (k + 1) * ppm)
        large.append(pltpu.make_async_copy(wjoin_hbm.at[:, :, lines, :], wjoin.at[k], sems.at[1, count + k]))
    large.append(pltpu.make_async_copy(conv_hbm, conv, sems.at[1, 2 * count]))
    ahead = 5
    for copy in small + large[:ahead]:
        copy.start()

    def ready(k):
        large[k].wait()
        if k + ahead < len(large):
            large[k + ahead].start()

    for copy in small:
        copy.wait()

    def along(ref, axis):
        high, low = split(ref[...])
        return dot(high, spread[axis]) + dot(low, spread[axis])

    grid = along(by_row, 0)[:, None, :] * along(by_col, 1)[None, :, :]
    grid_high, grid_low = split(grid.reshape(grid.shape[0] * grid.shape[1], -1))
    scale = row_scale[...] * col_scale[...]
    scale = jnp.broadcast_to(scale, (128, scale.shape[1])).T[:, :1]
    pooled = dot(table[...], parts[...]) * scale
    branches = []
    row = 0
    for index, level in enumerate(LEVELS):
        slots = SLOTS[level]
        high, low = split(pooled[row : row + 2 * slots])
        ready(index)
        both = dot(jnp.concatenate([high, low], axis=0), wpool[index])
        high, low = split(jnp.maximum(both[: 2 * slots] + both[2 * slots :], 0.0))
        branches.append(jnp.concatenate([high, low], axis=0))
        row += 2 * slots
    at = 0
    for index, level in enumerate(LEVELS):
        slots = SLOTS[level]
        ready(count + index)
        for a in range(3):
            for b in range(3):
                tap = dot(branches[index], wjoin[index, a, b])
                tap = tap[: 2 * slots] + tap[2 * slots :]
                start = at + (a * 3 + b) * slots
                for s in range(2):
                    taps[s, start : start + slots, :] = tap[s * slots : (s + 1) * slots]
        at += TAPS * slots
    ready(2 * count)
    results = [pltpu.make_async_copy(out.at[s], out_hbm.at[s], sems.at[2, s]) for s in range(2)]
    for s in range(2):
        high, low = split(taps[s])
        total = conv[s] + dot(grid_high, high) + dot(grid_low, high) + dot(grid_high, low)
        out[s] = total.astype(bf16)
        results[s].start()
    for copy in results:
        copy.wait()


def cost(flops, nbytes, transcendentals=0):
    return pl.CostEstimate(flops=int(flops), bytes_accessed=int(nbytes), transcendentals=int(transcendentals))


def params(mib):
    return pltpu.CompilerParams(vmem_limit_bytes=mib * 2**20)


def whole(shape):
    return pl.BlockSpec(shape, lambda *_: (0,) * len(shape))


def in_hbm(x):
    return pltpu.with_memory_space_constraint(x, pltpu.HBM)


def shifts(axis):
    count = lax.axis_size(axis)
    forward = [(i, i + 1) for i in range(count - 1)]
    return forward, [(j, i) for i, j in forward]


def layer(tokens, norm_gain, w_query, w_kv, w_out, w_pool, w_join):
    sheets, rows, cols, width = tokens.shape
    inner = w_query.shape[1]
    wide = w_kv.shape[1]
    out_ch = w_join.shape[-1]
    ppm = w_pool.shape[-1]
    area = rows * cols
    row_count, col_count = lax.axis_size("row"), lax.axis_size("col")
    r, c = lax.axis_index("row"), lax.axis_index("col")
    grid_h, grid_w = rows * row_count, cols * col_count
    gain = norm_gain.reshape(1, width)
    tables = pool_tables(rows, row_count, cols, col_count)
    row_masks, col_masks, strip_table, near_table, bin_table, row_scale, col_scale = tables
    by_row, by_col, spread = upsample_tables(rows, row_count, cols, col_count)
    masks = np.concatenate([row_masks, col_masks], axis=-1).reshape(row_count * col_count, UNITS, rows + cols)

    at = jnp.stack([r, c]).astype(jnp.int32)
    row_fwd, row_bwd = shifts("row")
    col_fwd, col_bwd = shifts("col")
    above = lax.ppermute(tokens[:, rows - HALO :], "row", row_fwd)
    below = lax.ppermute(tokens[:, :HALO], "row", row_bwd)

    def edges(first):
        return jnp.concatenate([x[:, :, first : first + HALO] for x in (above, tokens, below)], axis=1)

    west = lax.ppermute(edges(cols - HALO), "col", col_fwd)
    east = lax.ppermute(edges(0), "col", col_bwd)

    def per_sheet(*dims):
        return pl.BlockSpec((None,) + dims, lambda s: (s,) + (0,) * len(dims))

    wq_near = pltpu.with_memory_space_constraint(w_query, pltpu.VMEM)
    wkv_near = pltpu.with_memory_space_constraint(w_kv, pltpu.VMEM)
    gain = pl.pallas_call(
        warm_kernel,
        in_specs=[pl.BlockSpec(memory_space=pltpu.VMEM)] * 3,
        out_specs=pl.BlockSpec(memory_space=pltpu.VMEM),
        out_shape=jax.ShapeDtypeStruct((1, width), f32),
        compiler_params=params(4),
        name="warm",
    )(gain, wq_near, wkv_near)
    flat = tokens.reshape(sheets, area, width)
    edge = HALO * cols
    q, kv = pl.pallas_call(
        project_kernel,
        grid=(sheets,),
        in_specs=[
            per_sheet(area, width), per_sheet(edge, width), per_sheet(edge, width),
            whole((1, width)), pl.BlockSpec(memory_space=pltpu.VMEM), pl.BlockSpec(memory_space=pltpu.VMEM),
        ],
        out_specs=[per_sheet(rows, cols, inner), per_sheet(rows + 2 * HALO, cols, wide)],
        out_shape=[
            jax.ShapeDtypeStruct((sheets, rows, cols, inner), f32),
            jax.ShapeDtypeStruct((sheets, rows + 2 * HALO, cols, wide), f32),
        ],
        compiler_params=params(28),
        cost_estimate=cost(2 * sheets * area * width * (inner + wide), 2 * (width * (inner + wide) + 5 * sheets * area * width)),
        name="project",
    )(flat, above.reshape(sheets, edge, width), below.reshape(sheets, edge, width), gain, wq_near, wkv_near)

    blank = jnp.zeros((sheets, rows + 2 * HALO, BLOCK - 2 * HALO, width), bf16)
    sides = jnp.concatenate([east, blank, west], axis=2).reshape(sheets, (rows + 2 * HALO) * BLOCK, width)
    blocks = (rows // BLOCK) * (cols // BLOCK)
    keys = (BLOCK + 2 * HALO) ** 2

    def fixed(*dims):
        return whole(dims)

    attended, sums = pl.pallas_call(
        lambda *refs: attend_kernel((grid_h, grid_w), *refs),
        grid_spec=pltpu.PrefetchScalarGridSpec(
            num_scalar_prefetch=1,
            grid=(sheets,),
            in_specs=[
                pl.BlockSpec((None, rows, cols, inner), lambda s, _: (s, 0, 0, 0)),
                pl.BlockSpec((None, rows + 2 * HALO, cols, wide), lambda s, _: (s, 0, 0, 0)),
                fixed(sheets, (rows + 2 * HALO) * BLOCK, width),
                pl.BlockSpec((None, area, width), lambda s, _: (s, 0, 0)),
                fixed(1, width), pl.BlockSpec(memory_space=pltpu.VMEM), fixed(inner, width),
                pl.BlockSpec((None, UNITS, rows + cols), lambda s, p: (p[0] * col_count + p[1], 0, 0)),
            ],
            out_specs=[
                pl.BlockSpec((None, area, width), lambda s, _: (s, 0, 0)),
                pl.BlockSpec((row_count, UNITS, width), lambda s, _: (0, s, 0)),
            ],
            scratch_shapes=[
                pltpu.VMEM((sheets, rows + 2 * HALO, BLOCK, wide), f32),
                pltpu.VMEM((rows, cols, inner), f32),
                pltpu.VMEM((rows // BLOCK, cols // BLOCK, keys, 128), f32),
                pltpu.VMEM((UNITS, area), bf16),
                pltpu.VMEM((2, inner // 128, keys, 256), f32),
                pltpu.VMEM((2, inner // 128, keys, 256), bf16),
            ],
        ),
        out_shape=[
            jax.ShapeDtypeStruct((sheets, area, width), bf16),
            jax.ShapeDtypeStruct((row_count, sheets * UNITS, width), bf16),
        ],
        compiler_params=params(32),
        cost_estimate=cost(2 * sheets * area * inner * width * 4, 2 * sheets * area * width * 4, sheets * blocks * keys * 1024),
        name="attend",
    )(at, q, kv, sides, flat, gain, wkv_near, w_out, masks)

    att = attended.reshape(sheets, rows, cols, width)
    strip_rows = sheets * STRIP_UNITS
    att_above = lax.ppermute(att[:, rows - 1 :], "row", row_fwd)
    att_below = lax.ppermute(att[:, :1], "row", row_bwd)
    parts = lax.all_to_all(sums, "row", 0, 0, tiled=True).reshape(row_count * sheets * UNITS, width)

    def att_edges(first):
        return jnp.concatenate([x[:, :, first] for x in (att_above, att, att_below)], axis=1)

    att_west = lax.ppermute(att_edges(cols - 1), "col", col_fwd)
    att_east = lax.ppermute(att_edges(0), "col", col_bwd)
    pad = ((0, 0), (0, 6), (0, 0))
    att_west, att_east = jnp.pad(att_west, pad), jnp.pad(att_east, pad)

    strips = pl.pallas_call(
        combine_kernel,
        grid_spec=pltpu.PrefetchScalarGridSpec(
            num_scalar_prefetch=1,
            grid=(1,),
            in_specs=[
                pl.BlockSpec((None,) + near_table.shape[1:], lambda k, p: (p[0], 0, 0)),
                pl.BlockSpec((None,) + strip_table.shape[1:], lambda k, p: (p[1], 0, 0)),
                fixed(row_count * sheets * UNITS, width),
            ],
            out_specs=fixed(col_count, strip_rows, width),
        ),
        out_shape=jax.ShapeDtypeStruct((col_count, strip_rows, width), bf16),
        compiler_params=params(8),
        name="combine",
    )(at, near_table.astype(bf16), strip_table.astype(bf16), parts)
    strips = lax.all_to_all(strips, "col", 0, 0, tiled=True).reshape(col_count * strip_rows, width)

    conv = pl.pallas_call(
        conv_kernel,
        in_specs=[pl.BlockSpec(memory_space=pl.ANY)] * 6,
        out_specs=pl.BlockSpec(memory_space=pl.ANY),
        out_shape=pltpu.HBM((sheets, area, out_ch), f32),
        scratch_shapes=[
            pltpu.VMEM((sheets, area + 2 * cols, width), bf16),
            pltpu.VMEM((2, sheets, rows + 8, width), bf16),
            pltpu.VMEM((3, 3, width, out_ch), bf16),
            pltpu.VMEM((sheets, area, out_ch), f32),
            pltpu.SemaphoreType.DMA((7, 3)),
        ],
        compiler_params=params(24),
        cost_estimate=cost(2 * sheets * area * width * 9 * out_ch, 2 * 9 * width * out_ch + 2 * sheets * area * width),
        name="conv",
    )(
        attended, att_above.reshape(sheets, cols, width), att_below.reshape(sheets, cols, width),
        att_west, att_east, in_hbm(w_join),
    )

    depth = TAPS * sum(SLOTS.values())
    bin_rows = 2 * sum(SLOTS.values())
    out = pl.pallas_call(
        tail_kernel,
        grid_spec=pltpu.PrefetchScalarGridSpec(
            num_scalar_prefetch=1,
            grid=(1,),
            in_specs=[
                pl.BlockSpec(memory_space=pl.ANY) for _ in range(10)
            ],
            out_specs=pl.BlockSpec(memory_space=pl.ANY),
            scratch_shapes=[
                pltpu.VMEM(bin_table.shape[1:], bf16),
                pltpu.VMEM((1, bin_rows), f32),
                pltpu.VMEM((1, bin_rows), f32),
                pltpu.VMEM((col_count * strip_rows, width), bf16),
                pltpu.VMEM((rows, 64), f32),
                pltpu.VMEM((cols, 64), f32),
                pltpu.VMEM((2, 64, depth), bf16),
                pltpu.VMEM(w_pool.shape, bf16),
                pltpu.VMEM((len(LEVELS), 3, 3, ppm, out_ch), bf16),
                pltpu.VMEM((sheets, area, out_ch), f32),
                pltpu.VMEM((sheets, depth, out_ch), f32),
                pltpu.VMEM((sheets, area, out_ch), bf16),
                pltpu.SemaphoreType.DMA((3, 2 * len(LEVELS) + 1)),
            ],
        ),
        out_shape=jax.ShapeDtypeStruct((sheets, area, out_ch), bf16),
        compiler_params=params(40),
        cost_estimate=cost(4e9, 2 * (w_pool.size + 9 * 4 * ppm * out_ch)),
        name="tail",
    )(
        at, bin_table.astype(bf16), row_scale, col_scale, strips, in_hbm(w_pool), in_hbm(w_join),
        by_row, by_col, spread.astype(bf16), in_hbm(conv),
    )
    return out.reshape(sheets, rows, cols, out_ch)


def solution(mesh):
    placed = (P(None, "row", "col", None), P(), P(), P(), P(), P(), P())
    return jax.shard_map(layer, mesh=mesh, in_specs=placed, out_specs=P(None, "row", "col", None), check_vma=False)
```

```python
import math

import jax
import jax.numpy as jnp
import numpy as np
from jax import lax
from jax.experimental import pallas as pl
from jax.experimental.pallas import tpu as pltpu
from jax.sharding import PartitionSpec as P

HEAD_DIM = 32
BLOCK = 8
HALO = 2
EPS = 1e-05
LEVELS = (1, 2, 3, 6)
CODED = (6, 3, 2)
UNITS = 8
STRIP_ALL = 24
STRIP_ALL_AT = {6: 0, 3: 12, 2: 18}
STRIP_UNITS = 16
STRIP_AT = {6: 0, 3: 6, 2: 12}
NEAR = {1: 1, 2: 2, 3: 3, 6: 3}
SLOTS = {1: 8, 2: 8, 3: 16, 6: 16}
TAPS = 9
f32 = jnp.float32
bf16 = jnp.bfloat16


def bins_of(level, length, first, count):
    places = first + np.arange(count)
    found = []
    for cell in range(level):
        start = cell * length // level
        end = ((cell + 1) * length + level - 1) // level
        mask = (places >= start) & (places < end)
        if mask.any():
            found.append((cell, mask))
    return found


def lower_bin(level, length, place):
    return max((2 * place + 1) * level - length, 0) // (2 * length)


def first_bin(level, length, first, count):
    start = min(lower_bin(level, length, first - 1), level - NEAR[level])
    assert min(lower_bin(level, length, first + count) + 1, level - 1) < start + NEAR[level]
    return start


def pool_tables(rows, row_strips, cols, col_strips):
    grid_h, grid_w = rows * row_strips, cols * col_strips
    row_masks = np.zeros((row_strips, col_strips, UNITS, rows), np.float32)
    col_masks = np.zeros((row_strips, col_strips, UNITS, cols), np.float32)
    strip = np.zeros((col_strips, 2 * STRIP_ALL, row_strips, 2 * UNITS), np.float32)
    near = np.zeros((row_strips, 2 * STRIP_UNITS, 2 * STRIP_ALL), np.float32)
    slots = 2 * sum(SLOTS.values())
    bins = np.zeros((col_strips, slots, col_strips, 2 * STRIP_UNITS), np.float32)
    row_scale = np.zeros((row_strips, 1, slots), np.float32)
    col_scale = np.zeros((col_strips, 1, slots), np.float32)
    for c in range(col_strips):
        for r in range(row_strips):
            units = []
            for level in CODED:
                for i, row_mask in bins_of(level, grid_h, r * rows, rows):
                    for g, (j, col_mask) in enumerate(bins_of(level, grid_w, c * cols, cols)):
                        key = (row_mask.tobytes(), col_mask.tobytes())
                        if key not in units:
                            units.append(key)
                            at = len(units) - 1
                            row_masks[r, c, at] = row_mask
                            col_masks[r, c, at] = col_mask
                        at = units.index(key)
                        width = 1 if level == 2 else 2
                        for s in range(2):
                            target = s * STRIP_ALL + STRIP_ALL_AT[level] + i * width + g
                            strip[c, target, r, s * UNITS + at] = 1.0
            assert len(units) <= UNITS
    for r in range(row_strips):
        for level in CODED:
            width = 1 if level == 2 else 2
            start = first_bin(level, grid_h, r * rows, rows)
            for k in range(NEAR[level] * width):
                for s in range(2):
                    source = s * STRIP_ALL + STRIP_ALL_AT[level] + start * width + k
                    near[r, s * STRIP_UNITS + STRIP_AT[level] + k, source] = 1.0
    for c in range(col_strips):
        base = 0
        for level in LEVELS:
            source = 2 if level == 1 else level
            width = 1 if source == 2 else 2
            start = first_bin(level, grid_w, c * cols, cols)
            for p in range(col_strips):
                for g, (j, _) in enumerate(bins_of(source, grid_w, p * cols, cols)):
                    j = 0 if level == 1 else j - start
                    if not 0 <= j < NEAR[level]:
                        continue
                    for i in range(NEAR[source]):
                        for s in range(2):
                            cell = 0 if level == 1 else i * NEAR[level] + j
                            at = base + s * SLOTS[level] + cell
                            bins[c, at, p, s * STRIP_UNITS + STRIP_AT[source] + i * width + g] = 1.0
            base += 2 * SLOTS[level]
    for table, strips, size, along_rows in ((row_scale, row_strips, rows, True), (col_scale, col_strips, cols, False)):
        for at in range(strips):
            base = 0
            for level in LEVELS:
                length = size * strips
                start = first_bin(level, length, at * size, size)
                sizes = [mask.sum() for _, mask in bins_of(level, length, 0, length)]
                for i in range(NEAR[level]):
                    for j in range(NEAR[level]):
                        for s in range(2):
                            k = base + s * SLOTS[level] + i * NEAR[level] + j
                            table[at, 0, k] = 1.0 / sizes[start + (i if along_rows else j)]
                base += 2 * SLOTS[level]
    strip = strip.reshape(col_strips, 2 * STRIP_ALL, -1)
    return row_masks, col_masks, strip, near, bins.reshape(col_strips, slots, -1), row_scale, col_scale


def upsample_weights(level, length, first, count):
    places = first + np.arange(count)
    numer = np.maximum((2 * places + 1) * level - length, 0)
    lower = numer // (2 * length)
    frac = (numer - lower * 2 * length).astype(np.float32) / np.float32(2.0 * length)
    upper = np.minimum(lower + 1, level - 1)
    cells = np.arange(level)[None, :]
    weight = (cells == lower[:, None]) * (1.0 - frac)[:, None] + (cells == upper[:, None]) * frac[:, None]
    inside = (places >= 0) & (places < length)
    return (weight * inside[:, None]).astype(np.float32)


def upsample_tables(rows, row_strips, cols, col_strips):
    width = TAPS * sum(SLOTS.values())
    cells = sum(NEAR.values())
    spread = np.zeros((2, 64, width), np.float32)

    def strips_of(size, strips):
        table = np.zeros((strips, size, 64), np.float32)
        length = size * strips
        for strip in range(strips):
            first = 0
            for level in LEVELS:
                start = first_bin(level, length, strip * size, size)
                for a in range(3):
                    w = upsample_weights(level, length, strip * size + a - 1, size)
                    at = a * cells + first
                    table[strip, :, at : at + NEAR[level]] = w[:, start : start + NEAR[level]]
                first += NEAR[level]
        return table

    base, first = 0, 0
    for level in LEVELS:
        for a in range(3):
            for c in range(3):
                for i in range(NEAR[level]):
                    for j in range(NEAR[level]):
                        at = base + (a * 3 + c) * SLOTS[level] + i * NEAR[level] + j
                        spread[0, a * cells + first + i, at] = 1.0
                        spread[1, c * cells + first + j, at] = 1.0
        base += TAPS * SLOTS[level]
        first += NEAR[level]
    return strips_of(rows, row_strips), strips_of(cols, col_strips), spread


def layer_norm(tokens, gain):
    x = tokens.astype(f32)
    center = jnp.mean(x, axis=-1, keepdims=True)
    x = x - center
    spread = jnp.mean(x * x, axis=-1, keepdims=True)
    return (x * lax.rsqrt(spread + EPS) * gain).astype(bf16)


def dot(a, b):
    return jnp.dot(a, b, preferred_element_type=f32)


def warm_kernel(gain_ref, wq_ref, wkv_ref, out_ref):
    out_ref[...] = gain_ref[...]


def project_kernel(tokens_ref, above_ref, below_ref, gain_ref, wq, wkv, q_ref, kv_ref):
    rows, cols, inner = q_ref.shape
    gain = gain_ref[...]
    normed = layer_norm(tokens_ref[...], gain)
    q_ref[...] = dot(normed, wq[...]).astype(bf16).astype(f32).reshape(rows, cols, inner)
    kv_ref[HALO : rows + HALO] = dot(normed, wkv[...]).astype(bf16).astype(f32).reshape(rows, cols, -1)
    edge = layer_norm(jnp.concatenate([above_ref[...], below_ref[...]], axis=0), gain)
    edge = dot(edge, wkv[...]).astype(bf16).astype(f32).reshape(2 * HALO, cols, -1)
    kv_ref[0:HALO] = edge[:HALO]
    kv_ref[rows + HALO :] = edge[HALO:]


def window_bias(bias, first_row, first_col, grid_h, grid_w):
    span = BLOCK + 2 * HALO
    key = lax.broadcasted_iota(jnp.int32, bias.shape[2:], 0)
    extra = key - span * BLOCK
    lane = extra & 7
    odd = ((lane >= 2) & (lane < 6)).astype(jnp.int32)
    west = (lane >= 6) | ((lane >= 2) & (lane < 4))
    main = key < span * BLOCK
    row = jnp.where(main, key >> 3, 2 * (extra >> 3) + odd) - HALO
    col = jnp.where(main, key & 7, (key & 1) + jnp.where(west, -HALO, BLOCK))
    for a in range(bias.shape[0]):
        at = row + (first_row + a * BLOCK)
        row_ok = (at >= 0) & (at < grid_h)
        for b in range(bias.shape[1]):
            at = col + (first_col + b * BLOCK)
            bias[a, b] = jnp.where(row_ok & (at >= 0) & (at < grid_w), 0.0, -1e30)


def attend_kernel(
    grid_shape, place_ref, q_ref, kv_ref, sides_ref, tokens_ref, gain_ref, wkv_ref, wout_ref, masks_ref,
    attended_ref, sums_ref, first_row_ref, last_row_ref, first_col_ref, last_col_ref, sides, context, bias, pool, scores, weights,
):
    rows, cols, inner = q_ref.shape
    groups = cols // BLOCK
    span = BLOCK + 2 * HALO

    @pl.when(pl.program_id(0) == 0)
    def _():
        window_bias(bias, place_ref[0] * rows, place_ref[1] * cols, *grid_shape)
        masks = masks_ref[...].astype(bf16)
        unit = lax.broadcasted_iota(jnp.int32, (masks.shape[1], rows * cols), 0)
        token = lax.broadcasted_iota(jnp.int32, (masks.shape[1], rows * cols), 1)
        to_row = (unit == token // cols).astype(f32).astype(bf16)
        to_col = (unit - rows == token % cols).astype(f32).astype(bf16)
        pool[...] = (dot(masks, to_row) * dot(masks, to_col)).astype(bf16)
        ends = layer_norm(sides_ref[...].reshape(-1, sides_ref.shape[-1]), gain_ref[...])
        ends = dot(ends, wkv_ref[...]).astype(bf16).astype(f32)
        sides[...] = ends.reshape(sides.shape)

    sheet = pl.program_id(0)
    count = BLOCK * BLOCK
    heads = 128 // HEAD_DIM
    head_of_row = lax.broadcasted_iota(jnp.int32, (heads, count, 128), 0)
    head_of_lane = lax.broadcasted_iota(jnp.int32, (heads, count, 128), 2) // HEAD_DIM
    own = (head_of_row == head_of_lane).astype(f32).astype(bf16).reshape(heads * count, 128)
    lane = lax.broadcasted_iota(jnp.int32, (count, 128), 1)
    place = lax.broadcasted_iota(jnp.int32, (span // 2, BLOCK, 128), 1)
    factor = math.log2(math.e) / math.sqrt(HEAD_DIM)

    def band(a, carry):
        at = pl.multiple_of(a * BLOCK, BLOCK)

        def keys_of(b, lanes):
            mid = slice(b * BLOCK, (b + 1) * BLOCK)
            main = kv_ref[pl.ds(at, span), mid, lanes].reshape(span * BLOCK, 128)

            def beside(g):
                if g < 0 or g >= groups:
                    found = sides[sheet, pl.ds(at, span), :, lanes]
                else:
                    found = kv_ref[pl.ds(at, span), g * BLOCK : (g + 1) * BLOCK, lanes]
                return found.reshape(span // 2, 2, BLOCK, 128)

            west, east = beside(b - 1), beside(b + 1)
            even = jnp.where(place >= 6, west[:, 0], east[:, 0])
            odd = pltpu.roll(jnp.where(place >= 6, west[:, 1], east[:, 1]), 4, 1)
            extra = jnp.where((place >= 6) | (place < 2), even, odd).reshape(span * 4, 128)
            return jnp.concatenate([main, extra], axis=0).astype(bf16)

        tiles = inner // 128

        def score(b, slot):
            mid = slice(b * BLOCK, (b + 1) * BLOCK)
            low = bias[a, b]
            for t in range(tiles):
                lanes = slice(t * 128, (t + 1) * 128)
                q = q_ref[pl.ds(at, BLOCK), mid, lanes].reshape(count, 128).astype(bf16)
                q = jnp.concatenate([q] * heads, axis=0) * own
                found = lax.dot_general(keys_of(b, lanes), q, (((1,), (1,)), ((), ())), preferred_element_type=f32)
                scores[slot, t] = found + jnp.concatenate([low] * (heads * count // 128), axis=1)

        def soften(slot):
            for t in range(tiles):
                for h in range(heads * count // 128):
                    lanes = slice(h * 128, (h + 1) * 128)
                    found = scores[slot, t, :, lanes]
                    top = jnp.max(found, axis=0, keepdims=True)
                    expon = jnp.exp2((found - top) * factor)
                    weights[slot, t, :, lanes] = (expon * (1.0 / jnp.sum(expon, axis=0, keepdims=True))).astype(bf16)

        def mix(b, slot):
            mid = slice(b * BLOCK, (b + 1) * BLOCK)
            for t in range(tiles):
                lanes = slice(t * 128, (t + 1) * 128)
                values = keys_of(b, slice(inner + t * 128, inner + (t + 1) * 128))
                mixed = lax.dot_general(weights[slot, t], values, (((0,), (0,)), ((), ())), preferred_element_type=f32)
                mixed = mixed.reshape(heads, count, 128)
                piece = mixed[0]
                for k in range(1, heads):
                    piece = jnp.where(lane >= k * HEAD_DIM, mixed[k], piece)
                context[pl.ds(at, BLOCK), mid, lanes] = piece.reshape(BLOCK, BLOCK, 128)

        score(0, 0)
        for b in range(groups):
            if b + 1 < groups:
                score(b + 1, (b + 1) % 2)
            soften(b % 2)
            mix(b, b % 2)
        return carry

    lax.fori_loop(0, rows // BLOCK, band, 0)
    mixed = context[...].reshape(rows * cols, inner).astype(bf16)
    attended = (tokens_ref[...].astype(f32) + dot(mixed, wout_ref[...])).astype(bf16)
    attended_ref[...] = attended
    first_row_ref[...] = attended[:cols]
    last_row_ref[...] = attended[(rows - 1) * cols :]
    by_place = attended.astype(f32).reshape(rows, cols, attended.shape[-1])
    first_col_ref[...] = by_place[:, 0].astype(bf16)
    last_col_ref[...] = by_place[:, cols - 1].astype(bf16)
    sums = dot(pool[...], attended).astype(bf16)
    sums_ref[...] = jnp.broadcast_to(sums[None], sums_ref.shape)


def combine_kernel(place_ref, near_ref, table_ref, parts_ref, out_ref):
    table = dot(near_ref[...], table_ref[...]).astype(bf16)
    added = dot(table, parts_ref[...]).astype(bf16)
    out_ref[...] = jnp.broadcast_to(added[None], out_ref.shape)


def conv_kernel(attended_ref, top_ref, bottom_ref, left_ref, right_ref, w_ref, out_ref, ext):
    area, _ = attended_ref.shape
    cols = top_ref.shape[0]
    rows = area // cols
    out_ch = out_ref.shape[-1]
    s, step = pl.program_id(0), pl.program_id(1)

    def edge(ref):
        total = 0.0
        for a in range(3):
            total = total + dot(ref[...], w_ref[a])[a : a + rows]
        return total.reshape(rows, 1, out_ch)

    def middle():
        total = dot(ext[0:area], w_ref[0])
        for a in range(1, 3):
            total = total + dot(ext[a * cols : a * cols + area], w_ref[a])
        return total.reshape(rows, cols, out_ch)

    @pl.when(step == 0)
    def _():
        ext[0:cols] = top_ref[...]
        ext[cols : cols + area] = attended_ref[...]
        ext[cols + area :] = bottom_ref[...]
        place = lax.broadcasted_iota(jnp.int32, (rows, cols, out_ch), 1)
        part = jnp.where(place == 0, edge(left_ref), pltpu.roll(middle(), 1, 1))
        out_ref[s] = part.reshape(area, out_ch)

    @pl.when(step == 1)
    def _():
        out_ref[s] += middle().reshape(area, out_ch)

    @pl.when(step == 2)
    def _():
        place = lax.broadcasted_iota(jnp.int32, (rows, cols, out_ch), 1)
        part = jnp.where(place == cols - 1, edge(right_ref), pltpu.roll(middle(), cols - 1, 1))
        out_ref[s] += part.reshape(area, out_ch)


def split(x):
    high = x.astype(bf16)
    return high, (x - high.astype(f32)).astype(bf16)


def tail_kernel(
    place_ref, table_hbm, row_scale_hbm, col_scale_hbm, parts_hbm, wpool_hbm, wjoin_hbm, by_row_hbm, by_col_hbm,
    spread_hbm, conv, out_hbm,
    table, row_scale, col_scale, parts, by_row, by_col, spread, wpool, wjoin, taps, out, sems,
):
    width, ppm = wpool.shape[1], wpool.shape[2]
    count = len(LEVELS)
    r, c = place_ref[0], place_ref[1]
    small = [
        pltpu.make_async_copy(source, target, sems.at[0, k])
        for k, (source, target) in enumerate((
            (parts_hbm, parts), (table_hbm.at[c], table), (row_scale_hbm.at[r], row_scale),
            (col_scale_hbm.at[c], col_scale), (by_row_hbm.at[r], by_row), (by_col_hbm.at[c], by_col), (spread_hbm, spread),
        ))
    ]
    large = [pltpu.make_async_copy(wpool_hbm.at[k], wpool.at[k], sems.at[1, k]) for k in range(count)]
    for k in range(count):
        lines = slice(width + k * ppm, width + (k + 1) * ppm)
        large.append(pltpu.make_async_copy(wjoin_hbm.at[:, :, lines, :], wjoin.at[k], sems.at[1, count + k]))
    ahead = 5
    for copy in small + large[:ahead]:
        copy.start()

    def ready(k):
        large[k].wait()
        if k + ahead < len(large):
            large[k + ahead].start()

    for copy in small:
        copy.wait()

    def along(ref, axis):
        high, low = split(ref[...])
        return dot(high, spread[axis]) + dot(low, spread[axis])

    grid = along(by_row, 0)[:, None, :] * along(by_col, 1)[None, :, :]
    grid_high, grid_low = split(grid.reshape(grid.shape[0] * grid.shape[1], -1))
    scale = row_scale[...] * col_scale[...]
    scale = jnp.broadcast_to(scale, (128, scale.shape[1])).T[:, :1]
    pooled = dot(table[...], parts[...]) * scale
    branches = []
    row = 0
    for index, level in enumerate(LEVELS):
        slots = SLOTS[level]
        high, low = split(pooled[row : row + 2 * slots])
        ready(index)
        both = dot(jnp.concatenate([high, low], axis=0), wpool[index])
        high, low = split(jnp.maximum(both[: 2 * slots] + both[2 * slots :], 0.0))
        branches.append(jnp.concatenate([high, low], axis=0))
        row += 2 * slots
    at = 0
    for index, level in enumerate(LEVELS):
        slots = SLOTS[level]
        ready(count + index)
        for a in range(3):
            for b in range(3):
                tap = dot(branches[index], wjoin[index, a, b])
                tap = tap[: 2 * slots] + tap[2 * slots :]
                start = at + (a * 3 + b) * slots
                for s in range(2):
                    taps[s, start : start + slots, :] = tap[s * slots : (s + 1) * slots]
        at += TAPS * slots
    results = [pltpu.make_async_copy(out.at[s], out_hbm.at[s], sems.at[2, s]) for s in range(2)]
    for s in range(2):
        high, low = split(taps[s])
        total = conv[s] + dot(grid_high, high) + dot(grid_low, high) + dot(grid_high, low)
        out[s] = total.astype(bf16)
        results[s].start()
    for copy in results:
        copy.wait()


def cost(flops, nbytes, transcendentals=0):
    return pl.CostEstimate(flops=int(flops), bytes_accessed=int(nbytes), transcendentals=int(transcendentals))


def params(mib):
    return pltpu.CompilerParams(vmem_limit_bytes=mib * 2**20)


def whole(shape):
    return pl.BlockSpec(shape, lambda *_: (0,) * len(shape))


def in_hbm(x):
    return pltpu.with_memory_space_constraint(x, pltpu.HBM)


def shifts(axis):
    count = lax.axis_size(axis)
    forward = [(i, i + 1) for i in range(count - 1)]
    return forward, [(j, i) for i, j in forward]


def layer(tokens, norm_gain, w_query, w_kv, w_out, w_pool, w_join):
    sheets, rows, cols, width = tokens.shape
    inner = w_query.shape[1]
    wide = w_kv.shape[1]
    out_ch = w_join.shape[-1]
    ppm = w_pool.shape[-1]
    area = rows * cols
    row_count, col_count = lax.axis_size("row"), lax.axis_size("col")
    r, c = lax.axis_index("row"), lax.axis_index("col")
    grid_h, grid_w = rows * row_count, cols * col_count
    gain = norm_gain.reshape(1, width)
    tables = pool_tables(rows, row_count, cols, col_count)
    row_masks, col_masks, strip_table, near_table, bin_table, row_scale, col_scale = tables
    by_row, by_col, spread = upsample_tables(rows, row_count, cols, col_count)
    masks = np.concatenate([row_masks, col_masks], axis=-1).reshape(row_count * col_count, UNITS, rows + cols)

    at = jnp.stack([r, c]).astype(jnp.int32)
    row_fwd, row_bwd = shifts("row")
    col_fwd, col_bwd = shifts("col")
    above = lax.ppermute(tokens[:, rows - HALO :], "row", row_fwd)
    below = lax.ppermute(tokens[:, :HALO], "row", row_bwd)

    def edges(first):
        return jnp.concatenate([x[:, :, first : first + HALO] for x in (above, tokens, below)], axis=1)

    west = lax.ppermute(edges(cols - HALO), "col", col_fwd)
    east = lax.ppermute(edges(0), "col", col_bwd)

    def per_sheet(*dims):
        return pl.BlockSpec((None,) + dims, lambda s, *_: (s,) + (0,) * len(dims))

    wq_near = pltpu.with_memory_space_constraint(w_query, pltpu.VMEM)
    wkv_near = pltpu.with_memory_space_constraint(w_kv, pltpu.VMEM)
    gain = pl.pallas_call(
        warm_kernel,
        in_specs=[pl.BlockSpec(memory_space=pltpu.VMEM)] * 3,
        out_specs=pl.BlockSpec(memory_space=pltpu.VMEM),
        out_shape=jax.ShapeDtypeStruct((1, width), f32),
        compiler_params=params(4),
        name="warm",
    )(gain, wq_near, wkv_near)
    flat = tokens.reshape(sheets, area, width)
    edge = HALO * cols
    q, kv = pl.pallas_call(
        project_kernel,
        grid=(sheets,),
        in_specs=[
            per_sheet(area, width), per_sheet(edge, width), per_sheet(edge, width),
            whole((1, width)), pl.BlockSpec(memory_space=pltpu.VMEM), pl.BlockSpec(memory_space=pltpu.VMEM),
        ],
        out_specs=[per_sheet(rows, cols, inner), per_sheet(rows + 2 * HALO, cols, wide)],
        out_shape=[
            jax.ShapeDtypeStruct((sheets, rows, cols, inner), f32),
            jax.ShapeDtypeStruct((sheets, rows + 2 * HALO, cols, wide), f32),
        ],
        compiler_params=params(28),
        cost_estimate=cost(2 * sheets * area * width * (inner + wide), 2 * (width * (inner + wide) + 5 * sheets * area * width)),
        name="project",
    )(flat, above.reshape(sheets, edge, width), below.reshape(sheets, edge, width), gain, wq_near, wkv_near)

    blank = jnp.zeros((sheets, rows + 2 * HALO, BLOCK - 2 * HALO, width), bf16)
    sides = jnp.concatenate([east, blank, west], axis=2).reshape(sheets, (rows + 2 * HALO) * BLOCK, width)
    blocks = (rows // BLOCK) * (cols // BLOCK)
    keys = (BLOCK + 2 * HALO) ** 2

    def fixed(*dims):
        return whole(dims)

    attended, sums, first_row, last_row, first_col, last_col = pl.pallas_call(
        lambda *refs: attend_kernel((grid_h, grid_w), *refs),
        grid_spec=pltpu.PrefetchScalarGridSpec(
            num_scalar_prefetch=1,
            grid=(sheets,),
            in_specs=[
                pl.BlockSpec((None, rows, cols, inner), lambda s, _: (s, 0, 0, 0)),
                pl.BlockSpec((None, rows + 2 * HALO, cols, wide), lambda s, _: (s, 0, 0, 0)),
                fixed(sheets, (rows + 2 * HALO) * BLOCK, width),
                pl.BlockSpec((None, area, width), lambda s, _: (s, 0, 0)),
                fixed(1, width), pl.BlockSpec(memory_space=pltpu.VMEM), fixed(inner, width),
                pl.BlockSpec((None, UNITS, rows + cols), lambda s, p: (p[0] * col_count + p[1], 0, 0)),
            ],
            out_specs=[
                pl.BlockSpec((None, area, width), lambda s, _: (s, 0, 0)),
                pl.BlockSpec((row_count, UNITS, width), lambda s, _: (0, s, 0)),
                per_sheet(cols, width), per_sheet(cols, width), per_sheet(rows, width), per_sheet(rows, width),
            ],
            scratch_shapes=[
                pltpu.VMEM((sheets, rows + 2 * HALO, BLOCK, wide), f32),
                pltpu.VMEM((rows, cols, inner), f32),
                pltpu.VMEM((rows // BLOCK, cols // BLOCK, keys, 128), f32),
                pltpu.VMEM((UNITS, area), bf16),
                pltpu.VMEM((2, inner // 128, keys, 256), f32),
                pltpu.VMEM((2, inner // 128, keys, 256), bf16),
            ],
        ),
        out_shape=[
            pltpu.HBM((sheets, area, width), bf16),
            jax.ShapeDtypeStruct((row_count, sheets * UNITS, width), bf16),
            jax.ShapeDtypeStruct((sheets, cols, width), bf16),
            jax.ShapeDtypeStruct((sheets, cols, width), bf16),
            jax.ShapeDtypeStruct((sheets, rows, width), bf16),
            jax.ShapeDtypeStruct((sheets, rows, width), bf16),
        ],
        compiler_params=params(32),
        cost_estimate=cost(2 * sheets * area * inner * width * 4, 2 * sheets * area * width * 4, sheets * blocks * keys * 1024),
        name="attend",
    )(at, q, kv, sides, flat, gain, wkv_near, w_out, masks)

    strip_rows = sheets * STRIP_UNITS
    att_above = lax.ppermute(last_row, "row", row_fwd)
    att_below = lax.ppermute(first_row, "row", row_bwd)
    parts = lax.all_to_all(sums, "row", 0, 0, tiled=True).reshape(row_count * sheets * UNITS, width)

    def att_edges(middle, at):
        return jnp.concatenate([att_above[:, at : at + 1], middle, att_below[:, at : at + 1]], axis=1)

    att_west = lax.ppermute(att_edges(last_col, cols - 1), "col", col_fwd)
    att_east = lax.ppermute(att_edges(first_col, 0), "col", col_bwd)
    pad = ((0, 0), (0, 6), (0, 0))
    att_west, att_east = jnp.pad(att_west, pad), jnp.pad(att_east, pad)

    strips = pl.pallas_call(
        combine_kernel,
        grid_spec=pltpu.PrefetchScalarGridSpec(
            num_scalar_prefetch=1,
            grid=(1,),
            in_specs=[
                pl.BlockSpec((None,) + near_table.shape[1:], lambda k, p: (p[0], 0, 0)),
                pl.BlockSpec((None,) + strip_table.shape[1:], lambda k, p: (p[1], 0, 0)),
                fixed(row_count * sheets * UNITS, width),
            ],
            out_specs=fixed(col_count, strip_rows, width),
        ),
        out_shape=jax.ShapeDtypeStruct((col_count, strip_rows, width), bf16),
        compiler_params=params(8),
        name="combine",
    )(at, near_table.astype(bf16), strip_table.astype(bf16), parts)
    strips = lax.all_to_all(strips, "col", 0, 0, tiled=True).reshape(col_count * strip_rows, width)

    conv = pl.pallas_call(
        conv_kernel,
        grid=(sheets, 3),
        in_specs=[
            per_sheet(area, width), per_sheet(cols, width), per_sheet(cols, width),
            per_sheet(rows + 8, width), per_sheet(rows + 8, width),
            pl.BlockSpec((3, None, width, out_ch), lambda s, k: (0, k, 0, 0)),
        ],
        out_specs=pl.BlockSpec(memory_space=pltpu.VMEM),
        out_shape=pltpu.VMEM((sheets, area, out_ch), f32),
        scratch_shapes=[pltpu.VMEM((area + 2 * cols, width), bf16)],
        compiler_params=params(20),
        cost_estimate=cost(2 * sheets * area * width * 9 * out_ch, 2 * 9 * width * out_ch + 2 * sheets * area * width),
        name="conv",
    )(in_hbm(attended), att_above, att_below, att_west, att_east, in_hbm(w_join))
    conv = pltpu.with_memory_space_constraint(conv, pltpu.VMEM)

    depth = TAPS * sum(SLOTS.values())
    bin_rows = 2 * sum(SLOTS.values())
    out = pl.pallas_call(
        tail_kernel,
        grid_spec=pltpu.PrefetchScalarGridSpec(
            num_scalar_prefetch=1,
            grid=(1,),
            in_specs=[pl.BlockSpec(memory_space=pl.ANY) for _ in range(9)] + [pl.BlockSpec(memory_space=pltpu.VMEM)],
            out_specs=pl.BlockSpec(memory_space=pl.ANY),
            scratch_shapes=[
                pltpu.VMEM(bin_table.shape[1:], bf16),
                pltpu.VMEM((1, bin_rows), f32),
                pltpu.VMEM((1, bin_rows), f32),
                pltpu.VMEM((col_count * strip_rows, width), bf16),
                pltpu.VMEM((rows, 64), f32),
                pltpu.VMEM((cols, 64), f32),
                pltpu.VMEM((2, 64, depth), bf16),
                pltpu.VMEM(w_pool.shape, bf16),
                pltpu.VMEM((len(LEVELS), 3, 3, ppm, out_ch), bf16),
                pltpu.VMEM((sheets, depth, out_ch), f32),
                pltpu.VMEM((sheets, area, out_ch), bf16),
                pltpu.SemaphoreType.DMA((3, 2 * len(LEVELS))),
            ],
        ),
        out_shape=jax.ShapeDtypeStruct((sheets, area, out_ch), bf16),
        compiler_params=params(40),
        cost_estimate=cost(4e9, 2 * (w_pool.size + 9 * 4 * ppm * out_ch)),
        name="tail",
    )(
        at, bin_table.astype(bf16), row_scale, col_scale, strips, in_hbm(w_pool), in_hbm(w_join),
        by_row, by_col, spread.astype(bf16), conv,
    )
    return out.reshape(sheets, rows, cols, out_ch)


def solution(mesh):
    placed = (P(None, "row", "col", None), P(), P(), P(), P(), P(), P())
    return jax.shard_map(layer, mesh=mesh, in_specs=placed, out_specs=P(None, "row", "col", None), check_vma=False)
```

```python
import math

import jax
import jax.numpy as jnp
import numpy as np
from jax import lax
from jax.experimental import pallas as pl
from jax.experimental.pallas import tpu as pltpu
from jax.sharding import PartitionSpec as P

HEAD_DIM = 32
BLOCK = 8
HALO = 2
EPS = 1e-05
LEVELS = (1, 2, 3, 6)
CODED = (6, 3, 2)
UNITS = 8
STRIP_ALL = 24
STRIP_ALL_AT = {6: 0, 3: 12, 2: 18}
STRIP_UNITS = 16
STRIP_AT = {6: 0, 3: 6, 2: 12}
NEAR = {1: 1, 2: 2, 3: 3, 6: 3}
SLOTS = {1: 8, 2: 8, 3: 16, 6: 16}
TAPS = 9
f32 = jnp.float32
bf16 = jnp.bfloat16


def bins_of(level, length, first, count):
    places = first + np.arange(count)
    found = []
    for cell in range(level):
        start = cell * length // level
        end = ((cell + 1) * length + level - 1) // level
        mask = (places >= start) & (places < end)
        if mask.any():
            found.append((cell, mask))
    return found


def lower_bin(level, length, place):
    return max((2 * place + 1) * level - length, 0) // (2 * length)


def first_bin(level, length, first, count):
    start = min(lower_bin(level, length, first - 1), level - NEAR[level])
    assert min(lower_bin(level, length, first + count) + 1, level - 1) < start + NEAR[level]
    return start


def pool_tables(rows, row_strips, cols, col_strips):
    grid_h, grid_w = rows * row_strips, cols * col_strips
    row_masks = np.zeros((row_strips, col_strips, UNITS, rows), np.float32)
    col_masks = np.zeros((row_strips, col_strips, UNITS, cols), np.float32)
    strip = np.zeros((col_strips, 2 * STRIP_ALL, row_strips, 2 * UNITS), np.float32)
    near = np.zeros((row_strips, 2 * STRIP_UNITS, 2 * STRIP_ALL), np.float32)
    slots = 2 * sum(SLOTS.values())
    bins = np.zeros((col_strips, slots, col_strips, 2 * STRIP_UNITS), np.float32)
    row_scale = np.zeros((row_strips, 1, slots), np.float32)
    col_scale = np.zeros((col_strips, 1, slots), np.float32)
    for c in range(col_strips):
        for r in range(row_strips):
            units = []
            for level in CODED:
                for i, row_mask in bins_of(level, grid_h, r * rows, rows):
                    for g, (j, col_mask) in enumerate(bins_of(level, grid_w, c * cols, cols)):
                        key = (row_mask.tobytes(), col_mask.tobytes())
                        if key not in units:
                            units.append(key)
                            at = len(units) - 1
                            row_masks[r, c, at] = row_mask
                            col_masks[r, c, at] = col_mask
                        at = units.index(key)
                        width = 1 if level == 2 else 2
                        for s in range(2):
                            target = s * STRIP_ALL + STRIP_ALL_AT[level] + i * width + g
                            strip[c, target, r, s * UNITS + at] = 1.0
            assert len(units) <= UNITS
    for r in range(row_strips):
        for level in CODED:
            width = 1 if level == 2 else 2
            start = first_bin(level, grid_h, r * rows, rows)
            for k in range(NEAR[level] * width):
                for s in range(2):
                    source = s * STRIP_ALL + STRIP_ALL_AT[level] + start * width + k
                    near[r, s * STRIP_UNITS + STRIP_AT[level] + k, source] = 1.0
    for c in range(col_strips):
        base = 0
        for level in LEVELS:
            source = 2 if level == 1 else level
            width = 1 if source == 2 else 2
            start = first_bin(level, grid_w, c * cols, cols)
            for p in range(col_strips):
                for g, (j, _) in enumerate(bins_of(source, grid_w, p * cols, cols)):
                    j = 0 if level == 1 else j - start
                    if not 0 <= j < NEAR[level]:
                        continue
                    for i in range(NEAR[source]):
                        for s in range(2):
                            cell = 0 if level == 1 else i * NEAR[level] + j
                            at = base + s * SLOTS[level] + cell
                            bins[c, at, p, s * STRIP_UNITS + STRIP_AT[source] + i * width + g] = 1.0
            base += 2 * SLOTS[level]
    for table, strips, size, along_rows in ((row_scale, row_strips, rows, True), (col_scale, col_strips, cols, False)):
        for at in range(strips):
            base = 0
            for level in LEVELS:
                length = size * strips
                start = first_bin(level, length, at * size, size)
                sizes = [mask.sum() for _, mask in bins_of(level, length, 0, length)]
                for i in range(NEAR[level]):
                    for j in range(NEAR[level]):
                        for s in range(2):
                            k = base + s * SLOTS[level] + i * NEAR[level] + j
                            table[at, 0, k] = 1.0 / sizes[start + (i if along_rows else j)]
                base += 2 * SLOTS[level]
    strip = strip.reshape(col_strips, 2 * STRIP_ALL, -1)
    return row_masks, col_masks, strip, near, bins.reshape(col_strips, slots, -1), row_scale, col_scale


def upsample_weights(level, length, first, count):
    places = first + np.arange(count)
    numer = np.maximum((2 * places + 1) * level - length, 0)
    lower = numer // (2 * length)
    frac = (numer - lower * 2 * length).astype(np.float32) / np.float32(2.0 * length)
    upper = np.minimum(lower + 1, level - 1)
    cells = np.arange(level)[None, :]
    weight = (cells == lower[:, None]) * (1.0 - frac)[:, None] + (cells == upper[:, None]) * frac[:, None]
    inside = (places >= 0) & (places < length)
    return (weight * inside[:, None]).astype(np.float32)


def upsample_tables(rows, row_strips, cols, col_strips):
    width = TAPS * sum(SLOTS.values())
    cells = sum(NEAR.values())
    spread = np.zeros((2, 64, width), np.float32)

    def strips_of(size, strips):
        table = np.zeros((strips, size, 64), np.float32)
        length = size * strips
        for strip in range(strips):
            first = 0
            for level in LEVELS:
                start = first_bin(level, length, strip * size, size)
                for a in range(3):
                    w = upsample_weights(level, length, strip * size + a - 1, size)
                    at = a * cells + first
                    table[strip, :, at : at + NEAR[level]] = w[:, start : start + NEAR[level]]
                first += NEAR[level]
        return table

    base, first = 0, 0
    for level in LEVELS:
        for a in range(3):
            for c in range(3):
                for i in range(NEAR[level]):
                    for j in range(NEAR[level]):
                        at = base + (a * 3 + c) * SLOTS[level] + i * NEAR[level] + j
                        spread[0, a * cells + first + i, at] = 1.0
                        spread[1, c * cells + first + j, at] = 1.0
        base += TAPS * SLOTS[level]
        first += NEAR[level]
    return strips_of(rows, row_strips), strips_of(cols, col_strips), spread


def layer_norm(tokens, gain):
    x = tokens.astype(f32)
    center = jnp.mean(x, axis=-1, keepdims=True)
    x = x - center
    spread = jnp.mean(x * x, axis=-1, keepdims=True)
    return (x * lax.rsqrt(spread + EPS) * gain).astype(bf16)


def dot(a, b):
    return jnp.dot(a, b, preferred_element_type=f32)


def warm_kernel(gain_ref, wq_ref, wkv_ref, out_ref):
    out_ref[...] = gain_ref[...]


def project_kernel(tokens_ref, above_ref, below_ref, gain_ref, wq, wkv, q_ref, kv_ref):
    rows, cols, inner = q_ref.shape[1:]
    s = pl.program_id(0)
    gain = gain_ref[...]
    normed = layer_norm(tokens_ref[s], gain)
    q_ref[s] = dot(normed, wq[...]).astype(bf16).astype(f32).reshape(rows, cols, inner)
    kv_ref[s, HALO : rows + HALO] = dot(normed, wkv[...]).astype(bf16).astype(f32).reshape(rows, cols, -1)
    edge = layer_norm(jnp.concatenate([above_ref[s], below_ref[s]], axis=0), gain)
    edge = dot(edge, wkv[...]).astype(bf16).astype(f32).reshape(2 * HALO, cols, -1)
    kv_ref[s, 0:HALO] = edge[:HALO]
    kv_ref[s, rows + HALO :] = edge[HALO:]


def window_bias(bias, first_row, first_col, grid_h, grid_w):
    span = BLOCK + 2 * HALO
    key = lax.broadcasted_iota(jnp.int32, bias.shape[2:], 0)
    extra = key - span * BLOCK
    lane = extra & 7
    odd = ((lane >= 2) & (lane < 6)).astype(jnp.int32)
    west = (lane >= 6) | ((lane >= 2) & (lane < 4))
    main = key < span * BLOCK
    row = jnp.where(main, key >> 3, 2 * (extra >> 3) + odd) - HALO
    col = jnp.where(main, key & 7, (key & 1) + jnp.where(west, -HALO, BLOCK))
    for a in range(bias.shape[0]):
        at = row + (first_row + a * BLOCK)
        row_ok = (at >= 0) & (at < grid_h)
        for b in range(bias.shape[1]):
            at = col + (first_col + b * BLOCK)
            bias[a, b] = jnp.where(row_ok & (at >= 0) & (at < grid_w), 0.0, -1e30)


def attend_kernel(
    grid_shape, place_ref, q_ref, kv_ref, sides_ref, tokens_ref, gain_ref, wkv_ref, wout_ref, masks_ref,
    attended_ref, sums_ref, first_row_ref, last_row_ref, first_col_ref, last_col_ref, sides, context, bias, pool, scores, weights,
):
    rows, cols, inner = q_ref.shape[1:]
    groups = cols // BLOCK
    span = BLOCK + 2 * HALO

    @pl.when(pl.program_id(0) == 0)
    def _():
        window_bias(bias, place_ref[0] * rows, place_ref[1] * cols, *grid_shape)
        masks = masks_ref[...].astype(bf16)
        unit = lax.broadcasted_iota(jnp.int32, (masks.shape[1], rows * cols), 0)
        token = lax.broadcasted_iota(jnp.int32, (masks.shape[1], rows * cols), 1)
        to_row = (unit == token // cols).astype(f32).astype(bf16)
        to_col = (unit - rows == token % cols).astype(f32).astype(bf16)
        pool[...] = (dot(masks, to_row) * dot(masks, to_col)).astype(bf16)
        ends = layer_norm(sides_ref[...].reshape(-1, sides_ref.shape[-1]), gain_ref[...])
        ends = dot(ends, wkv_ref[...]).astype(bf16).astype(f32)
        sides[...] = ends.reshape(sides.shape)

    sheet = pl.program_id(0)
    count = BLOCK * BLOCK
    heads = 128 // HEAD_DIM
    head_of_row = lax.broadcasted_iota(jnp.int32, (heads, count, 128), 0)
    head_of_lane = lax.broadcasted_iota(jnp.int32, (heads, count, 128), 2) // HEAD_DIM
    own = (head_of_row == head_of_lane).astype(f32).astype(bf16).reshape(heads * count, 128)
    lane = lax.broadcasted_iota(jnp.int32, (count, 128), 1)
    place = lax.broadcasted_iota(jnp.int32, (span // 2, BLOCK, 128), 1)
    factor = math.log2(math.e) / math.sqrt(HEAD_DIM)

    def band(a, carry):
        at = pl.multiple_of(a * BLOCK, BLOCK)

        def keys_of(b, lanes):
            mid = slice(b * BLOCK, (b + 1) * BLOCK)
            main = kv_ref[sheet, pl.ds(at, span), mid, lanes].reshape(span * BLOCK, 128)

            def beside(g):
                if g < 0 or g >= groups:
                    found = sides[sheet, pl.ds(at, span), :, lanes]
                else:
                    found = kv_ref[sheet, pl.ds(at, span), g * BLOCK : (g + 1) * BLOCK, lanes]
                return found.reshape(span // 2, 2, BLOCK, 128)

            west, east = beside(b - 1), beside(b + 1)
            even = jnp.where(place >= 6, west[:, 0], east[:, 0])
            odd = pltpu.roll(jnp.where(place >= 6, west[:, 1], east[:, 1]), 4, 1)
            extra = jnp.where((place >= 6) | (place < 2), even, odd).reshape(span * 4, 128)
            return jnp.concatenate([main, extra], axis=0).astype(bf16)

        tiles = inner // 128

        def score(b, slot):
            mid = slice(b * BLOCK, (b + 1) * BLOCK)
            low = bias[a, b]
            for t in range(tiles):
                lanes = slice(t * 128, (t + 1) * 128)
                q = q_ref[sheet, pl.ds(at, BLOCK), mid, lanes].reshape(count, 128).astype(bf16)
                q = jnp.concatenate([q] * heads, axis=0) * own
                found = lax.dot_general(keys_of(b, lanes), q, (((1,), (1,)), ((), ())), preferred_element_type=f32)
                scores[slot, t] = found + jnp.concatenate([low] * (heads * count // 128), axis=1)

        def soften(slot):
            for t in range(tiles):
                for h in range(heads * count // 128):
                    lanes = slice(h * 128, (h + 1) * 128)
                    found = scores[slot, t, :, lanes]
                    top = jnp.max(found, axis=0, keepdims=True)
                    expon = jnp.exp2((found - top) * factor)
                    weights[slot, t, :, lanes] = (expon * (1.0 / jnp.sum(expon, axis=0, keepdims=True))).astype(bf16)

        def mix(b, slot):
            mid = slice(b * BLOCK, (b + 1) * BLOCK)
            for t in range(tiles):
                lanes = slice(t * 128, (t + 1) * 128)
                values = keys_of(b, slice(inner + t * 128, inner + (t + 1) * 128))
                mixed = lax.dot_general(weights[slot, t], values, (((0,), (0,)), ((), ())), preferred_element_type=f32)
                mixed = mixed.reshape(heads, count, 128)
                piece = mixed[0]
                for k in range(1, heads):
                    piece = jnp.where(lane >= k * HEAD_DIM, mixed[k], piece)
                context[pl.ds(at, BLOCK), mid, lanes] = piece.reshape(BLOCK, BLOCK, 128)

        score(0, 0)
        for b in range(groups):
            if b + 1 < groups:
                score(b + 1, (b + 1) % 2)
            soften(b % 2)
            mix(b, b % 2)
        return carry

    lax.fori_loop(0, rows // BLOCK, band, 0)
    mixed = context[...].reshape(rows * cols, inner).astype(bf16)
    attended = (tokens_ref[sheet].astype(f32) + dot(mixed, wout_ref[...])).astype(bf16)
    attended_ref[...] = attended
    first_row_ref[...] = attended[:cols]
    last_row_ref[...] = attended[(rows - 1) * cols :]
    by_place = attended.astype(f32).reshape(rows, cols, attended.shape[-1])
    first_col_ref[...] = by_place[:, 0].astype(bf16)
    last_col_ref[...] = by_place[:, cols - 1].astype(bf16)
    sums = dot(pool[...], attended).astype(bf16)
    sums_ref[...] = jnp.broadcast_to(sums[None], sums_ref.shape)


def combine_kernel(place_ref, near_ref, table_ref, parts_ref, out_ref):
    table = dot(near_ref[...], table_ref[...]).astype(bf16)
    added = dot(table, parts_ref[...]).astype(bf16)
    out_ref[...] = jnp.broadcast_to(added[None], out_ref.shape)


def conv_kernel(attended_ref, top_ref, bottom_ref, left_ref, right_ref, taps_ref, w_hbm, out_ref, ext, w, sems):
    area, width = attended_ref.shape
    cols = top_ref.shape[0]
    rows = area // cols
    out_ch = out_ref.shape[-1]
    s, step = pl.program_id(0), pl.program_id(1)

    fetches = [
        pltpu.make_async_copy(w_hbm.at[:, k, 0:width, :], w.at[k - 1], sems.at[k - 1]) for k in (1, 2)
    ]

    @pl.when((s == 0) & (step == 0))
    def _():
        for fetch in fetches:
            fetch.start()

    for k, fetch in enumerate(fetches):

        @pl.when((s == 0) & (step == k + 1))
        def _():
            fetch.wait()

    def edge(ref, w_ref):
        total = 0.0
        for a in range(3):
            total = total + dot(ref[...], w_ref[a])[a : a + rows]
        return total.reshape(rows, 1, out_ch)

    def middle(w_ref):
        total = dot(ext[0:area], w_ref[0])
        for a in range(1, 3):
            total = total + dot(ext[a * cols : a * cols + area], w_ref[a])
        return total.reshape(rows, cols, out_ch)

    @pl.when(step == 0)
    def _():
        ext[0:cols] = top_ref[...]
        ext[cols : cols + area] = attended_ref[...]
        ext[cols + area :] = bottom_ref[...]
        place = lax.broadcasted_iota(jnp.int32, (rows, cols, out_ch), 1)
        part = jnp.where(place == 0, edge(left_ref, taps_ref), pltpu.roll(middle(taps_ref), 1, 1))
        out_ref[s] = part.reshape(area, out_ch)

    @pl.when(step == 1)
    def _():
        out_ref[s] += middle(w.at[0]).reshape(area, out_ch)

    @pl.when(step == 2)
    def _():
        place = lax.broadcasted_iota(jnp.int32, (rows, cols, out_ch), 1)
        part = jnp.where(place == cols - 1, edge(right_ref, w.at[1]), pltpu.roll(middle(w.at[1]), cols - 1, 1))
        out_ref[s] += part.reshape(area, out_ch)


def split(x):
    high = x.astype(bf16)
    return high, (x - high.astype(f32)).astype(bf16)


def tail_kernel(
    place_ref, table_hbm, row_scale_hbm, col_scale_hbm, parts_hbm, wpool_hbm, wjoin_hbm, by_row_hbm, by_col_hbm,
    spread_hbm, conv_ref, out_hbm,
    table, row_scale, col_scale, parts, by_row, by_col, spread, wpool, wjoin, conv, taps, out, sems,
):
    width, ppm = wpool.shape[1], wpool.shape[2]
    count = len(LEVELS)
    r, c = place_ref[0], place_ref[1]
    small = [
        pltpu.make_async_copy(source, target, sems.at[0, k])
        for k, (source, target) in enumerate((
            (parts_hbm, parts), (table_hbm.at[c], table), (row_scale_hbm.at[r], row_scale),
            (col_scale_hbm.at[c], col_scale), (by_row_hbm.at[r], by_row), (by_col_hbm.at[c], by_col), (spread_hbm, spread),
        ))
    ]
    large = [pltpu.make_async_copy(wpool_hbm.at[k], wpool.at[k], sems.at[1, k]) for k in range(count)]
    for k in range(count):
        lines = slice(width + k * ppm, width + (k + 1) * ppm)
        large.append(pltpu.make_async_copy(wjoin_hbm.at[:, :, lines, :], wjoin.at[k], sems.at[1, count + k]))
    ahead = 5
    for copy in small + large[:ahead]:
        copy.start()

    def ready(k):
        large[k].wait()
        if k + ahead < len(large):
            large[k + ahead].start()

    for copy in small:
        copy.wait()

    def along(ref, axis):
        high, low = split(ref[...])
        return dot(high, spread[axis]) + dot(low, spread[axis])

    grid = along(by_row, 0)[:, None, :] * along(by_col, 1)[None, :, :]
    grid_high, grid_low = split(grid.reshape(grid.shape[0] * grid.shape[1], -1))
    scale = row_scale[...] * col_scale[...]
    scale = jnp.broadcast_to(scale, (128, scale.shape[1])).T[:, :1]
    pooled = dot(table[...], parts[...]) * scale
    branches = []
    row = 0
    for index, level in enumerate(LEVELS):
        slots = SLOTS[level]
        high, low = split(pooled[row : row + 2 * slots])
        ready(index)
        both = dot(jnp.concatenate([high, low], axis=0), wpool[index])
        high, low = split(jnp.maximum(both[: 2 * slots] + both[2 * slots :], 0.0))
        branches.append(jnp.concatenate([high, low], axis=0))
        row += 2 * slots
    results = [pltpu.make_async_copy(out.at[s], out_hbm.at[s], sems.at[2, s]) for s in range(2)]

    def spread_over(s, part):
        high, low = split(taps[s, part])
        lines = dot(grid_high[:, part], high) + dot(grid_low[:, part], high)
        return lines + dot(grid_high[:, part], low)

    at = 0
    for index, level in enumerate(LEVELS):
        slots = SLOTS[level]
        last = index == count - 1
        if last:
            for s in range(2):
                conv[s] = conv_ref[s] + spread_over(s, slice(0, at))
        ready(count + index)
        for a in range(3):
            for b in range(3):
                tap = dot(branches[index], wjoin[index, a, b])
                tap = tap[: 2 * slots] + tap[2 * slots :]
                start = at + (a * 3 + b) * slots
                for s in range(2):
                    taps[s, start : start + slots, :] = tap[s * slots : (s + 1) * slots]
        if last:
            for s in range(2):
                out[s] = (conv[s] + spread_over(s, slice(at, at + TAPS * slots))).astype(bf16)
                results[s].start()
        at += TAPS * slots
    for copy in results:
        copy.wait()


def cost(flops, nbytes, transcendentals=0):
    return pl.CostEstimate(flops=int(flops), bytes_accessed=int(nbytes), transcendentals=int(transcendentals))


def params(mib):
    return pltpu.CompilerParams(vmem_limit_bytes=mib * 2**20)


def whole(shape):
    return pl.BlockSpec(shape, lambda *_: (0,) * len(shape))


def in_vmem(x):
    return pltpu.with_memory_space_constraint(x, pltpu.VMEM)


def in_hbm(x):
    return pltpu.with_memory_space_constraint(x, pltpu.HBM)


def shifts(axis):
    count = lax.axis_size(axis)
    forward = [(i, i + 1) for i in range(count - 1)]
    return forward, [(j, i) for i, j in forward]


def layer(tokens, norm_gain, w_query, w_kv, w_out, w_pool, w_join):
    sheets, rows, cols, width = tokens.shape
    inner = w_query.shape[1]
    wide = w_kv.shape[1]
    out_ch = w_join.shape[-1]
    ppm = w_pool.shape[-1]
    area = rows * cols
    row_count, col_count = lax.axis_size("row"), lax.axis_size("col")
    r, c = lax.axis_index("row"), lax.axis_index("col")
    grid_h, grid_w = rows * row_count, cols * col_count
    gain = norm_gain.reshape(1, width)
    tables = pool_tables(rows, row_count, cols, col_count)
    row_masks, col_masks, strip_table, near_table, bin_table, row_scale, col_scale = tables
    by_row, by_col, spread = upsample_tables(rows, row_count, cols, col_count)
    masks = np.concatenate([row_masks, col_masks], axis=-1).reshape(row_count * col_count, UNITS, rows + cols)

    at = jnp.stack([r, c]).astype(jnp.int32)
    row_fwd, row_bwd = shifts("row")
    col_fwd, col_bwd = shifts("col")
    above = lax.ppermute(tokens[:, rows - HALO :], "row", row_fwd)
    below = lax.ppermute(tokens[:, :HALO], "row", row_bwd)

    def edges(first):
        return jnp.concatenate([x[:, :, first : first + HALO] for x in (above, tokens, below)], axis=1)

    west = lax.ppermute(edges(cols - HALO), "col", col_fwd)
    east = lax.ppermute(edges(0), "col", col_bwd)

    def per_sheet(*dims):
        return pl.BlockSpec((None,) + dims, lambda s, *_: (s,) + (0,) * len(dims))

    near = pl.BlockSpec(memory_space=pltpu.VMEM)
    far = pl.BlockSpec(memory_space=pl.ANY)
    wq_near, wkv_near = in_vmem(w_query), in_vmem(w_kv)
    gain = pl.pallas_call(
        warm_kernel,
        in_specs=[pl.BlockSpec(memory_space=pltpu.VMEM)] * 3,
        out_specs=pl.BlockSpec(memory_space=pltpu.VMEM),
        out_shape=jax.ShapeDtypeStruct((1, width), f32),
        compiler_params=params(4),
        name="warm",
    )(gain, wq_near, wkv_near)
    flat = in_vmem(tokens.reshape(sheets, area, width))
    edge = HALO * cols
    q, kv = pl.pallas_call(
        project_kernel,
        grid=(sheets,),
        in_specs=[near] * 6,
        out_specs=[near] * 2,
        out_shape=[
            pltpu.VMEM((sheets, rows, cols, inner), f32), pltpu.VMEM((sheets, rows + 2 * HALO, cols, wide), f32),
        ],
        compiler_params=params(28),
        cost_estimate=cost(2 * sheets * area * width * (inner + wide), 2 * (width * (inner + wide) + 5 * sheets * area * width)),
        name="project",
    )(
        flat, in_vmem(above.reshape(sheets, edge, width)), in_vmem(below.reshape(sheets, edge, width)),
        in_vmem(gain), wq_near, wkv_near,
    )

    blank = jnp.zeros((sheets, rows + 2 * HALO, BLOCK - 2 * HALO, width), bf16)
    sides = jnp.concatenate([east, blank, west], axis=2).reshape(sheets, (rows + 2 * HALO) * BLOCK, width)
    blocks = (rows // BLOCK) * (cols // BLOCK)
    keys = (BLOCK + 2 * HALO) ** 2

    def fixed(*dims):
        return whole(dims)

    attended, sums, first_row, last_row, first_col, last_col = pl.pallas_call(
        lambda *refs: attend_kernel((grid_h, grid_w), *refs),
        grid_spec=pltpu.PrefetchScalarGridSpec(
            num_scalar_prefetch=1,
            grid=(sheets,),
            in_specs=[
                near, near, near, near, near, near, fixed(inner, width),
                pl.BlockSpec((None, UNITS, rows + cols), lambda s, p: (p[0] * col_count + p[1], 0, 0)),
            ],
            out_specs=[
                pl.BlockSpec((None, area, width), lambda s, _: (s, 0, 0)),
                pl.BlockSpec((row_count, UNITS, width), lambda s, _: (0, s, 0)),
                per_sheet(cols, width), per_sheet(cols, width), per_sheet(rows, width), per_sheet(rows, width),
            ],
            scratch_shapes=[
                pltpu.VMEM((sheets, rows + 2 * HALO, BLOCK, wide), f32),
                pltpu.VMEM((rows, cols, inner), f32),
                pltpu.VMEM((rows // BLOCK, cols // BLOCK, keys, 128), f32),
                pltpu.VMEM((UNITS, area), bf16),
                pltpu.VMEM((2, inner // 128, keys, 256), f32),
                pltpu.VMEM((2, inner // 128, keys, 256), bf16),
            ],
        ),
        out_shape=[
            pltpu.HBM((sheets, area, width), bf16),
            jax.ShapeDtypeStruct((row_count, sheets * UNITS, width), bf16),
            jax.ShapeDtypeStruct((sheets, cols, width), bf16),
            jax.ShapeDtypeStruct((sheets, cols, width), bf16),
            jax.ShapeDtypeStruct((sheets, rows, width), bf16),
            jax.ShapeDtypeStruct((sheets, rows, width), bf16),
        ],
        compiler_params=params(32),
        cost_estimate=cost(2 * sheets * area * inner * width * 4, 2 * sheets * area * width * 4, sheets * blocks * keys * 1024),
        name="attend",
    )(
        at, in_vmem(q), in_vmem(kv), in_vmem(sides), flat, in_vmem(gain), wkv_near, w_out, masks,
    )

    strip_rows = sheets * STRIP_UNITS
    att_above = lax.ppermute(last_row, "row", row_fwd)
    att_below = lax.ppermute(first_row, "row", row_bwd)
    parts = lax.all_to_all(sums, "row", 0, 0, tiled=True).reshape(row_count * sheets * UNITS, width)

    def att_edges(middle, at):
        return jnp.concatenate([att_above[:, at : at + 1], middle, att_below[:, at : at + 1]], axis=1)

    att_west = lax.ppermute(att_edges(last_col, cols - 1), "col", col_fwd)
    att_east = lax.ppermute(att_edges(first_col, 0), "col", col_bwd)
    pad = ((0, 0), (0, 6), (0, 0))
    att_west, att_east = jnp.pad(att_west, pad), jnp.pad(att_east, pad)

    strips = pl.pallas_call(
        combine_kernel,
        grid_spec=pltpu.PrefetchScalarGridSpec(
            num_scalar_prefetch=1,
            grid=(1,),
            in_specs=[
                pl.BlockSpec((None,) + near_table.shape[1:], lambda k, p: (p[0], 0, 0)),
                pl.BlockSpec((None,) + strip_table.shape[1:], lambda k, p: (p[1], 0, 0)),
                fixed(row_count * sheets * UNITS, width),
            ],
            out_specs=fixed(col_count, strip_rows, width),
        ),
        out_shape=jax.ShapeDtypeStruct((col_count, strip_rows, width), bf16),
        compiler_params=params(8),
        name="combine",
    )(at, near_table.astype(bf16), strip_table.astype(bf16), parts)
    strips = lax.all_to_all(strips, "col", 0, 0, tiled=True).reshape(col_count * strip_rows, width)

    conv = pl.pallas_call(
        conv_kernel,
        grid=(sheets, 3),
        in_specs=[
            per_sheet(area, width), per_sheet(cols, width), per_sheet(cols, width),
            per_sheet(rows + 8, width), per_sheet(rows + 8, width),
            pl.BlockSpec((3, None, width, out_ch), lambda *_: (0, 0, 0, 0)), far,
        ],
        out_specs=pl.BlockSpec(memory_space=pltpu.VMEM),
        out_shape=pltpu.VMEM((sheets, area, out_ch), f32),
        scratch_shapes=[
            pltpu.VMEM((area + 2 * cols, width), bf16), pltpu.VMEM((2, 3, width, out_ch), bf16),
            pltpu.SemaphoreType.DMA((2,)),
        ],
        compiler_params=params(20),
        cost_estimate=cost(2 * sheets * area * width * 9 * out_ch, 2 * 9 * width * out_ch + 2 * sheets * area * width),
        name="conv",
    )(in_hbm(attended), att_above, att_below, att_west, att_east, in_hbm(w_join), in_hbm(w_join))
    conv = in_vmem(conv)

    depth = TAPS * sum(SLOTS.values())
    bin_rows = 2 * sum(SLOTS.values())
    out = pl.pallas_call(
        tail_kernel,
        grid_spec=pltpu.PrefetchScalarGridSpec(
            num_scalar_prefetch=1,
            grid=(1,),
            in_specs=[pl.BlockSpec(memory_space=pl.ANY) for _ in range(9)] + [pl.BlockSpec(memory_space=pltpu.VMEM)],
            out_specs=pl.BlockSpec(memory_space=pl.ANY),
            scratch_shapes=[
                pltpu.VMEM(bin_table.shape[1:], bf16),
                pltpu.VMEM((1, bin_rows), f32),
                pltpu.VMEM((1, bin_rows), f32),
                pltpu.VMEM((col_count * strip_rows, width), bf16),
                pltpu.VMEM((rows, 64), f32),
                pltpu.VMEM((cols, 64), f32),
                pltpu.VMEM((2, 64, depth), bf16),
                pltpu.VMEM(w_pool.shape, bf16),
                pltpu.VMEM((len(LEVELS), 3, 3, ppm, out_ch), bf16),
                pltpu.VMEM((sheets, area, out_ch), f32),
                pltpu.VMEM((sheets, depth, out_ch), f32),
                pltpu.VMEM((sheets, area, out_ch), bf16),
                pltpu.SemaphoreType.DMA((3, 2 * len(LEVELS))),
            ],
        ),
        out_shape=jax.ShapeDtypeStruct((sheets, area, out_ch), bf16),
        compiler_params=params(40),
        cost_estimate=cost(4e9, 2 * (w_pool.size + 9 * 4 * ppm * out_ch)),
        name="tail",
    )(
        at, bin_table.astype(bf16), row_scale, col_scale, strips, in_hbm(w_pool), in_hbm(w_join),
        by_row, by_col, spread.astype(bf16), conv,
    )
    return out.reshape(sheets, rows, cols, out_ch)


def solution(mesh):
    placed = (P(None, "row", "col", None), P(), P(), P(), P(), P(), P())
    return jax.shard_map(layer, mesh=mesh, in_specs=placed, out_specs=P(None, "row", "col", None), check_vma=False)
```

```python
import math

import jax
import jax.numpy as jnp
import numpy as np
from jax import lax
from jax.experimental import pallas as pl
from jax.experimental.pallas import tpu as pltpu
from jax.sharding import PartitionSpec as P

HEAD_DIM = 32
BLOCK = 8
HALO = 2
EPS = 1e-05
LEVELS = (1, 2, 3, 6)
CODED = (6, 3, 2)
UNITS = 8
STRIP_ALL = 24
STRIP_ALL_AT = {6: 0, 3: 12, 2: 18}
STRIP_UNITS = 16
STRIP_AT = {6: 0, 3: 6, 2: 12}
NEAR = {1: 1, 2: 2, 3: 3, 6: 3}
SLOTS = {1: 8, 2: 8, 3: 16, 6: 16}
TAPS = 9
f32 = jnp.float32
bf16 = jnp.bfloat16


def bins_of(level, length, first, count):
    places = first + np.arange(count)
    found = []
    for cell in range(level):
        start = cell * length // level
        end = ((cell + 1) * length + level - 1) // level
        mask = (places >= start) & (places < end)
        if mask.any():
            found.append((cell, mask))
    return found


def lower_bin(level, length, place):
    return max((2 * place + 1) * level - length, 0) // (2 * length)


def first_bin(level, length, first, count):
    start = min(lower_bin(level, length, first - 1), level - NEAR[level])
    assert min(lower_bin(level, length, first + count) + 1, level - 1) < start + NEAR[level]
    return start


def pool_tables(rows, row_strips, cols, col_strips):
    grid_h, grid_w = rows * row_strips, cols * col_strips
    row_masks = np.zeros((row_strips, col_strips, UNITS, rows), np.float32)
    col_masks = np.zeros((row_strips, col_strips, UNITS, cols), np.float32)
    strip = np.zeros((col_strips, 2 * STRIP_ALL, row_strips, 2 * UNITS), np.float32)
    near = np.zeros((row_strips, 2 * STRIP_UNITS, 2 * STRIP_ALL), np.float32)
    slots = 2 * sum(SLOTS.values())
    bins = np.zeros((col_strips, slots, col_strips, 2 * STRIP_UNITS), np.float32)
    row_scale = np.zeros((row_strips, 1, slots), np.float32)
    col_scale = np.zeros((col_strips, 1, slots), np.float32)
    for c in range(col_strips):
        for r in range(row_strips):
            units = []
            for level in CODED:
                for i, row_mask in bins_of(level, grid_h, r * rows, rows):
                    for g, (j, col_mask) in enumerate(bins_of(level, grid_w, c * cols, cols)):
                        key = (row_mask.tobytes(), col_mask.tobytes())
                        if key not in units:
                            units.append(key)
                            at = len(units) - 1
                            row_masks[r, c, at] = row_mask
                            col_masks[r, c, at] = col_mask
                        at = units.index(key)
                        width = 1 if level == 2 else 2
                        for s in range(2):
                            target = s * STRIP_ALL + STRIP_ALL_AT[level] + i * width + g
                            strip[c, target, r, s * UNITS + at] = 1.0
            assert len(units) <= UNITS
    for r in range(row_strips):
        for level in CODED:
            width = 1 if level == 2 else 2
            start = first_bin(level, grid_h, r * rows, rows)
            for k in range(NEAR[level] * width):
                for s in range(2):
                    source = s * STRIP_ALL + STRIP_ALL_AT[level] + start * width + k
                    near[r, s * STRIP_UNITS + STRIP_AT[level] + k, source] = 1.0
    for c in range(col_strips):
        base = 0
        for level in LEVELS:
            source = 2 if level == 1 else level
            width = 1 if source == 2 else 2
            start = first_bin(level, grid_w, c * cols, cols)
            for p in range(col_strips):
                for g, (j, _) in enumerate(bins_of(source, grid_w, p * cols, cols)):
                    j = 0 if level == 1 else j - start
                    if not 0 <= j < NEAR[level]:
                        continue
                    for i in range(NEAR[source]):
                        for s in range(2):
                            cell = 0 if level == 1 else i * NEAR[level] + j
                            at = base + s * SLOTS[level] + cell
                            bins[c, at, p, s * STRIP_UNITS + STRIP_AT[source] + i * width + g] = 1.0
            base += 2 * SLOTS[level]
    for table, strips, size, along_rows in ((row_scale, row_strips, rows, True), (col_scale, col_strips, cols, False)):
        for at in range(strips):
            base = 0
            for level in LEVELS:
                length = size * strips
                start = first_bin(level, length, at * size, size)
                sizes = [mask.sum() for _, mask in bins_of(level, length, 0, length)]
                for i in range(NEAR[level]):
                    for j in range(NEAR[level]):
                        for s in range(2):
                            k = base + s * SLOTS[level] + i * NEAR[level] + j
                            table[at, 0, k] = 1.0 / sizes[start + (i if along_rows else j)]
                base += 2 * SLOTS[level]
    strip = strip.reshape(col_strips, 2 * STRIP_ALL, -1)
    return row_masks, col_masks, strip, near, bins.reshape(col_strips, slots, -1), row_scale, col_scale


def upsample_weights(level, length, first, count):
    places = first + np.arange(count)
    numer = np.maximum((2 * places + 1) * level - length, 0)
    lower = numer // (2 * length)
    frac = (numer - lower * 2 * length).astype(np.float32) / np.float32(2.0 * length)
    upper = np.minimum(lower + 1, level - 1)
    cells = np.arange(level)[None, :]
    weight = (cells == lower[:, None]) * (1.0 - frac)[:, None] + (cells == upper[:, None]) * frac[:, None]
    inside = (places >= 0) & (places < length)
    return (weight * inside[:, None]).astype(np.float32)


def upsample_tables(rows, row_strips, cols, col_strips):
    width = TAPS * sum(SLOTS.values())
    cells = sum(NEAR.values())
    spread = np.zeros((2, 64, width), np.float32)

    def strips_of(size, strips):
        table = np.zeros((strips, size, 64), np.float32)
        length = size * strips
        for strip in range(strips):
            first = 0
            for level in LEVELS:
                start = first_bin(level, length, strip * size, size)
                for a in range(3):
                    w = upsample_weights(level, length, strip * size + a - 1, size)
                    at = a * cells + first
                    table[strip, :, at : at + NEAR[level]] = w[:, start : start + NEAR[level]]
                first += NEAR[level]
        return table

    base, first = 0, 0
    for level in LEVELS:
        for a in range(3):
            for c in range(3):
                for i in range(NEAR[level]):
                    for j in range(NEAR[level]):
                        at = base + (a * 3 + c) * SLOTS[level] + i * NEAR[level] + j
                        spread[0, a * cells + first + i, at] = 1.0
                        spread[1, c * cells + first + j, at] = 1.0
        base += TAPS * SLOTS[level]
        first += NEAR[level]
    return strips_of(rows, row_strips), strips_of(cols, col_strips), spread


def layer_norm(tokens, gain):
    x = tokens.astype(f32)
    center = jnp.mean(x, axis=-1, keepdims=True)
    x = x - center
    spread = jnp.mean(x * x, axis=-1, keepdims=True)
    return (x * lax.rsqrt(spread + EPS) * gain).astype(bf16)


def dot(a, b):
    return jnp.dot(a, b, preferred_element_type=f32)


def warm_kernel(gain_ref, wq_ref, wkv_ref, out_ref):
    out_ref[...] = gain_ref[...]


def project_kernel(tokens_ref, above_ref, below_ref, gain_ref, wq, wkv, q_ref, kv_ref):
    rows, cols, inner = q_ref.shape[1:]
    s = pl.program_id(0)
    gain = gain_ref[...]
    normed = layer_norm(tokens_ref[s], gain)
    q_ref[s] = dot(normed, wq[...]).astype(bf16).astype(f32).reshape(rows, cols, inner)
    kv_ref[s, HALO : rows + HALO] = dot(normed, wkv[...]).astype(bf16).astype(f32).reshape(rows, cols, -1)
    edge = layer_norm(jnp.concatenate([above_ref[s], below_ref[s]], axis=0), gain)
    edge = dot(edge, wkv[...]).astype(bf16).astype(f32).reshape(2 * HALO, cols, -1)
    kv_ref[s, 0:HALO] = edge[:HALO]
    kv_ref[s, rows + HALO :] = edge[HALO:]


def window_bias(bias, first_row, first_col, grid_h, grid_w):
    span = BLOCK + 2 * HALO
    key = lax.broadcasted_iota(jnp.int32, bias.shape[2:], 0)
    extra = key - span * BLOCK
    lane = extra & 7
    odd = ((lane >= 2) & (lane < 6)).astype(jnp.int32)
    west = (lane >= 6) | ((lane >= 2) & (lane < 4))
    main = key < span * BLOCK
    row = jnp.where(main, key >> 3, 2 * (extra >> 3) + odd) - HALO
    col = jnp.where(main, key & 7, (key & 1) + jnp.where(west, -HALO, BLOCK))
    for a in range(bias.shape[0]):
        at = row + (first_row + a * BLOCK)
        row_ok = (at >= 0) & (at < grid_h)
        for b in range(bias.shape[1]):
            at = col + (first_col + b * BLOCK)
            bias[a, b] = jnp.where(row_ok & (at >= 0) & (at < grid_w), 0.0, -1e30)


def attend_kernel(
    grid_shape, place_ref, q_ref, kv_ref, sides_ref, tokens_ref, gain_ref, wkv_ref, wout_ref, masks_ref,
    attended_ref, sums_ref, first_row_ref, last_row_ref, first_col_ref, last_col_ref, sides, context, bias, pool, scores, weights,
):
    rows, cols, inner = q_ref.shape[1:]
    groups = cols // BLOCK
    span = BLOCK + 2 * HALO

    @pl.when(pl.program_id(0) == 0)
    def _():
        window_bias(bias, place_ref[0] * rows, place_ref[1] * cols, *grid_shape)
        masks = masks_ref[...].astype(bf16)
        unit = lax.broadcasted_iota(jnp.int32, (masks.shape[1], rows * cols), 0)
        token = lax.broadcasted_iota(jnp.int32, (masks.shape[1], rows * cols), 1)
        to_row = (unit == token // cols).astype(f32).astype(bf16)
        to_col = (unit - rows == token % cols).astype(f32).astype(bf16)
        pool[...] = (dot(masks, to_row) * dot(masks, to_col)).astype(bf16)
        ends = layer_norm(sides_ref[...].reshape(-1, sides_ref.shape[-1]), gain_ref[...])
        ends = dot(ends, wkv_ref[...]).astype(bf16).astype(f32)
        sides[...] = ends.reshape(sides.shape)

    sheet = pl.program_id(0)
    count = BLOCK * BLOCK
    heads = 128 // HEAD_DIM
    head_of_row = lax.broadcasted_iota(jnp.int32, (heads, count, 128), 0)
    head_of_lane = lax.broadcasted_iota(jnp.int32, (heads, count, 128), 2) // HEAD_DIM
    own = (head_of_row == head_of_lane).astype(f32).astype(bf16).reshape(heads * count, 128)
    lane = lax.broadcasted_iota(jnp.int32, (count, 128), 1)
    place = lax.broadcasted_iota(jnp.int32, (span // 2, BLOCK, 128), 1)
    factor = math.log2(math.e) / math.sqrt(HEAD_DIM)

    def band(a, carry):
        at = pl.multiple_of(a * BLOCK, BLOCK)

        def keys_of(b, lanes):
            mid = slice(b * BLOCK, (b + 1) * BLOCK)
            main = kv_ref[sheet, pl.ds(at, span), mid, lanes].reshape(span * BLOCK, 128)

            def beside(g):
                if g < 0 or g >= groups:
                    found = sides[sheet, pl.ds(at, span), :, lanes]
                else:
                    found = kv_ref[sheet, pl.ds(at, span), g * BLOCK : (g + 1) * BLOCK, lanes]
                return found.reshape(span // 2, 2, BLOCK, 128)

            west, east = beside(b - 1), beside(b + 1)
            even = jnp.where(place >= 6, west[:, 0], east[:, 0])
            odd = pltpu.roll(jnp.where(place >= 6, west[:, 1], east[:, 1]), 4, 1)
            extra = jnp.where((place >= 6) | (place < 2), even, odd).reshape(span * 4, 128)
            return jnp.concatenate([main, extra], axis=0).astype(bf16)

        tiles = inner // 128

        def score(b, slot):
            mid = slice(b * BLOCK, (b + 1) * BLOCK)
            low = bias[a, b]
            for t in range(tiles):
                lanes = slice(t * 128, (t + 1) * 128)
                q = q_ref[sheet, pl.ds(at, BLOCK), mid, lanes].reshape(count, 128).astype(bf16)
                q = jnp.concatenate([q] * heads, axis=0) * own
                found = lax.dot_general(keys_of(b, lanes), q, (((1,), (1,)), ((), ())), preferred_element_type=f32)
                scores[slot, t] = found + jnp.concatenate([low] * (heads * count // 128), axis=1)

        def soften(slot):
            for t in range(tiles):
                for h in range(heads * count // 128):
                    lanes = slice(h * 128, (h + 1) * 128)
                    found = scores[slot, t, :, lanes]
                    top = jnp.max(found, axis=0, keepdims=True)
                    expon = jnp.exp2((found - top) * factor)
                    weights[slot, t, :, lanes] = (expon * (1.0 / jnp.sum(expon, axis=0, keepdims=True))).astype(bf16)

        def mix(b, slot):
            mid = slice(b * BLOCK, (b + 1) * BLOCK)
            for t in range(tiles):
                lanes = slice(t * 128, (t + 1) * 128)
                values = keys_of(b, slice(inner + t * 128, inner + (t + 1) * 128))
                mixed = lax.dot_general(weights[slot, t], values, (((0,), (0,)), ((), ())), preferred_element_type=f32)
                mixed = mixed.reshape(heads, count, 128)
                piece = mixed[0]
                for k in range(1, heads):
                    piece = jnp.where(lane >= k * HEAD_DIM, mixed[k], piece)
                context[pl.ds(at, BLOCK), mid, lanes] = piece.reshape(BLOCK, BLOCK, 128)

        score(0, 0)
        for b in range(groups):
            if b + 1 < groups:
                score(b + 1, (b + 1) % 2)
            soften(b % 2)
            mix(b, b % 2)
        return carry

    lax.fori_loop(0, rows // BLOCK, band, 0)
    mixed = context[...].reshape(rows * cols, inner).astype(bf16)
    attended = (tokens_ref[sheet].astype(f32) + dot(mixed, wout_ref[...])).astype(bf16)
    attended_ref[...] = attended
    first_row_ref[...] = attended[:cols]
    last_row_ref[...] = attended[(rows - 1) * cols :]
    by_place = attended.astype(f32).reshape(rows, cols, attended.shape[-1])
    first_col_ref[...] = by_place[:, 0].astype(bf16)
    last_col_ref[...] = by_place[:, cols - 1].astype(bf16)
    sums = dot(pool[...], attended).astype(bf16)
    sums_ref[...] = jnp.broadcast_to(sums[None], sums_ref.shape)


def combine_kernel(place_ref, near_ref, table_ref, parts_ref, out_ref):
    table = dot(near_ref[...], table_ref[...]).astype(bf16)
    added = dot(table, parts_ref[...]).astype(bf16)
    out_ref[...] = jnp.broadcast_to(added[None], out_ref.shape)


def conv_kernel(attended_ref, top_ref, bottom_ref, left_ref, right_ref, taps_ref, w_hbm, out_ref, ext, w, sems):
    area, width = attended_ref.shape
    cols = top_ref.shape[0]
    rows = area // cols
    out_ch = out_ref.shape[-1]
    s, step = pl.program_id(0), pl.program_id(1)

    fetches = [
        pltpu.make_async_copy(w_hbm.at[:, k, 0:width, :], w.at[k - 1], sems.at[k - 1]) for k in (1, 2)
    ]

    @pl.when((s == 0) & (step == 0))
    def _():
        for fetch in fetches:
            fetch.start()

    for k, fetch in enumerate(fetches):

        @pl.when((s == 0) & (step == k + 1))
        def _():
            fetch.wait()

    def edge(ref, w_ref):
        total = 0.0
        for a in range(3):
            total = total + dot(ref[...], w_ref[a])[a : a + rows]
        return total.reshape(rows, 1, out_ch)

    def middle(w_ref):
        total = dot(ext[0:area], w_ref[0])
        for a in range(1, 3):
            total = total + dot(ext[a * cols : a * cols + area], w_ref[a])
        return total.reshape(rows, cols, out_ch)

    @pl.when(step == 0)
    def _():
        ext[0:cols] = top_ref[...]
        ext[cols : cols + area] = attended_ref[...]
        ext[cols + area :] = bottom_ref[...]
        place = lax.broadcasted_iota(jnp.int32, (rows, cols, out_ch), 1)
        part = jnp.where(place == 0, edge(left_ref, taps_ref), pltpu.roll(middle(taps_ref), 1, 1))
        out_ref[s] = part.reshape(area, out_ch)

    @pl.when(step == 1)
    def _():
        out_ref[s] += middle(w.at[0]).reshape(area, out_ch)

    @pl.when(step == 2)
    def _():
        place = lax.broadcasted_iota(jnp.int32, (rows, cols, out_ch), 1)
        part = jnp.where(place == cols - 1, edge(right_ref, w.at[1]), pltpu.roll(middle(w.at[1]), cols - 1, 1))
        out_ref[s] += part.reshape(area, out_ch)


def split(x):
    high = x.astype(bf16)
    return high, (x - high.astype(f32)).astype(bf16)


def tail_kernel(
    place_ref, table_hbm, row_scale_hbm, col_scale_hbm, parts_hbm, wpool_hbm, wjoin_hbm, by_row_hbm, by_col_hbm,
    spread_hbm, conv, out_hbm,
    table, row_scale, col_scale, parts, by_row, by_col, spread, wpool, wjoin, taps, out, sems,
):
    width, ppm = wpool.shape[1], wpool.shape[2]
    count = len(LEVELS)
    r, c = place_ref[0], place_ref[1]
    small = [
        pltpu.make_async_copy(source, target, sems.at[0, k])
        for k, (source, target) in enumerate((
            (parts_hbm, parts), (table_hbm.at[c], table), (row_scale_hbm.at[r], row_scale),
            (col_scale_hbm.at[c], col_scale), (by_row_hbm.at[r], by_row), (by_col_hbm.at[c], by_col), (spread_hbm, spread),
        ))
    ]
    large = [pltpu.make_async_copy(wpool_hbm.at[k], wpool.at[k], sems.at[1, k]) for k in range(count)]
    for k in range(count):
        lines = slice(width + k * ppm, width + (k + 1) * ppm)
        large.append(pltpu.make_async_copy(wjoin_hbm.at[:, :, lines, :], wjoin.at[k], sems.at[1, count + k]))
    ahead = 5
    for copy in small + large[:ahead]:
        copy.start()

    def ready(k):
        large[k].wait()
        if k + ahead < len(large):
            large[k + ahead].start()

    for copy in small:
        copy.wait()

    def along(ref, axis):
        high, low = split(ref[...])
        return dot(high, spread[axis]) + dot(low, spread[axis])

    grid = along(by_row, 0)[:, None, :] * along(by_col, 1)[None, :, :]
    grid_high, grid_low = split(grid.reshape(grid.shape[0] * grid.shape[1], -1))
    scale = row_scale[...] * col_scale[...]
    scale = jnp.broadcast_to(scale, (128, scale.shape[1])).T[:, :1]
    pooled = dot(table[...], parts[...]) * scale
    branches = []
    row = 0
    for index, level in enumerate(LEVELS):
        slots = SLOTS[level]
        high, low = split(pooled[row : row + 2 * slots])
        ready(index)
        both = dot(jnp.concatenate([high, low], axis=0), wpool[index])
        high, low = split(jnp.maximum(both[: 2 * slots] + both[2 * slots :], 0.0))
        branches.append(jnp.concatenate([high, low], axis=0))
        row += 2 * slots
    results = [pltpu.make_async_copy(out.at[s], out_hbm.at[s], sems.at[2, s]) for s in range(2)]

    at = 0
    for index, level in enumerate(LEVELS):
        slots = SLOTS[level]
        ready(count + index)
        for a in range(3):
            for b in range(3):
                tap = dot(branches[index], wjoin[index, a, b])
                tap = tap[: 2 * slots] + tap[2 * slots :]
                start = at + (a * 3 + b) * slots
                for s in range(2):
                    taps[s, start : start + slots, :] = tap[s * slots : (s + 1) * slots]
        at += TAPS * slots
    for s in range(2):
        high, low = split(taps[s])
        total = conv[s] + dot(grid_high, high) + dot(grid_low, high) + dot(grid_high, low)
        out[s] = total.astype(bf16)
        results[s].start()
    for copy in results:
        copy.wait()


def cost(flops, nbytes, transcendentals=0):
    return pl.CostEstimate(flops=int(flops), bytes_accessed=int(nbytes), transcendentals=int(transcendentals))


def params(mib):
    return pltpu.CompilerParams(vmem_limit_bytes=mib * 2**20)


def whole(shape):
    return pl.BlockSpec(shape, lambda *_: (0,) * len(shape))


def in_vmem(x):
    return pltpu.with_memory_space_constraint(x, pltpu.VMEM)


def in_hbm(x):
    return pltpu.with_memory_space_constraint(x, pltpu.HBM)


def shifts(axis):
    count = lax.axis_size(axis)
    forward = [(i, i + 1) for i in range(count - 1)]
    return forward, [(j, i) for i, j in forward]


def layer(tokens, norm_gain, w_query, w_kv, w_out, w_pool, w_join):
    sheets, rows, cols, width = tokens.shape
    inner = w_query.shape[1]
    wide = w_kv.shape[1]
    out_ch = w_join.shape[-1]
    ppm = w_pool.shape[-1]
    area = rows * cols
    row_count, col_count = lax.axis_size("row"), lax.axis_size("col")
    r, c = lax.axis_index("row"), lax.axis_index("col")
    grid_h, grid_w = rows * row_count, cols * col_count
    gain = norm_gain.reshape(1, width)
    tables = pool_tables(rows, row_count, cols, col_count)
    row_masks, col_masks, strip_table, near_table, bin_table, row_scale, col_scale = tables
    by_row, by_col, spread = upsample_tables(rows, row_count, cols, col_count)
    masks = np.concatenate([row_masks, col_masks], axis=-1).reshape(row_count * col_count, UNITS, rows + cols)

    at = jnp.stack([r, c]).astype(jnp.int32)
    row_fwd, row_bwd = shifts("row")
    col_fwd, col_bwd = shifts("col")
    above = lax.ppermute(tokens[:, rows - HALO :], "row", row_fwd)
    below = lax.ppermute(tokens[:, :HALO], "row", row_bwd)

    def edges(first):
        return jnp.concatenate([x[:, :, first : first + HALO] for x in (above, tokens, below)], axis=1)

    west = lax.ppermute(edges(cols - HALO), "col", col_fwd)
    east = lax.ppermute(edges(0), "col", col_bwd)

    def per_sheet(*dims):
        return pl.BlockSpec((None,) + dims, lambda s, *_: (s,) + (0,) * len(dims))

    near = pl.BlockSpec(memory_space=pltpu.VMEM)
    far = pl.BlockSpec(memory_space=pl.ANY)
    wq_near, wkv_near = in_vmem(w_query), in_vmem(w_kv)
    gain = pl.pallas_call(
        warm_kernel,
        in_specs=[pl.BlockSpec(memory_space=pltpu.VMEM)] * 3,
        out_specs=pl.BlockSpec(memory_space=pltpu.VMEM),
        out_shape=jax.ShapeDtypeStruct((1, width), f32),
        compiler_params=params(4),
        name="warm",
    )(gain, wq_near, wkv_near)
    flat = in_vmem(tokens.reshape(sheets, area, width))
    edge = HALO * cols
    q, kv = pl.pallas_call(
        project_kernel,
        grid=(sheets,),
        in_specs=[near] * 6,
        out_specs=[near] * 2,
        out_shape=[
            pltpu.VMEM((sheets, rows, cols, inner), f32), pltpu.VMEM((sheets, rows + 2 * HALO, cols, wide), f32),
        ],
        compiler_params=params(28),
        cost_estimate=cost(2 * sheets * area * width * (inner + wide), 2 * (width * (inner + wide) + 5 * sheets * area * width)),
        name="project",
    )(
        flat, in_vmem(above.reshape(sheets, edge, width)), in_vmem(below.reshape(sheets, edge, width)),
        in_vmem(gain), wq_near, wkv_near,
    )

    blank = jnp.zeros((sheets, rows + 2 * HALO, BLOCK - 2 * HALO, width), bf16)
    sides = jnp.concatenate([east, blank, west], axis=2).reshape(sheets, (rows + 2 * HALO) * BLOCK, width)
    blocks = (rows // BLOCK) * (cols // BLOCK)
    keys = (BLOCK + 2 * HALO) ** 2

    def fixed(*dims):
        return whole(dims)

    attended, sums, first_row, last_row, first_col, last_col = pl.pallas_call(
        lambda *refs: attend_kernel((grid_h, grid_w), *refs),
        grid_spec=pltpu.PrefetchScalarGridSpec(
            num_scalar_prefetch=1,
            grid=(sheets,),
            in_specs=[
                near, near, near, near, near, near, fixed(inner, width),
                pl.BlockSpec((None, UNITS, rows + cols), lambda s, p: (p[0] * col_count + p[1], 0, 0)),
            ],
            out_specs=[
                pl.BlockSpec((None, area, width), lambda s, _: (s, 0, 0)),
                pl.BlockSpec((row_count, UNITS, width), lambda s, _: (0, s, 0)),
                per_sheet(cols, width), per_sheet(cols, width), per_sheet(rows, width), per_sheet(rows, width),
            ],
            scratch_shapes=[
                pltpu.VMEM((sheets, rows + 2 * HALO, BLOCK, wide), f32),
                pltpu.VMEM((rows, cols, inner), f32),
                pltpu.VMEM((rows // BLOCK, cols // BLOCK, keys, 128), f32),
                pltpu.VMEM((UNITS, area), bf16),
                pltpu.VMEM((2, inner // 128, keys, 256), f32),
                pltpu.VMEM((2, inner // 128, keys, 256), bf16),
            ],
        ),
        out_shape=[
            pltpu.HBM((sheets, area, width), bf16),
            jax.ShapeDtypeStruct((row_count, sheets * UNITS, width), bf16),
            jax.ShapeDtypeStruct((sheets, cols, width), bf16),
            jax.ShapeDtypeStruct((sheets, cols, width), bf16),
            jax.ShapeDtypeStruct((sheets, rows, width), bf16),
            jax.ShapeDtypeStruct((sheets, rows, width), bf16),
        ],
        compiler_params=params(32),
        cost_estimate=cost(2 * sheets * area * inner * width * 4, 2 * sheets * area * width * 4, sheets * blocks * keys * 1024),
        name="attend",
    )(
        at, in_vmem(q), in_vmem(kv), in_vmem(sides), flat, in_vmem(gain), wkv_near, w_out, masks,
    )

    strip_rows = sheets * STRIP_UNITS
    att_above = lax.ppermute(last_row, "row", row_fwd)
    att_below = lax.ppermute(first_row, "row", row_bwd)
    parts = lax.all_to_all(sums, "row", 0, 0, tiled=True).reshape(row_count * sheets * UNITS, width)

    def att_edges(middle, at):
        return jnp.concatenate([att_above[:, at : at + 1], middle, att_below[:, at : at + 1]], axis=1)

    att_west = lax.ppermute(att_edges(last_col, cols - 1), "col", col_fwd)
    att_east = lax.ppermute(att_edges(first_col, 0), "col", col_bwd)
    pad = ((0, 0), (0, 6), (0, 0))
    att_west, att_east = jnp.pad(att_west, pad), jnp.pad(att_east, pad)

    strips = pl.pallas_call(
        combine_kernel,
        grid_spec=pltpu.PrefetchScalarGridSpec(
            num_scalar_prefetch=1,
            grid=(1,),
            in_specs=[
                pl.BlockSpec((None,) + near_table.shape[1:], lambda k, p: (p[0], 0, 0)),
                pl.BlockSpec((None,) + strip_table.shape[1:], lambda k, p: (p[1], 0, 0)),
                fixed(row_count * sheets * UNITS, width),
            ],
            out_specs=fixed(col_count, strip_rows, width),
        ),
        out_shape=jax.ShapeDtypeStruct((col_count, strip_rows, width), bf16),
        compiler_params=params(8),
        name="combine",
    )(at, near_table.astype(bf16), strip_table.astype(bf16), parts)
    strips = lax.all_to_all(strips, "col", 0, 0, tiled=True).reshape(col_count * strip_rows, width)

    conv = pl.pallas_call(
        conv_kernel,
        grid=(sheets, 3),
        in_specs=[
            per_sheet(area, width), per_sheet(cols, width), per_sheet(cols, width),
            per_sheet(rows + 8, width), per_sheet(rows + 8, width),
            pl.BlockSpec((3, None, width, out_ch), lambda *_: (0, 0, 0, 0)), far,
        ],
        out_specs=pl.BlockSpec(memory_space=pltpu.VMEM),
        out_shape=pltpu.VMEM((sheets, area, out_ch), f32),
        scratch_shapes=[
            pltpu.VMEM((area + 2 * cols, width), bf16), pltpu.VMEM((2, 3, width, out_ch), bf16),
            pltpu.SemaphoreType.DMA((2,)),
        ],
        compiler_params=params(20),
        cost_estimate=cost(2 * sheets * area * width * 9 * out_ch, 2 * 9 * width * out_ch + 2 * sheets * area * width),
        name="conv",
    )(in_hbm(attended), att_above, att_below, att_west, att_east, in_hbm(w_join), in_hbm(w_join))
    conv = in_vmem(conv)

    depth = TAPS * sum(SLOTS.values())
    bin_rows = 2 * sum(SLOTS.values())
    out = pl.pallas_call(
        tail_kernel,
        grid_spec=pltpu.PrefetchScalarGridSpec(
            num_scalar_prefetch=1,
            grid=(1,),
            in_specs=[pl.BlockSpec(memory_space=pl.ANY) for _ in range(9)] + [pl.BlockSpec(memory_space=pltpu.VMEM)],
            out_specs=pl.BlockSpec(memory_space=pl.ANY),
            scratch_shapes=[
                pltpu.VMEM(bin_table.shape[1:], bf16),
                pltpu.VMEM((1, bin_rows), f32),
                pltpu.VMEM((1, bin_rows), f32),
                pltpu.VMEM((col_count * strip_rows, width), bf16),
                pltpu.VMEM((rows, 64), f32),
                pltpu.VMEM((cols, 64), f32),
                pltpu.VMEM((2, 64, depth), bf16),
                pltpu.VMEM(w_pool.shape, bf16),
                pltpu.VMEM((len(LEVELS), 3, 3, ppm, out_ch), bf16),
                pltpu.VMEM((sheets, depth, out_ch), f32),
                pltpu.VMEM((sheets, area, out_ch), bf16),
                pltpu.SemaphoreType.DMA((3, 2 * len(LEVELS))),
            ],
        ),
        out_shape=jax.ShapeDtypeStruct((sheets, area, out_ch), bf16),
        compiler_params=params(40),
        cost_estimate=cost(4e9, 2 * (w_pool.size + 9 * 4 * ppm * out_ch)),
        name="tail",
    )(
        at, bin_table.astype(bf16), row_scale, col_scale, strips, in_hbm(w_pool), in_hbm(w_join),
        by_row, by_col, spread.astype(bf16), conv,
    )
    return out.reshape(sheets, rows, cols, out_ch)


def solution(mesh):
    placed = (P(None, "row", "col", None), P(), P(), P(), P(), P(), P())
    return jax.shard_map(layer, mesh=mesh, in_specs=placed, out_specs=P(None, "row", "col", None), check_vma=False)
```

```python
import math

import jax
import jax.numpy as jnp
import numpy as np
from jax import lax
from jax.experimental import pallas as pl
from jax.experimental.pallas import tpu as pltpu
from jax.sharding import PartitionSpec as P

HEAD_DIM = 32
BLOCK = 8
HALO = 2
EPS = 1e-05
LEVELS = (1, 2, 3, 6)
CODED = (6, 3, 2)
UNITS = 8
STRIP_ALL = 24
STRIP_ALL_AT = {6: 0, 3: 12, 2: 18}
STRIP_UNITS = 16
STRIP_AT = {6: 0, 3: 6, 2: 12}
NEAR = {1: 1, 2: 2, 3: 3, 6: 3}
SLOTS = {1: 8, 2: 8, 3: 16, 6: 16}
TAPS = 9
f32 = jnp.float32
bf16 = jnp.bfloat16


def bins_of(level, length, first, count):
    places = first + np.arange(count)
    found = []
    for cell in range(level):
        start = cell * length // level
        end = ((cell + 1) * length + level - 1) // level
        mask = (places >= start) & (places < end)
        if mask.any():
            found.append((cell, mask))
    return found


def lower_bin(level, length, place):
    return max((2 * place + 1) * level - length, 0) // (2 * length)


def first_bin(level, length, first, count):
    start = min(lower_bin(level, length, first - 1), level - NEAR[level])
    assert min(lower_bin(level, length, first + count) + 1, level - 1) < start + NEAR[level]
    return start


def pool_tables(rows, row_strips, cols, col_strips):
    grid_h, grid_w = rows * row_strips, cols * col_strips
    row_masks = np.zeros((row_strips, col_strips, UNITS, rows), np.float32)
    col_masks = np.zeros((row_strips, col_strips, UNITS, cols), np.float32)
    strip = np.zeros((col_strips, 2 * STRIP_ALL, row_strips, 2 * UNITS), np.float32)
    near = np.zeros((row_strips, 2 * STRIP_UNITS, 2 * STRIP_ALL), np.float32)
    slots = 2 * sum(SLOTS.values())
    bins = np.zeros((col_strips, slots, col_strips, 2 * STRIP_UNITS), np.float32)
    row_scale = np.zeros((row_strips, 1, slots), np.float32)
    col_scale = np.zeros((col_strips, 1, slots), np.float32)
    for c in range(col_strips):
        for r in range(row_strips):
            units = []
            for level in CODED:
                for i, row_mask in bins_of(level, grid_h, r * rows, rows):
                    for g, (j, col_mask) in enumerate(bins_of(level, grid_w, c * cols, cols)):
                        key = (row_mask.tobytes(), col_mask.tobytes())
                        if key not in units:
                            units.append(key)
                            at = len(units) - 1
                            row_masks[r, c, at] = row_mask
                            col_masks[r, c, at] = col_mask
                        at = units.index(key)
                        width = 1 if level == 2 else 2
                        for s in range(2):
                            target = s * STRIP_ALL + STRIP_ALL_AT[level] + i * width + g
                            strip[c, target, r, s * UNITS + at] = 1.0
            assert len(units) <= UNITS
    for r in range(row_strips):
        for level in CODED:
            width = 1 if level == 2 else 2
            start = first_bin(level, grid_h, r * rows, rows)
            for k in range(NEAR[level] * width):
                for s in range(2):
                    source = s * STRIP_ALL + STRIP_ALL_AT[level] + start * width + k
                    near[r, s * STRIP_UNITS + STRIP_AT[level] + k, source] = 1.0
    for c in range(col_strips):
        base = 0
        for level in LEVELS:
            source = 2 if level == 1 else level
            width = 1 if source == 2 else 2
            start = first_bin(level, grid_w, c * cols, cols)
            for p in range(col_strips):
                for g, (j, _) in enumerate(bins_of(source, grid_w, p * cols, cols)):
                    j = 0 if level == 1 else j - start
                    if not 0 <= j < NEAR[level]:
                        continue
                    for i in range(NEAR[source]):
                        for s in range(2):
                            cell = 0 if level == 1 else i * NEAR[level] + j
                            at = base + s * SLOTS[level] + cell
                            bins[c, at, p, s * STRIP_UNITS + STRIP_AT[source] + i * width + g] = 1.0
            base += 2 * SLOTS[level]
    for table, strips, size, along_rows in ((row_scale, row_strips, rows, True), (col_scale, col_strips, cols, False)):
        for at in range(strips):
            base = 0
            for level in LEVELS:
                length = size * strips
                start = first_bin(level, length, at * size, size)
                sizes = [mask.sum() for _, mask in bins_of(level, length, 0, length)]
                for i in range(NEAR[level]):
                    for j in range(NEAR[level]):
                        for s in range(2):
                            k = base + s * SLOTS[level] + i * NEAR[level] + j
                            table[at, 0, k] = 1.0 / sizes[start + (i if along_rows else j)]
                base += 2 * SLOTS[level]
    strip = strip.reshape(col_strips, 2 * STRIP_ALL, -1)
    return row_masks, col_masks, strip, near, bins.reshape(col_strips, slots, -1), row_scale, col_scale


def upsample_weights(level, length, first, count):
    places = first + np.arange(count)
    numer = np.maximum((2 * places + 1) * level - length, 0)
    lower = numer // (2 * length)
    frac = (numer - lower * 2 * length).astype(np.float32) / np.float32(2.0 * length)
    upper = np.minimum(lower + 1, level - 1)
    cells = np.arange(level)[None, :]
    weight = (cells == lower[:, None]) * (1.0 - frac)[:, None] + (cells == upper[:, None]) * frac[:, None]
    inside = (places >= 0) & (places < length)
    return (weight * inside[:, None]).astype(np.float32)


def upsample_tables(rows, row_strips, cols, col_strips):
    width = TAPS * sum(SLOTS.values())
    cells = sum(NEAR.values())
    spread = np.zeros((2, 64, width), np.float32)

    def strips_of(size, strips):
        table = np.zeros((strips, size, 64), np.float32)
        length = size * strips
        for strip in range(strips):
            first = 0
            for level in LEVELS:
                start = first_bin(level, length, strip * size, size)
                for a in range(3):
                    w = upsample_weights(level, length, strip * size + a - 1, size)
                    at = a * cells + first
                    table[strip, :, at : at + NEAR[level]] = w[:, start : start + NEAR[level]]
                first += NEAR[level]
        return table

    base, first = 0, 0
    for level in LEVELS:
        for a in range(3):
            for c in range(3):
                for i in range(NEAR[level]):
                    for j in range(NEAR[level]):
                        at = base + (a * 3 + c) * SLOTS[level] + i * NEAR[level] + j
                        spread[0, a * cells + first + i, at] = 1.0
                        spread[1, c * cells + first + j, at] = 1.0
        base += TAPS * SLOTS[level]
        first += NEAR[level]
    return strips_of(rows, row_strips), strips_of(cols, col_strips), spread


def layer_norm(tokens, gain):
    x = tokens.astype(f32)
    center = jnp.mean(x, axis=-1, keepdims=True)
    x = x - center
    spread = jnp.mean(x * x, axis=-1, keepdims=True)
    return (x * lax.rsqrt(spread + EPS) * gain).astype(bf16)


def dot(a, b):
    return jnp.dot(a, b, preferred_element_type=f32)


def warm_kernel(gain_ref, wq_ref, wkv_ref, out_ref):
    out_ref[...] = gain_ref[...]


def pool_members(masks_ref, pool, cols):
    masks = masks_ref[...].astype(bf16)
    _, count = masks.shape
    area = pool.shape[1]
    rows = count - cols
    unit = lax.broadcasted_iota(jnp.int32, (count, area), 0)
    token = lax.broadcasted_iota(jnp.int32, (count, area), 1)
    to_row = (unit == token // cols).astype(f32).astype(bf16)
    to_col = (unit - rows == token % cols).astype(f32).astype(bf16)
    pool[...] = (dot(masks, to_row) * dot(masks, to_col)).astype(bf16)


def project_kernel(
    grid_shape, place_ref, tokens_ref, above_ref, below_ref, gain_ref, wq, wkv, masks_ref,
    q_ref, kv_ref, bias, pool, context, scores, weights,
):
    rows, cols, inner = q_ref.shape[1:]
    s = pl.program_id(0)
    gain = gain_ref[...]
    normed = layer_norm(tokens_ref[s], gain)
    q_ref[s] = dot(normed, wq[...]).astype(bf16).astype(f32).reshape(rows, cols, inner)
    kv_ref[s, HALO : rows + HALO] = dot(normed, wkv[...]).astype(bf16).astype(f32).reshape(rows, cols, -1)
    edge = layer_norm(jnp.concatenate([above_ref[s], below_ref[s]], axis=0), gain)
    edge = dot(edge, wkv[...]).astype(bf16).astype(f32).reshape(2 * HALO, cols, -1)
    kv_ref[s, 0:HALO] = edge[:HALO]
    kv_ref[s, rows + HALO :] = edge[HALO:]

    @pl.when(s == 0)
    def _():
        window_bias(bias, place_ref[0] * rows, place_ref[1] * cols, *grid_shape)
        pool_members(masks_ref, pool, cols)

    def store(at, b, lanes, piece):
        context[s, at : at + BLOCK, (b - 1) * BLOCK : b * BLOCK, lanes] = piece

    middle = range(1, cols // BLOCK - 1)
    attend_blocks(middle, s, q_ref, kv_ref, None, bias, scores, weights, store)


def window_bias(bias, first_row, first_col, grid_h, grid_w):
    span = BLOCK + 2 * HALO
    key = lax.broadcasted_iota(jnp.int32, bias.shape[2:], 0)
    extra = key - span * BLOCK
    lane = extra & 7
    odd = ((lane >= 2) & (lane < 6)).astype(jnp.int32)
    west = (lane >= 6) | ((lane >= 2) & (lane < 4))
    main = key < span * BLOCK
    row = jnp.where(main, key >> 3, 2 * (extra >> 3) + odd) - HALO
    col = jnp.where(main, key & 7, (key & 1) + jnp.where(west, -HALO, BLOCK))
    for a in range(bias.shape[0]):
        at = row + (first_row + a * BLOCK)
        row_ok = (at >= 0) & (at < grid_h)
        for b in range(bias.shape[1]):
            at = col + (first_col + b * BLOCK)
            bias[a, b] = jnp.where(row_ok & (at >= 0) & (at < grid_w), 0.0, -1e30)


def attend_blocks(columns, sheet, q_ref, kv_ref, sides, bias, scores, weights, store):
    rows, cols, inner = q_ref.shape[1:]
    groups = cols // BLOCK
    span = BLOCK + 2 * HALO
    tiles = inner // 128
    count = BLOCK * BLOCK
    heads = 128 // HEAD_DIM
    head_of_row = lax.broadcasted_iota(jnp.int32, (heads, count, 128), 0)
    head_of_lane = lax.broadcasted_iota(jnp.int32, (heads, count, 128), 2) // HEAD_DIM
    own = (head_of_row == head_of_lane).astype(f32).astype(bf16).reshape(heads * count, 128)
    lane = lax.broadcasted_iota(jnp.int32, (count, 128), 1)
    place = lax.broadcasted_iota(jnp.int32, (span // 2, BLOCK, 128), 1)
    factor = math.log2(math.e) / math.sqrt(HEAD_DIM)

    def keys_of(at, b, lanes):
        main = kv_ref[sheet, at : at + span, b * BLOCK : (b + 1) * BLOCK, lanes].reshape(span * BLOCK, 128)

        def beside(g):
            if g < 0 or g >= groups:
                found = sides[sheet, at : at + span, :, lanes]
            else:
                found = kv_ref[sheet, at : at + span, g * BLOCK : (g + 1) * BLOCK, lanes]
            return found.reshape(span // 2, 2, BLOCK, 128)

        west, east = beside(b - 1), beside(b + 1)
        even = jnp.where(place >= 6, west[:, 0], east[:, 0])
        odd = pltpu.roll(jnp.where(place >= 6, west[:, 1], east[:, 1]), 4, 1)
        extra = jnp.where((place >= 6) | (place < 2), even, odd).reshape(span * 4, 128)
        return jnp.concatenate([main, extra], axis=0).astype(bf16)

    def score(at, b, slot):
        low = bias[at // BLOCK, b]
        for t in range(tiles):
            lanes = slice(t * 128, (t + 1) * 128)
            q = q_ref[sheet, at : at + BLOCK, b * BLOCK : (b + 1) * BLOCK, lanes].reshape(count, 128).astype(bf16)
            q = jnp.concatenate([q] * heads, axis=0) * own
            found = lax.dot_general(keys_of(at, b, lanes), q, (((1,), (1,)), ((), ())), preferred_element_type=f32)
            scores[slot, t] = found + jnp.concatenate([low] * (heads * count // 128), axis=1)

    def soften(slot):
        for t in range(tiles):
            for h in range(heads * count // 128):
                lanes = slice(h * 128, (h + 1) * 128)
                found = scores[slot, t, :, lanes]
                top = jnp.max(found, axis=0, keepdims=True)
                expon = jnp.exp2((found - top) * factor)
                weights[slot, t, :, lanes] = (expon * (1.0 / jnp.sum(expon, axis=0, keepdims=True))).astype(bf16)

    def mix(at, b, slot):
        for t in range(tiles):
            lanes = slice(t * 128, (t + 1) * 128)
            values = keys_of(at, b, slice(inner + t * 128, inner + (t + 1) * 128))
            mixed = lax.dot_general(weights[slot, t], values, (((0,), (0,)), ((), ())), preferred_element_type=f32)
            mixed = mixed.reshape(heads, count, 128)
            piece = mixed[0]
            for k in range(1, heads):
                piece = jnp.where(lane >= k * HEAD_DIM, mixed[k], piece)
            store(at, b, lanes, piece.reshape(BLOCK, BLOCK, 128))

    blocks = [(at, b) for at in range(0, rows, BLOCK) for b in columns]
    score(*blocks[0], 0)
    for k, block in enumerate(blocks):
        if k + 1 < len(blocks):
            score(*blocks[k + 1], (k + 1) % 2)
        soften(k % 2)
        mix(*block, k % 2)


def attend_kernel(
    q_ref, kv_ref, sides_ref, tokens_ref, gain_ref, wkv_ref, middle_ref, bias, pool, wout_ref,
    attended_ref, sums_ref, first_row_ref, last_row_ref, first_col_ref, last_col_ref, sides, outer, scores, weights,
):
    rows, cols, inner = q_ref.shape[1:]
    sheet = pl.program_id(0)

    @pl.when(sheet == 0)
    def _():
        ends = layer_norm(sides_ref[...].reshape(-1, sides_ref.shape[-1]), gain_ref[...])
        ends = dot(ends, wkv_ref[...]).astype(bf16).astype(f32)
        sides[...] = ends.reshape(sides.shape)

    last = cols // BLOCK - 1

    def store(at, b, lanes, piece):
        outer[b // last, at : at + BLOCK, :, lanes] = piece

    attend_blocks((0, last), sheet, q_ref, kv_ref, sides, bias, scores, weights, store)
    mixed = jnp.concatenate([outer[0], middle_ref[sheet], outer[1]], axis=1)
    mixed = mixed.reshape(rows * cols, inner).astype(bf16)
    attended = (tokens_ref[sheet].astype(f32) + dot(mixed, wout_ref[...])).astype(bf16)
    attended_ref[...] = attended
    first_row_ref[...] = attended[:cols]
    last_row_ref[...] = attended[(rows - 1) * cols :]
    by_place = attended.astype(f32).reshape(rows, cols, attended.shape[-1])
    first_col_ref[...] = by_place[:, 0].astype(bf16)
    last_col_ref[...] = by_place[:, cols - 1].astype(bf16)
    sums = dot(pool[...], attended).astype(bf16)
    sums_ref[...] = jnp.broadcast_to(sums[None], sums_ref.shape)


def combine_kernel(place_ref, near_ref, table_ref, parts_ref, out_ref):
    table = dot(near_ref[...], table_ref[...]).astype(bf16)
    added = dot(table, parts_ref[...]).astype(bf16)
    out_ref[...] = jnp.broadcast_to(added[None], out_ref.shape)


def conv_kernel(attended_ref, top_ref, bottom_ref, left_ref, right_ref, taps_ref, w_hbm, out_ref, ext, w, sems):
    area, width = attended_ref.shape
    cols = top_ref.shape[0]
    rows = area // cols
    out_ch = out_ref.shape[-1]
    s, step = pl.program_id(0), pl.program_id(1)

    fetches = [
        pltpu.make_async_copy(w_hbm.at[:, k, 0:width, :], w.at[k - 1], sems.at[k - 1]) for k in (1, 2)
    ]

    @pl.when((s == 0) & (step == 0))
    def _():
        for fetch in fetches:
            fetch.start()

    for k, fetch in enumerate(fetches):

        @pl.when((s == 0) & (step == k + 1))
        def _():
            fetch.wait()

    def edge(ref, w_ref):
        total = 0.0
        for a in range(3):
            total = total + dot(ref[...], w_ref[a])[a : a + rows]
        return total.reshape(rows, 1, out_ch)

    def middle(w_ref):
        total = dot(ext[0:area], w_ref[0])
        for a in range(1, 3):
            total = total + dot(ext[a * cols : a * cols + area], w_ref[a])
        return total.reshape(rows, cols, out_ch)

    @pl.when(step == 0)
    def _():
        ext[0:cols] = top_ref[...]
        ext[cols : cols + area] = attended_ref[...]
        ext[cols + area :] = bottom_ref[...]
        place = lax.broadcasted_iota(jnp.int32, (rows, cols, out_ch), 1)
        part = jnp.where(place == 0, edge(left_ref, taps_ref), pltpu.roll(middle(taps_ref), 1, 1))
        out_ref[s] = part.reshape(area, out_ch)

    @pl.when(step == 1)
    def _():
        out_ref[s] += middle(w.at[0]).reshape(area, out_ch)

    @pl.when(step == 2)
    def _():
        place = lax.broadcasted_iota(jnp.int32, (rows, cols, out_ch), 1)
        part = jnp.where(place == cols - 1, edge(right_ref, w.at[1]), pltpu.roll(middle(w.at[1]), cols - 1, 1))
        out_ref[s] += part.reshape(area, out_ch)


def split(x):
    high = x.astype(bf16)
    return high, (x - high.astype(f32)).astype(bf16)


def tail_kernel(
    place_ref, table_hbm, row_scale_hbm, col_scale_hbm, parts_hbm, wpool_hbm, wjoin_hbm, by_row_hbm, by_col_hbm,
    spread_hbm, conv, out_hbm,
    table, row_scale, col_scale, parts, by_row, by_col, spread, wpool, wjoin, taps, out, sems,
):
    width, ppm = wpool.shape[1], wpool.shape[2]
    count = len(LEVELS)
    r, c = place_ref[0], place_ref[1]
    small = [
        pltpu.make_async_copy(source, target, sems.at[0, k])
        for k, (source, target) in enumerate((
            (parts_hbm, parts), (table_hbm.at[c], table), (row_scale_hbm.at[r], row_scale),
            (col_scale_hbm.at[c], col_scale), (by_row_hbm.at[r], by_row), (by_col_hbm.at[c], by_col), (spread_hbm, spread),
        ))
    ]
    large = [pltpu.make_async_copy(wpool_hbm.at[k], wpool.at[k], sems.at[1, k]) for k in range(count)]
    for k in range(count):
        lines = slice(width + k * ppm, width + (k + 1) * ppm)
        large.append(pltpu.make_async_copy(wjoin_hbm.at[:, :, lines, :], wjoin.at[k], sems.at[1, count + k]))
    ahead = 5
    for copy in small + large[:ahead]:
        copy.start()

    def ready(k):
        large[k].wait()
        if k + ahead < len(large):
            large[k + ahead].start()

    for copy in small:
        copy.wait()

    def along(ref, axis):
        high, low = split(ref[...])
        return dot(high, spread[axis]) + dot(low, spread[axis])

    grid = along(by_row, 0)[:, None, :] * along(by_col, 1)[None, :, :]
    grid_high, grid_low = split(grid.reshape(grid.shape[0] * grid.shape[1], -1))
    scale = row_scale[...] * col_scale[...]
    scale = jnp.broadcast_to(scale, (128, scale.shape[1])).T[:, :1]
    pooled = dot(table[...], parts[...]) * scale
    branches = []
    row = 0
    for index, level in enumerate(LEVELS):
        slots = SLOTS[level]
        high, low = split(pooled[row : row + 2 * slots])
        ready(index)
        both = dot(jnp.concatenate([high, low], axis=0), wpool[index])
        high, low = split(jnp.maximum(both[: 2 * slots] + both[2 * slots :], 0.0))
        branches.append(jnp.concatenate([high, low], axis=0))
        row += 2 * slots
    results = [pltpu.make_async_copy(out.at[s], out_hbm.at[s], sems.at[2, s]) for s in range(2)]

    at = 0
    for index, level in enumerate(LEVELS):
        slots = SLOTS[level]
        ready(count + index)
        for a in range(3):
            for b in range(3):
                tap = dot(branches[index], wjoin[index, a, b])
                tap = tap[: 2 * slots] + tap[2 * slots :]
                start = at + (a * 3 + b) * slots
                for s in range(2):
                    taps[s, start : start + slots, :] = tap[s * slots : (s + 1) * slots]
        at += TAPS * slots
    for s in range(2):
        high, low = split(taps[s])
        total = conv[s] + dot(grid_high, high) + dot(grid_low, high) + dot(grid_high, low)
        out[s] = total.astype(bf16)
        results[s].start()
    for copy in results:
        copy.wait()


def cost(flops, nbytes, transcendentals=0):
    return pl.CostEstimate(flops=int(flops), bytes_accessed=int(nbytes), transcendentals=int(transcendentals))


def params(mib):
    return pltpu.CompilerParams(vmem_limit_bytes=mib * 2**20)


def whole(shape):
    return pl.BlockSpec(shape, lambda *_: (0,) * len(shape))


def in_vmem(x):
    return pltpu.with_memory_space_constraint(x, pltpu.VMEM)


def in_hbm(x):
    return pltpu.with_memory_space_constraint(x, pltpu.HBM)


def shifts(axis):
    count = lax.axis_size(axis)
    forward = [(i, i + 1) for i in range(count - 1)]
    return forward, [(j, i) for i, j in forward]


def layer(tokens, norm_gain, w_query, w_kv, w_out, w_pool, w_join):
    sheets, rows, cols, width = tokens.shape
    inner = w_query.shape[1]
    wide = w_kv.shape[1]
    out_ch = w_join.shape[-1]
    ppm = w_pool.shape[-1]
    area = rows * cols
    row_count, col_count = lax.axis_size("row"), lax.axis_size("col")
    r, c = lax.axis_index("row"), lax.axis_index("col")
    grid_h, grid_w = rows * row_count, cols * col_count
    gain = norm_gain.reshape(1, width)
    tables = pool_tables(rows, row_count, cols, col_count)
    row_masks, col_masks, strip_table, near_table, bin_table, row_scale, col_scale = tables
    by_row, by_col, spread = upsample_tables(rows, row_count, cols, col_count)
    masks = np.concatenate([row_masks, col_masks], axis=-1).reshape(row_count * col_count, UNITS, rows + cols)

    at = jnp.stack([r, c]).astype(jnp.int32)
    row_fwd, row_bwd = shifts("row")
    col_fwd, col_bwd = shifts("col")
    above = lax.ppermute(tokens[:, rows - HALO :], "row", row_fwd)
    below = lax.ppermute(tokens[:, :HALO], "row", row_bwd)

    def edges(first):
        return jnp.concatenate([x[:, :, first : first + HALO] for x in (above, tokens, below)], axis=1)

    west = lax.ppermute(edges(cols - HALO), "col", col_fwd)
    east = lax.ppermute(edges(0), "col", col_bwd)

    def per_sheet(*dims):
        return pl.BlockSpec((None,) + dims, lambda s, *_: (s,) + (0,) * len(dims))

    near = pl.BlockSpec(memory_space=pltpu.VMEM)
    far = pl.BlockSpec(memory_space=pl.ANY)
    wq_near, wkv_near = in_vmem(w_query), in_vmem(w_kv)
    gain = pl.pallas_call(
        warm_kernel,
        in_specs=[pl.BlockSpec(memory_space=pltpu.VMEM)] * 3,
        out_specs=pl.BlockSpec(memory_space=pltpu.VMEM),
        out_shape=jax.ShapeDtypeStruct((1, width), f32),
        compiler_params=params(4),
        name="warm",
    )(gain, wq_near, wkv_near)
    flat = in_vmem(tokens.reshape(sheets, area, width))
    edge = HALO * cols
    blocks = (rows // BLOCK) * (cols // BLOCK)
    keys = (BLOCK + 2 * HALO) ** 2
    stage = [pltpu.VMEM((2, inner // 128, keys, 256), f32), pltpu.VMEM((2, inner // 128, keys, 256), bf16)]
    q, kv, bias, pool, middle = pl.pallas_call(
        lambda *refs: project_kernel((grid_h, grid_w), *refs),
        grid_spec=pltpu.PrefetchScalarGridSpec(
            num_scalar_prefetch=1,
            grid=(sheets,),
            in_specs=[near] * 6 + [
                pl.BlockSpec((None, UNITS, rows + cols), lambda s, p: (p[0] * col_count + p[1], 0, 0)),
            ],
            out_specs=[near] * 5,
            scratch_shapes=stage,
        ),
        out_shape=[
            pltpu.VMEM((sheets, rows, cols, inner), f32), pltpu.VMEM((sheets, rows + 2 * HALO, cols, wide), f32),
            pltpu.VMEM((rows // BLOCK, cols // BLOCK, keys, 128), f32), pltpu.VMEM((UNITS, area), bf16),
            pltpu.VMEM((sheets, rows, cols - 2 * BLOCK, inner), f32),
        ],
        compiler_params=params(16),
        cost_estimate=cost(2 * sheets * area * width * (inner + wide), 2 * (width * (inner + wide) + 5 * sheets * area * width)),
        name="project",
    )(
        at, flat, in_vmem(above.reshape(sheets, edge, width)), in_vmem(below.reshape(sheets, edge, width)),
        in_vmem(gain), wq_near, wkv_near, masks,
    )

    blank = jnp.zeros((sheets, rows + 2 * HALO, BLOCK - 2 * HALO, width), bf16)
    sides = jnp.concatenate([east, blank, west], axis=2).reshape(sheets, (rows + 2 * HALO) * BLOCK, width)

    def fixed(*dims):
        return whole(dims)

    attended, sums, first_row, last_row, first_col, last_col = pl.pallas_call(
        attend_kernel,
        grid=(sheets,),
        in_specs=[near] * 9 + [fixed(inner, width)],
        out_specs=[
            per_sheet(area, width),
            pl.BlockSpec((row_count, UNITS, width), lambda s: (0, s, 0)),
            per_sheet(cols, width), per_sheet(cols, width), per_sheet(rows, width), per_sheet(rows, width),
        ],
        scratch_shapes=[
            pltpu.VMEM((sheets, rows + 2 * HALO, BLOCK, wide), f32), pltpu.VMEM((2, rows, BLOCK, inner), f32),
        ] + stage,
        out_shape=[
            pltpu.HBM((sheets, area, width), bf16),
            jax.ShapeDtypeStruct((row_count, sheets * UNITS, width), bf16),
            jax.ShapeDtypeStruct((sheets, cols, width), bf16),
            jax.ShapeDtypeStruct((sheets, cols, width), bf16),
            jax.ShapeDtypeStruct((sheets, rows, width), bf16),
            jax.ShapeDtypeStruct((sheets, rows, width), bf16),
        ],
        compiler_params=params(20),
        cost_estimate=cost(2 * sheets * area * inner * width * 4, 2 * sheets * area * width * 4, sheets * blocks * keys * 1024),
        name="attend",
    )(
        in_vmem(q), in_vmem(kv), in_vmem(sides), flat, in_vmem(gain), wkv_near, in_vmem(middle), in_vmem(bias),
        in_vmem(pool), w_out,
    )

    strip_rows = sheets * STRIP_UNITS
    att_above = lax.ppermute(last_row, "row", row_fwd)
    att_below = lax.ppermute(first_row, "row", row_bwd)
    parts = lax.all_to_all(sums, "row", 0, 0, tiled=True).reshape(row_count * sheets * UNITS, width)

    def att_edges(middle, at):
        return jnp.concatenate([att_above[:, at : at + 1], middle, att_below[:, at : at + 1]], axis=1)

    att_west = lax.ppermute(att_edges(last_col, cols - 1), "col", col_fwd)
    att_east = lax.ppermute(att_edges(first_col, 0), "col", col_bwd)
    pad = ((0, 0), (0, 6), (0, 0))
    att_west, att_east = jnp.pad(att_west, pad), jnp.pad(att_east, pad)

    strips = pl.pallas_call(
        combine_kernel,
        grid_spec=pltpu.PrefetchScalarGridSpec(
            num_scalar_prefetch=1,
            grid=(1,),
            in_specs=[
                pl.BlockSpec((None,) + near_table.shape[1:], lambda k, p: (p[0], 0, 0)),
                pl.BlockSpec((None,) + strip_table.shape[1:], lambda k, p: (p[1], 0, 0)),
                fixed(row_count * sheets * UNITS, width),
            ],
            out_specs=fixed(col_count, strip_rows, width),
        ),
        out_shape=jax.ShapeDtypeStruct((col_count, strip_rows, width), bf16),
        compiler_params=params(8),
        name="combine",
    )(at, near_table.astype(bf16), strip_table.astype(bf16), parts)
    strips = lax.all_to_all(strips, "col", 0, 0, tiled=True).reshape(col_count * strip_rows, width)

    conv = pl.pallas_call(
        conv_kernel,
        grid=(sheets, 3),
        in_specs=[
            per_sheet(area, width), per_sheet(cols, width), per_sheet(cols, width),
            per_sheet(rows + 8, width), per_sheet(rows + 8, width),
            pl.BlockSpec((3, None, width, out_ch), lambda *_: (0, 0, 0, 0)), far,
        ],
        out_specs=pl.BlockSpec(memory_space=pltpu.VMEM),
        out_shape=pltpu.VMEM((sheets, area, out_ch), f32),
        scratch_shapes=[
            pltpu.VMEM((area + 2 * cols, width), bf16), pltpu.VMEM((2, 3, width, out_ch), bf16),
            pltpu.SemaphoreType.DMA((2,)),
        ],
        compiler_params=params(20),
        cost_estimate=cost(2 * sheets * area * width * 9 * out_ch, 2 * 9 * width * out_ch + 2 * sheets * area * width),
        name="conv",
    )(in_hbm(attended), att_above, att_below, att_west, att_east, in_hbm(w_join), in_hbm(w_join))
    conv = in_vmem(conv)

    depth = TAPS * sum(SLOTS.values())
    bin_rows = 2 * sum(SLOTS.values())
    out = pl.pallas_call(
        tail_kernel,
        grid_spec=pltpu.PrefetchScalarGridSpec(
            num_scalar_prefetch=1,
            grid=(1,),
            in_specs=[pl.BlockSpec(memory_space=pl.ANY) for _ in range(9)] + [pl.BlockSpec(memory_space=pltpu.VMEM)],
            out_specs=pl.BlockSpec(memory_space=pl.ANY),
            scratch_shapes=[
                pltpu.VMEM(bin_table.shape[1:], bf16),
                pltpu.VMEM((1, bin_rows), f32),
                pltpu.VMEM((1, bin_rows), f32),
                pltpu.VMEM((col_count * strip_rows, width), bf16),
                pltpu.VMEM((rows, 64), f32),
                pltpu.VMEM((cols, 64), f32),
                pltpu.VMEM((2, 64, depth), bf16),
                pltpu.VMEM(w_pool.shape, bf16),
                pltpu.VMEM((len(LEVELS), 3, 3, ppm, out_ch), bf16),
                pltpu.VMEM((sheets, depth, out_ch), f32),
                pltpu.VMEM((sheets, area, out_ch), bf16),
                pltpu.SemaphoreType.DMA((3, 2 * len(LEVELS))),
            ],
        ),
        out_shape=jax.ShapeDtypeStruct((sheets, area, out_ch), bf16),
        compiler_params=params(40),
        cost_estimate=cost(4e9, 2 * (w_pool.size + 9 * 4 * ppm * out_ch)),
        name="tail",
    )(
        at, bin_table.astype(bf16), row_scale, col_scale, strips, in_hbm(w_pool), in_hbm(w_join),
        by_row, by_col, spread.astype(bf16), conv,
    )
    return out.reshape(sheets, rows, cols, out_ch)


def solution(mesh):
    placed = (P(None, "row", "col", None), P(), P(), P(), P(), P(), P())
    return jax.shard_map(layer, mesh=mesh, in_specs=placed, out_specs=P(None, "row", "col", None), check_vma=False)
```

```python
import math

import jax
import jax.numpy as jnp
import numpy as np
from jax import lax
from jax.experimental import pallas as pl
from jax.experimental.pallas import tpu as pltpu
from jax.sharding import PartitionSpec as P

HEAD_DIM = 32
BLOCK = 8
HALO = 2
EPS = 1e-05
LEVELS = (1, 2, 3, 6)
CODED = (6, 3, 2)
UNITS = 8
STRIP_ALL = 24
STRIP_ALL_AT = {6: 0, 3: 12, 2: 18}
STRIP_UNITS = 16
STRIP_AT = {6: 0, 3: 6, 2: 12}
NEAR = {1: 1, 2: 2, 3: 3, 6: 3}
SLOTS = {1: 8, 2: 8, 3: 16, 6: 16}
TAPS = 9
f32 = jnp.float32
bf16 = jnp.bfloat16


def bins_of(level, length, first, count):
    places = first + np.arange(count)
    found = []
    for cell in range(level):
        start = cell * length // level
        end = ((cell + 1) * length + level - 1) // level
        mask = (places >= start) & (places < end)
        if mask.any():
            found.append((cell, mask))
    return found


def lower_bin(level, length, place):
    return max((2 * place + 1) * level - length, 0) // (2 * length)


def first_bin(level, length, first, count):
    start = min(lower_bin(level, length, first - 1), level - NEAR[level])
    assert min(lower_bin(level, length, first + count) + 1, level - 1) < start + NEAR[level]
    return start


def pool_tables(rows, row_strips, cols, col_strips):
    grid_h, grid_w = rows * row_strips, cols * col_strips
    row_masks = np.zeros((row_strips, col_strips, UNITS, rows), np.float32)
    col_masks = np.zeros((row_strips, col_strips, UNITS, cols), np.float32)
    strip = np.zeros((col_strips, 2 * STRIP_ALL, row_strips, 2 * UNITS), np.float32)
    near = np.zeros((row_strips, 2 * STRIP_UNITS, 2 * STRIP_ALL), np.float32)
    slots = 2 * sum(SLOTS.values())
    bins = np.zeros((col_strips, slots, col_strips, 2 * STRIP_UNITS), np.float32)
    row_scale = np.zeros((row_strips, 1, slots), np.float32)
    col_scale = np.zeros((col_strips, 1, slots), np.float32)
    for c in range(col_strips):
        for r in range(row_strips):
            units = []
            for level in CODED:
                for i, row_mask in bins_of(level, grid_h, r * rows, rows):
                    for g, (j, col_mask) in enumerate(bins_of(level, grid_w, c * cols, cols)):
                        key = (row_mask.tobytes(), col_mask.tobytes())
                        if key not in units:
                            units.append(key)
                            at = len(units) - 1
                            row_masks[r, c, at] = row_mask
                            col_masks[r, c, at] = col_mask
                        at = units.index(key)
                        width = 1 if level == 2 else 2
                        for s in range(2):
                            target = s * STRIP_ALL + STRIP_ALL_AT[level] + i * width + g
                            strip[c, target, r, s * UNITS + at] = 1.0
            assert len(units) <= UNITS
    for r in range(row_strips):
        for level in CODED:
            width = 1 if level == 2 else 2
            start = first_bin(level, grid_h, r * rows, rows)
            for k in range(NEAR[level] * width):
                for s in range(2):
                    source = s * STRIP_ALL + STRIP_ALL_AT[level] + start * width + k
                    near[r, s * STRIP_UNITS + STRIP_AT[level] + k, source] = 1.0
    for c in range(col_strips):
        base = 0
        for level in LEVELS:
            source = 2 if level == 1 else level
            width = 1 if source == 2 else 2
            start = first_bin(level, grid_w, c * cols, cols)
            for p in range(col_strips):
                for g, (j, _) in enumerate(bins_of(source, grid_w, p * cols, cols)):
                    j = 0 if level == 1 else j - start
                    if not 0 <= j < NEAR[level]:
                        continue
                    for i in range(NEAR[source]):
                        for s in range(2):
                            cell = 0 if level == 1 else i * NEAR[level] + j
                            at = base + s * SLOTS[level] + cell
                            bins[c, at, p, s * STRIP_UNITS + STRIP_AT[source] + i * width + g] = 1.0
            base += 2 * SLOTS[level]
    for table, strips, size, along_rows in ((row_scale, row_strips, rows, True), (col_scale, col_strips, cols, False)):
        for at in range(strips):
            base = 0
            for level in LEVELS:
                length = size * strips
                start = first_bin(level, length, at * size, size)
                sizes = [mask.sum() for _, mask in bins_of(level, length, 0, length)]
                for i in range(NEAR[level]):
                    for j in range(NEAR[level]):
                        for s in range(2):
                            k = base + s * SLOTS[level] + i * NEAR[level] + j
                            table[at, 0, k] = 1.0 / sizes[start + (i if along_rows else j)]
                base += 2 * SLOTS[level]
    strip = strip.reshape(col_strips, 2 * STRIP_ALL, -1)
    return row_masks, col_masks, strip, near, bins.reshape(col_strips, slots, -1), row_scale, col_scale


def upsample_weights(level, length, first, count):
    places = first + np.arange(count)
    numer = np.maximum((2 * places + 1) * level - length, 0)
    lower = numer // (2 * length)
    frac = (numer - lower * 2 * length).astype(np.float32) / np.float32(2.0 * length)
    upper = np.minimum(lower + 1, level - 1)
    cells = np.arange(level)[None, :]
    weight = (cells == lower[:, None]) * (1.0 - frac)[:, None] + (cells == upper[:, None]) * frac[:, None]
    inside = (places >= 0) & (places < length)
    return (weight * inside[:, None]).astype(np.float32)


def upsample_tables(rows, row_strips, cols, col_strips):
    width = TAPS * sum(SLOTS.values())
    cells = sum(NEAR.values())
    spread = np.zeros((2, 64, width), np.float32)

    def strips_of(size, strips):
        table = np.zeros((strips, size, 64), np.float32)
        length = size * strips
        for strip in range(strips):
            first = 0
            for level in LEVELS:
                start = first_bin(level, length, strip * size, size)
                for a in range(3):
                    w = upsample_weights(level, length, strip * size + a - 1, size)
                    at = a * cells + first
                    table[strip, :, at : at + NEAR[level]] = w[:, start : start + NEAR[level]]
                first += NEAR[level]
        return table

    base, first = 0, 0
    for level in LEVELS:
        for a in range(3):
            for c in range(3):
                for i in range(NEAR[level]):
                    for j in range(NEAR[level]):
                        at = base + (a * 3 + c) * SLOTS[level] + i * NEAR[level] + j
                        spread[0, a * cells + first + i, at] = 1.0
                        spread[1, c * cells + first + j, at] = 1.0
        base += TAPS * SLOTS[level]
        first += NEAR[level]
    return strips_of(rows, row_strips), strips_of(cols, col_strips), spread


def layer_norm(tokens, gain):
    x = tokens.astype(f32)
    center = jnp.mean(x, axis=-1, keepdims=True)
    x = x - center
    spread = jnp.mean(x * x, axis=-1, keepdims=True)
    return (x * lax.rsqrt(spread + EPS) * gain).astype(bf16)


def dot(a, b):
    return jnp.dot(a, b, preferred_element_type=f32)


def project_kernel(tokens_ref, gain_ref, wq, wkv, q_ref, kv_ref):
    rows, cols, inner = q_ref.shape[1:]
    s = pl.program_id(0)
    normed = layer_norm(tokens_ref[s], gain_ref[...])
    q_ref[s] = dot(normed, wq[...]).astype(bf16).astype(f32).reshape(rows, cols, inner)
    kv_ref[s] = dot(normed, wkv[...]).astype(bf16).astype(f32).reshape(rows, cols, -1)


def pool_members(masks_ref, pool, cols):
    masks = masks_ref[...].astype(bf16)
    _, count = masks.shape
    area = pool.shape[1]
    rows = count - cols
    unit = lax.broadcasted_iota(jnp.int32, (count, area), 0)
    token = lax.broadcasted_iota(jnp.int32, (count, area), 1)
    to_row = (unit == token // cols).astype(f32).astype(bf16)
    to_col = (unit - rows == token % cols).astype(f32).astype(bf16)
    pool[...] = (dot(masks, to_row) * dot(masks, to_col)).astype(bf16)


def middle_kernel(
    grid_shape, place_ref, q_ref, kv_ref, above_ref, below_ref, gain_ref, wkv, masks_ref,
    halo_ref, bias, pool, context, scores, weights,
):
    rows, cols = q_ref.shape[1:3]
    s = pl.program_id(0)

    @pl.when(s == 0)
    def _():
        window_bias(bias, place_ref[0] * rows, place_ref[1] * cols, *grid_shape)
        pool_members(masks_ref, pool, cols)
        edge = jnp.concatenate([above_ref[...], below_ref[...]], axis=1)
        edge = layer_norm(edge.reshape(-1, edge.shape[-1]), gain_ref[...])
        halo_ref[...] = dot(edge, wkv[...]).astype(bf16).astype(f32).reshape(halo_ref.shape)

    def store(at, b, lanes, piece):
        context[s, at : at + BLOCK, (b - 1) * BLOCK : b * BLOCK, lanes] = piece

    middle = range(1, cols // BLOCK - 1)
    attend_blocks(middle, s, q_ref, kv_ref, halo_ref, None, bias, scores, weights, store)


def window_bias(bias, first_row, first_col, grid_h, grid_w):
    span = BLOCK + 2 * HALO
    key = lax.broadcasted_iota(jnp.int32, bias.shape[2:], 0)
    extra = key - span * BLOCK
    lane = extra & 7
    odd = ((lane >= 2) & (lane < 6)).astype(jnp.int32)
    west = (lane >= 6) | ((lane >= 2) & (lane < 4))
    main = key < span * BLOCK
    row = jnp.where(main, key >> 3, 2 * (extra >> 3) + odd) - HALO
    col = jnp.where(main, key & 7, (key & 1) + jnp.where(west, -HALO, BLOCK))
    for a in range(bias.shape[0]):
        at = row + (first_row + a * BLOCK)
        row_ok = (at >= 0) & (at < grid_h)
        for b in range(bias.shape[1]):
            at = col + (first_col + b * BLOCK)
            bias[a, b] = jnp.where(row_ok & (at >= 0) & (at < grid_w), 0.0, -1e30)


def attend_blocks(columns, sheet, q_ref, kv_ref, halo_ref, sides, bias, scores, weights, store):
    rows, cols, inner = q_ref.shape[1:]
    groups = cols // BLOCK
    span = BLOCK + 2 * HALO
    tiles = inner // 128
    count = BLOCK * BLOCK
    heads = 128 // HEAD_DIM
    head_of_row = lax.broadcasted_iota(jnp.int32, (heads, count, 128), 0)
    head_of_lane = lax.broadcasted_iota(jnp.int32, (heads, count, 128), 2) // HEAD_DIM
    own = (head_of_row == head_of_lane).astype(f32).astype(bf16).reshape(heads * count, 128)
    lane = lax.broadcasted_iota(jnp.int32, (count, 128), 1)
    place = lax.broadcasted_iota(jnp.int32, (span // 2, BLOCK, 128), 1)
    factor = math.log2(math.e) / math.sqrt(HEAD_DIM)

    def rows_of(at, g, lanes):
        places = slice(g * BLOCK, (g + 1) * BLOCK)
        parts = [kv_ref[sheet, max(at - HALO, 0) : min(at + BLOCK + HALO, rows), places, lanes]]
        if at == 0:
            parts = [halo_ref[sheet, 0:HALO, places, lanes]] + parts
        if at + BLOCK == rows:
            parts = parts + [halo_ref[sheet, HALO:, places, lanes]]
        return jnp.concatenate(parts, axis=0)

    def keys_of(at, b, lanes):
        main = rows_of(at, b, lanes).reshape(span * BLOCK, 128)

        def beside(g):
            if g < 0 or g >= groups:
                found = sides[sheet, at : at + span, :, lanes]
            else:
                found = rows_of(at, g, lanes)
            return found.reshape(span // 2, 2, BLOCK, 128)

        west, east = beside(b - 1), beside(b + 1)
        even = jnp.where(place >= 6, west[:, 0], east[:, 0])
        odd = pltpu.roll(jnp.where(place >= 6, west[:, 1], east[:, 1]), 4, 1)
        extra = jnp.where((place >= 6) | (place < 2), even, odd).reshape(span * 4, 128)
        return jnp.concatenate([main, extra], axis=0).astype(bf16)

    def score(at, b, slot):
        low = bias[at // BLOCK, b]
        for t in range(tiles):
            lanes = slice(t * 128, (t + 1) * 128)
            q = q_ref[sheet, at : at + BLOCK, b * BLOCK : (b + 1) * BLOCK, lanes].reshape(count, 128).astype(bf16)
            q = jnp.concatenate([q] * heads, axis=0) * own
            found = lax.dot_general(keys_of(at, b, lanes), q, (((1,), (1,)), ((), ())), preferred_element_type=f32)
            scores[slot, t] = found + jnp.concatenate([low] * (heads * count // 128), axis=1)

    def soften(slot):
        for t in range(tiles):
            for h in range(heads * count // 128):
                lanes = slice(h * 128, (h + 1) * 128)
                found = scores[slot, t, :, lanes]
                top = jnp.max(found, axis=0, keepdims=True)
                expon = jnp.exp2((found - top) * factor)
                weights[slot, t, :, lanes] = (expon * (1.0 / jnp.sum(expon, axis=0, keepdims=True))).astype(bf16)

    def mix(at, b, slot):
        for t in range(tiles):
            lanes = slice(t * 128, (t + 1) * 128)
            values = keys_of(at, b, slice(inner + t * 128, inner + (t + 1) * 128))
            mixed = lax.dot_general(weights[slot, t], values, (((0,), (0,)), ((), ())), preferred_element_type=f32)
            mixed = mixed.reshape(heads, count, 128)
            piece = mixed[0]
            for k in range(1, heads):
                piece = jnp.where(lane >= k * HEAD_DIM, mixed[k], piece)
            store(at, b, lanes, piece.reshape(BLOCK, BLOCK, 128))

    blocks = [(at, b) for at in range(0, rows, BLOCK) for b in columns]
    score(*blocks[0], 0)
    for k, block in enumerate(blocks):
        if k + 1 < len(blocks):
            score(*blocks[k + 1], (k + 1) % 2)
        soften(k % 2)
        mix(*block, k % 2)


def attend_kernel(
    q_ref, kv_ref, halo_ref, sides_ref, tokens_ref, gain_ref, wkv_ref, middle_ref, bias, pool, wout_ref,
    attended_ref, sums_ref, first_row_ref, last_row_ref, first_col_ref, last_col_ref, sides, outer, scores, weights,
):
    rows, cols, inner = q_ref.shape[1:]
    sheet = pl.program_id(0)

    @pl.when(sheet == 0)
    def _():
        ends = layer_norm(sides_ref[...].reshape(-1, sides_ref.shape[-1]), gain_ref[...])
        ends = dot(ends, wkv_ref[...]).astype(bf16).astype(f32)
        sides[...] = ends.reshape(sides.shape)

    last = cols // BLOCK - 1

    def store(at, b, lanes, piece):
        outer[b // last, at : at + BLOCK, :, lanes] = piece

    attend_blocks((0, last), sheet, q_ref, kv_ref, halo_ref, sides, bias, scores, weights, store)
    mixed = jnp.concatenate([outer[0], middle_ref[sheet], outer[1]], axis=1)
    mixed = mixed.reshape(rows * cols, inner).astype(bf16)
    attended = (tokens_ref[sheet].astype(f32) + dot(mixed, wout_ref[...])).astype(bf16)
    attended_ref[...] = attended
    first_row_ref[...] = attended[:cols]
    last_row_ref[...] = attended[(rows - 1) * cols :]
    by_place = attended.astype(f32).reshape(rows, cols, attended.shape[-1])
    first_col_ref[...] = by_place[:, 0].astype(bf16)
    last_col_ref[...] = by_place[:, cols - 1].astype(bf16)
    sums = dot(pool[...], attended).astype(bf16)
    sums_ref[...] = jnp.broadcast_to(sums[None], sums_ref.shape)


def combine_kernel(place_ref, near_ref, table_ref, parts_ref, out_ref):
    table = dot(near_ref[...], table_ref[...]).astype(bf16)
    added = dot(table, parts_ref[...]).astype(bf16)
    out_ref[...] = jnp.broadcast_to(added[None], out_ref.shape)


def conv_kernel(attended_ref, top_ref, bottom_ref, left_ref, right_ref, taps_ref, w_hbm, out_ref, ext, w, sems):
    area, width = attended_ref.shape
    cols = top_ref.shape[0]
    rows = area // cols
    out_ch = out_ref.shape[-1]
    s, step = pl.program_id(0), pl.program_id(1)

    fetches = [
        pltpu.make_async_copy(w_hbm.at[:, k, 0:width, :], w.at[k - 1], sems.at[k - 1]) for k in (1, 2)
    ]

    @pl.when((s == 0) & (step == 0))
    def _():
        for fetch in fetches:
            fetch.start()

    for k, fetch in enumerate(fetches):

        @pl.when((s == 0) & (step == k + 1))
        def _():
            fetch.wait()

    def edge(ref, w_ref):
        total = 0.0
        for a in range(3):
            total = total + dot(ref[...], w_ref[a])[a : a + rows]
        return total.reshape(rows, 1, out_ch)

    def middle(w_ref):
        total = dot(ext[0:area], w_ref[0])
        for a in range(1, 3):
            total = total + dot(ext[a * cols : a * cols + area], w_ref[a])
        return total.reshape(rows, cols, out_ch)

    @pl.when(step == 0)
    def _():
        ext[0:cols] = top_ref[...]
        ext[cols : cols + area] = attended_ref[...]
        ext[cols + area :] = bottom_ref[...]
        place = lax.broadcasted_iota(jnp.int32, (rows, cols, out_ch), 1)
        part = jnp.where(place == 0, edge(left_ref, taps_ref), pltpu.roll(middle(taps_ref), 1, 1))
        out_ref[s] = part.reshape(area, out_ch)

    @pl.when(step == 1)
    def _():
        out_ref[s] += middle(w.at[0]).reshape(area, out_ch)

    @pl.when(step == 2)
    def _():
        place = lax.broadcasted_iota(jnp.int32, (rows, cols, out_ch), 1)
        part = jnp.where(place == cols - 1, edge(right_ref, w.at[1]), pltpu.roll(middle(w.at[1]), cols - 1, 1))
        out_ref[s] += part.reshape(area, out_ch)


def split(x):
    high = x.astype(bf16)
    return high, (x - high.astype(f32)).astype(bf16)


def tail_kernel(
    place_ref, table_hbm, row_scale_hbm, col_scale_hbm, parts_hbm, wpool_hbm, wjoin_hbm, by_row_hbm, by_col_hbm,
    spread_hbm, conv, out_hbm,
    table, row_scale, col_scale, parts, by_row, by_col, spread, wpool, wjoin, taps, out, sems,
):
    width, ppm = wpool.shape[1], wpool.shape[2]
    count = len(LEVELS)
    r, c = place_ref[0], place_ref[1]
    small = [
        pltpu.make_async_copy(source, target, sems.at[0, k])
        for k, (source, target) in enumerate((
            (parts_hbm, parts), (table_hbm.at[c], table), (row_scale_hbm.at[r], row_scale),
            (col_scale_hbm.at[c], col_scale), (by_row_hbm.at[r], by_row), (by_col_hbm.at[c], by_col), (spread_hbm, spread),
        ))
    ]
    large = [pltpu.make_async_copy(wpool_hbm.at[k], wpool.at[k], sems.at[1, k]) for k in range(count)]
    for k in range(count):
        lines = slice(width + k * ppm, width + (k + 1) * ppm)
        large.append(pltpu.make_async_copy(wjoin_hbm.at[:, :, lines, :], wjoin.at[k], sems.at[1, count + k]))
    ahead = 5
    for copy in small + large[:ahead]:
        copy.start()

    def ready(k):
        large[k].wait()
        if k + ahead < len(large):
            large[k + ahead].start()

    for copy in small:
        copy.wait()

    def along(ref, axis):
        high, low = split(ref[...])
        return dot(high, spread[axis]) + dot(low, spread[axis])

    grid = along(by_row, 0)[:, None, :] * along(by_col, 1)[None, :, :]
    grid_high, grid_low = split(grid.reshape(grid.shape[0] * grid.shape[1], -1))
    scale = row_scale[...] * col_scale[...]
    scale = jnp.broadcast_to(scale, (128, scale.shape[1])).T[:, :1]
    pooled = dot(table[...], parts[...]) * scale
    branches = []
    row = 0
    for index, level in enumerate(LEVELS):
        slots = SLOTS[level]
        high, low = split(pooled[row : row + 2 * slots])
        ready(index)
        both = dot(jnp.concatenate([high, low], axis=0), wpool[index])
        high, low = split(jnp.maximum(both[: 2 * slots] + both[2 * slots :], 0.0))
        branches.append(jnp.concatenate([high, low], axis=0))
        row += 2 * slots
    results = [pltpu.make_async_copy(out.at[s], out_hbm.at[s], sems.at[2, s]) for s in range(2)]

    at = 0
    for index, level in enumerate(LEVELS):
        slots = SLOTS[level]
        ready(count + index)
        for a in range(3):
            for b in range(3):
                tap = dot(branches[index], wjoin[index, a, b])
                tap = tap[: 2 * slots] + tap[2 * slots :]
                start = at + (a * 3 + b) * slots
                for s in range(2):
                    taps[s, start : start + slots, :] = tap[s * slots : (s + 1) * slots]
        at += TAPS * slots
    for s in range(2):
        high, low = split(taps[s])
        total = conv[s] + dot(grid_high, high) + dot(grid_low, high) + dot(grid_high, low)
        out[s] = total.astype(bf16)
        results[s].start()
    for copy in results:
        copy.wait()


def cost(flops, nbytes, transcendentals=0):
    return pl.CostEstimate(flops=int(flops), bytes_accessed=int(nbytes), transcendentals=int(transcendentals))


def params(mib):
    return pltpu.CompilerParams(vmem_limit_bytes=mib * 2**20)


def whole(shape):
    return pl.BlockSpec(shape, lambda *_: (0,) * len(shape))


def in_vmem(x):
    return pltpu.with_memory_space_constraint(x, pltpu.VMEM)


def in_hbm(x):
    return pltpu.with_memory_space_constraint(x, pltpu.HBM)


def shifts(axis):
    count = lax.axis_size(axis)
    forward = [(i, i + 1) for i in range(count - 1)]
    return forward, [(j, i) for i, j in forward]


def layer(tokens, norm_gain, w_query, w_kv, w_out, w_pool, w_join):
    sheets, rows, cols, width = tokens.shape
    inner = w_query.shape[1]
    wide = w_kv.shape[1]
    out_ch = w_join.shape[-1]
    ppm = w_pool.shape[-1]
    area = rows * cols
    row_count, col_count = lax.axis_size("row"), lax.axis_size("col")
    r, c = lax.axis_index("row"), lax.axis_index("col")
    grid_h, grid_w = rows * row_count, cols * col_count
    gain = norm_gain.reshape(1, width)
    tables = pool_tables(rows, row_count, cols, col_count)
    row_masks, col_masks, strip_table, near_table, bin_table, row_scale, col_scale = tables
    by_row, by_col, spread = upsample_tables(rows, row_count, cols, col_count)
    masks = np.concatenate([row_masks, col_masks], axis=-1).reshape(row_count * col_count, UNITS, rows + cols)

    at = jnp.stack([r, c]).astype(jnp.int32)
    row_fwd, row_bwd = shifts("row")
    col_fwd, col_bwd = shifts("col")
    above = lax.ppermute(tokens[:, rows - HALO :], "row", row_fwd)
    below = lax.ppermute(tokens[:, :HALO], "row", row_bwd)

    def edges(first):
        return jnp.concatenate([x[:, :, first : first + HALO] for x in (above, tokens, below)], axis=1)

    west = lax.ppermute(edges(cols - HALO), "col", col_fwd)
    east = lax.ppermute(edges(0), "col", col_bwd)

    def per_sheet(*dims):
        return pl.BlockSpec((None,) + dims, lambda s, *_: (s,) + (0,) * len(dims))

    near = pl.BlockSpec(memory_space=pltpu.VMEM)
    far = pl.BlockSpec(memory_space=pl.ANY)
    wq_near, wkv_near = in_vmem(w_query), in_vmem(w_kv)
    flat = in_vmem(tokens.reshape(sheets, area, width))
    edge = HALO * cols
    blocks = (rows // BLOCK) * (cols // BLOCK)
    keys = (BLOCK + 2 * HALO) ** 2
    stage = [pltpu.VMEM((2, inner // 128, keys, 256), f32), pltpu.VMEM((2, inner // 128, keys, 256), bf16)]
    gain = in_vmem(gain)
    q, kv = pl.pallas_call(
        project_kernel,
        grid=(sheets,),
        in_specs=[near] * 4,
        out_specs=[near] * 2,
        out_shape=[pltpu.VMEM((sheets, rows, cols, inner), f32), pltpu.VMEM((sheets, rows, cols, wide), f32)],
        compiler_params=params(16),
        cost_estimate=cost(2 * sheets * area * width * (inner + wide), 2 * (width * (inner + wide) + 5 * sheets * area * width)),
        name="project",
    )(flat, gain, wq_near, wkv_near)
    q, kv = in_vmem(q), in_vmem(kv)
    halo, bias, pool, middle = pl.pallas_call(
        lambda *refs: middle_kernel((grid_h, grid_w), *refs),
        grid_spec=pltpu.PrefetchScalarGridSpec(
            num_scalar_prefetch=1,
            grid=(sheets,),
            in_specs=[near] * 6 + [
                pl.BlockSpec((None, UNITS, rows + cols), lambda s, p: (p[0] * col_count + p[1], 0, 0)),
            ],
            out_specs=[near] * 4,
            scratch_shapes=stage,
        ),
        out_shape=[
            pltpu.VMEM((sheets, 2 * HALO, cols, wide), f32),
            pltpu.VMEM((rows // BLOCK, cols // BLOCK, keys, 128), f32), pltpu.VMEM((UNITS, area), bf16),
            pltpu.VMEM((sheets, rows, cols - 2 * BLOCK, inner), f32),
        ],
        compiler_params=params(16),
        cost_estimate=cost(2 * sheets * area * width * wide, 8 * sheets * area * width, sheets * blocks * keys * 512),
        name="middle",
    )(
        at, q, kv, in_vmem(above.reshape(sheets, edge, width)), in_vmem(below.reshape(sheets, edge, width)),
        gain, wkv_near, masks,
    )

    blank = jnp.zeros((sheets, rows + 2 * HALO, BLOCK - 2 * HALO, width), bf16)
    sides = jnp.concatenate([east, blank, west], axis=2).reshape(sheets, (rows + 2 * HALO) * BLOCK, width)

    def fixed(*dims):
        return whole(dims)

    attended, sums, first_row, last_row, first_col, last_col = pl.pallas_call(
        attend_kernel,
        grid=(sheets,),
        in_specs=[near] * 10 + [fixed(inner, width)],
        out_specs=[
            per_sheet(area, width),
            pl.BlockSpec((row_count, UNITS, width), lambda s: (0, s, 0)),
            per_sheet(cols, width), per_sheet(cols, width), per_sheet(rows, width), per_sheet(rows, width),
        ],
        scratch_shapes=[
            pltpu.VMEM((sheets, rows + 2 * HALO, BLOCK, wide), f32), pltpu.VMEM((2, rows, BLOCK, inner), f32),
        ] + stage,
        out_shape=[
            pltpu.HBM((sheets, area, width), bf16),
            jax.ShapeDtypeStruct((row_count, sheets * UNITS, width), bf16),
            jax.ShapeDtypeStruct((sheets, cols, width), bf16),
            jax.ShapeDtypeStruct((sheets, cols, width), bf16),
            jax.ShapeDtypeStruct((sheets, rows, width), bf16),
            jax.ShapeDtypeStruct((sheets, rows, width), bf16),
        ],
        compiler_params=params(20),
        cost_estimate=cost(2 * sheets * area * inner * width * 4, 2 * sheets * area * width * 4, sheets * blocks * keys * 1024),
        name="attend",
    )(
        q, kv, in_vmem(halo), in_vmem(sides), flat, gain, wkv_near, in_vmem(middle), in_vmem(bias),
        in_vmem(pool), w_out,
    )

    strip_rows = sheets * STRIP_UNITS
    att_above = lax.ppermute(last_row, "row", row_fwd)
    att_below = lax.ppermute(first_row, "row", row_bwd)
    parts = lax.all_to_all(sums, "row", 0, 0, tiled=True).reshape(row_count * sheets * UNITS, width)

    def att_edges(middle, at):
        return jnp.concatenate([att_above[:, at : at + 1], middle, att_below[:, at : at + 1]], axis=1)

    att_west = lax.ppermute(att_edges(last_col, cols - 1), "col", col_fwd)
    att_east = lax.ppermute(att_edges(first_col, 0), "col", col_bwd)
    pad = ((0, 0), (0, 6), (0, 0))
    att_west, att_east = jnp.pad(att_west, pad), jnp.pad(att_east, pad)

    strips = pl.pallas_call(
        combine_kernel,
        grid_spec=pltpu.PrefetchScalarGridSpec(
            num_scalar_prefetch=1,
            grid=(1,),
            in_specs=[
                pl.BlockSpec((None,) + near_table.shape[1:], lambda k, p: (p[0], 0, 0)),
                pl.BlockSpec((None,) + strip_table.shape[1:], lambda k, p: (p[1], 0, 0)),
                fixed(row_count * sheets * UNITS, width),
            ],
            out_specs=fixed(col_count, strip_rows, width),
        ),
        out_shape=jax.ShapeDtypeStruct((col_count, strip_rows, width), bf16),
        compiler_params=params(8),
        name="combine",
    )(at, near_table.astype(bf16), strip_table.astype(bf16), parts)
    strips = lax.all_to_all(strips, "col", 0, 0, tiled=True).reshape(col_count * strip_rows, width)

    conv = pl.pallas_call(
        conv_kernel,
        grid=(sheets, 3),
        in_specs=[
            per_sheet(area, width), per_sheet(cols, width), per_sheet(cols, width),
            per_sheet(rows + 8, width), per_sheet(rows + 8, width),
            pl.BlockSpec((3, None, width, out_ch), lambda *_: (0, 0, 0, 0)), far,
        ],
        out_specs=pl.BlockSpec(memory_space=pltpu.VMEM),
        out_shape=pltpu.VMEM((sheets, area, out_ch), f32),
        scratch_shapes=[
            pltpu.VMEM((area + 2 * cols, width), bf16), pltpu.VMEM((2, 3, width, out_ch), bf16),
            pltpu.SemaphoreType.DMA((2,)),
        ],
        compiler_params=params(20),
        cost_estimate=cost(2 * sheets * area * width * 9 * out_ch, 2 * 9 * width * out_ch + 2 * sheets * area * width),
        name="conv",
    )(in_hbm(attended), att_above, att_below, att_west, att_east, in_hbm(w_join), in_hbm(w_join))
    conv = in_vmem(conv)

    depth = TAPS * sum(SLOTS.values())
    bin_rows = 2 * sum(SLOTS.values())
    out = pl.pallas_call(
        tail_kernel,
        grid_spec=pltpu.PrefetchScalarGridSpec(
            num_scalar_prefetch=1,
            grid=(1,),
            in_specs=[pl.BlockSpec(memory_space=pl.ANY) for _ in range(9)] + [pl.BlockSpec(memory_space=pltpu.VMEM)],
            out_specs=pl.BlockSpec(memory_space=pl.ANY),
            scratch_shapes=[
                pltpu.VMEM(bin_table.shape[1:], bf16),
                pltpu.VMEM((1, bin_rows), f32),
                pltpu.VMEM((1, bin_rows), f32),
                pltpu.VMEM((col_count * strip_rows, width), bf16),
                pltpu.VMEM((rows, 64), f32),
                pltpu.VMEM((cols, 64), f32),
                pltpu.VMEM((2, 64, depth), bf16),
                pltpu.VMEM(w_pool.shape, bf16),
                pltpu.VMEM((len(LEVELS), 3, 3, ppm, out_ch), bf16),
                pltpu.VMEM((sheets, depth, out_ch), f32),
                pltpu.VMEM((sheets, area, out_ch), bf16),
                pltpu.SemaphoreType.DMA((3, 2 * len(LEVELS))),
            ],
        ),
        out_shape=jax.ShapeDtypeStruct((sheets, area, out_ch), bf16),
        compiler_params=params(40),
        cost_estimate=cost(4e9, 2 * (w_pool.size + 9 * 4 * ppm * out_ch)),
        name="tail",
    )(
        at, bin_table.astype(bf16), row_scale, col_scale, strips, in_hbm(w_pool), in_hbm(w_join),
        by_row, by_col, spread.astype(bf16), conv,
    )
    return out.reshape(sheets, rows, cols, out_ch)


def solution(mesh):
    placed = (P(None, "row", "col", None), P(), P(), P(), P(), P(), P())
    return jax.shard_map(layer, mesh=mesh, in_specs=placed, out_specs=P(None, "row", "col", None), check_vma=False)
```

```python
import math

import jax
import jax.numpy as jnp
import numpy as np
from jax import lax
from jax.experimental import pallas as pl
from jax.experimental.pallas import tpu as pltpu
from jax.sharding import PartitionSpec as P

HEAD_DIM = 32
BLOCK = 8
HALO = 2
EPS = 1e-05
LEVELS = (1, 2, 3, 6)
CODED = (6, 3, 2)
UNITS = 8
STRIP_ALL = 24
STRIP_ALL_AT = {6: 0, 3: 12, 2: 18}
STRIP_UNITS = 16
STRIP_AT = {6: 0, 3: 6, 2: 12}
NEAR = {1: 1, 2: 2, 3: 3, 6: 3}
SLOTS = {1: 8, 2: 8, 3: 16, 6: 16}
TAPS = 9
f32 = jnp.float32
bf16 = jnp.bfloat16


def bins_of(level, length, first, count):
    places = first + np.arange(count)
    found = []
    for cell in range(level):
        start = cell * length // level
        end = ((cell + 1) * length + level - 1) // level
        mask = (places >= start) & (places < end)
        if mask.any():
            found.append((cell, mask))
    return found


def lower_bin(level, length, place):
    return max((2 * place + 1) * level - length, 0) // (2 * length)


def first_bin(level, length, first, count):
    start = min(lower_bin(level, length, first - 1), level - NEAR[level])
    assert min(lower_bin(level, length, first + count) + 1, level - 1) < start + NEAR[level]
    return start


def pool_tables(rows, row_strips, cols, col_strips):
    grid_h, grid_w = rows * row_strips, cols * col_strips
    row_masks = np.zeros((row_strips, col_strips, UNITS, rows), np.float32)
    col_masks = np.zeros((row_strips, col_strips, UNITS, cols), np.float32)
    strip = np.zeros((col_strips, 2 * STRIP_ALL, row_strips, 2 * UNITS), np.float32)
    near = np.zeros((row_strips, 2 * STRIP_UNITS, 2 * STRIP_ALL), np.float32)
    slots = 2 * sum(SLOTS.values())
    bins = np.zeros((col_strips, slots, col_strips, 2 * STRIP_UNITS), np.float32)
    row_scale = np.zeros((row_strips, 1, slots), np.float32)
    col_scale = np.zeros((col_strips, 1, slots), np.float32)
    for c in range(col_strips):
        for r in range(row_strips):
            units = []
            for level in CODED:
                for i, row_mask in bins_of(level, grid_h, r * rows, rows):
                    for g, (j, col_mask) in enumerate(bins_of(level, grid_w, c * cols, cols)):
                        key = (row_mask.tobytes(), col_mask.tobytes())
                        if key not in units:
                            units.append(key)
                            at = len(units) - 1
                            row_masks[r, c, at] = row_mask
                            col_masks[r, c, at] = col_mask
                        at = units.index(key)
                        width = 1 if level == 2 else 2
                        for s in range(2):
                            target = s * STRIP_ALL + STRIP_ALL_AT[level] + i * width + g
                            strip[c, target, r, s * UNITS + at] = 1.0
            assert len(units) <= UNITS
    for r in range(row_strips):
        for level in CODED:
            width = 1 if level == 2 else 2
            start = first_bin(level, grid_h, r * rows, rows)
            for k in range(NEAR[level] * width):
                for s in range(2):
                    source = s * STRIP_ALL + STRIP_ALL_AT[level] + start * width + k
                    near[r, s * STRIP_UNITS + STRIP_AT[level] + k, source] = 1.0
    for c in range(col_strips):
        base = 0
        for level in LEVELS:
            source = 2 if level == 1 else level
            width = 1 if source == 2 else 2
            start = first_bin(level, grid_w, c * cols, cols)
            for p in range(col_strips):
                for g, (j, _) in enumerate(bins_of(source, grid_w, p * cols, cols)):
                    j = 0 if level == 1 else j - start
                    if not 0 <= j < NEAR[level]:
                        continue
                    for i in range(NEAR[source]):
                        for s in range(2):
                            cell = 0 if level == 1 else i * NEAR[level] + j
                            at = base + s * SLOTS[level] + cell
                            bins[c, at, p, s * STRIP_UNITS + STRIP_AT[source] + i * width + g] = 1.0
            base += 2 * SLOTS[level]
    for table, strips, size, along_rows in ((row_scale, row_strips, rows, True), (col_scale, col_strips, cols, False)):
        for at in range(strips):
            base = 0
            for level in LEVELS:
                length = size * strips
                start = first_bin(level, length, at * size, size)
                sizes = [mask.sum() for _, mask in bins_of(level, length, 0, length)]
                for i in range(NEAR[level]):
                    for j in range(NEAR[level]):
                        for s in range(2):
                            k = base + s * SLOTS[level] + i * NEAR[level] + j
                            table[at, 0, k] = 1.0 / sizes[start + (i if along_rows else j)]
                base += 2 * SLOTS[level]
    strip = strip.reshape(col_strips, 2 * STRIP_ALL, -1)
    return row_masks, col_masks, strip, near, bins.reshape(col_strips, slots, -1), row_scale, col_scale


def upsample_weights(level, length, first, count):
    places = first + np.arange(count)
    numer = np.maximum((2 * places + 1) * level - length, 0)
    lower = numer // (2 * length)
    frac = (numer - lower * 2 * length).astype(np.float32) / np.float32(2.0 * length)
    upper = np.minimum(lower + 1, level - 1)
    cells = np.arange(level)[None, :]
    weight = (cells == lower[:, None]) * (1.0 - frac)[:, None] + (cells == upper[:, None]) * frac[:, None]
    inside = (places >= 0) & (places < length)
    return (weight * inside[:, None]).astype(np.float32)


def upsample_tables(rows, row_strips, cols, col_strips):
    width = TAPS * sum(SLOTS.values())
    cells = sum(NEAR.values())
    spread = np.zeros((2, 64, width), np.float32)

    def strips_of(size, strips):
        table = np.zeros((strips, size, 64), np.float32)
        length = size * strips
        for strip in range(strips):
            first = 0
            for level in LEVELS:
                start = first_bin(level, length, strip * size, size)
                for a in range(3):
                    w = upsample_weights(level, length, strip * size + a - 1, size)
                    at = a * cells + first
                    table[strip, :, at : at + NEAR[level]] = w[:, start : start + NEAR[level]]
                first += NEAR[level]
        return table

    base, first = 0, 0
    for level in LEVELS:
        for a in range(3):
            for c in range(3):
                for i in range(NEAR[level]):
                    for j in range(NEAR[level]):
                        at = base + (a * 3 + c) * SLOTS[level] + i * NEAR[level] + j
                        spread[0, a * cells + first + i, at] = 1.0
                        spread[1, c * cells + first + j, at] = 1.0
        base += TAPS * SLOTS[level]
        first += NEAR[level]
    return strips_of(rows, row_strips), strips_of(cols, col_strips), spread


def layer_norm(tokens, gain):
    x = tokens.astype(f32)
    center = jnp.mean(x, axis=-1, keepdims=True)
    x = x - center
    spread = jnp.mean(x * x, axis=-1, keepdims=True)
    return (x * lax.rsqrt(spread + EPS) * gain).astype(bf16)


def dot(a, b):
    return jnp.dot(a, b, preferred_element_type=f32)


def project_kernel(tokens_ref, gain_ref, wkv, normed_ref, kv_ref):
    rows, cols, wide = kv_ref.shape[1:]
    s = pl.program_id(0)
    normed = layer_norm(tokens_ref[...], gain_ref[...])
    normed_ref[s] = normed
    kv_ref[s] = dot(normed, wkv[...]).astype(bf16).astype(f32).reshape(rows, cols, wide)


def pool_members(masks_ref, pool, cols):
    masks = masks_ref[...].astype(bf16)
    _, count = masks.shape
    area = pool.shape[1]
    rows = count - cols
    unit = lax.broadcasted_iota(jnp.int32, (count, area), 0)
    token = lax.broadcasted_iota(jnp.int32, (count, area), 1)
    to_row = (unit == token // cols).astype(f32).astype(bf16)
    to_col = (unit - rows == token % cols).astype(f32).astype(bf16)
    pool[...] = (dot(masks, to_row) * dot(masks, to_col)).astype(bf16)


def middle_kernel(
    grid_shape, place_ref, normed_ref, kv_ref, above_ref, below_ref, gain_ref, wq, wkv, masks_ref,
    q_ref, halo_ref, bias, pool, context, scores, weights,
):
    rows, cols, inner = q_ref.shape[1:]
    s = pl.program_id(0)
    q_ref[s] = dot(normed_ref[s], wq[...]).astype(bf16).astype(f32).reshape(rows, cols, inner)

    @pl.when(s == 0)
    def _():
        window_bias(bias, place_ref[0] * rows, place_ref[1] * cols, *grid_shape)
        pool_members(masks_ref, pool, cols)
        edge = jnp.concatenate([above_ref[...], below_ref[...]], axis=1)
        edge = layer_norm(edge.reshape(-1, edge.shape[-1]), gain_ref[...])
        halo_ref[...] = dot(edge, wkv[...]).astype(bf16).astype(f32).reshape(halo_ref.shape)

    def store(at, b, lanes, piece):
        context[s, at : at + BLOCK, (b - 1) * BLOCK : b * BLOCK, lanes] = piece

    middle = range(1, cols // BLOCK - 1)
    attend_blocks(middle, s, q_ref, kv_ref, halo_ref, None, bias, scores, weights, store)


def window_bias(bias, first_row, first_col, grid_h, grid_w):
    span = BLOCK + 2 * HALO
    key = lax.broadcasted_iota(jnp.int32, bias.shape[2:], 0)
    extra = key - span * BLOCK
    lane = extra & 7
    odd = ((lane >= 2) & (lane < 6)).astype(jnp.int32)
    west = (lane >= 6) | ((lane >= 2) & (lane < 4))
    main = key < span * BLOCK
    row = jnp.where(main, key >> 3, 2 * (extra >> 3) + odd) - HALO
    col = jnp.where(main, key & 7, (key & 1) + jnp.where(west, -HALO, BLOCK))
    for a in range(bias.shape[0]):
        at = row + (first_row + a * BLOCK)
        row_ok = (at >= 0) & (at < grid_h)
        for b in range(bias.shape[1]):
            at = col + (first_col + b * BLOCK)
            bias[a, b] = jnp.where(row_ok & (at >= 0) & (at < grid_w), 0.0, -1e30)


def attend_blocks(columns, sheet, q_ref, kv_ref, halo_ref, sides, bias, scores, weights, store):
    rows, cols, inner = q_ref.shape[1:]
    groups = cols // BLOCK
    span = BLOCK + 2 * HALO
    tiles = inner // 128
    count = BLOCK * BLOCK
    heads = 128 // HEAD_DIM
    head_of_row = lax.broadcasted_iota(jnp.int32, (heads, count, 128), 0)
    head_of_lane = lax.broadcasted_iota(jnp.int32, (heads, count, 128), 2) // HEAD_DIM
    own = (head_of_row == head_of_lane).astype(f32).astype(bf16).reshape(heads * count, 128)
    lane = lax.broadcasted_iota(jnp.int32, (count, 128), 1)
    place = lax.broadcasted_iota(jnp.int32, (span // 2, BLOCK, 128), 1)
    factor = math.log2(math.e) / math.sqrt(HEAD_DIM)

    def rows_of(at, g, lanes):
        places = slice(g * BLOCK, (g + 1) * BLOCK)
        parts = [kv_ref[sheet, max(at - HALO, 0) : min(at + BLOCK + HALO, rows), places, lanes]]
        if at == 0:
            parts = [halo_ref[sheet, 0:HALO, places, lanes]] + parts
        if at + BLOCK == rows:
            parts = parts + [halo_ref[sheet, HALO:, places, lanes]]
        return jnp.concatenate(parts, axis=0)

    def keys_of(at, b, lanes):
        main = rows_of(at, b, lanes).reshape(span * BLOCK, 128)

        def beside(g):
            if g < 0 or g >= groups:
                found = sides[sheet, at : at + span, :, lanes]
            else:
                found = rows_of(at, g, lanes)
            return found.reshape(span // 2, 2, BLOCK, 128)

        west, east = beside(b - 1), beside(b + 1)
        even = jnp.where(place >= 6, west[:, 0], east[:, 0])
        odd = pltpu.roll(jnp.where(place >= 6, west[:, 1], east[:, 1]), 4, 1)
        extra = jnp.where((place >= 6) | (place < 2), even, odd).reshape(span * 4, 128)
        return jnp.concatenate([main, extra], axis=0).astype(bf16)

    def score(at, b, slot):
        low = bias[at // BLOCK, b]
        for t in range(tiles):
            lanes = slice(t * 128, (t + 1) * 128)
            q = q_ref[sheet, at : at + BLOCK, b * BLOCK : (b + 1) * BLOCK, lanes].reshape(count, 128).astype(bf16)
            q = jnp.concatenate([q] * heads, axis=0) * own
            found = lax.dot_general(keys_of(at, b, lanes), q, (((1,), (1,)), ((), ())), preferred_element_type=f32)
            scores[slot, t] = found + jnp.concatenate([low] * (heads * count // 128), axis=1)

    def soften(slot):
        for t in range(tiles):
            for h in range(heads * count // 128):
                lanes = slice(h * 128, (h + 1) * 128)
                found = scores[slot, t, :, lanes]
                top = jnp.max(found, axis=0, keepdims=True)
                expon = jnp.exp2((found - top) * factor)
                weights[slot, t, :, lanes] = (expon * (1.0 / jnp.sum(expon, axis=0, keepdims=True))).astype(bf16)

    def mix(at, b, slot):
        for t in range(tiles):
            lanes = slice(t * 128, (t + 1) * 128)
            values = keys_of(at, b, slice(inner + t * 128, inner + (t + 1) * 128))
            mixed = lax.dot_general(weights[slot, t], values, (((0,), (0,)), ((), ())), preferred_element_type=f32)
            mixed = mixed.reshape(heads, count, 128)
            piece = mixed[0]
            for k in range(1, heads):
                piece = jnp.where(lane >= k * HEAD_DIM, mixed[k], piece)
            store(at, b, lanes, piece.reshape(BLOCK, BLOCK, 128))

    blocks = [(at, b) for at in range(0, rows, BLOCK) for b in columns]
    score(*blocks[0], 0)
    for k, block in enumerate(blocks):
        if k + 1 < len(blocks):
            score(*blocks[k + 1], (k + 1) % 2)
        soften(k % 2)
        mix(*block, k % 2)


def attend_kernel(
    q_ref, kv_ref, halo_ref, sides_ref, tokens_ref, gain_ref, wkv_ref, middle_ref, bias, pool, wout_ref,
    attended_ref, sums_ref, first_row_ref, last_row_ref, first_col_ref, last_col_ref, sides, outer, scores, weights,
):
    rows, cols, inner = q_ref.shape[1:]
    sheet = pl.program_id(0)

    @pl.when(sheet == 0)
    def _():
        ends = layer_norm(sides_ref[...].reshape(-1, sides_ref.shape[-1]), gain_ref[...])
        ends = dot(ends, wkv_ref[...]).astype(bf16).astype(f32)
        sides[...] = ends.reshape(sides.shape)

    last = cols // BLOCK - 1

    def store(at, b, lanes, piece):
        outer[b // last, at : at + BLOCK, :, lanes] = piece

    attend_blocks((0, last), sheet, q_ref, kv_ref, halo_ref, sides, bias, scores, weights, store)
    mixed = jnp.concatenate([outer[0], middle_ref[sheet], outer[1]], axis=1)
    mixed = mixed.reshape(rows * cols, inner).astype(bf16)
    attended = (tokens_ref[sheet].astype(f32) + dot(mixed, wout_ref[...])).astype(bf16)
    attended_ref[...] = attended
    first_row_ref[...] = attended[:cols]
    last_row_ref[...] = attended[(rows - 1) * cols :]
    by_place = attended.astype(f32).reshape(rows, cols, attended.shape[-1])
    first_col_ref[...] = by_place[:, 0].astype(bf16)
    last_col_ref[...] = by_place[:, cols - 1].astype(bf16)
    sums = dot(pool[...], attended).astype(bf16)
    sums_ref[...] = jnp.broadcast_to(sums[None], sums_ref.shape)


def combine_kernel(place_ref, near_ref, table_ref, parts_ref, out_ref):
    table = dot(near_ref[...], table_ref[...]).astype(bf16)
    added = dot(table, parts_ref[...]).astype(bf16)
    out_ref[...] = jnp.broadcast_to(added[None], out_ref.shape)


def conv_kernel(attended_ref, top_ref, bottom_ref, left_ref, right_ref, taps_ref, w_hbm, out_ref, ext, w, sems):
    area, width = attended_ref.shape
    cols = top_ref.shape[0]
    rows = area // cols
    out_ch = out_ref.shape[-1]
    s, step = pl.program_id(0), pl.program_id(1)

    fetches = [
        pltpu.make_async_copy(w_hbm.at[:, k, 0:width, :], w.at[k - 1], sems.at[k - 1]) for k in (1, 2)
    ]

    @pl.when((s == 0) & (step == 0))
    def _():
        for fetch in fetches:
            fetch.start()

    for k, fetch in enumerate(fetches):

        @pl.when((s == 0) & (step == k + 1))
        def _():
            fetch.wait()

    def edge(ref, w_ref):
        total = 0.0
        for a in range(3):
            total = total + dot(ref[...], w_ref[a])[a : a + rows]
        return total.reshape(rows, 1, out_ch)

    def middle(w_ref):
        total = dot(ext[0:area], w_ref[0])
        for a in range(1, 3):
            total = total + dot(ext[a * cols : a * cols + area], w_ref[a])
        return total.reshape(rows, cols, out_ch)

    @pl.when(step == 0)
    def _():
        ext[0:cols] = top_ref[...]
        ext[cols : cols + area] = attended_ref[...]
        ext[cols + area :] = bottom_ref[...]
        place = lax.broadcasted_iota(jnp.int32, (rows, cols, out_ch), 1)
        part = jnp.where(place == 0, edge(left_ref, taps_ref), pltpu.roll(middle(taps_ref), 1, 1))
        out_ref[s] = part.reshape(area, out_ch)

    @pl.when(step == 1)
    def _():
        out_ref[s] += middle(w.at[0]).reshape(area, out_ch)

    @pl.when(step == 2)
    def _():
        place = lax.broadcasted_iota(jnp.int32, (rows, cols, out_ch), 1)
        part = jnp.where(place == cols - 1, edge(right_ref, w.at[1]), pltpu.roll(middle(w.at[1]), cols - 1, 1))
        out_ref[s] += part.reshape(area, out_ch)


def split(x):
    high = x.astype(bf16)
    return high, (x - high.astype(f32)).astype(bf16)


def tail_kernel(
    place_ref, table_hbm, row_scale_hbm, col_scale_hbm, parts_hbm, wpool_hbm, wjoin_hbm, by_row_hbm, by_col_hbm,
    spread_hbm, conv, out_hbm,
    table, row_scale, col_scale, parts, by_row, by_col, spread, wpool, wjoin, taps, out, sems,
):
    width, ppm = wpool.shape[1], wpool.shape[2]
    count = len(LEVELS)
    r, c = place_ref[0], place_ref[1]
    small = [
        pltpu.make_async_copy(source, target, sems.at[0, k])
        for k, (source, target) in enumerate((
            (parts_hbm, parts), (table_hbm.at[c], table), (row_scale_hbm.at[r], row_scale),
            (col_scale_hbm.at[c], col_scale), (by_row_hbm.at[r], by_row), (by_col_hbm.at[c], by_col), (spread_hbm, spread),
        ))
    ]
    large = [pltpu.make_async_copy(wpool_hbm.at[k], wpool.at[k], sems.at[1, k]) for k in range(count)]
    for k in range(count):
        lines = slice(width + k * ppm, width + (k + 1) * ppm)
        large.append(pltpu.make_async_copy(wjoin_hbm.at[:, :, lines, :], wjoin.at[k], sems.at[1, count + k]))
    ahead = 5
    for copy in small + large[:ahead]:
        copy.start()

    def ready(k):
        large[k].wait()
        if k + ahead < len(large):
            large[k + ahead].start()

    for copy in small:
        copy.wait()

    def along(ref, axis):
        high, low = split(ref[...])
        return dot(high, spread[axis]) + dot(low, spread[axis])

    grid = along(by_row, 0)[:, None, :] * along(by_col, 1)[None, :, :]
    grid_high, grid_low = split(grid.reshape(grid.shape[0] * grid.shape[1], -1))
    scale = row_scale[...] * col_scale[...]
    scale = jnp.broadcast_to(scale, (128, scale.shape[1])).T[:, :1]
    pooled = dot(table[...], parts[...]) * scale
    branches = []
    row = 0
    for index, level in enumerate(LEVELS):
        slots = SLOTS[level]
        high, low = split(pooled[row : row + 2 * slots])
        ready(index)
        both = dot(jnp.concatenate([high, low], axis=0), wpool[index])
        high, low = split(jnp.maximum(both[: 2 * slots] + both[2 * slots :], 0.0))
        branches.append(jnp.concatenate([high, low], axis=0))
        row += 2 * slots
    results = [pltpu.make_async_copy(out.at[s], out_hbm.at[s], sems.at[2, s]) for s in range(2)]

    at = 0
    for index, level in enumerate(LEVELS):
        slots = SLOTS[level]
        ready(count + index)
        for a in range(3):
            for b in range(3):
                tap = dot(branches[index], wjoin[index, a, b])
                tap = tap[: 2 * slots] + tap[2 * slots :]
                start = at + (a * 3 + b) * slots
                for s in range(2):
                    taps[s, start : start + slots, :] = tap[s * slots : (s + 1) * slots]
        at += TAPS * slots
    for s in range(2):
        high, low = split(taps[s])
        total = conv[s] + dot(grid_high, high) + dot(grid_low, high) + dot(grid_high, low)
        out[s] = total.astype(bf16)
        results[s].start()
    for copy in results:
        copy.wait()


def cost(flops, nbytes, transcendentals=0):
    return pl.CostEstimate(flops=int(flops), bytes_accessed=int(nbytes), transcendentals=int(transcendentals))


def params(mib):
    return pltpu.CompilerParams(vmem_limit_bytes=mib * 2**20)


def whole(shape):
    return pl.BlockSpec(shape, lambda *_: (0,) * len(shape))


def in_vmem(x):
    return pltpu.with_memory_space_constraint(x, pltpu.VMEM)


def in_hbm(x):
    return pltpu.with_memory_space_constraint(x, pltpu.HBM)


def shifts(axis):
    count = lax.axis_size(axis)
    forward = [(i, i + 1) for i in range(count - 1)]
    return forward, [(j, i) for i, j in forward]


def layer(tokens, norm_gain, w_query, w_kv, w_out, w_pool, w_join):
    sheets, rows, cols, width = tokens.shape
    inner = w_query.shape[1]
    wide = w_kv.shape[1]
    out_ch = w_join.shape[-1]
    ppm = w_pool.shape[-1]
    area = rows * cols
    row_count, col_count = lax.axis_size("row"), lax.axis_size("col")
    r, c = lax.axis_index("row"), lax.axis_index("col")
    grid_h, grid_w = rows * row_count, cols * col_count
    gain = norm_gain.reshape(1, width)
    tables = pool_tables(rows, row_count, cols, col_count)
    row_masks, col_masks, strip_table, near_table, bin_table, row_scale, col_scale = tables
    by_row, by_col, spread = upsample_tables(rows, row_count, cols, col_count)
    masks = np.concatenate([row_masks, col_masks], axis=-1).reshape(row_count * col_count, UNITS, rows + cols)

    at = jnp.stack([r, c]).astype(jnp.int32)
    row_fwd, row_bwd = shifts("row")
    col_fwd, col_bwd = shifts("col")
    above = lax.ppermute(tokens[:, rows - HALO :], "row", row_fwd)
    below = lax.ppermute(tokens[:, :HALO], "row", row_bwd)

    def edges(first):
        return jnp.concatenate([x[:, :, first : first + HALO] for x in (above, tokens, below)], axis=1)

    west = lax.ppermute(edges(cols - HALO), "col", col_fwd)
    east = lax.ppermute(edges(0), "col", col_bwd)

    def per_sheet(*dims):
        return pl.BlockSpec((None,) + dims, lambda s, *_: (s,) + (0,) * len(dims))

    near = pl.BlockSpec(memory_space=pltpu.VMEM)
    far = pl.BlockSpec(memory_space=pl.ANY)
    wq_near, wkv_near = in_vmem(w_query), in_vmem(w_kv)
    flat = in_vmem(tokens.reshape(sheets, area, width))
    edge = HALO * cols
    blocks = (rows // BLOCK) * (cols // BLOCK)
    keys = (BLOCK + 2 * HALO) ** 2
    stage = [pltpu.VMEM((2, inner // 128, keys, 256), f32), pltpu.VMEM((2, inner // 128, keys, 256), bf16)]
    gain = in_vmem(gain)
    normed, kv = pl.pallas_call(
        project_kernel,
        grid=(sheets,),
        in_specs=[per_sheet(area, width), near, near],
        out_specs=[near] * 2,
        out_shape=[pltpu.VMEM((sheets, area, width), bf16), pltpu.VMEM((sheets, rows, cols, wide), f32)],
        compiler_params=params(16),
        cost_estimate=cost(2 * sheets * area * width * wide, 2 * (width * (inner + wide) + 5 * sheets * area * width)),
        name="project",
    )(in_hbm(tokens.reshape(sheets, area, width)), gain, wkv_near)
    kv = in_vmem(kv)
    q, halo, bias, pool, middle = pl.pallas_call(
        lambda *refs: middle_kernel((grid_h, grid_w), *refs),
        grid_spec=pltpu.PrefetchScalarGridSpec(
            num_scalar_prefetch=1,
            grid=(sheets,),
            in_specs=[near] * 7 + [
                pl.BlockSpec((None, UNITS, rows + cols), lambda s, p: (p[0] * col_count + p[1], 0, 0)),
            ],
            out_specs=[near] * 5,
            scratch_shapes=stage,
        ),
        out_shape=[
            pltpu.VMEM((sheets, rows, cols, inner), f32), pltpu.VMEM((sheets, 2 * HALO, cols, wide), f32),
            pltpu.VMEM((rows // BLOCK, cols // BLOCK, keys, 128), f32), pltpu.VMEM((UNITS, area), bf16),
            pltpu.VMEM((sheets, rows, cols - 2 * BLOCK, inner), f32),
        ],
        compiler_params=params(16),
        cost_estimate=cost(2 * sheets * area * width * wide, 8 * sheets * area * width, sheets * blocks * keys * 512),
        name="middle",
    )(
        at, in_vmem(normed), kv, in_vmem(above.reshape(sheets, edge, width)),
        in_vmem(below.reshape(sheets, edge, width)), gain, wq_near, wkv_near, masks,
    )

    blank = jnp.zeros((sheets, rows + 2 * HALO, BLOCK - 2 * HALO, width), bf16)
    sides = jnp.concatenate([east, blank, west], axis=2).reshape(sheets, (rows + 2 * HALO) * BLOCK, width)

    def fixed(*dims):
        return whole(dims)

    attended, sums, first_row, last_row, first_col, last_col = pl.pallas_call(
        attend_kernel,
        grid=(sheets,),
        in_specs=[near] * 10 + [fixed(inner, width)],
        out_specs=[
            per_sheet(area, width),
            pl.BlockSpec((row_count, UNITS, width), lambda s: (0, s, 0)),
            per_sheet(cols, width), per_sheet(cols, width), per_sheet(rows, width), per_sheet(rows, width),
        ],
        scratch_shapes=[
            pltpu.VMEM((sheets, rows + 2 * HALO, BLOCK, wide), f32), pltpu.VMEM((2, rows, BLOCK, inner), f32),
        ] + stage,
        out_shape=[
            pltpu.HBM((sheets, area, width), bf16),
            jax.ShapeDtypeStruct((row_count, sheets * UNITS, width), bf16),
            jax.ShapeDtypeStruct((sheets, cols, width), bf16),
            jax.ShapeDtypeStruct((sheets, cols, width), bf16),
            jax.ShapeDtypeStruct((sheets, rows, width), bf16),
            jax.ShapeDtypeStruct((sheets, rows, width), bf16),
        ],
        compiler_params=params(20),
        cost_estimate=cost(2 * sheets * area * inner * width * 4, 2 * sheets * area * width * 4, sheets * blocks * keys * 1024),
        name="attend",
    )(
        in_vmem(q), kv, in_vmem(halo), in_vmem(sides), flat, gain, wkv_near, in_vmem(middle), in_vmem(bias),
        in_vmem(pool), w_out,
    )

    strip_rows = sheets * STRIP_UNITS
    att_above = lax.ppermute(last_row, "row", row_fwd)
    att_below = lax.ppermute(first_row, "row", row_bwd)
    parts = lax.all_to_all(sums, "row", 0, 0, tiled=True).reshape(row_count * sheets * UNITS, width)

    def att_edges(middle, at):
        return jnp.concatenate([att_above[:, at : at + 1], middle, att_below[:, at : at + 1]], axis=1)

    att_west = lax.ppermute(att_edges(last_col, cols - 1), "col", col_fwd)
    att_east = lax.ppermute(att_edges(first_col, 0), "col", col_bwd)
    pad = ((0, 0), (0, 6), (0, 0))
    att_west, att_east = jnp.pad(att_west, pad), jnp.pad(att_east, pad)

    strips = pl.pallas_call(
        combine_kernel,
        grid_spec=pltpu.PrefetchScalarGridSpec(
            num_scalar_prefetch=1,
            grid=(1,),
            in_specs=[
                pl.BlockSpec((None,) + near_table.shape[1:], lambda k, p: (p[0], 0, 0)),
                pl.BlockSpec((None,) + strip_table.shape[1:], lambda k, p: (p[1], 0, 0)),
                fixed(row_count * sheets * UNITS, width),
            ],
            out_specs=fixed(col_count, strip_rows, width),
        ),
        out_shape=jax.ShapeDtypeStruct((col_count, strip_rows, width), bf16),
        compiler_params=params(8),
        name="combine",
    )(at, near_table.astype(bf16), strip_table.astype(bf16), parts)
    strips = lax.all_to_all(strips, "col", 0, 0, tiled=True).reshape(col_count * strip_rows, width)

    conv = pl.pallas_call(
        conv_kernel,
        grid=(sheets, 3),
        in_specs=[
            per_sheet(area, width), per_sheet(cols, width), per_sheet(cols, width),
            per_sheet(rows + 8, width), per_sheet(rows + 8, width),
            pl.BlockSpec((3, None, width, out_ch), lambda *_: (0, 0, 0, 0)), far,
        ],
        out_specs=pl.BlockSpec(memory_space=pltpu.VMEM),
        out_shape=pltpu.VMEM((sheets, area, out_ch), f32),
        scratch_shapes=[
            pltpu.VMEM((area + 2 * cols, width), bf16), pltpu.VMEM((2, 3, width, out_ch), bf16),
            pltpu.SemaphoreType.DMA((2,)),
        ],
        compiler_params=params(20),
        cost_estimate=cost(2 * sheets * area * width * 9 * out_ch, 2 * 9 * width * out_ch + 2 * sheets * area * width),
        name="conv",
    )(in_hbm(attended), att_above, att_below, att_west, att_east, in_hbm(w_join), in_hbm(w_join))
    conv = in_vmem(conv)

    depth = TAPS * sum(SLOTS.values())
    bin_rows = 2 * sum(SLOTS.values())
    out = pl.pallas_call(
        tail_kernel,
        grid_spec=pltpu.PrefetchScalarGridSpec(
            num_scalar_prefetch=1,
            grid=(1,),
            in_specs=[pl.BlockSpec(memory_space=pl.ANY) for _ in range(9)] + [pl.BlockSpec(memory_space=pltpu.VMEM)],
            out_specs=pl.BlockSpec(memory_space=pl.ANY),
            scratch_shapes=[
                pltpu.VMEM(bin_table.shape[1:], bf16),
                pltpu.VMEM((1, bin_rows), f32),
                pltpu.VMEM((1, bin_rows), f32),
                pltpu.VMEM((col_count * strip_rows, width), bf16),
                pltpu.VMEM((rows, 64), f32),
                pltpu.VMEM((cols, 64), f32),
                pltpu.VMEM((2, 64, depth), bf16),
                pltpu.VMEM(w_pool.shape, bf16),
                pltpu.VMEM((len(LEVELS), 3, 3, ppm, out_ch), bf16),
                pltpu.VMEM((sheets, depth, out_ch), f32),
                pltpu.VMEM((sheets, area, out_ch), bf16),
                pltpu.SemaphoreType.DMA((3, 2 * len(LEVELS))),
            ],
        ),
        out_shape=jax.ShapeDtypeStruct((sheets, area, out_ch), bf16),
        compiler_params=params(40),
        cost_estimate=cost(4e9, 2 * (w_pool.size + 9 * 4 * ppm * out_ch)),
        name="tail",
    )(
        at, bin_table.astype(bf16), row_scale, col_scale, strips, in_hbm(w_pool), in_hbm(w_join),
        by_row, by_col, spread.astype(bf16), conv,
    )
    return out.reshape(sheets, rows, cols, out_ch)


def solution(mesh):
    placed = (P(None, "row", "col", None), P(), P(), P(), P(), P(), P())
    return jax.shard_map(layer, mesh=mesh, in_specs=placed, out_specs=P(None, "row", "col", None), check_vma=False)
```

```python
import math

import jax
import jax.numpy as jnp
import numpy as np
from jax import lax
from jax.experimental import pallas as pl
from jax.experimental.pallas import tpu as pltpu
from jax.sharding import PartitionSpec as P

HEAD_DIM = 32
BLOCK = 8
HALO = 2
EPS = 1e-05
LEVELS = (1, 2, 3, 6)
CODED = (6, 3, 2)
UNITS = 8
STRIP_ALL = 24
STRIP_ALL_AT = {6: 0, 3: 12, 2: 18}
STRIP_UNITS = 16
STRIP_AT = {6: 0, 3: 6, 2: 12}
NEAR = {1: 1, 2: 2, 3: 3, 6: 3}
SLOTS = {1: 8, 2: 8, 3: 16, 6: 16}
TAPS = 9
f32 = jnp.float32
bf16 = jnp.bfloat16


def bins_of(level, length, first, count):
    places = first + np.arange(count)
    found = []
    for cell in range(level):
        start = cell * length // level
        end = ((cell + 1) * length + level - 1) // level
        mask = (places >= start) & (places < end)
        if mask.any():
            found.append((cell, mask))
    return found


def lower_bin(level, length, place):
    return max((2 * place + 1) * level - length, 0) // (2 * length)


def first_bin(level, length, first, count):
    start = min(lower_bin(level, length, first - 1), level - NEAR[level])
    assert min(lower_bin(level, length, first + count) + 1, level - 1) < start + NEAR[level]
    return start


def pool_tables(rows, row_strips, cols, col_strips):
    grid_h, grid_w = rows * row_strips, cols * col_strips
    row_masks = np.zeros((row_strips, col_strips, UNITS, rows), np.float32)
    col_masks = np.zeros((row_strips, col_strips, UNITS, cols), np.float32)
    strip = np.zeros((col_strips, 2 * STRIP_ALL, row_strips, 2 * UNITS), np.float32)
    near = np.zeros((row_strips, 2 * STRIP_UNITS, 2 * STRIP_ALL), np.float32)
    slots = 2 * sum(SLOTS.values())
    bins = np.zeros((col_strips, slots, col_strips, 2 * STRIP_UNITS), np.float32)
    row_scale = np.zeros((row_strips, 1, slots), np.float32)
    col_scale = np.zeros((col_strips, 1, slots), np.float32)
    for c in range(col_strips):
        for r in range(row_strips):
            units = []
            for level in CODED:
                for i, row_mask in bins_of(level, grid_h, r * rows, rows):
                    for g, (j, col_mask) in enumerate(bins_of(level, grid_w, c * cols, cols)):
                        key = (row_mask.tobytes(), col_mask.tobytes())
                        if key not in units:
                            units.append(key)
                            at = len(units) - 1
                            row_masks[r, c, at] = row_mask
                            col_masks[r, c, at] = col_mask
                        at = units.index(key)
                        width = 1 if level == 2 else 2
                        for s in range(2):
                            target = s * STRIP_ALL + STRIP_ALL_AT[level] + i * width + g
                            strip[c, target, r, s * UNITS + at] = 1.0
            assert len(units) <= UNITS
    for r in range(row_strips):
        for level in CODED:
            width = 1 if level == 2 else 2
            start = first_bin(level, grid_h, r * rows, rows)
            for k in range(NEAR[level] * width):
                for s in range(2):
                    source = s * STRIP_ALL + STRIP_ALL_AT[level] + start * width + k
                    near[r, s * STRIP_UNITS + STRIP_AT[level] + k, source] = 1.0
    for c in range(col_strips):
        base = 0
        for level in LEVELS:
            source = 2 if level == 1 else level
            width = 1 if source == 2 else 2
            start = first_bin(level, grid_w, c * cols, cols)
            for p in range(col_strips):
                for g, (j, _) in enumerate(bins_of(source, grid_w, p * cols, cols)):
                    j = 0 if level == 1 else j - start
                    if not 0 <= j < NEAR[level]:
                        continue
                    for i in range(NEAR[source]):
                        for s in range(2):
                            cell = 0 if level == 1 else i * NEAR[level] + j
                            at = base + s * SLOTS[level] + cell
                            bins[c, at, p, s * STRIP_UNITS + STRIP_AT[source] + i * width + g] = 1.0
            base += 2 * SLOTS[level]
    for table, strips, size, along_rows in ((row_scale, row_strips, rows, True), (col_scale, col_strips, cols, False)):
        for at in range(strips):
            base = 0
            for level in LEVELS:
                length = size * strips
                start = first_bin(level, length, at * size, size)
                sizes = [mask.sum() for _, mask in bins_of(level, length, 0, length)]
                for i in range(NEAR[level]):
                    for j in range(NEAR[level]):
                        for s in range(2):
                            k = base + s * SLOTS[level] + i * NEAR[level] + j
                            table[at, 0, k] = 1.0 / sizes[start + (i if along_rows else j)]
                base += 2 * SLOTS[level]
    strip = strip.reshape(col_strips, 2 * STRIP_ALL, -1)
    return row_masks, col_masks, strip, near, bins.reshape(col_strips, slots, -1), row_scale, col_scale


def upsample_weights(level, length, first, count):
    places = first + np.arange(count)
    numer = np.maximum((2 * places + 1) * level - length, 0)
    lower = numer // (2 * length)
    frac = (numer - lower * 2 * length).astype(np.float32) / np.float32(2.0 * length)
    upper = np.minimum(lower + 1, level - 1)
    cells = np.arange(level)[None, :]
    weight = (cells == lower[:, None]) * (1.0 - frac)[:, None] + (cells == upper[:, None]) * frac[:, None]
    inside = (places >= 0) & (places < length)
    return (weight * inside[:, None]).astype(np.float32)


def upsample_tables(rows, row_strips, cols, col_strips):
    width = TAPS * sum(SLOTS.values())
    cells = sum(NEAR.values())
    spread = np.zeros((2, 64, width), np.float32)

    def strips_of(size, strips):
        table = np.zeros((strips, size, 64), np.float32)
        length = size * strips
        for strip in range(strips):
            first = 0
            for level in LEVELS:
                start = first_bin(level, length, strip * size, size)
                for a in range(3):
                    w = upsample_weights(level, length, strip * size + a - 1, size)
                    at = a * cells + first
                    table[strip, :, at : at + NEAR[level]] = w[:, start : start + NEAR[level]]
                first += NEAR[level]
        return table

    base, first = 0, 0
    for level in LEVELS:
        for a in range(3):
            for c in range(3):
                for i in range(NEAR[level]):
                    for j in range(NEAR[level]):
                        at = base + (a * 3 + c) * SLOTS[level] + i * NEAR[level] + j
                        spread[0, a * cells + first + i, at] = 1.0
                        spread[1, c * cells + first + j, at] = 1.0
        base += TAPS * SLOTS[level]
        first += NEAR[level]
    return strips_of(rows, row_strips), strips_of(cols, col_strips), spread


def layer_norm(tokens, gain):
    x = tokens.astype(f32)
    center = jnp.mean(x, axis=-1, keepdims=True)
    x = x - center
    spread = jnp.mean(x * x, axis=-1, keepdims=True)
    return (x * lax.rsqrt(spread + EPS) * gain).astype(bf16)


def dot(a, b):
    return jnp.dot(a, b, preferred_element_type=f32)


def project_kernel(tokens_ref, gain_ref, wkv, normed_ref, kv_ref, first_ref, last_ref):
    rows, cols, wide = kv_ref.shape[1:]
    s = pl.program_id(0)
    by_place = tokens_ref[...].astype(f32).reshape(rows, cols, tokens_ref.shape[-1])
    for k in range(HALO):
        first_ref[s, k] = by_place[:, k].astype(bf16)
        last_ref[s, k] = by_place[:, cols - HALO + k].astype(bf16)
    normed = layer_norm(tokens_ref[...], gain_ref[...])
    normed_ref[s] = normed
    kv_ref[s] = dot(normed, wkv[...]).astype(bf16).astype(f32).reshape(rows, cols, wide)


def pool_members(masks_ref, pool, cols):
    masks = masks_ref[...].astype(bf16)
    _, count = masks.shape
    area = pool.shape[1]
    rows = count - cols
    unit = lax.broadcasted_iota(jnp.int32, (count, area), 0)
    token = lax.broadcasted_iota(jnp.int32, (count, area), 1)
    to_row = (unit == token // cols).astype(f32).astype(bf16)
    to_col = (unit - rows == token % cols).astype(f32).astype(bf16)
    pool[...] = (dot(masks, to_row) * dot(masks, to_col)).astype(bf16)


def middle_kernel(
    grid_shape, place_ref, normed_ref, kv_ref, above_ref, below_ref, gain_ref, wq, wkv, masks_ref,
    q_ref, halo_ref, bias, pool, context, scores, weights,
):
    rows, cols, inner = q_ref.shape[1:]
    s = pl.program_id(0)
    q_ref[s] = dot(normed_ref[s], wq[...]).astype(bf16).astype(f32).reshape(rows, cols, inner)

    @pl.when(s == 0)
    def _():
        window_bias(bias, place_ref[0] * rows, place_ref[1] * cols, *grid_shape)
        pool_members(masks_ref, pool, cols)
        edge = jnp.concatenate([above_ref[...], below_ref[...]], axis=1)
        edge = layer_norm(edge.reshape(-1, edge.shape[-1]), gain_ref[...])
        halo_ref[...] = dot(edge, wkv[...]).astype(bf16).astype(f32).reshape(halo_ref.shape)

    def store(at, b, lanes, piece):
        context[s, at : at + BLOCK, (b - 1) * BLOCK : b * BLOCK, lanes] = piece

    middle = range(1, cols // BLOCK - 1)
    attend_blocks(middle, s, q_ref, kv_ref, halo_ref, None, bias, scores, weights, store)


def window_bias(bias, first_row, first_col, grid_h, grid_w):
    span = BLOCK + 2 * HALO
    key = lax.broadcasted_iota(jnp.int32, bias.shape[2:], 0)
    extra = key - span * BLOCK
    lane = extra & 7
    odd = ((lane >= 2) & (lane < 6)).astype(jnp.int32)
    west = (lane >= 6) | ((lane >= 2) & (lane < 4))
    main = key < span * BLOCK
    row = jnp.where(main, key >> 3, 2 * (extra >> 3) + odd) - HALO
    col = jnp.where(main, key & 7, (key & 1) + jnp.where(west, -HALO, BLOCK))
    for a in range(bias.shape[0]):
        at = row + (first_row + a * BLOCK)
        row_ok = (at >= 0) & (at < grid_h)
        for b in range(bias.shape[1]):
            at = col + (first_col + b * BLOCK)
            bias[a, b] = jnp.where(row_ok & (at >= 0) & (at < grid_w), 0.0, -1e30)


def attend_blocks(columns, sheet, q_ref, kv_ref, halo_ref, sides, bias, scores, weights, store):
    rows, cols, inner = q_ref.shape[1:]
    groups = cols // BLOCK
    span = BLOCK + 2 * HALO
    tiles = inner // 128
    count = BLOCK * BLOCK
    heads = 128 // HEAD_DIM
    head_of_row = lax.broadcasted_iota(jnp.int32, (heads, count, 128), 0)
    head_of_lane = lax.broadcasted_iota(jnp.int32, (heads, count, 128), 2) // HEAD_DIM
    own = (head_of_row == head_of_lane).astype(f32).astype(bf16).reshape(heads * count, 128)
    lane = lax.broadcasted_iota(jnp.int32, (count, 128), 1)
    place = lax.broadcasted_iota(jnp.int32, (span // 2, BLOCK, 128), 1)
    factor = math.log2(math.e) / math.sqrt(HEAD_DIM)

    def rows_of(at, g, lanes):
        places = slice(g * BLOCK, (g + 1) * BLOCK)
        parts = [kv_ref[sheet, max(at - HALO, 0) : min(at + BLOCK + HALO, rows), places, lanes]]
        if at == 0:
            parts = [halo_ref[sheet, 0:HALO, places, lanes]] + parts
        if at + BLOCK == rows:
            parts = parts + [halo_ref[sheet, HALO:, places, lanes]]
        return jnp.concatenate(parts, axis=0)

    def keys_of(at, b, lanes):
        main = rows_of(at, b, lanes).reshape(span * BLOCK, 128)

        def beside(g):
            if g < 0 or g >= groups:
                found = sides[sheet, at : at + span, :, lanes]
            else:
                found = rows_of(at, g, lanes)
            return found.reshape(span // 2, 2, BLOCK, 128)

        west, east = beside(b - 1), beside(b + 1)
        even = jnp.where(place >= 6, west[:, 0], east[:, 0])
        odd = pltpu.roll(jnp.where(place >= 6, west[:, 1], east[:, 1]), 4, 1)
        extra = jnp.where((place >= 6) | (place < 2), even, odd).reshape(span * 4, 128)
        return jnp.concatenate([main, extra], axis=0).astype(bf16)

    def score(at, b, slot):
        low = bias[at // BLOCK, b]
        for t in range(tiles):
            lanes = slice(t * 128, (t + 1) * 128)
            q = q_ref[sheet, at : at + BLOCK, b * BLOCK : (b + 1) * BLOCK, lanes].reshape(count, 128).astype(bf16)
            q = jnp.concatenate([q] * heads, axis=0) * own
            found = lax.dot_general(keys_of(at, b, lanes), q, (((1,), (1,)), ((), ())), preferred_element_type=f32)
            scores[slot, t] = found + jnp.concatenate([low] * (heads * count // 128), axis=1)

    def soften(slot):
        for t in range(tiles):
            for h in range(heads * count // 128):
                lanes = slice(h * 128, (h + 1) * 128)
                found = scores[slot, t, :, lanes]
                top = jnp.max(found, axis=0, keepdims=True)
                expon = jnp.exp2((found - top) * factor)
                weights[slot, t, :, lanes] = (expon * (1.0 / jnp.sum(expon, axis=0, keepdims=True))).astype(bf16)

    def mix(at, b, slot):
        for t in range(tiles):
            lanes = slice(t * 128, (t + 1) * 128)
            values = keys_of(at, b, slice(inner + t * 128, inner + (t + 1) * 128))
            mixed = lax.dot_general(weights[slot, t], values, (((0,), (0,)), ((), ())), preferred_element_type=f32)
            mixed = mixed.reshape(heads, count, 128)
            piece = mixed[0]
            for k in range(1, heads):
                piece = jnp.where(lane >= k * HEAD_DIM, mixed[k], piece)
            store(at, b, lanes, piece.reshape(BLOCK, BLOCK, 128))

    blocks = [(at, b) for at in range(0, rows, BLOCK) for b in columns]
    score(*blocks[0], 0)
    for k, block in enumerate(blocks):
        if k + 1 < len(blocks):
            score(*blocks[k + 1], (k + 1) % 2)
        soften(k % 2)
        mix(*block, k % 2)


def attend_kernel(
    q_ref, kv_ref, halo_ref, sides_ref, tokens_ref, gain_ref, wkv_ref, middle_ref, bias, pool, wout_ref,
    attended_ref, sums_ref, first_row_ref, last_row_ref, first_col_ref, last_col_ref, sides, outer, scores, weights,
):
    rows, cols, inner = q_ref.shape[1:]
    sheet = pl.program_id(0)

    @pl.when(sheet == 0)
    def _():
        ends = layer_norm(sides_ref[...].reshape(-1, sides_ref.shape[-1]), gain_ref[...])
        ends = dot(ends, wkv_ref[...]).astype(bf16).astype(f32)
        sides[...] = ends.reshape(sides.shape)

    last = cols // BLOCK - 1

    def store(at, b, lanes, piece):
        outer[b // last, at : at + BLOCK, :, lanes] = piece

    attend_blocks((0, last), sheet, q_ref, kv_ref, halo_ref, sides, bias, scores, weights, store)
    mixed = jnp.concatenate([outer[0], middle_ref[sheet], outer[1]], axis=1)
    mixed = mixed.reshape(rows * cols, inner).astype(bf16)
    attended = (tokens_ref[sheet].astype(f32) + dot(mixed, wout_ref[...])).astype(bf16)
    attended_ref[...] = attended
    first_row_ref[...] = attended[:cols]
    last_row_ref[...] = attended[(rows - 1) * cols :]
    by_place = attended.astype(f32).reshape(rows, cols, attended.shape[-1])
    first_col_ref[...] = by_place[:, 0].astype(bf16)
    last_col_ref[...] = by_place[:, cols - 1].astype(bf16)
    sums = dot(pool[...], attended).astype(bf16)
    sums_ref[...] = jnp.broadcast_to(sums[None], sums_ref.shape)


def combine_kernel(place_ref, near_ref, table_ref, parts_ref, out_ref):
    table = dot(near_ref[...], table_ref[...]).astype(bf16)
    added = dot(table, parts_ref[...]).astype(bf16)
    out_ref[...] = jnp.broadcast_to(added[None], out_ref.shape)


def conv_kernel(attended_ref, top_ref, bottom_ref, left_ref, right_ref, taps_ref, w_hbm, out_ref, ext, w, sems):
    area, width = attended_ref.shape
    cols = top_ref.shape[0]
    rows = area // cols
    out_ch = out_ref.shape[-1]
    s, step = pl.program_id(0), pl.program_id(1)

    fetches = [
        pltpu.make_async_copy(w_hbm.at[:, k, 0:width, :], w.at[k - 1], sems.at[k - 1]) for k in (1, 2)
    ]

    @pl.when((s == 0) & (step == 0))
    def _():
        for fetch in fetches:
            fetch.start()

    for k, fetch in enumerate(fetches):

        @pl.when((s == 0) & (step == k + 1))
        def _():
            fetch.wait()

    def edge(ref, w_ref):
        total = 0.0
        for a in range(3):
            total = total + dot(ref[...], w_ref[a])[a : a + rows]
        return total.reshape(rows, 1, out_ch)

    def middle(w_ref):
        total = dot(ext[0:area], w_ref[0])
        for a in range(1, 3):
            total = total + dot(ext[a * cols : a * cols + area], w_ref[a])
        return total.reshape(rows, cols, out_ch)

    @pl.when(step == 0)
    def _():
        ext[0:cols] = top_ref[...]
        ext[cols : cols + area] = attended_ref[...]
        ext[cols + area :] = bottom_ref[...]
        place = lax.broadcasted_iota(jnp.int32, (rows, cols, out_ch), 1)
        part = jnp.where(place == 0, edge(left_ref, taps_ref), pltpu.roll(middle(taps_ref), 1, 1))
        out_ref[s] = part.reshape(area, out_ch)

    @pl.when(step == 1)
    def _():
        out_ref[s] += middle(w.at[0]).reshape(area, out_ch)

    @pl.when(step == 2)
    def _():
        place = lax.broadcasted_iota(jnp.int32, (rows, cols, out_ch), 1)
        part = jnp.where(place == cols - 1, edge(right_ref, w.at[1]), pltpu.roll(middle(w.at[1]), cols - 1, 1))
        out_ref[s] += part.reshape(area, out_ch)


def split(x):
    high = x.astype(bf16)
    return high, (x - high.astype(f32)).astype(bf16)


def tail_kernel(
    place_ref, table_hbm, row_scale_hbm, col_scale_hbm, parts_hbm, wpool_hbm, wjoin_hbm, by_row_hbm, by_col_hbm,
    spread_hbm, conv, out_hbm,
    table, row_scale, col_scale, parts, by_row, by_col, spread, wpool, wjoin, taps, out, sems,
):
    width, ppm = wpool.shape[1], wpool.shape[2]
    count = len(LEVELS)
    r, c = place_ref[0], place_ref[1]
    small = [
        pltpu.make_async_copy(source, target, sems.at[0, k])
        for k, (source, target) in enumerate((
            (parts_hbm, parts), (table_hbm.at[c], table), (row_scale_hbm.at[r], row_scale),
            (col_scale_hbm.at[c], col_scale), (by_row_hbm.at[r], by_row), (by_col_hbm.at[c], by_col), (spread_hbm, spread),
        ))
    ]
    large = [pltpu.make_async_copy(wpool_hbm.at[k], wpool.at[k], sems.at[1, k]) for k in range(count)]
    for k in range(count):
        lines = slice(width + k * ppm, width + (k + 1) * ppm)
        large.append(pltpu.make_async_copy(wjoin_hbm.at[:, :, lines, :], wjoin.at[k], sems.at[1, count + k]))
    ahead = len(large)
    for copy in small + large[:ahead]:
        copy.start()

    def ready(k):
        large[k].wait()
        if k + ahead < len(large):
            large[k + ahead].start()

    for copy in small:
        copy.wait()

    def along(ref, axis):
        high, low = split(ref[...])
        return dot(high, spread[axis]) + dot(low, spread[axis])

    grid = along(by_row, 0)[:, None, :] * along(by_col, 1)[None, :, :]
    grid_high, grid_low = split(grid.reshape(grid.shape[0] * grid.shape[1], -1))
    scale = row_scale[...] * col_scale[...]
    scale = jnp.broadcast_to(scale, (128, scale.shape[1])).T[:, :1]
    pooled = dot(table[...], parts[...]) * scale
    branches = []
    row = 0
    for index, level in enumerate(LEVELS):
        slots = SLOTS[level]
        high, low = split(pooled[row : row + 2 * slots])
        ready(index)
        both = dot(jnp.concatenate([high, low], axis=0), wpool[index])
        high, low = split(jnp.maximum(both[: 2 * slots] + both[2 * slots :], 0.0))
        branches.append(jnp.concatenate([high, low], axis=0))
        row += 2 * slots
    results = [pltpu.make_async_copy(out.at[s], out_hbm.at[s], sems.at[2, s]) for s in range(2)]

    at = 0
    for index, level in enumerate(LEVELS):
        slots = SLOTS[level]
        ready(count + index)
        for a in range(3):
            for b in range(3):
                tap = dot(branches[index], wjoin[index, a, b])
                tap = tap[: 2 * slots] + tap[2 * slots :]
                start = at + (a * 3 + b) * slots
                for s in range(2):
                    taps[s, start : start + slots, :] = tap[s * slots : (s + 1) * slots]
        at += TAPS * slots
    for s in range(2):
        high, low = split(taps[s])
        total = conv[s] + dot(grid_high, high) + dot(grid_low, high) + dot(grid_high, low)
        out[s] = total.astype(bf16)
        results[s].start()
    for copy in results:
        copy.wait()


def cost(flops, nbytes, transcendentals=0):
    return pl.CostEstimate(flops=int(flops), bytes_accessed=int(nbytes), transcendentals=int(transcendentals))


def params(mib):
    return pltpu.CompilerParams(vmem_limit_bytes=mib * 2**20)


def whole(shape):
    return pl.BlockSpec(shape, lambda *_: (0,) * len(shape))


def in_vmem(x):
    return pltpu.with_memory_space_constraint(x, pltpu.VMEM)


def in_hbm(x):
    return pltpu.with_memory_space_constraint(x, pltpu.HBM)


def shifts(axis):
    count = lax.axis_size(axis)
    forward = [(i, i + 1) for i in range(count - 1)]
    return forward, [(j, i) for i, j in forward]


def layer(tokens, norm_gain, w_query, w_kv, w_out, w_pool, w_join):
    sheets, rows, cols, width = tokens.shape
    inner = w_query.shape[1]
    wide = w_kv.shape[1]
    out_ch = w_join.shape[-1]
    ppm = w_pool.shape[-1]
    area = rows * cols
    row_count, col_count = lax.axis_size("row"), lax.axis_size("col")
    r, c = lax.axis_index("row"), lax.axis_index("col")
    grid_h, grid_w = rows * row_count, cols * col_count
    gain = norm_gain.reshape(1, width)
    tables = pool_tables(rows, row_count, cols, col_count)
    row_masks, col_masks, strip_table, near_table, bin_table, row_scale, col_scale = tables
    by_row, by_col, spread = upsample_tables(rows, row_count, cols, col_count)
    masks = np.concatenate([row_masks, col_masks], axis=-1).reshape(row_count * col_count, UNITS, rows + cols)

    at = jnp.stack([r, c]).astype(jnp.int32)
    row_fwd, row_bwd = shifts("row")
    col_fwd, col_bwd = shifts("col")
    edge = HALO * cols
    flat_above = lax.ppermute(tokens[:, rows - HALO :].reshape(sheets, edge, width), "row", row_fwd)
    flat_below = lax.ppermute(tokens[:, :HALO].reshape(sheets, edge, width), "row", row_bwd)
    above = flat_above.reshape(sheets, HALO, cols, width)
    below = flat_below.reshape(sheets, HALO, cols, width)

    def per_sheet(*dims):
        return pl.BlockSpec((None,) + dims, lambda s, *_: (s,) + (0,) * len(dims))

    near = pl.BlockSpec(memory_space=pltpu.VMEM)
    far = pl.BlockSpec(memory_space=pl.ANY)
    wq_near, wkv_near = in_vmem(w_query), in_vmem(w_kv)
    flat = in_vmem(tokens.reshape(sheets, area, width))
    blocks = (rows // BLOCK) * (cols // BLOCK)
    keys = (BLOCK + 2 * HALO) ** 2
    stage = [pltpu.VMEM((2, inner // 128, keys, 256), f32), pltpu.VMEM((2, inner // 128, keys, 256), bf16)]
    gain = in_vmem(gain)
    normed, kv, first_cols, last_cols = pl.pallas_call(
        project_kernel,
        grid=(sheets,),
        in_specs=[per_sheet(area, width), near, near],
        out_specs=[near] * 4,
        out_shape=[
            pltpu.VMEM((sheets, area, width), bf16), pltpu.VMEM((sheets, rows, cols, wide), f32),
            pltpu.VMEM((sheets, HALO, rows, width), bf16), pltpu.VMEM((sheets, HALO, rows, width), bf16),
        ],
        compiler_params=params(16),
        cost_estimate=cost(2 * sheets * area * width * wide, 2 * (width * (inner + wide) + 5 * sheets * area * width)),
        name="project",
    )(in_hbm(tokens.reshape(sheets, area, width)), gain, wkv_near)
    kv = in_vmem(kv)

    def edges(own, first):
        own = jnp.swapaxes(own, 1, 2)
        return jnp.concatenate([above[:, :, first : first + HALO], own, below[:, :, first : first + HALO]], axis=1)

    west = lax.ppermute(edges(last_cols, cols - HALO), "col", col_fwd)
    east = lax.ppermute(edges(first_cols, 0), "col", col_bwd)

    q, halo, bias, pool, middle = pl.pallas_call(
        lambda *refs: middle_kernel((grid_h, grid_w), *refs),
        grid_spec=pltpu.PrefetchScalarGridSpec(
            num_scalar_prefetch=1,
            grid=(sheets,),
            in_specs=[near] * 7 + [
                pl.BlockSpec((None, UNITS, rows + cols), lambda s, p: (p[0] * col_count + p[1], 0, 0)),
            ],
            out_specs=[near] * 5,
            scratch_shapes=stage,
        ),
        out_shape=[
            pltpu.VMEM((sheets, rows, cols, inner), f32), pltpu.VMEM((sheets, 2 * HALO, cols, wide), f32),
            pltpu.VMEM((rows // BLOCK, cols // BLOCK, keys, 128), f32), pltpu.VMEM((UNITS, area), bf16),
            pltpu.VMEM((sheets, rows, cols - 2 * BLOCK, inner), f32),
        ],
        compiler_params=params(16),
        cost_estimate=cost(2 * sheets * area * width * wide, 8 * sheets * area * width, sheets * blocks * keys * 512),
        name="middle",
    )(
        at, in_vmem(normed), kv, in_vmem(flat_above),
        in_vmem(flat_below), gain, wq_near, wkv_near, masks,
    )

    blank = jnp.zeros((sheets, rows + 2 * HALO, BLOCK - 2 * HALO, width), bf16)
    sides = jnp.concatenate([east, blank, west], axis=2).reshape(sheets, (rows + 2 * HALO) * BLOCK, width)

    def fixed(*dims):
        return whole(dims)

    attended, sums, first_row, last_row, first_col, last_col = pl.pallas_call(
        attend_kernel,
        grid=(sheets,),
        in_specs=[near] * 10 + [fixed(inner, width)],
        out_specs=[
            per_sheet(area, width),
            pl.BlockSpec((row_count, UNITS, width), lambda s: (0, s, 0)),
            per_sheet(cols, width), per_sheet(cols, width), per_sheet(rows, width), per_sheet(rows, width),
        ],
        scratch_shapes=[
            pltpu.VMEM((sheets, rows + 2 * HALO, BLOCK, wide), f32), pltpu.VMEM((2, rows, BLOCK, inner), f32),
        ] + stage,
        out_shape=[
            pltpu.HBM((sheets, area, width), bf16),
            jax.ShapeDtypeStruct((row_count, sheets * UNITS, width), bf16),
            jax.ShapeDtypeStruct((sheets, cols, width), bf16),
            jax.ShapeDtypeStruct((sheets, cols, width), bf16),
            jax.ShapeDtypeStruct((sheets, rows, width), bf16),
            jax.ShapeDtypeStruct((sheets, rows, width), bf16),
        ],
        compiler_params=params(20),
        cost_estimate=cost(2 * sheets * area * inner * width * 4, 2 * sheets * area * width * 4, sheets * blocks * keys * 1024),
        name="attend",
    )(
        in_vmem(q), kv, in_vmem(halo), in_vmem(sides), flat, gain, wkv_near, in_vmem(middle), in_vmem(bias),
        in_vmem(pool), w_out,
    )

    strip_rows = sheets * STRIP_UNITS
    att_above = lax.ppermute(last_row, "row", row_fwd)
    att_below = lax.ppermute(first_row, "row", row_bwd)
    parts = lax.all_to_all(sums, "row", 0, 0, tiled=True).reshape(row_count * sheets * UNITS, width)

    def att_edges(middle, at):
        return jnp.concatenate([att_above[:, at : at + 1], middle, att_below[:, at : at + 1]], axis=1)

    att_west = lax.ppermute(att_edges(last_col, cols - 1), "col", col_fwd)
    att_east = lax.ppermute(att_edges(first_col, 0), "col", col_bwd)
    pad = ((0, 0), (0, 6), (0, 0))
    att_west, att_east = jnp.pad(att_west, pad), jnp.pad(att_east, pad)

    strips = pl.pallas_call(
        combine_kernel,
        grid_spec=pltpu.PrefetchScalarGridSpec(
            num_scalar_prefetch=1,
            grid=(1,),
            in_specs=[
                pl.BlockSpec((None,) + near_table.shape[1:], lambda k, p: (p[0], 0, 0)),
                pl.BlockSpec((None,) + strip_table.shape[1:], lambda k, p: (p[1], 0, 0)),
                fixed(row_count * sheets * UNITS, width),
            ],
            out_specs=fixed(col_count, strip_rows, width),
        ),
        out_shape=jax.ShapeDtypeStruct((col_count, strip_rows, width), bf16),
        compiler_params=params(8),
        name="combine",
    )(at, near_table.astype(bf16), strip_table.astype(bf16), parts)
    strips = lax.all_to_all(strips, "col", 0, 0, tiled=True).reshape(col_count * strip_rows, width)

    conv = pl.pallas_call(
        conv_kernel,
        grid=(sheets, 3),
        in_specs=[
            per_sheet(area, width), per_sheet(cols, width), per_sheet(cols, width),
            per_sheet(rows + 8, width), per_sheet(rows + 8, width),
            pl.BlockSpec((3, None, width, out_ch), lambda *_: (0, 0, 0, 0)), far,
        ],
        out_specs=pl.BlockSpec(memory_space=pltpu.VMEM),
        out_shape=pltpu.VMEM((sheets, area, out_ch), f32),
        scratch_shapes=[
            pltpu.VMEM((area + 2 * cols, width), bf16), pltpu.VMEM((2, 3, width, out_ch), bf16),
            pltpu.SemaphoreType.DMA((2,)),
        ],
        compiler_params=params(20),
        cost_estimate=cost(2 * sheets * area * width * 9 * out_ch, 2 * 9 * width * out_ch + 2 * sheets * area * width),
        name="conv",
    )(in_hbm(attended), att_above, att_below, att_west, att_east, in_hbm(w_join), in_hbm(w_join))
    conv = in_vmem(conv)

    depth = TAPS * sum(SLOTS.values())
    bin_rows = 2 * sum(SLOTS.values())
    out = pl.pallas_call(
        tail_kernel,
        grid_spec=pltpu.PrefetchScalarGridSpec(
            num_scalar_prefetch=1,
            grid=(1,),
            in_specs=[pl.BlockSpec(memory_space=pl.ANY) for _ in range(9)] + [pl.BlockSpec(memory_space=pltpu.VMEM)],
            out_specs=pl.BlockSpec(memory_space=pl.ANY),
            scratch_shapes=[
                pltpu.VMEM(bin_table.shape[1:], bf16),
                pltpu.VMEM((1, bin_rows), f32),
                pltpu.VMEM((1, bin_rows), f32),
                pltpu.VMEM((col_count * strip_rows, width), bf16),
                pltpu.VMEM((rows, 64), f32),
                pltpu.VMEM((cols, 64), f32),
                pltpu.VMEM((2, 64, depth), bf16),
                pltpu.VMEM(w_pool.shape, bf16),
                pltpu.VMEM((len(LEVELS), 3, 3, ppm, out_ch), bf16),
                pltpu.VMEM((sheets, depth, out_ch), f32),
                pltpu.VMEM((sheets, area, out_ch), bf16),
                pltpu.SemaphoreType.DMA((3, 2 * len(LEVELS))),
            ],
        ),
        out_shape=jax.ShapeDtypeStruct((sheets, area, out_ch), bf16),
        compiler_params=params(40),
        cost_estimate=cost(4e9, 2 * (w_pool.size + 9 * 4 * ppm * out_ch)),
        name="tail",
    )(
        at, bin_table.astype(bf16), row_scale, col_scale, strips, in_hbm(w_pool), in_hbm(w_join),
        by_row, by_col, spread.astype(bf16), conv,
    )
    return out.reshape(sheets, rows, cols, out_ch)


def solution(mesh):
    placed = (P(None, "row", "col", None), P(), P(), P(), P(), P(), P())
    return jax.shard_map(layer, mesh=mesh, in_specs=placed, out_specs=P(None, "row", "col", None), check_vma=False)
```

```python
import math

import jax
import jax.numpy as jnp
import numpy as np
from jax import lax
from jax.experimental import pallas as pl
from jax.experimental.pallas import tpu as pltpu
from jax.sharding import PartitionSpec as P

HEAD_DIM = 32
BLOCK = 8
HALO = 2
EPS = 1e-05
LEVELS = (1, 2, 3, 6)
CODED = (6, 3, 2)
UNITS = 8
STRIP_ALL = 24
STRIP_ALL_AT = {6: 0, 3: 12, 2: 18}
STRIP_UNITS = 16
STRIP_AT = {6: 0, 3: 6, 2: 12}
NEAR = {1: 1, 2: 2, 3: 3, 6: 3}
SLOTS = {1: 8, 2: 8, 3: 16, 6: 16}
TAPS = 9
f32 = jnp.float32
bf16 = jnp.bfloat16


def bins_of(level, length, first, count):
    places = first + np.arange(count)
    found = []
    for cell in range(level):
        start = cell * length // level
        end = ((cell + 1) * length + level - 1) // level
        mask = (places >= start) & (places < end)
        if mask.any():
            found.append((cell, mask))
    return found


def lower_bin(level, length, place):
    return max((2 * place + 1) * level - length, 0) // (2 * length)


def first_bin(level, length, first, count):
    start = min(lower_bin(level, length, first - 1), level - NEAR[level])
    assert min(lower_bin(level, length, first + count) + 1, level - 1) < start + NEAR[level]
    return start


def pool_tables(rows, row_strips, cols, col_strips):
    grid_h, grid_w = rows * row_strips, cols * col_strips
    row_masks = np.zeros((row_strips, col_strips, UNITS, rows), np.float32)
    col_masks = np.zeros((row_strips, col_strips, UNITS, cols), np.float32)
    strip = np.zeros((col_strips, 2 * STRIP_ALL, row_strips, 2 * UNITS), np.float32)
    near = np.zeros((row_strips, 2 * STRIP_UNITS, 2 * STRIP_ALL), np.float32)
    slots = 2 * sum(SLOTS.values())
    bins = np.zeros((col_strips, slots, col_strips, 2 * STRIP_UNITS), np.float32)
    row_scale = np.zeros((row_strips, 1, slots), np.float32)
    col_scale = np.zeros((col_strips, 1, slots), np.float32)
    for c in range(col_strips):
        for r in range(row_strips):
            units = []
            for level in CODED:
                for i, row_mask in bins_of(level, grid_h, r * rows, rows):
                    for g, (j, col_mask) in enumerate(bins_of(level, grid_w, c * cols, cols)):
                        key = (row_mask.tobytes(), col_mask.tobytes())
                        if key not in units:
                            units.append(key)
                            at = len(units) - 1
                            row_masks[r, c, at] = row_mask
                            col_masks[r, c, at] = col_mask
                        at = units.index(key)
                        width = 1 if level == 2 else 2
                        for s in range(2):
                            target = s * STRIP_ALL + STRIP_ALL_AT[level] + i * width + g
                            strip[c, target, r, s * UNITS + at] = 1.0
            assert len(units) <= UNITS
    for r in range(row_strips):
        for level in CODED:
            width = 1 if level == 2 else 2
            start = first_bin(level, grid_h, r * rows, rows)
            for k in range(NEAR[level] * width):
                for s in range(2):
                    source = s * STRIP_ALL + STRIP_ALL_AT[level] + start * width + k
                    near[r, s * STRIP_UNITS + STRIP_AT[level] + k, source] = 1.0
    for c in range(col_strips):
        base = 0
        for level in LEVELS:
            source = 2 if level == 1 else level
            width = 1 if source == 2 else 2
            start = first_bin(level, grid_w, c * cols, cols)
            for p in range(col_strips):
                for g, (j, _) in enumerate(bins_of(source, grid_w, p * cols, cols)):
                    j = 0 if level == 1 else j - start
                    if not 0 <= j < NEAR[level]:
                        continue
                    for i in range(NEAR[source]):
                        for s in range(2):
                            cell = 0 if level == 1 else i * NEAR[level] + j
                            at = base + s * SLOTS[level] + cell
                            bins[c, at, p, s * STRIP_UNITS + STRIP_AT[source] + i * width + g] = 1.0
            base += 2 * SLOTS[level]
    for table, strips, size, along_rows in ((row_scale, row_strips, rows, True), (col_scale, col_strips, cols, False)):
        for at in range(strips):
            base = 0
            for level in LEVELS:
                length = size * strips
                start = first_bin(level, length, at * size, size)
                sizes = [mask.sum() for _, mask in bins_of(level, length, 0, length)]
                for i in range(NEAR[level]):
                    for j in range(NEAR[level]):
                        for s in range(2):
                            k = base + s * SLOTS[level] + i * NEAR[level] + j
                            table[at, 0, k] = 1.0 / sizes[start + (i if along_rows else j)]
                base += 2 * SLOTS[level]
    strip = strip.reshape(col_strips, 2 * STRIP_ALL, -1)
    return row_masks, col_masks, strip, near, bins.reshape(col_strips, slots, -1), row_scale, col_scale


def upsample_weights(level, length, first, count):
    places = first + np.arange(count)
    numer = np.maximum((2 * places + 1) * level - length, 0)
    lower = numer // (2 * length)
    frac = (numer - lower * 2 * length).astype(np.float32) / np.float32(2.0 * length)
    upper = np.minimum(lower + 1, level - 1)
    cells = np.arange(level)[None, :]
    weight = (cells == lower[:, None]) * (1.0 - frac)[:, None] + (cells == upper[:, None]) * frac[:, None]
    inside = (places >= 0) & (places < length)
    return (weight * inside[:, None]).astype(np.float32)


def upsample_tables(rows, row_strips, cols, col_strips):
    width = TAPS * sum(SLOTS.values())
    cells = sum(NEAR.values())
    spread = np.zeros((2, 64, width), np.float32)

    def strips_of(size, strips):
        table = np.zeros((strips, size, 64), np.float32)
        length = size * strips
        for strip in range(strips):
            first = 0
            for level in LEVELS:
                start = first_bin(level, length, strip * size, size)
                for a in range(3):
                    w = upsample_weights(level, length, strip * size + a - 1, size)
                    at = a * cells + first
                    table[strip, :, at : at + NEAR[level]] = w[:, start : start + NEAR[level]]
                first += NEAR[level]
        return table

    base, first = 0, 0
    for level in LEVELS:
        for a in range(3):
            for c in range(3):
                for i in range(NEAR[level]):
                    for j in range(NEAR[level]):
                        at = base + (a * 3 + c) * SLOTS[level] + i * NEAR[level] + j
                        spread[0, a * cells + first + i, at] = 1.0
                        spread[1, c * cells + first + j, at] = 1.0
        base += TAPS * SLOTS[level]
        first += NEAR[level]
    return strips_of(rows, row_strips), strips_of(cols, col_strips), spread


def layer_norm(tokens, gain):
    x = tokens.astype(f32)
    center = jnp.mean(x, axis=-1, keepdims=True)
    x = x - center
    spread = jnp.mean(x * x, axis=-1, keepdims=True)
    return (x * lax.rsqrt(spread + EPS) * gain).astype(bf16)


def dot(a, b):
    return jnp.dot(a, b, preferred_element_type=f32)


def project_kernel(
    tokens_hbm, gain_hbm, wkv_hbm, normed_ref, kv_ref, first_ref, last_ref, tokens_ref, gain_ref, wkv_ref, sems,
):
    rows, cols, wide = kv_ref.shape[1:]
    s = pl.program_id(0)
    sheets = tokens_ref.shape[0]
    gain_copy = pltpu.make_async_copy(gain_hbm, gain_ref, sems.at[sheets])
    wkv_copy = pltpu.make_async_copy(wkv_hbm, wkv_ref, sems.at[sheets + 1])
    token_copies = [pltpu.make_async_copy(tokens_hbm.at[k], tokens_ref.at[k], sems.at[k]) for k in range(sheets)]

    @pl.when(s == 0)
    def _():
        gain_copy.start()
        token_copies[0].start()
        wkv_copy.start()
        for copy in token_copies[1:]:
            copy.start()
        gain_copy.wait()

    for k, copy in enumerate(token_copies):

        @pl.when(s == k)
        def _():
            copy.wait()

    by_place = tokens_ref[s].astype(f32).reshape(rows, cols, tokens_ref.shape[-1])
    for k in range(HALO):
        first_ref[s, k] = by_place[:, k].astype(bf16)
        last_ref[s, k] = by_place[:, cols - HALO + k].astype(bf16)
    normed = layer_norm(tokens_ref[s], gain_ref[...])
    normed_ref[s] = normed

    @pl.when(s == 0)
    def _():
        wkv_copy.wait()

    kv_ref[s] = dot(normed_ref[s], wkv_ref[...]).astype(bf16).astype(f32).reshape(rows, cols, wide)


def pool_members(masks_ref, pool, cols):
    masks = masks_ref[...].astype(bf16)
    _, count = masks.shape
    area = pool.shape[1]
    rows = count - cols
    unit = lax.broadcasted_iota(jnp.int32, (count, area), 0)
    token = lax.broadcasted_iota(jnp.int32, (count, area), 1)
    to_row = (unit == token // cols).astype(f32).astype(bf16)
    to_col = (unit - rows == token % cols).astype(f32).astype(bf16)
    pool[...] = (dot(masks, to_row) * dot(masks, to_col)).astype(bf16)


def middle_kernel(
    grid_shape, place_ref, normed_ref, kv_ref, above_ref, below_ref, gain_ref, wq, wkv, masks_ref,
    q_ref, halo_ref, bias, pool, context, scores, weights,
):
    rows, cols, inner = q_ref.shape[1:]
    s = pl.program_id(0)
    q_ref[s] = dot(normed_ref[s], wq[...]).astype(bf16).astype(f32).reshape(rows, cols, inner)

    @pl.when(s == 0)
    def _():
        window_bias(bias, place_ref[0] * rows, place_ref[1] * cols, *grid_shape)
        pool_members(masks_ref, pool, cols)
        edge = jnp.concatenate([above_ref[...], below_ref[...]], axis=1)
        edge = layer_norm(edge.reshape(-1, edge.shape[-1]), gain_ref[...])
        halo_ref[...] = dot(edge, wkv[...]).astype(bf16).astype(f32).reshape(halo_ref.shape)

    def store(at, b, lanes, piece):
        context[s, at : at + BLOCK, (b - 1) * BLOCK : b * BLOCK, lanes] = piece

    middle = range(1, cols // BLOCK - 1)
    attend_blocks(middle, s, q_ref, kv_ref, halo_ref, None, bias, scores, weights, store)


def window_bias(bias, first_row, first_col, grid_h, grid_w):
    span = BLOCK + 2 * HALO
    key = lax.broadcasted_iota(jnp.int32, bias.shape[2:], 0)
    extra = key - span * BLOCK
    lane = extra & 7
    odd = ((lane >= 2) & (lane < 6)).astype(jnp.int32)
    west = (lane >= 6) | ((lane >= 2) & (lane < 4))
    main = key < span * BLOCK
    row = jnp.where(main, key >> 3, 2 * (extra >> 3) + odd) - HALO
    col = jnp.where(main, key & 7, (key & 1) + jnp.where(west, -HALO, BLOCK))
    for a in range(bias.shape[0]):
        at = row + (first_row + a * BLOCK)
        row_ok = (at >= 0) & (at < grid_h)
        for b in range(bias.shape[1]):
            at = col + (first_col + b * BLOCK)
            bias[a, b] = jnp.where(row_ok & (at >= 0) & (at < grid_w), 0.0, -1e30)


def attend_blocks(columns, sheet, q_ref, kv_ref, halo_ref, sides, bias, scores, weights, store):
    rows, cols, inner = q_ref.shape[1:]
    groups = cols // BLOCK
    span = BLOCK + 2 * HALO
    tiles = inner // 128
    count = BLOCK * BLOCK
    heads = 128 // HEAD_DIM
    head_of_row = lax.broadcasted_iota(jnp.int32, (heads, count, 128), 0)
    head_of_lane = lax.broadcasted_iota(jnp.int32, (heads, count, 128), 2) // HEAD_DIM
    own = (head_of_row == head_of_lane).astype(f32).astype(bf16).reshape(heads * count, 128)
    lane = lax.broadcasted_iota(jnp.int32, (count, 128), 1)
    place = lax.broadcasted_iota(jnp.int32, (span // 2, BLOCK, 128), 1)
    factor = math.log2(math.e) / math.sqrt(HEAD_DIM)

    def rows_of(at, g, lanes):
        places = slice(g * BLOCK, (g + 1) * BLOCK)
        parts = [kv_ref[sheet, max(at - HALO, 0) : min(at + BLOCK + HALO, rows), places, lanes]]
        if at == 0:
            parts = [halo_ref[sheet, 0:HALO, places, lanes]] + parts
        if at + BLOCK == rows:
            parts = parts + [halo_ref[sheet, HALO:, places, lanes]]
        return jnp.concatenate(parts, axis=0)

    def keys_of(at, b, lanes):
        main = rows_of(at, b, lanes).reshape(span * BLOCK, 128)

        def beside(g):
            if g < 0 or g >= groups:
                found = sides[sheet, at : at + span, :, lanes]
            else:
                found = rows_of(at, g, lanes)
            return found.reshape(span // 2, 2, BLOCK, 128)

        west, east = beside(b - 1), beside(b + 1)
        even = jnp.where(place >= 6, west[:, 0], east[:, 0])
        odd = pltpu.roll(jnp.where(place >= 6, west[:, 1], east[:, 1]), 4, 1)
        extra = jnp.where((place >= 6) | (place < 2), even, odd).reshape(span * 4, 128)
        return jnp.concatenate([main, extra], axis=0).astype(bf16)

    def score(at, b, slot):
        low = bias[at // BLOCK, b]
        for t in range(tiles):
            lanes = slice(t * 128, (t + 1) * 128)
            q = q_ref[sheet, at : at + BLOCK, b * BLOCK : (b + 1) * BLOCK, lanes].reshape(count, 128).astype(bf16)
            q = jnp.concatenate([q] * heads, axis=0) * own
            found = lax.dot_general(keys_of(at, b, lanes), q, (((1,), (1,)), ((), ())), preferred_element_type=f32)
            scores[slot, t] = found + jnp.concatenate([low] * (heads * count // 128), axis=1)

    def soften(slot):
        for t in range(tiles):
            for h in range(heads * count // 128):
                lanes = slice(h * 128, (h + 1) * 128)
                found = scores[slot, t, :, lanes]
                top = jnp.max(found, axis=0, keepdims=True)
                expon = jnp.exp2((found - top) * factor)
                weights[slot, t, :, lanes] = (expon * (1.0 / jnp.sum(expon, axis=0, keepdims=True))).astype(bf16)

    def mix(at, b, slot):
        for t in range(tiles):
            lanes = slice(t * 128, (t + 1) * 128)
            values = keys_of(at, b, slice(inner + t * 128, inner + (t + 1) * 128))
            mixed = lax.dot_general(weights[slot, t], values, (((0,), (0,)), ((), ())), preferred_element_type=f32)
            mixed = mixed.reshape(heads, count, 128)
            piece = mixed[0]
            for k in range(1, heads):
                piece = jnp.where(lane >= k * HEAD_DIM, mixed[k], piece)
            store(at, b, lanes, piece.reshape(BLOCK, BLOCK, 128))

    blocks = [(at, b) for at in range(0, rows, BLOCK) for b in columns]
    score(*blocks[0], 0)
    for k, block in enumerate(blocks):
        if k + 1 < len(blocks):
            score(*blocks[k + 1], (k + 1) % 2)
        soften(k % 2)
        mix(*block, k % 2)


def attend_kernel(
    q_ref, kv_ref, halo_ref, sides_ref, tokens_ref, gain_ref, wkv_ref, middle_ref, bias, pool, wout_ref,
    attended_ref, sums_ref, first_row_ref, last_row_ref, first_col_ref, last_col_ref, sides, outer, scores, weights,
):
    rows, cols, inner = q_ref.shape[1:]
    sheet = pl.program_id(0)

    @pl.when(sheet == 0)
    def _():
        ends = layer_norm(sides_ref[...].reshape(-1, sides_ref.shape[-1]), gain_ref[...])
        ends = dot(ends, wkv_ref[...]).astype(bf16).astype(f32)
        sides[...] = ends.reshape(sides.shape)

    last = cols // BLOCK - 1

    def store(at, b, lanes, piece):
        outer[b // last, at : at + BLOCK, :, lanes] = piece

    attend_blocks((0, last), sheet, q_ref, kv_ref, halo_ref, sides, bias, scores, weights, store)
    mixed = jnp.concatenate([outer[0], middle_ref[sheet], outer[1]], axis=1)
    mixed = mixed.reshape(rows * cols, inner).astype(bf16)
    attended = (tokens_ref[sheet].astype(f32) + dot(mixed, wout_ref[...])).astype(bf16)
    attended_ref[...] = attended
    first_row_ref[...] = attended[:cols]
    last_row_ref[...] = attended[(rows - 1) * cols :]
    by_place = attended.astype(f32).reshape(rows, cols, attended.shape[-1])
    first_col_ref[...] = by_place[:, 0].astype(bf16)
    last_col_ref[...] = by_place[:, cols - 1].astype(bf16)
    sums = dot(pool[...], attended).astype(bf16)
    sums_ref[...] = jnp.broadcast_to(sums[None], sums_ref.shape)


def combine_kernel(place_ref, near_ref, table_ref, parts_ref, out_ref):
    table = dot(near_ref[...], table_ref[...]).astype(bf16)
    added = dot(table, parts_ref[...]).astype(bf16)
    out_ref[...] = jnp.broadcast_to(added[None], out_ref.shape)


def conv_kernel(attended_ref, top_ref, bottom_ref, left_ref, right_ref, taps_ref, w_hbm, out_ref, ext, w, sems):
    area, width = attended_ref.shape
    cols = top_ref.shape[0]
    rows = area // cols
    out_ch = out_ref.shape[-1]
    s, step = pl.program_id(0), pl.program_id(1)

    fetches = [
        pltpu.make_async_copy(w_hbm.at[:, k, 0:width, :], w.at[k - 1], sems.at[k - 1]) for k in (1, 2)
    ]

    @pl.when((s == 0) & (step == 0))
    def _():
        for fetch in fetches:
            fetch.start()

    for k, fetch in enumerate(fetches):

        @pl.when((s == 0) & (step == k + 1))
        def _():
            fetch.wait()

    def edge(ref, w_ref):
        total = 0.0
        for a in range(3):
            total = total + dot(ref[...], w_ref[a])[a : a + rows]
        return total.reshape(rows, 1, out_ch)

    def middle(w_ref):
        total = dot(ext[0:area], w_ref[0])
        for a in range(1, 3):
            total = total + dot(ext[a * cols : a * cols + area], w_ref[a])
        return total.reshape(rows, cols, out_ch)

    @pl.when(step == 0)
    def _():
        ext[0:cols] = top_ref[...]
        ext[cols : cols + area] = attended_ref[...]
        ext[cols + area :] = bottom_ref[...]
        place = lax.broadcasted_iota(jnp.int32, (rows, cols, out_ch), 1)
        part = jnp.where(place == 0, edge(left_ref, taps_ref), pltpu.roll(middle(taps_ref), 1, 1))
        out_ref[s] = part.reshape(area, out_ch)

    @pl.when(step == 1)
    def _():
        out_ref[s] += middle(w.at[0]).reshape(area, out_ch)

    @pl.when(step == 2)
    def _():
        place = lax.broadcasted_iota(jnp.int32, (rows, cols, out_ch), 1)
        part = jnp.where(place == cols - 1, edge(right_ref, w.at[1]), pltpu.roll(middle(w.at[1]), cols - 1, 1))
        out_ref[s] += part.reshape(area, out_ch)


def split(x):
    high = x.astype(bf16)
    return high, (x - high.astype(f32)).astype(bf16)


def tail_kernel(
    place_ref, table_hbm, row_scale_hbm, col_scale_hbm, parts_hbm, wpool_hbm, wjoin_hbm, by_row_hbm, by_col_hbm,
    spread_hbm, conv, out_hbm,
    table, row_scale, col_scale, parts, by_row, by_col, spread, wpool, wjoin, taps, out, sems,
):
    width, ppm = wpool.shape[1], wpool.shape[2]
    count = len(LEVELS)
    r, c = place_ref[0], place_ref[1]
    small = [
        pltpu.make_async_copy(source, target, sems.at[0, k])
        for k, (source, target) in enumerate((
            (parts_hbm, parts), (table_hbm.at[c], table), (row_scale_hbm.at[r], row_scale),
            (col_scale_hbm.at[c], col_scale), (by_row_hbm.at[r], by_row), (by_col_hbm.at[c], by_col), (spread_hbm, spread),
        ))
    ]
    large = [pltpu.make_async_copy(wpool_hbm.at[k], wpool.at[k], sems.at[1, k]) for k in range(count)]
    for k in range(count):
        lines = slice(width + k * ppm, width + (k + 1) * ppm)
        large.append(pltpu.make_async_copy(wjoin_hbm.at[:, :, lines, :], wjoin.at[k], sems.at[1, count + k]))
    ahead = len(large)
    for copy in small + large[:ahead]:
        copy.start()

    def ready(k):
        large[k].wait()
        if k + ahead < len(large):
            large[k + ahead].start()

    for copy in small:
        copy.wait()

    def along(ref, axis):
        high, low = split(ref[...])
        return dot(high, spread[axis]) + dot(low, spread[axis])

    grid = along(by_row, 0)[:, None, :] * along(by_col, 1)[None, :, :]
    grid_high, grid_low = split(grid.reshape(grid.shape[0] * grid.shape[1], -1))
    scale = row_scale[...] * col_scale[...]
    scale = jnp.broadcast_to(scale, (128, scale.shape[1])).T[:, :1]
    pooled = dot(table[...], parts[...]) * scale
    branches = []
    row = 0
    for index, level in enumerate(LEVELS):
        slots = SLOTS[level]
        high, low = split(pooled[row : row + 2 * slots])
        ready(index)
        both = dot(jnp.concatenate([high, low], axis=0), wpool[index])
        high, low = split(jnp.maximum(both[: 2 * slots] + both[2 * slots :], 0.0))
        branches.append(jnp.concatenate([high, low], axis=0))
        row += 2 * slots
    results = [pltpu.make_async_copy(out.at[s], out_hbm.at[s], sems.at[2, s]) for s in range(2)]

    at = 0
    for index, level in enumerate(LEVELS):
        slots = SLOTS[level]
        ready(count + index)
        for a in range(3):
            for b in range(3):
                tap = dot(branches[index], wjoin[index, a, b])
                tap = tap[: 2 * slots] + tap[2 * slots :]
                start = at + (a * 3 + b) * slots
                for s in range(2):
                    taps[s, start : start + slots, :] = tap[s * slots : (s + 1) * slots]
        at += TAPS * slots
    for s in range(2):
        high, low = split(taps[s])
        total = conv[s] + dot(grid_high, high) + dot(grid_low, high) + dot(grid_high, low)
        out[s] = total.astype(bf16)
        results[s].start()
    for copy in results:
        copy.wait()


def cost(flops, nbytes, transcendentals=0):
    return pl.CostEstimate(flops=int(flops), bytes_accessed=int(nbytes), transcendentals=int(transcendentals))


def params(mib):
    return pltpu.CompilerParams(vmem_limit_bytes=mib * 2**20)


def whole(shape):
    return pl.BlockSpec(shape, lambda *_: (0,) * len(shape))


def in_vmem(x):
    return pltpu.with_memory_space_constraint(x, pltpu.VMEM)


def in_hbm(x):
    return pltpu.with_memory_space_constraint(x, pltpu.HBM)


def shifts(axis):
    count = lax.axis_size(axis)
    forward = [(i, i + 1) for i in range(count - 1)]
    return forward, [(j, i) for i, j in forward]


def layer(tokens, norm_gain, w_query, w_kv, w_out, w_pool, w_join):
    sheets, rows, cols, width = tokens.shape
    inner = w_query.shape[1]
    wide = w_kv.shape[1]
    out_ch = w_join.shape[-1]
    ppm = w_pool.shape[-1]
    area = rows * cols
    row_count, col_count = lax.axis_size("row"), lax.axis_size("col")
    r, c = lax.axis_index("row"), lax.axis_index("col")
    grid_h, grid_w = rows * row_count, cols * col_count
    gain = norm_gain.reshape(1, width)
    tables = pool_tables(rows, row_count, cols, col_count)
    row_masks, col_masks, strip_table, near_table, bin_table, row_scale, col_scale = tables
    by_row, by_col, spread = upsample_tables(rows, row_count, cols, col_count)
    masks = np.concatenate([row_masks, col_masks], axis=-1).reshape(row_count * col_count, UNITS, rows + cols)

    at = jnp.stack([r, c]).astype(jnp.int32)
    row_fwd, row_bwd = shifts("row")
    col_fwd, col_bwd = shifts("col")
    edge = HALO * cols
    flat_above = lax.ppermute(tokens[:, rows - HALO :].reshape(sheets, edge, width), "row", row_fwd)
    flat_below = lax.ppermute(tokens[:, :HALO].reshape(sheets, edge, width), "row", row_bwd)
    above = flat_above.reshape(sheets, HALO, cols, width)
    below = flat_below.reshape(sheets, HALO, cols, width)

    def per_sheet(*dims):
        return pl.BlockSpec((None,) + dims, lambda s, *_: (s,) + (0,) * len(dims))

    near = pl.BlockSpec(memory_space=pltpu.VMEM)
    far = pl.BlockSpec(memory_space=pl.ANY)
    wq_near = in_vmem(w_query)
    blocks = (rows // BLOCK) * (cols // BLOCK)
    keys = (BLOCK + 2 * HALO) ** 2
    stage = [pltpu.VMEM((2, inner // 128, keys, 256), f32), pltpu.VMEM((2, inner // 128, keys, 256), bf16)]
    normed, kv, first_cols, last_cols, flat, gain, wkv_near = pl.pallas_call(
        project_kernel,
        grid=(sheets,),
        in_specs=[far] * 3,
        out_specs=[near] * 7,
        out_shape=[
            pltpu.VMEM((sheets, area, width), bf16), pltpu.VMEM((sheets, rows, cols, wide), f32),
            pltpu.VMEM((sheets, HALO, rows, width), bf16), pltpu.VMEM((sheets, HALO, rows, width), bf16),
            pltpu.VMEM((sheets, area, width), bf16), pltpu.VMEM((1, width), f32), pltpu.VMEM((width, wide), bf16),
        ],
        scratch_shapes=[pltpu.SemaphoreType.DMA((sheets + 2,))],
        compiler_params=params(16),
        cost_estimate=cost(2 * sheets * area * width * wide, 2 * (width * (inner + wide) + 5 * sheets * area * width)),
        name="project",
    )(in_hbm(tokens.reshape(sheets, area, width)), in_hbm(gain), in_hbm(w_kv))
    kv, flat, gain, wkv_near = in_vmem(kv), in_vmem(flat), in_vmem(gain), in_vmem(wkv_near)

    def edges(own, first):
        own = jnp.swapaxes(own, 1, 2)
        return jnp.concatenate([above[:, :, first : first + HALO], own, below[:, :, first : first + HALO]], axis=1)

    west = lax.ppermute(edges(last_cols, cols - HALO), "col", col_fwd)
    east = lax.ppermute(edges(first_cols, 0), "col", col_bwd)

    q, halo, bias, pool, middle = pl.pallas_call(
        lambda *refs: middle_kernel((grid_h, grid_w), *refs),
        grid_spec=pltpu.PrefetchScalarGridSpec(
            num_scalar_prefetch=1,
            grid=(sheets,),
            in_specs=[near] * 7 + [
                pl.BlockSpec((None, UNITS, rows + cols), lambda s, p: (p[0] * col_count + p[1], 0, 0)),
            ],
            out_specs=[near] * 5,
            scratch_shapes=stage,
        ),
        out_shape=[
            pltpu.VMEM((sheets, rows, cols, inner), f32), pltpu.VMEM((sheets, 2 * HALO, cols, wide), f32),
            pltpu.VMEM((rows // BLOCK, cols // BLOCK, keys, 128), f32), pltpu.VMEM((UNITS, area), bf16),
            pltpu.VMEM((sheets, rows, cols - 2 * BLOCK, inner), f32),
        ],
        compiler_params=params(16),
        cost_estimate=cost(2 * sheets * area * width * wide, 8 * sheets * area * width, sheets * blocks * keys * 512),
        name="middle",
    )(
        at, in_vmem(normed), kv, in_vmem(flat_above),
        in_vmem(flat_below), gain, wq_near, wkv_near, masks,
    )

    blank = jnp.zeros((sheets, rows + 2 * HALO, BLOCK - 2 * HALO, width), bf16)
    sides = jnp.concatenate([east, blank, west], axis=2).reshape(sheets, (rows + 2 * HALO) * BLOCK, width)

    def fixed(*dims):
        return whole(dims)

    attended, sums, first_row, last_row, first_col, last_col = pl.pallas_call(
        attend_kernel,
        grid=(sheets,),
        in_specs=[near] * 10 + [fixed(inner, width)],
        out_specs=[
            per_sheet(area, width),
            pl.BlockSpec((row_count, UNITS, width), lambda s: (0, s, 0)),
            per_sheet(cols, width), per_sheet(cols, width), per_sheet(rows, width), per_sheet(rows, width),
        ],
        scratch_shapes=[
            pltpu.VMEM((sheets, rows + 2 * HALO, BLOCK, wide), f32), pltpu.VMEM((2, rows, BLOCK, inner), f32),
        ] + stage,
        out_shape=[
            pltpu.HBM((sheets, area, width), bf16),
            jax.ShapeDtypeStruct((row_count, sheets * UNITS, width), bf16),
            jax.ShapeDtypeStruct((sheets, cols, width), bf16),
            jax.ShapeDtypeStruct((sheets, cols, width), bf16),
            jax.ShapeDtypeStruct((sheets, rows, width), bf16),
            jax.ShapeDtypeStruct((sheets, rows, width), bf16),
        ],
        compiler_params=params(20),
        cost_estimate=cost(2 * sheets * area * inner * width * 4, 2 * sheets * area * width * 4, sheets * blocks * keys * 1024),
        name="attend",
    )(
        in_vmem(q), kv, in_vmem(halo), in_vmem(sides), flat, gain, wkv_near, in_vmem(middle), in_vmem(bias),
        in_vmem(pool), w_out,
    )

    strip_rows = sheets * STRIP_UNITS
    att_above = lax.ppermute(last_row, "row", row_fwd)
    att_below = lax.ppermute(first_row, "row", row_bwd)
    parts = lax.all_to_all(sums, "row", 0, 0, tiled=True).reshape(row_count * sheets * UNITS, width)

    def att_edges(middle, at):
        return jnp.concatenate([att_above[:, at : at + 1], middle, att_below[:, at : at + 1]], axis=1)

    att_west = lax.ppermute(att_edges(last_col, cols - 1), "col", col_fwd)
    att_east = lax.ppermute(att_edges(first_col, 0), "col", col_bwd)
    pad = ((0, 0), (0, 6), (0, 0))
    att_west, att_east = jnp.pad(att_west, pad), jnp.pad(att_east, pad)

    strips = pl.pallas_call(
        combine_kernel,
        grid_spec=pltpu.PrefetchScalarGridSpec(
            num_scalar_prefetch=1,
            grid=(1,),
            in_specs=[
                pl.BlockSpec((None,) + near_table.shape[1:], lambda k, p: (p[0], 0, 0)),
                pl.BlockSpec((None,) + strip_table.shape[1:], lambda k, p: (p[1], 0, 0)),
                fixed(row_count * sheets * UNITS, width),
            ],
            out_specs=fixed(col_count, strip_rows, width),
        ),
        out_shape=jax.ShapeDtypeStruct((col_count, strip_rows, width), bf16),
        compiler_params=params(8),
        name="combine",
    )(at, near_table.astype(bf16), strip_table.astype(bf16), parts)
    strips = lax.all_to_all(strips, "col", 0, 0, tiled=True).reshape(col_count * strip_rows, width)

    conv = pl.pallas_call(
        conv_kernel,
        grid=(sheets, 3),
        in_specs=[
            per_sheet(area, width), per_sheet(cols, width), per_sheet(cols, width),
            per_sheet(rows + 8, width), per_sheet(rows + 8, width),
            pl.BlockSpec((3, None, width, out_ch), lambda *_: (0, 0, 0, 0)), far,
        ],
        out_specs=pl.BlockSpec(memory_space=pltpu.VMEM),
        out_shape=pltpu.VMEM((sheets, area, out_ch), f32),
        scratch_shapes=[
            pltpu.VMEM((area + 2 * cols, width), bf16), pltpu.VMEM((2, 3, width, out_ch), bf16),
            pltpu.SemaphoreType.DMA((2,)),
        ],
        compiler_params=params(20),
        cost_estimate=cost(2 * sheets * area * width * 9 * out_ch, 2 * 9 * width * out_ch + 2 * sheets * area * width),
        name="conv",
    )(in_hbm(attended), att_above, att_below, att_west, att_east, in_hbm(w_join), in_hbm(w_join))
    conv = in_vmem(conv)

    depth = TAPS * sum(SLOTS.values())
    bin_rows = 2 * sum(SLOTS.values())
    out = pl.pallas_call(
        tail_kernel,
        grid_spec=pltpu.PrefetchScalarGridSpec(
            num_scalar_prefetch=1,
            grid=(1,),
            in_specs=[pl.BlockSpec(memory_space=pl.ANY) for _ in range(9)] + [pl.BlockSpec(memory_space=pltpu.VMEM)],
            out_specs=pl.BlockSpec(memory_space=pl.ANY),
            scratch_shapes=[
                pltpu.VMEM(bin_table.shape[1:], bf16),
                pltpu.VMEM((1, bin_rows), f32),
                pltpu.VMEM((1, bin_rows), f32),
                pltpu.VMEM((col_count * strip_rows, width), bf16),
                pltpu.VMEM((rows, 64), f32),
                pltpu.VMEM((cols, 64), f32),
                pltpu.VMEM((2, 64, depth), bf16),
                pltpu.VMEM(w_pool.shape, bf16),
                pltpu.VMEM((len(LEVELS), 3, 3, ppm, out_ch), bf16),
                pltpu.VMEM((sheets, depth, out_ch), f32),
                pltpu.VMEM((sheets, area, out_ch), bf16),
                pltpu.SemaphoreType.DMA((3, 2 * len(LEVELS))),
            ],
        ),
        out_shape=jax.ShapeDtypeStruct((sheets, area, out_ch), bf16),
        compiler_params=params(40),
        cost_estimate=cost(4e9, 2 * (w_pool.size + 9 * 4 * ppm * out_ch)),
        name="tail",
    )(
        at, bin_table.astype(bf16), row_scale, col_scale, strips, in_hbm(w_pool), in_hbm(w_join),
        by_row, by_col, spread.astype(bf16), conv,
    )
    return out.reshape(sheets, rows, cols, out_ch)


def solution(mesh):
    placed = (P(None, "row", "col", None), P(), P(), P(), P(), P(), P())
    return jax.shard_map(layer, mesh=mesh, in_specs=placed, out_specs=P(None, "row", "col", None), check_vma=False)
```

```python
import math

import jax
import jax.numpy as jnp
import numpy as np
from jax import lax
from jax.experimental import pallas as pl
from jax.experimental.pallas import tpu as pltpu
from jax.sharding import PartitionSpec as P

HEAD_DIM = 32
BLOCK = 8
HALO = 2
EPS = 1e-05
LEVELS = (1, 2, 3, 6)
CODED = (6, 3, 2)
UNITS = 8
STRIP_ALL = 24
STRIP_ALL_AT = {6: 0, 3: 12, 2: 18}
STRIP_UNITS = 16
STRIP_AT = {6: 0, 3: 6, 2: 12}
NEAR = {1: 1, 2: 2, 3: 3, 6: 3}
SLOTS = {1: 8, 2: 8, 3: 16, 6: 16}
TAPS = 9
f32 = jnp.float32
bf16 = jnp.bfloat16


def bins_of(level, length, first, count):
    places = first + np.arange(count)
    found = []
    for cell in range(level):
        start = cell * length // level
        end = ((cell + 1) * length + level - 1) // level
        mask = (places >= start) & (places < end)
        if mask.any():
            found.append((cell, mask))
    return found


def lower_bin(level, length, place):
    return max((2 * place + 1) * level - length, 0) // (2 * length)


def first_bin(level, length, first, count):
    start = min(lower_bin(level, length, first - 1), level - NEAR[level])
    assert min(lower_bin(level, length, first + count) + 1, level - 1) < start + NEAR[level]
    return start


def pool_tables(rows, row_strips, cols, col_strips):
    grid_h, grid_w = rows * row_strips, cols * col_strips
    row_masks = np.zeros((row_strips, col_strips, UNITS, rows), np.float32)
    col_masks = np.zeros((row_strips, col_strips, UNITS, cols), np.float32)
    strip = np.zeros((col_strips, 2 * STRIP_ALL, row_strips, 2 * UNITS), np.float32)
    near = np.zeros((row_strips, 2 * STRIP_UNITS, 2 * STRIP_ALL), np.float32)
    slots = 2 * sum(SLOTS.values())
    bins = np.zeros((col_strips, slots, col_strips, 2 * STRIP_UNITS), np.float32)
    row_scale = np.zeros((row_strips, 1, slots), np.float32)
    col_scale = np.zeros((col_strips, 1, slots), np.float32)
    for c in range(col_strips):
        for r in range(row_strips):
            units = []
            for level in CODED:
                for i, row_mask in bins_of(level, grid_h, r * rows, rows):
                    for g, (j, col_mask) in enumerate(bins_of(level, grid_w, c * cols, cols)):
                        key = (row_mask.tobytes(), col_mask.tobytes())
                        if key not in units:
                            units.append(key)
                            at = len(units) - 1
                            row_masks[r, c, at] = row_mask
                            col_masks[r, c, at] = col_mask
                        at = units.index(key)
                        width = 1 if level == 2 else 2
                        for s in range(2):
                            target = s * STRIP_ALL + STRIP_ALL_AT[level] + i * width + g
                            strip[c, target, r, s * UNITS + at] = 1.0
            assert len(units) <= UNITS
    for r in range(row_strips):
        for level in CODED:
            width = 1 if level == 2 else 2
            start = first_bin(level, grid_h, r * rows, rows)
            for k in range(NEAR[level] * width):
                for s in range(2):
                    source = s * STRIP_ALL + STRIP_ALL_AT[level] + start * width + k
                    near[r, s * STRIP_UNITS + STRIP_AT[level] + k, source] = 1.0
    for c in range(col_strips):
        base = 0
        for level in LEVELS:
            source = 2 if level == 1 else level
            width = 1 if source == 2 else 2
            start = first_bin(level, grid_w, c * cols, cols)
            for p in range(col_strips):
                for g, (j, _) in enumerate(bins_of(source, grid_w, p * cols, cols)):
                    j = 0 if level == 1 else j - start
                    if not 0 <= j < NEAR[level]:
                        continue
                    for i in range(NEAR[source]):
                        for s in range(2):
                            cell = 0 if level == 1 else i * NEAR[level] + j
                            at = base + s * SLOTS[level] + cell
                            bins[c, at, p, s * STRIP_UNITS + STRIP_AT[source] + i * width + g] = 1.0
            base += 2 * SLOTS[level]
    for table, strips, size, along_rows in ((row_scale, row_strips, rows, True), (col_scale, col_strips, cols, False)):
        for at in range(strips):
            base = 0
            for level in LEVELS:
                length = size * strips
                start = first_bin(level, length, at * size, size)
                sizes = [mask.sum() for _, mask in bins_of(level, length, 0, length)]
                for i in range(NEAR[level]):
                    for j in range(NEAR[level]):
                        for s in range(2):
                            k = base + s * SLOTS[level] + i * NEAR[level] + j
                            table[at, 0, k] = 1.0 / sizes[start + (i if along_rows else j)]
                base += 2 * SLOTS[level]
    strip = strip.reshape(col_strips, 2 * STRIP_ALL, -1)
    return row_masks, col_masks, strip, near, bins.reshape(col_strips, slots, -1), row_scale, col_scale


def upsample_weights(level, length, first, count):
    places = first + np.arange(count)
    numer = np.maximum((2 * places + 1) * level - length, 0)
    lower = numer // (2 * length)
    frac = (numer - lower * 2 * length).astype(np.float32) / np.float32(2.0 * length)
    upper = np.minimum(lower + 1, level - 1)
    cells = np.arange(level)[None, :]
    weight = (cells == lower[:, None]) * (1.0 - frac)[:, None] + (cells == upper[:, None]) * frac[:, None]
    inside = (places >= 0) & (places < length)
    return (weight * inside[:, None]).astype(np.float32)


def upsample_tables(rows, row_strips, cols, col_strips):
    width = TAPS * sum(SLOTS.values())
    cells = sum(NEAR.values())
    spread = np.zeros((2, 64, width), np.float32)

    def strips_of(size, strips):
        table = np.zeros((strips, size, 64), np.float32)
        length = size * strips
        for strip in range(strips):
            first = 0
            for level in LEVELS:
                start = first_bin(level, length, strip * size, size)
                for a in range(3):
                    w = upsample_weights(level, length, strip * size + a - 1, size)
                    at = a * cells + first
                    table[strip, :, at : at + NEAR[level]] = w[:, start : start + NEAR[level]]
                first += NEAR[level]
        return table

    base, first = 0, 0
    for level in LEVELS:
        for a in range(3):
            for c in range(3):
                for i in range(NEAR[level]):
                    for j in range(NEAR[level]):
                        at = base + (a * 3 + c) * SLOTS[level] + i * NEAR[level] + j
                        spread[0, a * cells + first + i, at] = 1.0
                        spread[1, c * cells + first + j, at] = 1.0
        base += TAPS * SLOTS[level]
        first += NEAR[level]
    return strips_of(rows, row_strips), strips_of(cols, col_strips), spread


def layer_norm(tokens, gain):
    x = tokens.astype(f32)
    center = jnp.mean(x, axis=-1, keepdims=True)
    x = x - center
    spread = jnp.mean(x * x, axis=-1, keepdims=True)
    return (x * lax.rsqrt(spread + EPS) * gain).astype(bf16)


def dot(a, b):
    return jnp.dot(a, b, preferred_element_type=f32)


def project_kernel(
    tokens_hbm, gain_hbm, wkv_hbm, normed_ref, kv_ref, first_ref, last_ref, tokens_ref, gain_ref, wkv_ref, sems,
):
    rows, cols, wide = kv_ref.shape[1:]
    s = pl.program_id(0)
    sheets = tokens_ref.shape[0]
    gain_copy = pltpu.make_async_copy(gain_hbm, gain_ref, sems.at[sheets])
    wkv_copy = pltpu.make_async_copy(wkv_hbm, wkv_ref, sems.at[sheets + 1])
    token_copies = [pltpu.make_async_copy(tokens_hbm.at[k], tokens_ref.at[k], sems.at[k]) for k in range(sheets)]

    @pl.when(s == 0)
    def _():
        gain_copy.start()
        token_copies[0].start()
        wkv_copy.start()
        for copy in token_copies[1:]:
            copy.start()
        gain_copy.wait()

    for k, copy in enumerate(token_copies):

        @pl.when(s == k)
        def _():
            copy.wait()

    by_place = tokens_ref[s].astype(f32).reshape(rows, cols, tokens_ref.shape[-1])
    for k in range(HALO):
        first_ref[s, k] = by_place[:, k].astype(bf16)
        last_ref[s, k] = by_place[:, cols - HALO + k].astype(bf16)
    normed = layer_norm(tokens_ref[s], gain_ref[...])
    normed_ref[s] = normed

    @pl.when(s == 0)
    def _():
        wkv_copy.wait()

    kv_ref[s] = dot(normed_ref[s], wkv_ref[...]).astype(bf16).astype(f32).reshape(rows, cols, wide)


def pool_members(masks_ref, pool, cols):
    masks = masks_ref[...].astype(bf16)
    _, count = masks.shape
    area = pool.shape[1]
    rows = count - cols
    unit = lax.broadcasted_iota(jnp.int32, (count, area), 0)
    token = lax.broadcasted_iota(jnp.int32, (count, area), 1)
    to_row = (unit == token // cols).astype(f32).astype(bf16)
    to_col = (unit - rows == token % cols).astype(f32).astype(bf16)
    pool[...] = (dot(masks, to_row) * dot(masks, to_col)).astype(bf16)


def middle_kernel(
    grid_shape, place_ref, normed_ref, kv_ref, above_ref, below_ref, gain_ref, wq, wkv, masks_ref,
    q_ref, halo_ref, bias, pool, context, scores, weights,
):
    rows, cols, inner = q_ref.shape[1:]
    s = pl.program_id(0)
    q_ref[s] = dot(normed_ref[s], wq[...]).astype(bf16).astype(f32).reshape(rows, cols, inner)

    @pl.when(s == 0)
    def _():
        window_bias(bias, place_ref[0] * rows, place_ref[1] * cols, *grid_shape)
        pool_members(masks_ref, pool, cols)
        edge = jnp.concatenate([above_ref[...], below_ref[...]], axis=1)
        edge = layer_norm(edge.reshape(-1, edge.shape[-1]), gain_ref[...])
        halo_ref[...] = dot(edge, wkv[...]).astype(bf16).astype(f32).reshape(halo_ref.shape)

    def store(at, b, lanes, piece):
        context[s, at : at + BLOCK, (b - 1) * BLOCK : b * BLOCK, lanes] = piece

    middle = range(1, cols // BLOCK - 1)
    attend_blocks(middle, s, q_ref, kv_ref, halo_ref, None, bias, scores, weights, store)


def window_bias(bias, first_row, first_col, grid_h, grid_w):
    span = BLOCK + 2 * HALO
    key = lax.broadcasted_iota(jnp.int32, bias.shape[2:], 0)
    extra = key - span * BLOCK
    lane = extra & 7
    odd = ((lane >= 2) & (lane < 6)).astype(jnp.int32)
    west = (lane >= 6) | ((lane >= 2) & (lane < 4))
    main = key < span * BLOCK
    row = jnp.where(main, key >> 3, 2 * (extra >> 3) + odd) - HALO
    col = jnp.where(main, key & 7, (key & 1) + jnp.where(west, -HALO, BLOCK))
    for a in range(bias.shape[0]):
        at = row + (first_row + a * BLOCK)
        row_ok = (at >= 0) & (at < grid_h)
        for b in range(bias.shape[1]):
            at = col + (first_col + b * BLOCK)
            bias[a, b] = jnp.where(row_ok & (at >= 0) & (at < grid_w), 0.0, -1e30)


def attend_blocks(columns, sheet, q_ref, kv_ref, halo_ref, sides, bias, scores, weights, store):
    rows, cols, inner = q_ref.shape[1:]
    groups = cols // BLOCK
    span = BLOCK + 2 * HALO
    tiles = inner // 128
    count = BLOCK * BLOCK
    heads = 128 // HEAD_DIM
    head_of_row = lax.broadcasted_iota(jnp.int32, (heads, count, 128), 0)
    head_of_lane = lax.broadcasted_iota(jnp.int32, (heads, count, 128), 2) // HEAD_DIM
    own = (head_of_row == head_of_lane).astype(f32).astype(bf16).reshape(heads * count, 128)
    lane = lax.broadcasted_iota(jnp.int32, (count, 128), 1)
    place = lax.broadcasted_iota(jnp.int32, (span // 2, BLOCK, 128), 1)
    factor = math.log2(math.e) / math.sqrt(HEAD_DIM)

    def rows_of(at, g, lanes):
        places = slice(g * BLOCK, (g + 1) * BLOCK)
        parts = [kv_ref[sheet, max(at - HALO, 0) : min(at + BLOCK + HALO, rows), places, lanes]]
        if at == 0:
            parts = [halo_ref[sheet, 0:HALO, places, lanes]] + parts
        if at + BLOCK == rows:
            parts = parts + [halo_ref[sheet, HALO:, places, lanes]]
        return jnp.concatenate(parts, axis=0)

    def keys_of(at, b, lanes):
        main = rows_of(at, b, lanes).reshape(span * BLOCK, 128)

        def beside(g):
            if g < 0 or g >= groups:
                found = sides[sheet, at : at + span, :, lanes]
            else:
                found = rows_of(at, g, lanes)
            return found.reshape(span // 2, 2, BLOCK, 128)

        west, east = beside(b - 1), beside(b + 1)
        even = jnp.where(place >= 6, west[:, 0], east[:, 0])
        odd = pltpu.roll(jnp.where(place >= 6, west[:, 1], east[:, 1]), 4, 1)
        extra = jnp.where((place >= 6) | (place < 2), even, odd).reshape(span * 4, 128)
        return jnp.concatenate([main, extra], axis=0).astype(bf16)

    def score(at, b, slot):
        low = bias[at // BLOCK, b]
        for t in range(tiles):
            lanes = slice(t * 128, (t + 1) * 128)
            q = q_ref[sheet, at : at + BLOCK, b * BLOCK : (b + 1) * BLOCK, lanes].reshape(count, 128).astype(bf16)
            q = jnp.concatenate([q] * heads, axis=0) * own
            found = lax.dot_general(keys_of(at, b, lanes), q, (((1,), (1,)), ((), ())), preferred_element_type=f32)
            scores[slot, t] = found + jnp.concatenate([low] * (heads * count // 128), axis=1)

    def soften(slot):
        for t in range(tiles):
            for h in range(heads * count // 128):
                lanes = slice(h * 128, (h + 1) * 128)
                found = scores[slot, t, :, lanes]
                top = jnp.max(found, axis=0, keepdims=True)
                expon = jnp.exp2((found - top) * factor)
                weights[slot, t, :, lanes] = (expon * (1.0 / jnp.sum(expon, axis=0, keepdims=True))).astype(bf16)

    def mix(at, b, slot):
        for t in range(tiles):
            lanes = slice(t * 128, (t + 1) * 128)
            values = keys_of(at, b, slice(inner + t * 128, inner + (t + 1) * 128))
            mixed = lax.dot_general(weights[slot, t], values, (((0,), (0,)), ((), ())), preferred_element_type=f32)
            mixed = mixed.reshape(heads, count, 128)
            piece = mixed[0]
            for k in range(1, heads):
                piece = jnp.where(lane >= k * HEAD_DIM, mixed[k], piece)
            store(at, b, lanes, piece.reshape(BLOCK, BLOCK, 128))

    blocks = [(at, b) for at in range(0, rows, BLOCK) for b in columns]
    score(*blocks[0], 0)
    for k, block in enumerate(blocks):
        if k + 1 < len(blocks):
            score(*blocks[k + 1], (k + 1) % 2)
        soften(k % 2)
        mix(*block, k % 2)


def attend_kernel(
    q_ref, kv_ref, halo_ref, sides_ref, tokens_ref, gain_ref, wkv_ref, middle_ref, bias, pool, wout_ref,
    attended_ref, sums_ref, first_row_ref, last_row_ref, first_col_ref, last_col_ref, sides, outer, scores, weights,
):
    rows, cols, inner = q_ref.shape[1:]
    sheet = pl.program_id(0)

    @pl.when(sheet == 0)
    def _():
        ends = layer_norm(sides_ref[...].reshape(-1, sides_ref.shape[-1]), gain_ref[...])
        ends = dot(ends, wkv_ref[...]).astype(bf16).astype(f32)
        sides[...] = ends.reshape(sides.shape)

    last = cols // BLOCK - 1

    def store(at, b, lanes, piece):
        outer[b // last, at : at + BLOCK, :, lanes] = piece

    attend_blocks((0, last), sheet, q_ref, kv_ref, halo_ref, sides, bias, scores, weights, store)
    mixed = jnp.concatenate([outer[0], middle_ref[sheet], outer[1]], axis=1)
    mixed = mixed.reshape(rows * cols, inner).astype(bf16)
    attended = (tokens_ref[sheet].astype(f32) + dot(mixed, wout_ref[...])).astype(bf16)
    attended_ref[...] = attended
    first_row_ref[...] = attended[:cols]
    last_row_ref[...] = attended[(rows - 1) * cols :]
    by_place = attended.astype(f32).reshape(rows, cols, attended.shape[-1])
    first_col_ref[...] = by_place[:, 0].astype(bf16)
    last_col_ref[...] = by_place[:, cols - 1].astype(bf16)
    sums = dot(pool[...], attended).astype(bf16)
    sums_ref[...] = jnp.broadcast_to(sums[None], sums_ref.shape)


def combine_kernel(place_ref, near_ref, table_ref, parts_ref, out_ref):
    table = dot(near_ref[...], table_ref[...]).astype(bf16)
    added = dot(table, parts_ref[...]).astype(bf16)
    out_ref[...] = jnp.broadcast_to(added[None], out_ref.shape)


def conv_kernel(attended_ref, top_ref, bottom_ref, left_ref, right_ref, taps_ref, w_hbm, out_ref, ext, w, sems):
    area, width = attended_ref.shape
    cols = top_ref.shape[0]
    rows = area // cols
    out_ch = out_ref.shape[-1]
    s, step = pl.program_id(0), pl.program_id(1)

    fetches = [
        pltpu.make_async_copy(w_hbm.at[:, k, 0:width, :], w.at[k - 1], sems.at[k - 1]) for k in (1, 2)
    ]

    @pl.when((s == 0) & (step == 0))
    def _():
        for fetch in fetches:
            fetch.start()

    for k, fetch in enumerate(fetches):

        @pl.when((s == 0) & (step == k + 1))
        def _():
            fetch.wait()

    def middle(w_ref):
        total = dot(ext[0:area], w_ref[0])
        for a in range(1, 3):
            total = total + dot(ext[a * cols : a * cols + area], w_ref[a])
        return total.reshape(rows, cols, out_ch)

    def with_edge(w_ref, side_ref):
        total, edge = 0.0, 0.0
        for a in range(3):
            lines = jnp.concatenate([ext[a * cols : a * cols + area], side_ref[...]], axis=0)
            part = dot(lines, w_ref[a])
            total = total + part[:area]
            edge = edge + part[area + a : area + a + rows]
        return total.reshape(rows, cols, out_ch), edge.reshape(rows, 1, out_ch)

    @pl.when(step == 0)
    def _():
        ext[0:cols] = top_ref[...]
        ext[cols : cols + area] = attended_ref[...]
        ext[cols + area :] = bottom_ref[...]
        place = lax.broadcasted_iota(jnp.int32, (rows, cols, out_ch), 1)
        total, edge = with_edge(taps_ref, left_ref)
        part = jnp.where(place == 0, edge, pltpu.roll(total, 1, 1))
        out_ref[s] = part.reshape(area, out_ch)

    @pl.when(step == 1)
    def _():
        out_ref[s] += middle(w.at[0]).reshape(area, out_ch)

    @pl.when(step == 2)
    def _():
        place = lax.broadcasted_iota(jnp.int32, (rows, cols, out_ch), 1)
        total, edge = with_edge(w.at[1], right_ref)
        part = jnp.where(place == cols - 1, edge, pltpu.roll(total, cols - 1, 1))
        out_ref[s] += part.reshape(area, out_ch)


def split(x):
    high = x.astype(bf16)
    return high, (x - high.astype(f32)).astype(bf16)


def tail_kernel(
    place_ref, table_hbm, row_scale_hbm, col_scale_hbm, parts_hbm, wpool_hbm, wjoin_hbm, by_row_hbm, by_col_hbm,
    spread_hbm, conv, out_hbm,
    table, row_scale, col_scale, parts, by_row, by_col, spread, wpool, wjoin, taps, out, sems,
):
    width, ppm = wpool.shape[1], wpool.shape[2]
    count = len(LEVELS)
    r, c = place_ref[0], place_ref[1]
    small = [
        pltpu.make_async_copy(source, target, sems.at[0, k])
        for k, (source, target) in enumerate((
            (parts_hbm, parts), (table_hbm.at[c], table), (row_scale_hbm.at[r], row_scale),
            (col_scale_hbm.at[c], col_scale), (by_row_hbm.at[r], by_row), (by_col_hbm.at[c], by_col), (spread_hbm, spread),
        ))
    ]
    large = [pltpu.make_async_copy(wpool_hbm.at[k], wpool.at[k], sems.at[1, k]) for k in range(count)]
    for k in range(count):
        lines = slice(width + k * ppm, width + (k + 1) * ppm)
        large.append(pltpu.make_async_copy(wjoin_hbm.at[:, :, lines, :], wjoin.at[k], sems.at[1, count + k]))
    ahead = len(large)
    for copy in small + large[:ahead]:
        copy.start()

    def ready(k):
        large[k].wait()
        if k + ahead < len(large):
            large[k + ahead].start()

    for copy in small:
        copy.wait()

    def along(ref, axis):
        high, low = split(ref[...])
        return dot(high, spread[axis]) + dot(low, spread[axis])

    grid = along(by_row, 0)[:, None, :] * along(by_col, 1)[None, :, :]
    grid_high, grid_low = split(grid.reshape(grid.shape[0] * grid.shape[1], -1))
    scale = row_scale[...] * col_scale[...]
    scale = jnp.broadcast_to(scale, (128, scale.shape[1])).T[:, :1]
    pooled = dot(table[...], parts[...]) * scale
    branches = []
    row = 0
    for index, level in enumerate(LEVELS):
        slots = SLOTS[level]
        high, low = split(pooled[row : row + 2 * slots])
        ready(index)
        both = dot(jnp.concatenate([high, low], axis=0), wpool[index])
        high, low = split(jnp.maximum(both[: 2 * slots] + both[2 * slots :], 0.0))
        branches.append(jnp.concatenate([high, low], axis=0))
        row += 2 * slots
    results = [pltpu.make_async_copy(out.at[s], out_hbm.at[s], sems.at[2, s]) for s in range(2)]

    at = 0
    for index, level in enumerate(LEVELS):
        slots = SLOTS[level]
        ready(count + index)
        for a in range(3):
            for b in range(3):
                tap = dot(branches[index], wjoin[index, a, b])
                tap = tap[: 2 * slots] + tap[2 * slots :]
                start = at + (a * 3 + b) * slots
                for s in range(2):
                    taps[s, start : start + slots, :] = tap[s * slots : (s + 1) * slots]
        at += TAPS * slots
    for s in range(2):
        high, low = split(taps[s])
        total = conv[s] + dot(grid_high, high) + dot(grid_low, high) + dot(grid_high, low)
        out[s] = total.astype(bf16)
        results[s].start()
    for copy in results:
        copy.wait()


def cost(flops, nbytes, transcendentals=0):
    return pl.CostEstimate(flops=int(flops), bytes_accessed=int(nbytes), transcendentals=int(transcendentals))


def params(mib):
    return pltpu.CompilerParams(vmem_limit_bytes=mib * 2**20)


def whole(shape):
    return pl.BlockSpec(shape, lambda *_: (0,) * len(shape))


def in_vmem(x):
    return pltpu.with_memory_space_constraint(x, pltpu.VMEM)


def in_hbm(x):
    return pltpu.with_memory_space_constraint(x, pltpu.HBM)


def shifts(axis):
    count = lax.axis_size(axis)
    forward = [(i, i + 1) for i in range(count - 1)]
    return forward, [(j, i) for i, j in forward]


def layer(tokens, norm_gain, w_query, w_kv, w_out, w_pool, w_join):
    sheets, rows, cols, width = tokens.shape
    inner = w_query.shape[1]
    wide = w_kv.shape[1]
    out_ch = w_join.shape[-1]
    ppm = w_pool.shape[-1]
    area = rows * cols
    row_count, col_count = lax.axis_size("row"), lax.axis_size("col")
    r, c = lax.axis_index("row"), lax.axis_index("col")
    grid_h, grid_w = rows * row_count, cols * col_count
    gain = norm_gain.reshape(1, width)
    tables = pool_tables(rows, row_count, cols, col_count)
    row_masks, col_masks, strip_table, near_table, bin_table, row_scale, col_scale = tables
    by_row, by_col, spread = upsample_tables(rows, row_count, cols, col_count)
    masks = np.concatenate([row_masks, col_masks], axis=-1).reshape(row_count * col_count, UNITS, rows + cols)

    at = jnp.stack([r, c]).astype(jnp.int32)
    row_fwd, row_bwd = shifts("row")
    col_fwd, col_bwd = shifts("col")
    edge = HALO * cols
    flat_above = lax.ppermute(tokens[:, rows - HALO :].reshape(sheets, edge, width), "row", row_fwd)
    flat_below = lax.ppermute(tokens[:, :HALO].reshape(sheets, edge, width), "row", row_bwd)
    above = flat_above.reshape(sheets, HALO, cols, width)
    below = flat_below.reshape(sheets, HALO, cols, width)

    def per_sheet(*dims):
        return pl.BlockSpec((None,) + dims, lambda s, *_: (s,) + (0,) * len(dims))

    near = pl.BlockSpec(memory_space=pltpu.VMEM)
    far = pl.BlockSpec(memory_space=pl.ANY)
    wq_near = in_vmem(w_query)
    blocks = (rows // BLOCK) * (cols // BLOCK)
    keys = (BLOCK + 2 * HALO) ** 2
    stage = [pltpu.VMEM((2, inner // 128, keys, 256), f32), pltpu.VMEM((2, inner // 128, keys, 256), bf16)]
    normed, kv, first_cols, last_cols, flat, gain, wkv_near = pl.pallas_call(
        project_kernel,
        grid=(sheets,),
        in_specs=[far] * 3,
        out_specs=[near] * 7,
        out_shape=[
            pltpu.VMEM((sheets, area, width), bf16), pltpu.VMEM((sheets, rows, cols, wide), f32),
            pltpu.VMEM((sheets, HALO, rows, width), bf16), pltpu.VMEM((sheets, HALO, rows, width), bf16),
            pltpu.VMEM((sheets, area, width), bf16), pltpu.VMEM((1, width), f32), pltpu.VMEM((width, wide), bf16),
        ],
        scratch_shapes=[pltpu.SemaphoreType.DMA((sheets + 2,))],
        compiler_params=params(16),
        cost_estimate=cost(2 * sheets * area * width * wide, 2 * (width * (inner + wide) + 5 * sheets * area * width)),
        name="project",
    )(in_hbm(tokens.reshape(sheets, area, width)), in_hbm(gain), in_hbm(w_kv))
    kv, flat, gain, wkv_near = in_vmem(kv), in_vmem(flat), in_vmem(gain), in_vmem(wkv_near)

    def edges(own, first):
        own = jnp.swapaxes(own, 1, 2)
        return jnp.concatenate([above[:, :, first : first + HALO], own, below[:, :, first : first + HALO]], axis=1)

    west = lax.ppermute(edges(last_cols, cols - HALO), "col", col_fwd)
    east = lax.ppermute(edges(first_cols, 0), "col", col_bwd)

    q, halo, bias, pool, middle = pl.pallas_call(
        lambda *refs: middle_kernel((grid_h, grid_w), *refs),
        grid_spec=pltpu.PrefetchScalarGridSpec(
            num_scalar_prefetch=1,
            grid=(sheets,),
            in_specs=[near] * 7 + [
                pl.BlockSpec((None, UNITS, rows + cols), lambda s, p: (p[0] * col_count + p[1], 0, 0)),
            ],
            out_specs=[near] * 5,
            scratch_shapes=stage,
        ),
        out_shape=[
            pltpu.VMEM((sheets, rows, cols, inner), f32), pltpu.VMEM((sheets, 2 * HALO, cols, wide), f32),
            pltpu.VMEM((rows // BLOCK, cols // BLOCK, keys, 128), f32), pltpu.VMEM((UNITS, area), bf16),
            pltpu.VMEM((sheets, rows, cols - 2 * BLOCK, inner), f32),
        ],
        compiler_params=params(16),
        cost_estimate=cost(2 * sheets * area * width * wide, 8 * sheets * area * width, sheets * blocks * keys * 512),
        name="middle",
    )(
        at, in_vmem(normed), kv, in_vmem(flat_above),
        in_vmem(flat_below), gain, wq_near, wkv_near, masks,
    )

    blank = jnp.zeros((sheets, rows + 2 * HALO, BLOCK - 2 * HALO, width), bf16)
    sides = jnp.concatenate([east, blank, west], axis=2).reshape(sheets, (rows + 2 * HALO) * BLOCK, width)

    def fixed(*dims):
        return whole(dims)

    attended, sums, first_row, last_row, first_col, last_col = pl.pallas_call(
        attend_kernel,
        grid=(sheets,),
        in_specs=[near] * 10 + [fixed(inner, width)],
        out_specs=[
            per_sheet(area, width),
            pl.BlockSpec((row_count, UNITS, width), lambda s: (0, s, 0)),
            per_sheet(cols, width), per_sheet(cols, width), per_sheet(rows, width), per_sheet(rows, width),
        ],
        scratch_shapes=[
            pltpu.VMEM((sheets, rows + 2 * HALO, BLOCK, wide), f32), pltpu.VMEM((2, rows, BLOCK, inner), f32),
        ] + stage,
        out_shape=[
            pltpu.HBM((sheets, area, width), bf16),
            jax.ShapeDtypeStruct((row_count, sheets * UNITS, width), bf16),
            jax.ShapeDtypeStruct((sheets, cols, width), bf16),
            jax.ShapeDtypeStruct((sheets, cols, width), bf16),
            jax.ShapeDtypeStruct((sheets, rows, width), bf16),
            jax.ShapeDtypeStruct((sheets, rows, width), bf16),
        ],
        compiler_params=params(20),
        cost_estimate=cost(2 * sheets * area * inner * width * 4, 2 * sheets * area * width * 4, sheets * blocks * keys * 1024),
        name="attend",
    )(
        in_vmem(q), kv, in_vmem(halo), in_vmem(sides), flat, gain, wkv_near, in_vmem(middle), in_vmem(bias),
        in_vmem(pool), w_out,
    )

    strip_rows = sheets * STRIP_UNITS
    att_above = lax.ppermute(last_row, "row", row_fwd)
    att_below = lax.ppermute(first_row, "row", row_bwd)
    parts = lax.all_to_all(sums, "row", 0, 0, tiled=True).reshape(row_count * sheets * UNITS, width)

    def att_edges(middle, at):
        return jnp.concatenate([att_above[:, at : at + 1], middle, att_below[:, at : at + 1]], axis=1)

    att_west = lax.ppermute(att_edges(last_col, cols - 1), "col", col_fwd)
    att_east = lax.ppermute(att_edges(first_col, 0), "col", col_bwd)
    pad = ((0, 0), (0, 6), (0, 0))
    att_west, att_east = jnp.pad(att_west, pad), jnp.pad(att_east, pad)

    strips = pl.pallas_call(
        combine_kernel,
        grid_spec=pltpu.PrefetchScalarGridSpec(
            num_scalar_prefetch=1,
            grid=(1,),
            in_specs=[
                pl.BlockSpec((None,) + near_table.shape[1:], lambda k, p: (p[0], 0, 0)),
                pl.BlockSpec((None,) + strip_table.shape[1:], lambda k, p: (p[1], 0, 0)),
                fixed(row_count * sheets * UNITS, width),
            ],
            out_specs=fixed(col_count, strip_rows, width),
        ),
        out_shape=jax.ShapeDtypeStruct((col_count, strip_rows, width), bf16),
        compiler_params=params(8),
        name="combine",
    )(at, near_table.astype(bf16), strip_table.astype(bf16), parts)
    strips = lax.all_to_all(strips, "col", 0, 0, tiled=True).reshape(col_count * strip_rows, width)

    conv = pl.pallas_call(
        conv_kernel,
        grid=(sheets, 3),
        in_specs=[
            per_sheet(area, width), per_sheet(cols, width), per_sheet(cols, width),
            per_sheet(rows + 8, width), per_sheet(rows + 8, width),
            pl.BlockSpec((3, None, width, out_ch), lambda *_: (0, 0, 0, 0)), far,
        ],
        out_specs=pl.BlockSpec(memory_space=pltpu.VMEM),
        out_shape=pltpu.VMEM((sheets, area, out_ch), f32),
        scratch_shapes=[
            pltpu.VMEM((area + 2 * cols, width), bf16), pltpu.VMEM((2, 3, width, out_ch), bf16),
            pltpu.SemaphoreType.DMA((2,)),
        ],
        compiler_params=params(20),
        cost_estimate=cost(2 * sheets * area * width * 9 * out_ch, 2 * 9 * width * out_ch + 2 * sheets * area * width),
        name="conv",
    )(in_hbm(attended), att_above, att_below, att_west, att_east, in_hbm(w_join), in_hbm(w_join))
    conv = in_vmem(conv)

    depth = TAPS * sum(SLOTS.values())
    bin_rows = 2 * sum(SLOTS.values())
    out = pl.pallas_call(
        tail_kernel,
        grid_spec=pltpu.PrefetchScalarGridSpec(
            num_scalar_prefetch=1,
            grid=(1,),
            in_specs=[pl.BlockSpec(memory_space=pl.ANY) for _ in range(9)] + [pl.BlockSpec(memory_space=pltpu.VMEM)],
            out_specs=pl.BlockSpec(memory_space=pl.ANY),
            scratch_shapes=[
                pltpu.VMEM(bin_table.shape[1:], bf16),
                pltpu.VMEM((1, bin_rows), f32),
                pltpu.VMEM((1, bin_rows), f32),
                pltpu.VMEM((col_count * strip_rows, width), bf16),
                pltpu.VMEM((rows, 64), f32),
                pltpu.VMEM((cols, 64), f32),
                pltpu.VMEM((2, 64, depth), bf16),
                pltpu.VMEM(w_pool.shape, bf16),
                pltpu.VMEM((len(LEVELS), 3, 3, ppm, out_ch), bf16),
                pltpu.VMEM((sheets, depth, out_ch), f32),
                pltpu.VMEM((sheets, area, out_ch), bf16),
                pltpu.SemaphoreType.DMA((3, 2 * len(LEVELS))),
            ],
        ),
        out_shape=jax.ShapeDtypeStruct((sheets, area, out_ch), bf16),
        compiler_params=params(40),
        cost_estimate=cost(4e9, 2 * (w_pool.size + 9 * 4 * ppm * out_ch)),
        name="tail",
    )(
        at, bin_table.astype(bf16), row_scale, col_scale, strips, in_hbm(w_pool), in_hbm(w_join),
        by_row, by_col, spread.astype(bf16), conv,
    )
    return out.reshape(sheets, rows, cols, out_ch)


def solution(mesh):
    placed = (P(None, "row", "col", None), P(), P(), P(), P(), P(), P())
    return jax.shard_map(layer, mesh=mesh, in_specs=placed, out_specs=P(None, "row", "col", None), check_vma=False)
```
